32 devices in a mesh: clip: 8 (over z, x), freq: 4 (over y, core).
Axes of the slice: x: 2, y: 2, z: 4, core: 2. Of those that a mesh axis runs over, the one named last changes fastest.
Arguments:
- tokens: bfloat16 [24, 1192, 768], P('clip', 'freq'), may hold values from -6 to 6
- kept_counts: int32 [24, 4], P('clip', 'freq'), may hold values from 37 to 298, as said below
- attn_gain: bfloat16 [768], replicated, may hold values from 0.099609375 to 1.8984375
- attn_shift: bfloat16 [768], replicated, may hold values from -3 to 3
- qkv_weight: bfloat16 [768, 2304], replicated, may hold values from -0.3125 to 0.3125
- query_bias: bfloat16 [768], replicated, may hold values from -3 to 3
- value_bias: bfloat16 [768], replicated, may hold values from -3 to 3
- proj_weight: bfloat16 [768, 768], replicated, may hold values from -1.75 to 1.75
- proj_bias: bfloat16 [768], replicated, may hold values from -3 to 3
- mlp_gain: bfloat16 [768], replicated, may hold values from 0.099609375 to 1.8984375
- mlp_shift: bfloat16 [768], replicated, may hold values from -3 to 3
- fc1_weight: bfloat16 [768, 3072], replicated, may hold values from -0.21875 to 0.21875
- fc1_bias: bfloat16 [3072], replicated, may hold values from -3 to 3
- fc2_weight: bfloat16 [3072, 768], replicated, may hold values from -0.15625 to 0.15625
- fc2_bias: bfloat16 [768], replicated, may hold values from -3 to 3
- cotangent: bfloat16 [24, 1192, 768], P('clip', 'freq'), may hold values from -6 to 6
Outputs:
- layer_out: bfloat16 [24, 1192, 768], P('clip', 'freq')
- grad_tokens: float32 [24, 1192, 768], P('clip', 'freq')
- grad_attn_gain: float32 [768], replicated
- grad_attn_shift: float32 [768], replicated
- grad_qkv_weight: float32 [768, 2304], P('clip')
- grad_query_bias: float32 [768], replicated
- grad_value_bias: float32 [768], replicated
- grad_proj_weight: float32 [768, 768], P('clip')
- grad_proj_bias: float32 [768], replicated
- grad_mlp_gain: float32 [768], replicated
- grad_mlp_shift: float32 [768], replicated
- grad_fc1_weight: float32 [768, 3072], P('clip')
- grad_fc1_bias: float32 [3072], replicated
- grad_fc2_weight: float32 [3072, 768], P('clip')
- grad_fc2_bias: float32 [768], replicated
The draws below stay inside these ranges and needn't reach their ends.
Inputs may be any that keep to these rules, and one draw needn't show every extreme that they name: `kept_counts`: each clip keeps all 298 slots in every group, or between 37 and 149 in each group; clip 0 keeps all; kept tokens fill the first slots of a group.
All inputs are finite; a program needn't handle non-finite values.
Results may differ from the reference program's by a relative error of at most 0.015.
The reference program's roundings to bfloat16 on the way count: a program that leaves them out, or rounds other values in their place, can miss the bound.
Values may be sent and summed in bfloat16 or wider, within the bound.
A program may use at most 320 MiB of HBM per device.

```python
import jax
import jax.numpy as jnp
from jax import lax

D = 768
HEADS = 12
DH = 64
FF = 3072
CAP = 298
GROUPS = 4
SLOTS = 1192
CLIPS = 24


def draw_kept_counts(key, part):
    key_full = jax.random.fold_in(key, 11)
    key_part = jax.random.fold_in(key, 23)
    full_clip = jax.random.randint(key_full, (CLIPS, 1), 0, 2)
    full_clip = jnp.where(jnp.arange(CLIPS)[:, None] == 0, 1, full_clip)
    partial_rows = jax.random.randint(key_part, (CLIPS, GROUPS), CAP // 8, CAP // 2 + 1)
    return jnp.where(full_clip == 1, CAP, partial_rows).astype(jnp.int32)


def steps_of(rng, dims, split, low, top_value):
    level, own = 1.0, jax.random.fold_in(rng, 6)
    for axis_at, blocks in split:
        draws = jnp.exp(jax.random.uniform(jax.random.fold_in(own, axis_at), (blocks,), jnp.float32, low / len(split), top_value / len(split)))
        level = level * jnp.repeat(draws, dims[axis_at] // blocks).reshape([-1 if axis == axis_at else 1 for axis in range(len(dims))])
    return level


def bell_draw(rng, shape, deviation, bound, split=(), kind=jnp.bfloat16):
    entries = jax.random.normal(rng, shape, jnp.float32) * deviation
    if len(split) > 0:
        entries = steps_of(rng, shape, split, -0.22, 0.18) * entries
    return jnp.clip(entries, min=-bound, max=bound).astype(kind)


def setup_inputs(seed: int = 0) -> dict:
    keys = jax.random.split(jax.random.key(seed), 17)
    return {
        "tokens": bell_draw(keys[0], (CLIPS, SLOTS, D), 1.0, 6.0, ((0, 8), (1, 4))),
        "kept_counts": draw_kept_counts(jax.random.fold_in(keys[16], 71), 0),
        "attn_gain": jnp.clip(1.0 + 0.18 * jax.random.normal(keys[2], (D,), jnp.float32), 0.099609375, 1.8984375).astype(jnp.bfloat16),
        "attn_shift": bell_draw(keys[3], (D,), 0.3, 3.0),
        "qkv_weight": bell_draw(keys[4], (D, 3 * D), (D // 2) ** -0.5, 0.3125),
        "query_bias": bell_draw(keys[5], (D,), 0.3, 3.0),
        "value_bias": bell_draw(keys[6], (D,), 0.3, 3.0),
        "proj_weight": bell_draw(keys[7], (D, D), (D // 64) ** -0.5, 1.75),
        "proj_bias": bell_draw(keys[8], (D,), 0.3, 3.0),
        "mlp_gain": jnp.clip(1.0 + 0.18 * jax.random.normal(keys[9], (D,), jnp.float32), 0.099609375, 1.8984375).astype(jnp.bfloat16),
        "mlp_shift": bell_draw(keys[10], (D,), 0.3, 3.0),
        "fc1_weight": bell_draw(keys[11], (D, FF), D ** -0.5, 0.21875),
        "fc1_bias": bell_draw(keys[12], (FF,), 0.5, 3.0),
        "fc2_weight": bell_draw(keys[13], (FF, D), (FF // 2) ** -0.5, 0.15625),
        "fc2_bias": bell_draw(keys[14], (D,), 0.3, 3.0),
        "cotangent": bell_draw(keys[15], (CLIPS, SLOTS, D), 1.0, 6.0, ((0, 8), (1, 4))),
    }


@jax.custom_vjp
def low(v):
    return lax.optimization_barrier(v.astype(jnp.bfloat16)).astype(jnp.float32)

@jax.custom_vjp
def low_back(v):
    return v

def low_keep(v):
    return (low(v), None)

def low_pass(kept, grad):
    return (grad,)

def back_keep(v):
    return (v, None)

def back_low(kept, grad):
    return (low(grad),)
low.defvjp(low_keep, low_pass)
low_back.defvjp(back_keep, back_low)
high_precision = lax.Precision.HIGHEST
norm_eps = 1e-06
masked_value = -1000000000.0

def layer_norm(inputs, norm_gain, norm_shift):
    center = inputs - lax.optimization_barrier(jnp.mean(inputs, axis=-1, keepdims=True))
    spread = lax.optimization_barrier(jnp.mean(center * center, axis=-1, keepdims=True))
    return center * lax.rsqrt(spread + norm_eps) * norm_gain + norm_shift

def matmul(left, right):
    return jnp.dot(left, right, precision=high_precision)

def forward(tokens, params, live_slots):
    attn_gain, attn_shift, qkv_weight, query_bias, value_bias, proj_weight, proj_bias, mlp_gain, mlp_shift, fc1_weight, fc1_bias, fc2_weight, fc2_bias = params
    model_width = tokens.shape[-1]
    slot_count = tokens.shape[0]
    normed = low(layer_norm(tokens, attn_gain, attn_shift))
    packed = matmul(normed, qkv_weight)
    query_rows = low(low_back(packed[:, :model_width] + query_bias))
    key_rows = low(low_back(packed[:, model_width:2 * model_width]))
    value_rows = low(low_back(packed[:, 2 * model_width:] + value_bias))
    query_heads = query_rows.reshape(slot_count, HEADS, DH)
    key_heads = key_rows.reshape(slot_count, HEADS, DH)
    value_heads = value_rows.reshape(slot_count, HEADS, DH)
    scores = jnp.einsum('qhd,khd->hqk', query_heads, key_heads, precision=high_precision) * DH ** (-0.5)
    scores = low_back(scores)
    scores = jnp.where(live_slots[None, None, :] > 0.5, scores, masked_value)
    prob_rows = jax.nn.softmax(scores, axis=-1)
    attn_mixed = jnp.einsum('hqk,khd->qhd', low(prob_rows), value_heads, precision=high_precision)
    attn_mixed = low(low_back(attn_mixed.reshape(slot_count, model_width)))
    branch = low_back(matmul(attn_mixed, proj_weight) + proj_bias)
    middle = tokens + branch
    normed_two = low(layer_norm(middle, mlp_gain, mlp_shift))
    hidden = low_back(matmul(normed_two, fc1_weight) + fc1_bias)
    active = low(jax.nn.gelu(hidden, approximate=False))
    out_branch = low_back(matmul(active, fc2_weight) + fc2_bias)
    return (middle + out_branch) * live_slots[:, None]

def reference(tokens, kept_counts, attn_gain, attn_shift, qkv_weight, query_bias, value_bias, proj_weight, proj_bias, mlp_gain, mlp_shift, fc1_weight, fc1_bias, fc2_weight, fc2_bias, cotangent):
    params = tuple((member.astype(jnp.float32) for member in (attn_gain, attn_shift, qkv_weight, query_bias, value_bias, proj_weight, proj_bias, mlp_gain, mlp_shift, fc1_weight, fc1_bias, fc2_weight, fc2_bias)))
    slot_ids = jnp.arange(SLOTS, dtype=jnp.int32)
    slot_group = slot_ids // CAP
    offset = slot_ids % CAP

    def one_clip(totals, inputs):
        clip_tokens, clip_counts, clip_cot = inputs
        live_slots = (offset < jnp.take(clip_counts, slot_group)).astype(jnp.float32)

        def run_clip(clip_inputs, clip_params):
            return forward(clip_inputs, clip_params, live_slots)
        outputs, pullback = jax.vjp(run_clip, clip_tokens.astype(jnp.float32), params)
        grad_inputs, grad_params = pullback(clip_cot.astype(jnp.float32))
        totals = tuple((running + adding for running, adding in zip(totals, grad_params)))
        return (totals, (outputs.astype(jnp.bfloat16), grad_inputs))
    zeros = tuple((jnp.zeros_like(member) for member in params))
    totals, (layer_out, grad_tokens) = lax.scan(one_clip, zeros, (tokens, kept_counts, cotangent))
    return (layer_out, grad_tokens, totals[0], totals[1], totals[2], totals[3], totals[4], totals[5], totals[6], totals[7], totals[8], totals[9], totals[10], totals[11], totals[12])
```

```python
import functools
import math

import jax
import jax.numpy as jnp
from jax import lax
from jax.experimental import pallas as pl
from jax.experimental.pallas import tpu as pltpu
from jax.sharding import PartitionSpec as P

HEADS = 12
DH = 64
EPS = 1e-06
MASKED = -1000000000.0
VMEM_BYTES = 60 * 1024 * 1024

f32 = jnp.float32
bf16 = jnp.bfloat16
NN = (((1,), (0,)), ((), ()))
NT = (((1,), (1,)), ((), ()))
TN = (((0,), (0,)), ((), ()))


def dot(left, right, dims=NN):
    return lax.dot_general(left, right, dims, preferred_element_type=f32)


def center_scale(rows):
    center = rows - jnp.mean(rows, axis=-1, keepdims=True)
    inverse = lax.rsqrt(jnp.mean(center * center, axis=-1, keepdims=True) + EPS)
    return center * inverse, inverse


def norm_back(unit, inverse, gain, grad):
    scaled = grad * gain
    return inverse * (
        scaled
        - jnp.mean(scaled, axis=-1, keepdims=True)
        - unit * jnp.mean(scaled * unit, axis=-1, keepdims=True)
    )


def column_sums(rows):
    return jnp.sum(rows, axis=0, keepdims=True)


def own_lanes(shape, head):
    lane = lax.broadcasted_iota(jnp.int32, shape, len(shape) - 1)
    return lane < DH if head == 0 else lane >= DH


def only(rows, head):
    return jnp.where(own_lanes(rows.shape, head), rows, jnp.zeros_like(rows))


def full(shape):
    return pl.BlockSpec(shape, lambda *ids: (0,) * len(shape))


def params(**more):
    return pltpu.CompilerParams(vmem_limit_bytes=VMEM_BYTES, **more)


def forward_kernel(
    rows,
    own_ref, vert_ref, core_ref, diag_ref, mask_ref,
    qkv_ref, qb_ref, vb_ref, gain_ref, shift_ref, proj_ref, pb_ref, gain2_ref, shift2_ref,
    q_ref, k_ref, v_ref, normed_ref, mixed_ref, lse_ref, middle_ref, normed2_ref,
):
    pair = pl.program_id(0)
    width = own_ref.shape[-1]

    @pl.when(pair == 0)
    def project():
        for slot, source in enumerate((own_ref, vert_ref, core_ref, diag_ref)):
            unit, _ = center_scale(source[0].astype(f32))
            normed = (unit * gain_ref[...] + shift_ref[...]).astype(bf16)
            if slot == 0:
                normed_ref[0] = normed
                query = (dot(normed, qkv_ref[:, :width]) + qb_ref[...]).astype(bf16)
                q_ref[0] = query * jnp.asarray(DH ** -0.5, bf16)
            both = dot(normed, qkv_ref[:, width:])
            k_ref[0, slot * rows : (slot + 1) * rows] = both[:, :width].astype(bf16)
            v_ref[0, slot * rows : (slot + 1) * rows] = (both[:, width:] + vb_ref[...]).astype(bf16)

    lanes = pl.ds(pl.multiple_of(pair * 2 * DH, 2 * DH), 2 * DH)
    query = q_ref[0, :, lanes]
    keys = k_ref[0, :, lanes]
    values = v_ref[0, :, lanes]
    live = mask_ref[0] > 0.5
    outs, lses = [], []
    for head in range(2):
        scores = jnp.where(live, dot(only(query, head), keys, NT), MASKED)
        top = jnp.max(scores, axis=1, keepdims=True)
        exps = jnp.exp(scores - top)
        total = jnp.sum(exps, axis=1, keepdims=True)
        outs.append(dot(exps.astype(bf16), values) / total)
        lses.append(top + jnp.log(total))
    first = own_lanes(outs[0].shape, 0)
    mixed_ref[0, :, lanes] = jnp.where(first, outs[0], outs[1]).astype(bf16)
    lse_ref[0, :, lanes] = jnp.where(first, lses[0], lses[1])

    @pl.when(pair == pl.num_programs(0) - 1)
    def finish():
        middle = own_ref[0].astype(f32) + (dot(mixed_ref[0], proj_ref[...]) + pb_ref[...])
        middle_ref[0] = middle
        unit, _ = center_scale(middle)
        normed2_ref[0] = (unit * gain2_ref[...] + shift2_ref[...]).astype(bf16)


def forward_clip(own, vert, core, diag, mask, qkv_weight, vectors, proj_weight):
    _, rows, width = own.shape
    keys = 4 * rows
    pairs = HEADS // 2
    query_bias, value_bias, gain, shift, proj_bias, gain2, shift2 = vectors
    row = full((1, width))
    tok = full((1, rows, width))
    key = full((1, keys, width))
    flops = 2 * (4 * rows * width * 2 * width + rows * width * 2 * width + 2 * rows * keys * width)
    return pl.pallas_call(
        functools.partial(forward_kernel, rows),
        grid=(pairs,),
        in_specs=[tok] * 4
        + [full((1, 1, keys)), full(qkv_weight.shape), row, row, row, row]
        + [full(proj_weight.shape), row, row, row],
        out_specs=[tok, key, key, tok, tok, tok, tok, tok],
        out_shape=[
            jax.ShapeDtypeStruct((1, rows, width), bf16),
            jax.ShapeDtypeStruct((1, keys, width), bf16),
            jax.ShapeDtypeStruct((1, keys, width), bf16),
            jax.ShapeDtypeStruct((1, rows, width), bf16),
            jax.ShapeDtypeStruct((1, rows, width), bf16),
            jax.ShapeDtypeStruct((1, rows, width), f32),
            jax.ShapeDtypeStruct((1, rows, width), f32),
            jax.ShapeDtypeStruct((1, rows, width), bf16),
        ],
        compiler_params=params(),
        cost_estimate=pl.CostEstimate(
            flops=flops * 2, bytes_accessed=14_000_000, transcendentals=rows * keys * HEADS
        ),
        name="forward_clip",
    )(own, vert, core, diag, mask, qkv_weight, query_bias, value_bias, gain, shift,
      proj_weight, proj_bias, gain2, shift2)


def mlp_kernel(
    counts,
    n2_ref, middle_ref, cot_ref, live_ref, mixed_ref, fc1_ref, b1_ref, fc2_ref, b2_ref,
    gain_ref, shift_ref, proj_ref,
    out_ref, dfc1_ref, dfc2_ref, dproj_ref, db1_ref, small_ref, gmid_ref, gmixed_ref,
    n2t_ref, grad_ref, out_acc, dn_acc, hidden_ref, dact_ref, active_ref, dhid_ref,
):
    clips, slots, rows, tile = counts
    step = pl.program_id(0)
    width = n2_ref.shape[-1]
    chunk = fc1_ref.shape[-1]
    total = clips * rows

    @pl.when(step == 0)
    def start():
        n2t_ref[...] = n2_ref[...].T
        grad_ref[...] = (cot_ref[...].astype(f32) * live_ref[...]).astype(bf16)
        out_acc[...] = jnp.zeros_like(out_acc)
        dn_acc[...] = jnp.zeros_like(dn_acc)

    hidden_ref[...] = dot(n2_ref[...], fc1_ref[...])
    dact_ref[...] = dot(grad_ref[...], fc2_ref[...], NT)
    bias = b1_ref[...]

    def gelu_tile(index, sums):
        at = pl.ds(pl.multiple_of(index * tile, tile), tile)
        hidden = hidden_ref[at, :] + bias
        cdf = 0.5 * (1.0 + lax.erf(hidden * (0.5 ** 0.5)))
        active_ref[at, :] = (hidden * cdf).astype(bf16)
        slope = cdf + hidden * (jnp.exp(-0.5 * hidden * hidden) * (1.0 / math.sqrt(2.0 * math.pi)))
        dhid = (dact_ref[at, :] * slope).astype(bf16)
        dhid_ref[at, :] = dhid
        return sums + dhid.astype(f32)

    sums = lax.fori_loop(0, total // tile, gelu_tile, jnp.zeros((tile, chunk), f32))
    db1_ref[...] = column_sums(sums)
    active = active_ref[...]
    dhid = dhid_ref[...]
    out_acc[...] += dot(active, fc2_ref[...])
    dn_acc[...] += dot(dhid, fc1_ref[...], NT)
    dfc1_ref[0] = dot(n2t_ref[...], dhid).astype(bf16)
    dfc2 = dot(active, grad_ref[...], TN).astype(bf16)
    half = width // 2
    dfc2_ref[0] = dfc2[:, :half]
    dfc2_ref[1] = dfc2[:, half:]

    @pl.when(step == pl.num_programs(0) - 1)
    def finish():
        gain = gain_ref[...]
        sum_gain = jnp.zeros((1, width), f32)
        sum_shift = jnp.zeros((1, width), f32)
        sum_grad = jnp.zeros((1, width), f32)
        sum_proj = jnp.zeros((1, width), f32)
        for clip in range(clips):
            at = slice(clip * rows, (clip + 1) * rows)
            middle = middle_ref[at]
            live = live_ref[at]
            layer = live * (middle + (out_acc[at] + b2_ref[...]))
            out_ref[clip] = layer[:slots].astype(bf16)
            unit, inverse = center_scale(middle)
            grad = dn_acc[at]
            out_grad = cot_ref[at].astype(f32) * live
            gmid = out_grad + norm_back(unit, inverse, gain, grad)
            gmid_ref[at] = gmid
            low = gmid.astype(bf16)
            dhid_ref[at, :width] = low
            gmixed_ref[at] = dot(low, proj_ref[...], NT).astype(bf16)
            sum_gain += column_sums(grad * unit)
            sum_shift += column_sums(grad)
            sum_grad += column_sums(grad_ref[at].astype(f32))
            sum_proj += column_sums(low.astype(f32))
        dproj = dot(mixed_ref[...], dhid_ref[:, :width], TN).astype(bf16)
        dproj_ref[0] = dproj[:, :half]
        dproj_ref[1] = dproj[:, half:]
        small_ref[0:1] = sum_gain
        small_ref[1:2] = sum_shift
        small_ref[2:3] = sum_grad
        small_ref[3:4] = sum_proj


def mlp(n2, middle, cot, live, mixed, fc1, b1, fc2, b2, gain, shift, proj, shape):
    clips, slots, rows = shape
    total, width = n2.shape
    hidden = fc1.shape[1]
    chunk = 768
    steps = hidden // chunk
    half = steps // 2
    tile = 16
    row = full((1, width))
    one = pl.Buffered(buffer_count=1)
    big = pl.BlockSpec((total, width), lambda j: (0, 0), pipeline_mode=one)
    return pl.pallas_call(
        functools.partial(mlp_kernel, (clips, slots, rows, tile)),
        grid=(steps,),
        in_specs=[
            big, big, big,
            pl.BlockSpec((total, 1), lambda j: (0, 0), pipeline_mode=one),
            big,
            pl.BlockSpec((width, chunk), lambda j: (0, j)),
            pl.BlockSpec((1, chunk), lambda j: (0, j)),
            pl.BlockSpec((chunk, width), lambda j: (j, 0)),
            row, row, row,
            pl.BlockSpec((width, width), lambda j: (0, 0), pipeline_mode=one),
        ],
        out_specs=[
            full((clips, slots, width)),
            pl.BlockSpec((1, width, chunk), lambda j: (j // half, 0, j % half)),
            pl.BlockSpec((2, chunk, width // 2), lambda j: (0, j, 0)),
            full((2, width, width // 2)),
            pl.BlockSpec((1, chunk), lambda j: (0, j)),
            full((8, width)),
            full((total, width)),
            full((total, width)),
        ],
        out_shape=[
            jax.ShapeDtypeStruct((clips, slots, width), bf16),
            jax.ShapeDtypeStruct((2, width, hidden // 2), bf16),
            jax.ShapeDtypeStruct((2, hidden, width // 2), bf16),
            jax.ShapeDtypeStruct((2, width, width // 2), bf16),
            jax.ShapeDtypeStruct((1, hidden), f32),
            jax.ShapeDtypeStruct((8, width), f32),
            jax.ShapeDtypeStruct((total, width), f32),
            jax.ShapeDtypeStruct((total, width), bf16),
        ],
        scratch_shapes=[
            pltpu.VMEM((width, total), bf16),
            pltpu.VMEM((total, width), bf16),
            pltpu.VMEM((total, width), f32),
            pltpu.VMEM((total, width), f32),
            pltpu.VMEM((total, chunk), f32),
            pltpu.VMEM((total, chunk), f32),
            pltpu.VMEM((total, chunk), bf16),
            pltpu.VMEM((total, chunk), bf16),
        ],
        compiler_params=params(),
        cost_estimate=pl.CostEstimate(
            flops=12 * total * width * hidden, bytes_accessed=40_000_000, transcendentals=2 * total * hidden
        ),
        name="mlp",
    )(n2, middle, cot, live, mixed, fc1, b1, fc2, b2, gain, shift, proj)


def attend_back_kernel(q_ref, k_ref, v_ref, mask_ref, mixed_ref, lse_ref, grad_ref,
                       dq_ref, dkeep_ref, dsend_ref):
    query = q_ref[0]
    keys = k_ref[0]
    values = v_ref[0]
    grad = grad_ref[0]
    live = mask_ref[0] > 0.5
    product = grad.astype(f32) * mixed_ref[0].astype(f32)
    dqs, dk, dv = [], None, None
    for head in range(2):
        own_query = only(query, head)
        own_grad = only(grad, head)
        scores = jnp.where(live, dot(own_query, keys, NT), MASKED)
        probs = jnp.exp(scores - lse_ref[0, :, head * DH : head * DH + 1])
        delta = jnp.sum(only(product, head), axis=1, keepdims=True)
        dscores = (probs * (dot(own_grad, values, NT) - delta)).astype(bf16)
        dqs.append(dot(dscores, keys))
        more_k = dot(dscores, own_query, TN)
        more_v = dot(probs.astype(bf16), own_grad, TN)
        dk = more_k if dk is None else dk + more_k
        dv = more_v if dv is None else dv + more_v
    first = own_lanes(dqs[0].shape, 0)
    dq_ref[0] = (jnp.where(first, dqs[0], dqs[1]) * DH ** -0.5).astype(bf16)
    half = dk.shape[0] // 2
    dkeep_ref[0, 0] = dk[:half].astype(bf16)
    dkeep_ref[1, 0] = dv[:half].astype(bf16)
    dsend_ref[0, 0] = dk[half:].astype(bf16)
    dsend_ref[1, 0] = dv[half:].astype(bf16)


def attend_back(q, k, v, mask, mixed, lse, grad, first_pair, pairs):
    clips, rows, _ = q.shape
    keys = k.shape[1]
    lanes = 2 * DH
    tok = pl.BlockSpec((1, rows, lanes), lambda c, p: (c, 0, first_pair + p))
    key = pl.BlockSpec((1, keys, lanes), lambda c, p: (c, 0, first_pair + p))
    part = pl.BlockSpec((2, 1, keys // 2, lanes), lambda c, p: (0, c, 0, p))
    return pl.pallas_call(
        attend_back_kernel,
        grid=(clips, pairs),
        in_specs=[tok, key, key, pl.BlockSpec((1, 1, keys), lambda c, p: (c, 0, 0)), tok, tok, tok],
        out_specs=[pl.BlockSpec((1, rows, lanes), lambda c, p: (c, 0, p)), part, part],
        out_shape=[
            jax.ShapeDtypeStruct((clips, rows, pairs * lanes), bf16),
            jax.ShapeDtypeStruct((2, clips, keys // 2, pairs * lanes), bf16),
            jax.ShapeDtypeStruct((2, clips, keys // 2, pairs * lanes), bf16),
        ],
        compiler_params=params(),
        cost_estimate=pl.CostEstimate(
            flops=4 * 10 * clips * rows * keys * pairs * lanes,
            bytes_accessed=clips * pairs * lanes * (keys * 10 + rows * 12),
            transcendentals=clips * rows * keys * 2 * pairs,
        ),
        name="attend_back",
    )(q, k, v, mask, mixed, lse, grad)


def weight_kernel(normed_ref, dq_ref, dk0_ref, dk1_ref, dk2_ref, out_ref, dkv_ref, sums_ref):
    part = pl.program_id(0)
    @pl.when(part == 0)
    def query():
        grad = dq_ref[...]
        out_ref[0] = dot(normed_ref[...], grad, TN).astype(bf16)
        sums_ref[0] = column_sums(grad.astype(f32))
        dkv_ref[0] = jnp.zeros_like(dkv_ref[0])

    @pl.when(part > 0)
    def other():
        grad = (dk0_ref[0].astype(f32) + dk1_ref[0].astype(f32) + dk2_ref[0].astype(f32)).astype(bf16)
        dkv_ref[0] = grad
        out_ref[0] = dot(normed_ref[...], grad, TN).astype(bf16)
        sums_ref[0] = column_sums(grad.astype(f32))


def weight_grads(normed, dq, parts):
    total, width = normed.shape
    lanes = dq.shape[1]
    before = lambda j: (jnp.maximum(j - 1, 0), 0, 0)
    part = pl.BlockSpec((1, total, lanes), before)
    return pl.pallas_call(
        weight_kernel,
        grid=(3,),
        in_specs=[full((total, width)), full((total, lanes)), part, part, part],
        out_specs=[
            pl.BlockSpec((1, width, lanes), lambda j: (j, 0, 0)),
            part,
            pl.BlockSpec((1, 1, lanes), lambda j: (j, 0, 0)),
        ],
        out_shape=[
            jax.ShapeDtypeStruct((3, width, lanes), bf16),
            jax.ShapeDtypeStruct((2, total, lanes), bf16),
            jax.ShapeDtypeStruct((3, 1, lanes), f32),
        ],
        compiler_params=params(),
        cost_estimate=pl.CostEstimate(
            flops=6 * total * width * lanes, bytes_accessed=8_000_000, transcendentals=0
        ),
        name="weight_grads",
    )(normed, dq, *parts)


def input_kernel(counts, groups, *refs):
    clips, slots, rows = counts
    dqs = refs[:groups]
    dkvs = refs[groups : 2 * groups]
    qkv_ref, tok_ref, gmid_ref, gain_ref, shift_ref, out_ref, small_ref = refs[2 * groups :]
    clip = pl.program_id(0)
    width = tok_ref.shape[-1]
    lanes = width // groups
    grad = None
    for group in range(groups):
        for part in range(3):
            rows_grad = dqs[group][0] if part == 0 else dkvs[group][part - 1]
            at = part * width + group * lanes
            more = dot(rows_grad, qkv_ref[:, at : at + lanes], NT)
            grad = more if grad is None else grad + more
    unit, inverse = center_scale(tok_ref[0].astype(f32))
    result = gmid_ref[0] + norm_back(unit, inverse, gain_ref[...], grad)
    out_ref[0] = result[:slots]

    @pl.when(clip == 0)
    def start():
        small_ref[...] = jnp.zeros_like(small_ref)

    small_ref[0:1] += column_sums(grad * unit)
    small_ref[1:2] += column_sums(grad)


def input_grads(dqs, dkvs, qkv_weight, tokens, gmid, gain, shift, slots):
    clips, rows, width = tokens.shape
    groups = len(dqs)
    lanes = width // groups
    tok = pl.BlockSpec((1, rows, width), lambda c: (c, 0, 0))
    return pl.pallas_call(
        functools.partial(input_kernel, (clips, slots, rows), groups),
        grid=(clips,),
        in_specs=[pl.BlockSpec((1, rows, lanes), lambda c: (c, 0, 0))] * groups
        + [pl.BlockSpec((2, rows, lanes), lambda c: (0, c, 0))] * groups
        + [full(qkv_weight.shape), tok, tok, full((1, width)), full((1, width))],
        out_specs=[pl.BlockSpec((1, slots, width), lambda c: (c, 0, 0)), full((8, width))],
        out_shape=[
            jax.ShapeDtypeStruct((clips, slots, width), f32),
            jax.ShapeDtypeStruct((8, width), f32),
        ],
        compiler_params=params(),
        cost_estimate=pl.CostEstimate(
            flops=6 * clips * rows * width * width, bytes_accessed=16_000_000, transcendentals=0
        ),
        name="input_grads",
    )(*dqs, *dkvs, qkv_weight, tokens, gmid, gain, shift)


def swap_bit(array, axis, size, bit):
    return lax.ppermute(array, axis, [(i, i ^ (1 << bit)) for i in range(size)])


def add_low(left, right):
    return (left.astype(f32) + right.astype(f32)).astype(bf16)


def pick(array, index, dim):
    return lax.dynamic_index_in_dim(array, index, dim, keepdims=False)


def bit_of(axis, bit):
    return (lax.axis_index(axis) >> bit) & 1


def scatter_sum(split, clip_size, order):
    core = bit_of("freq", 0)
    vert = bit_of("freq", 1)
    bits = clip_size.bit_length() - 1
    lanes = split.shape[-1]
    value = add_low(pick(split, core, 0), swap_bit(pick(split, 1 - core, 0), "freq", 4, 0))
    rows = value.shape[0] // (2 * clip_size)
    value = value.reshape((2,) * bits + (2, rows, lanes))
    left = list(range(bits))[::-1]
    for bit in order:
        at = left.index(bit)
        mine = bit_of("clip", bit)
        value = add_low(
            pick(value, mine, at), swap_bit(pick(value, 1 - mine, at), "clip", clip_size, bit)
        )
        left.remove(bit)
    return add_low(pick(value, vert, 0), swap_bit(pick(value, 1 - vert, 0), "freq", 4, 1))


def gather_low(part):
    core = bit_of("freq", 0)
    vert = bit_of("freq", 1)
    other = swap_bit(part, "freq", 4, 1)
    tall = jnp.where(vert == 0, jnp.concatenate([part, other]), jnp.concatenate([other, part]))
    side = swap_bit(tall, "freq", 4, 0)
    return jnp.where(
        core == 0,
        jnp.concatenate([tall, side], axis=1),
        jnp.concatenate([side, tall], axis=1),
    ).astype(f32)


def total_sum(array, clip_size):
    for bit in range(2):
        array = array + swap_bit(array, "freq", 4, bit)
    for bit in range(clip_size.bit_length() - 1):
        array = array + swap_bit(array, "clip", clip_size, bit)
    return array


def on_device(
    clip_size, tokens, kept_counts, attn_gain, attn_shift, qkv_weight, query_bias, value_bias,
    proj_weight, proj_bias, mlp_gain, mlp_shift, fc1_weight, fc1_bias, fc2_weight, fc2_bias, cotangent,
):
    clips, slots, width = tokens.shape
    rows = -(-slots // 16) * 16
    total = clips * rows
    bits = clip_size.bit_length() - 1
    forward_order = list(range(bits))
    second_order = forward_order[1:2] + forward_order[:1] + forward_order[2:]
    pad = ((0, 0), (0, rows - slots), (0, 0))
    tok = jnp.pad(tokens, pad)
    vec = lambda v: v.astype(f32)[None, :]

    slot_ids = jnp.arange(rows, dtype=jnp.int32)
    counts = kept_counts
    counts_vert = swap_bit(counts, "freq", 4, 1)
    counts_core = swap_bit(counts, "freq", 4, 0)
    counts_diag = swap_bit(counts_vert, "freq", 4, 0)
    live_keys = [
        (slot_ids[None, :] < c).astype(f32) for c in (counts, counts_vert, counts_core, counts_diag)
    ]
    mask = jnp.concatenate(live_keys, axis=1)[:, None, :]
    live = live_keys[0].reshape(total, 1)

    vectors = [vec(v) for v in (query_bias, value_bias, attn_gain, attn_shift, proj_bias, mlp_gain, mlp_shift)]
    saved = []
    for clip in range(clips):
        own = tok[clip : clip + 1]
        vert = swap_bit(own, "freq", 4, 1)
        core = swap_bit(own, "freq", 4, 0)
        diag = swap_bit(vert, "freq", 4, 0)
        saved.append(
            forward_clip(own, vert, core, diag, mask[clip : clip + 1], qkv_weight, vectors, proj_weight)
        )
    q, k, v, normed, mixed, lse, middle, normed2 = [
        jnp.concatenate([entry[i] for entry in saved]) for i in range(8)
    ]
    flat = lambda a: a.reshape(total, width)
    cot = jnp.pad(cotangent, pad)
    layer_out, dfc1, dfc2, dproj, db1, small2, gmid, gmixed = mlp(
        flat(normed2), flat(middle), flat(cot), live, flat(mixed), fc1_weight, vec(fc1_bias),
        fc2_weight, vec(fc2_bias), vectors[5], vectors[6], proj_weight, (clips, slots, rows),
    )
    early = total_sum(jnp.concatenate([small2[:4].reshape(-1), db1.reshape(-1)])[None, :], clip_size)[0]
    sum_fc1 = gather_low(scatter_sum(dfc1, clip_size, forward_order))
    sum_fc2 = gather_low(scatter_sum(dfc2, clip_size, second_order))
    sum_proj = gather_low(scatter_sum(dproj, clip_size, forward_order))

    groups = 3
    pairs = HEADS // 2 // groups
    lanes = pairs * 2 * DH
    gmixed = gmixed.reshape(clips, rows, width)
    dqs, dkvs, sums, sharded = [], [], [], []
    for group in range(groups):
        dq, keep, send = attend_back(q, k, v, mask, mixed, lse, gmixed, group * pairs, pairs)
        got = swap_bit(send, "freq", 4, 0)
        across = swap_bit(add_low(keep[:, :, rows:], got[:, :, rows:]), "freq", 4, 1)
        parts = [a.reshape(2, total, lanes) for a in (keep[:, :, :rows], got[:, :, :rows], across)]
        dw, dkv, colsum = weight_grads(flat(normed), dq.reshape(total, lanes), parts)
        half = lanes // 2
        split = jnp.stack(
            [
                jnp.concatenate([dw[i, :, s * half : (s + 1) * half] for i in range(3)], axis=1)
                for s in range(2)
            ]
        )
        order = forward_order if group % 2 == 0 else second_order
        summed = gather_low(scatter_sum(split, clip_size, order))
        sharded.append(summed.reshape(summed.shape[0], 2, 3, half))
        dqs.append(dq)
        dkvs.append(dkv)
        sums.append(colsum)
    grad_tokens, small1 = input_grads(
        dqs, dkvs, qkv_weight, tok, gmid.reshape(clips, rows, width), vectors[2], vectors[3], slots
    )
    qkv = jnp.stack(sharded, axis=1)
    sum_qkv = qkv.transpose(0, 3, 1, 2, 4).reshape(qkv.shape[0], 3 * width)
    bias = jnp.concatenate(sums, axis=2)
    late = total_sum(
        jnp.concatenate([small1[0:1], small1[1:2], bias[0], bias[2]], axis=1), clip_size
    )[0]
    cut = lambda a, i: a[i * width : (i + 1) * width]
    return (
        layer_out, grad_tokens, cut(late, 0), cut(late, 1), sum_qkv, cut(late, 2), cut(late, 3),
        sum_proj, cut(early, 3), cut(early, 0), cut(early, 1), sum_fc1, early[4 * width :],
        sum_fc2, cut(early, 2),
    )


def solution(mesh):
    rows = P("clip", "freq", None)
    shard = P("clip", None)
    return jax.shard_map(
        functools.partial(on_device, mesh.shape["clip"]),
        mesh=mesh,
        in_specs=(rows, P("clip", "freq")) + (P(),) * 13 + (rows,),
        out_specs=(rows, rows, P(), P(), shard, P(), P(), shard, P(), P(), P(), shard, P(), shard, P()),
        check_vma=False,
    )
```

```python
import functools
import math

import jax
import jax.numpy as jnp
from jax import lax
from jax.experimental import pallas as pl
from jax.experimental.pallas import tpu as pltpu
from jax.sharding import PartitionSpec as P

HEADS = 12
DH = 64
EPS = 1e-06
MASKED = -1000000000.0
VMEM_BYTES = 60 * 1024 * 1024

f32 = jnp.float32
bf16 = jnp.bfloat16
NN = (((1,), (0,)), ((), ()))
NT = (((1,), (1,)), ((), ()))
TN = (((0,), (0,)), ((), ()))


def dot(left, right, dims=NN):
    return lax.dot_general(left, right, dims, preferred_element_type=f32)


def center_scale(rows):
    center = rows - jnp.mean(rows, axis=-1, keepdims=True)
    inverse = lax.rsqrt(jnp.mean(center * center, axis=-1, keepdims=True) + EPS)
    return center * inverse, inverse


def norm_back(unit, inverse, gain, grad):
    scaled = grad * gain
    return inverse * (
        scaled
        - jnp.mean(scaled, axis=-1, keepdims=True)
        - unit * jnp.mean(scaled * unit, axis=-1, keepdims=True)
    )


def column_sums(rows):
    return jnp.sum(rows, axis=0, keepdims=True)


def own_lanes(shape, head):
    lane = lax.broadcasted_iota(jnp.int32, shape, len(shape) - 1)
    return lane < DH if head == 0 else lane >= DH


def only(rows, head):
    return jnp.where(own_lanes(rows.shape, head), rows, jnp.zeros_like(rows))


def full(shape):
    return pl.BlockSpec(shape, lambda *ids: (0,) * len(shape))


def params(**more):
    return pltpu.CompilerParams(vmem_limit_bytes=VMEM_BYTES, **more)


def partner(kind):
    index = lax.axis_index("freq")
    if kind == "vert":
        return {"freq": (index + 2) % 4}
    return {"freq": index + 1 - 2 * (index % 2)}


def forward_kernel(
    counts,
    tok_ref, qkv_ref, qb_ref, vb_ref, gain_ref, shift_ref, proj_ref, pb_ref, gain2_ref, shift2_ref,
    q_ref, k_ref, v_ref, normed_ref, mixed_ref, lse_ref, middle_ref, normed2_ref, mask_ref,
    held, send_sem, recv_sem,
):
    clips, slots, rows = counts
    clip = pl.program_id(0)
    pair = pl.program_id(1)
    width = tok_ref.shape[-1]

    def copy(kind, index):
        at = {"vert": 0, "core": 1, "diag": 2}[kind]
        return pltpu.make_async_remote_copy(
            src_ref=held.at[index, 0] if kind == "diag" else tok_ref.at[index],
            dst_ref=held.at[index, at],
            send_sem=send_sem.at[index, at],
            recv_sem=recv_sem.at[index, at],
            device_id=partner(kind),
            device_id_type=pl.DeviceIdType.MESH,
        )

    def project(slot, source):
        unit, _ = center_scale(source.astype(f32))
        normed = (unit * gain_ref[...] + shift_ref[...]).astype(bf16)
        if slot == 0:
            normed_ref[0] = normed
            query = (dot(normed, qkv_ref[:, :width]) + qb_ref[...]).astype(bf16)
            q_ref[0] = query * jnp.asarray(DH ** -0.5, bf16)
        both = dot(normed, qkv_ref[:, width:])
        k_ref[0, slot * rows : (slot + 1) * rows] = both[:, :width].astype(bf16)
        v_ref[0, slot * rows : (slot + 1) * rows] = (both[:, width:] + vb_ref[...]).astype(bf16)
        first = (slots // 16) * 16
        kept = source[first:].astype(f32)[slots - first : slots - first + 1, 0:1] + slots // 2
        lane = lax.broadcasted_iota(jnp.int32, (1, rows), 1).astype(f32)
        return (lane < kept).astype(f32)

    @pl.when((clip == 0) & (pair == 0))
    def enter():
        barrier = pltpu.get_barrier_semaphore()
        for kind in ("vert", "core"):
            pl.semaphore_signal(
                barrier, inc=1, device_id=partner(kind), device_id_type=pl.DeviceIdType.MESH
            )
        pl.semaphore_wait(barrier, 2)
        copy("vert", 0).start()
        for index in range(clips):
            copy("core", index).start()

    def pass_on(index):
        copy("vert", index).wait_recv()
        copy("diag", index).start()
        copy("vert", index).wait_send()

        @pl.when(index + 1 < clips)
        def more():
            copy("vert", index + 1).start()

    @pl.when(pair == 0)
    def project_all():
        live_own = project(0, tok_ref[clip])
        copy("core", clip).wait_recv()
        live_core = project(2, held[clip, 1])

        @pl.when(clip == 0)
        def first_pass():
            pass_on(clip)

        live_vert = project(1, held[clip, 0])
        copy("diag", clip).wait_recv()
        live_diag = project(3, held[clip, 2])
        mask_ref[0] = jnp.concatenate([live_own, live_vert, live_core, live_diag], axis=1)

    @pl.when((pair == 3) & (clip + 1 < clips))
    def next_pass():
        pass_on(clip + 1)

    lanes = pl.ds(pl.multiple_of(pair * 2 * DH, 2 * DH), 2 * DH)
    query = q_ref[0, :, lanes]
    keys = k_ref[0, :, lanes]
    values = v_ref[0, :, lanes]
    live = mask_ref[0] > 0.5
    outs, lses = [], []
    for head in range(2):
        scores = jnp.where(live, dot(only(query, head), keys, NT), MASKED)
        top = jnp.max(scores, axis=1, keepdims=True)
        exps = jnp.exp(scores - top)
        total = jnp.sum(exps, axis=1, keepdims=True)
        outs.append(dot(exps.astype(bf16), values) / total)
        lses.append(top + jnp.log(total))
    first = own_lanes(outs[0].shape, 0)
    mixed_ref[0, :, lanes] = jnp.where(first, outs[0], outs[1]).astype(bf16)
    lse_ref[0, :, lanes] = jnp.where(first, lses[0], lses[1])

    @pl.when(pair == pl.num_programs(1) - 1)
    def finish():
        middle = tok_ref[clip].astype(f32) + (dot(mixed_ref[0], proj_ref[...]) + pb_ref[...])
        middle_ref[0] = middle
        unit, _ = center_scale(middle)
        normed2_ref[0] = (unit * gain2_ref[...] + shift2_ref[...]).astype(bf16)
        copy("core", clip).wait_send()
        copy("diag", clip).wait_send()


def forward(tok, slots, qkv_weight, vectors, proj_weight):
    clips, rows, width = tok.shape
    keys = 4 * rows
    pairs = HEADS // 2
    query_bias, value_bias, gain, shift, proj_bias, gain2, shift2 = vectors
    one = pl.Buffered(buffer_count=1)
    row = full((1, width))
    block = lambda n: pl.BlockSpec((1, n, width), lambda c, p: (c, 0, 0))
    flops = 2 * clips * (10 * rows * width * width + 2 * rows * keys * width)
    weight = lambda w: pl.BlockSpec(w.shape, lambda c, p: (0, 0), pipeline_mode=one)
    return pl.pallas_call(
        functools.partial(forward_kernel, (clips, slots, rows)),
        grid=(clips, pairs),
        in_specs=[
            pl.BlockSpec(tok.shape, lambda c, p: (0, 0, 0), pipeline_mode=one),
            weight(qkv_weight), row, row, row, row, weight(proj_weight), row, row, row,
        ],
        out_specs=[block(rows), block(keys), block(keys)] + [block(rows)] * 5
        + [pl.BlockSpec((1, 1, keys), lambda c, p: (c, 0, 0))],
        out_shape=[
            jax.ShapeDtypeStruct((clips, rows, width), bf16),
            jax.ShapeDtypeStruct((clips, keys, width), bf16),
            jax.ShapeDtypeStruct((clips, keys, width), bf16),
            jax.ShapeDtypeStruct((clips, rows, width), bf16),
            jax.ShapeDtypeStruct((clips, rows, width), bf16),
            jax.ShapeDtypeStruct((clips, rows, width), f32),
            jax.ShapeDtypeStruct((clips, rows, width), f32),
            jax.ShapeDtypeStruct((clips, rows, width), bf16),
            jax.ShapeDtypeStruct((clips, 1, keys), f32),
        ],
        scratch_shapes=[
            pltpu.VMEM((clips, 3, rows, width), bf16),
            pltpu.SemaphoreType.DMA((clips, 3)),
            pltpu.SemaphoreType.DMA((clips, 3)),
        ],
        compiler_params=params(collective_id=0, has_side_effects=True),
        cost_estimate=pl.CostEstimate(
            flops=flops, bytes_accessed=40_000_000, transcendentals=clips * rows * keys * HEADS
        ),
        name="forward",
    )(tok, qkv_weight, query_bias, value_bias, gain, shift, proj_weight, proj_bias, gain2, shift2)


def mlp_kernel(
    counts,
    n2_ref, middle_ref, cot_ref, live_ref, mixed_ref, fc1_ref, b1_ref, fc2_ref, b2_ref,
    gain_ref, shift_ref, proj_ref,
    out_ref, dfc1_ref, dfc2_ref, dproj_ref, db1_ref, small_ref, gmid_ref, gmixed_ref,
    n2t_ref, grad_ref, out_acc, dn_acc, hidden_ref, dact_ref, active_ref, dhid_ref,
):
    clips, slots, rows, tile = counts
    step = pl.program_id(0)
    width = n2_ref.shape[-1]
    chunk = fc1_ref.shape[-1]
    total = clips * rows

    @pl.when(step == 0)
    def start():
        n2t_ref[...] = n2_ref[...].T
        grad_ref[...] = (cot_ref[...].astype(f32) * live_ref[...]).astype(bf16)
        out_acc[...] = jnp.zeros_like(out_acc)
        dn_acc[...] = jnp.zeros_like(dn_acc)

    hidden_ref[...] = dot(n2_ref[...], fc1_ref[...])
    dact_ref[...] = dot(grad_ref[...], fc2_ref[...], NT)
    bias = b1_ref[...]

    def gelu_tile(index, sums):
        at = pl.ds(pl.multiple_of(index * tile, tile), tile)
        hidden = hidden_ref[at, :] + bias
        cdf = 0.5 * (1.0 + lax.erf(hidden * (0.5 ** 0.5)))
        active_ref[at, :] = (hidden * cdf).astype(bf16)
        slope = cdf + hidden * (jnp.exp(-0.5 * hidden * hidden) * (1.0 / math.sqrt(2.0 * math.pi)))
        dhid = (dact_ref[at, :] * slope).astype(bf16)
        dhid_ref[at, :] = dhid
        return sums + dhid.astype(f32)

    sums = lax.fori_loop(0, total // tile, gelu_tile, jnp.zeros((tile, chunk), f32))
    db1_ref[...] = column_sums(sums)
    active = active_ref[...]
    dhid = dhid_ref[...]
    out_acc[...] += dot(active, fc2_ref[...])
    dn_acc[...] += dot(dhid, fc1_ref[...], NT)
    dfc1_ref[0] = dot(n2t_ref[...], dhid).astype(bf16)
    dfc2 = dot(active, grad_ref[...], TN).astype(bf16)
    half = width // 2
    dfc2_ref[0] = dfc2[:, :half]
    dfc2_ref[1] = dfc2[:, half:]

    @pl.when(step == pl.num_programs(0) - 1)
    def finish():
        gain = gain_ref[...]
        sum_gain = jnp.zeros((1, width), f32)
        sum_shift = jnp.zeros((1, width), f32)
        sum_grad = jnp.zeros((1, width), f32)
        sum_proj = jnp.zeros((1, width), f32)
        for clip in range(clips):
            at = slice(clip * rows, (clip + 1) * rows)
            middle = middle_ref[at]
            live = live_ref[at]
            layer = live * (middle + (out_acc[at] + b2_ref[...]))
            out_ref[clip] = layer[:slots].astype(bf16)
            unit, inverse = center_scale(middle)
            grad = dn_acc[at]
            out_grad = cot_ref[at].astype(f32) * live
            gmid = out_grad + norm_back(unit, inverse, gain, grad)
            gmid_ref[at] = gmid
            low = gmid.astype(bf16)
            dhid_ref[at, :width] = low
            gmixed_ref[at] = dot(low, proj_ref[...], NT).astype(bf16)
            sum_gain += column_sums(grad * unit)
            sum_shift += column_sums(grad)
            sum_grad += column_sums(grad_ref[at].astype(f32))
            sum_proj += column_sums(low.astype(f32))
        dproj = dot(mixed_ref[...], dhid_ref[:, :width], TN).astype(bf16)
        dproj_ref[0] = dproj[:, :half]
        dproj_ref[1] = dproj[:, half:]
        small_ref[0:1] = sum_gain
        small_ref[1:2] = sum_shift
        small_ref[2:3] = sum_grad
        small_ref[3:4] = sum_proj


def mlp(n2, middle, cot, live, mixed, fc1, b1, fc2, b2, gain, shift, proj, shape):
    clips, slots, rows = shape
    total, width = n2.shape
    hidden = fc1.shape[1]
    chunk = 768
    steps = hidden // chunk
    half = steps // 2
    tile = 16
    row = full((1, width))
    one = pl.Buffered(buffer_count=1)
    big = pl.BlockSpec((total, width), lambda j: (0, 0), pipeline_mode=one)
    return pl.pallas_call(
        functools.partial(mlp_kernel, (clips, slots, rows, tile)),
        grid=(steps,),
        in_specs=[
            big, big, big,
            pl.BlockSpec((total, 1), lambda j: (0, 0), pipeline_mode=one),
            big,
            pl.BlockSpec((width, chunk), lambda j: (0, j)),
            pl.BlockSpec((1, chunk), lambda j: (0, j)),
            pl.BlockSpec((chunk, width), lambda j: (j, 0)),
            row, row, row,
            pl.BlockSpec((width, width), lambda j: (0, 0), pipeline_mode=one),
        ],
        out_specs=[
            full((clips, slots, width)),
            pl.BlockSpec((1, width, chunk), lambda j: (j // half, 0, j % half)),
            pl.BlockSpec((2, chunk, width // 2), lambda j: (0, j, 0)),
            full((2, width, width // 2)),
            pl.BlockSpec((1, chunk), lambda j: (0, j)),
            full((8, width)),
            full((total, width)),
            full((total, width)),
        ],
        out_shape=[
            jax.ShapeDtypeStruct((clips, slots, width), bf16),
            jax.ShapeDtypeStruct((2, width, hidden // 2), bf16),
            jax.ShapeDtypeStruct((2, hidden, width // 2), bf16),
            jax.ShapeDtypeStruct((2, width, width // 2), bf16),
            jax.ShapeDtypeStruct((1, hidden), f32),
            jax.ShapeDtypeStruct((8, width), f32),
            jax.ShapeDtypeStruct((total, width), f32),
            jax.ShapeDtypeStruct((total, width), bf16),
        ],
        scratch_shapes=[
            pltpu.VMEM((width, total), bf16),
            pltpu.VMEM((total, width), bf16),
            pltpu.VMEM((total, width), f32),
            pltpu.VMEM((total, width), f32),
            pltpu.VMEM((total, chunk), f32),
            pltpu.VMEM((total, chunk), f32),
            pltpu.VMEM((total, chunk), bf16),
            pltpu.VMEM((total, chunk), bf16),
        ],
        compiler_params=params(),
        cost_estimate=pl.CostEstimate(
            flops=12 * total * width * hidden, bytes_accessed=40_000_000, transcendentals=2 * total * hidden
        ),
        name="mlp",
    )(n2, middle, cot, live, mixed, fc1, b1, fc2, b2, gain, shift, proj)


def attend_back_kernel(q_ref, k_ref, v_ref, mask_ref, mixed_ref, lse_ref, grad_ref,
                       dq_ref, dkeep_ref, dsend_ref):
    query = q_ref[0]
    keys = k_ref[0]
    values = v_ref[0]
    grad = grad_ref[0]
    live = mask_ref[0] > 0.5
    product = grad.astype(f32) * mixed_ref[0].astype(f32)
    dqs, dk, dv = [], None, None
    for head in range(2):
        own_query = only(query, head)
        own_grad = only(grad, head)
        scores = jnp.where(live, dot(own_query, keys, NT), MASKED)
        probs = jnp.exp(scores - lse_ref[0, :, head * DH : head * DH + 1])
        delta = jnp.sum(only(product, head), axis=1, keepdims=True)
        dscores = (probs * (dot(own_grad, values, NT) - delta)).astype(bf16)
        dqs.append(dot(dscores, keys))
        more_k = dot(dscores, own_query, TN)
        more_v = dot(probs.astype(bf16), own_grad, TN)
        dk = more_k if dk is None else dk + more_k
        dv = more_v if dv is None else dv + more_v
    first = own_lanes(dqs[0].shape, 0)
    dq_ref[0] = (jnp.where(first, dqs[0], dqs[1]) * DH ** -0.5).astype(bf16)
    half = dk.shape[0] // 2
    dkeep_ref[0, 0] = dk[:half].astype(bf16)
    dkeep_ref[1, 0] = dv[:half].astype(bf16)
    dsend_ref[0, 0] = dk[half:].astype(bf16)
    dsend_ref[1, 0] = dv[half:].astype(bf16)


def attend_back(q, k, v, mask, mixed, lse, grad, first_pair, pairs):
    clips, rows, _ = q.shape
    keys = k.shape[1]
    lanes = 2 * DH
    tok = pl.BlockSpec((1, rows, lanes), lambda c, p: (c, 0, first_pair + p))
    key = pl.BlockSpec((1, keys, lanes), lambda c, p: (c, 0, first_pair + p))
    part = pl.BlockSpec((2, 1, keys // 2, lanes), lambda c, p: (0, c, 0, p))
    return pl.pallas_call(
        attend_back_kernel,
        grid=(clips, pairs),
        in_specs=[tok, key, key, pl.BlockSpec((1, 1, keys), lambda c, p: (c, 0, 0)), tok, tok, tok],
        out_specs=[pl.BlockSpec((1, rows, lanes), lambda c, p: (c, 0, p)), part, part],
        out_shape=[
            jax.ShapeDtypeStruct((clips, rows, pairs * lanes), bf16),
            jax.ShapeDtypeStruct((2, clips, keys // 2, pairs * lanes), bf16),
            jax.ShapeDtypeStruct((2, clips, keys // 2, pairs * lanes), bf16),
        ],
        compiler_params=params(),
        cost_estimate=pl.CostEstimate(
            flops=4 * 10 * clips * rows * keys * pairs * lanes,
            bytes_accessed=clips * pairs * lanes * (keys * 10 + rows * 12),
            transcendentals=clips * rows * keys * 2 * pairs,
        ),
        name="attend_back",
    )(q, k, v, mask, mixed, lse, grad)


def weight_kernel(normed_ref, dq_ref, dk0_ref, dk1_ref, dk2_ref, out_ref, dkv_ref, sums_ref):
    part = pl.program_id(0)
    @pl.when(part == 0)
    def query():
        grad = dq_ref[...]
        out_ref[0] = dot(normed_ref[...], grad, TN).astype(bf16)
        sums_ref[0] = column_sums(grad.astype(f32))
        dkv_ref[0] = jnp.zeros_like(dkv_ref[0])

    @pl.when(part > 0)
    def other():
        grad = (dk0_ref[0].astype(f32) + dk1_ref[0].astype(f32) + dk2_ref[0].astype(f32)).astype(bf16)
        dkv_ref[0] = grad
        out_ref[0] = dot(normed_ref[...], grad, TN).astype(bf16)
        sums_ref[0] = column_sums(grad.astype(f32))


def weight_grads(normed, dq, parts):
    total, width = normed.shape
    lanes = dq.shape[1]
    before = lambda j: (jnp.maximum(j - 1, 0), 0, 0)
    part = pl.BlockSpec((1, total, lanes), before)
    return pl.pallas_call(
        weight_kernel,
        grid=(3,),
        in_specs=[full((total, width)), full((total, lanes)), part, part, part],
        out_specs=[
            pl.BlockSpec((1, width, lanes), lambda j: (j, 0, 0)),
            part,
            pl.BlockSpec((1, 1, lanes), lambda j: (j, 0, 0)),
        ],
        out_shape=[
            jax.ShapeDtypeStruct((3, width, lanes), bf16),
            jax.ShapeDtypeStruct((2, total, lanes), bf16),
            jax.ShapeDtypeStruct((3, 1, lanes), f32),
        ],
        compiler_params=params(),
        cost_estimate=pl.CostEstimate(
            flops=6 * total * width * lanes, bytes_accessed=8_000_000, transcendentals=0
        ),
        name="weight_grads",
    )(normed, dq, *parts)


def input_kernel(counts, groups, *refs):
    clips, slots, rows = counts
    dqs = refs[:groups]
    dkvs = refs[groups : 2 * groups]
    qkv_ref, tok_ref, gmid_ref, gain_ref, shift_ref, out_ref, small_ref = refs[2 * groups :]
    clip = pl.program_id(0)
    width = tok_ref.shape[-1]
    lanes = width // groups
    grad = None
    for group in range(groups):
        for part in range(3):
            rows_grad = dqs[group][0] if part == 0 else dkvs[group][part - 1]
            at = part * width + group * lanes
            more = dot(rows_grad, qkv_ref[:, at : at + lanes], NT)
            grad = more if grad is None else grad + more
    unit, inverse = center_scale(tok_ref[0].astype(f32))
    result = gmid_ref[0] + norm_back(unit, inverse, gain_ref[...], grad)
    out_ref[0] = result[:slots]

    @pl.when(clip == 0)
    def start():
        small_ref[...] = jnp.zeros_like(small_ref)

    small_ref[0:1] += column_sums(grad * unit)
    small_ref[1:2] += column_sums(grad)


def input_grads(dqs, dkvs, qkv_weight, tokens, gmid, gain, shift, slots):
    clips, rows, width = tokens.shape
    groups = len(dqs)
    lanes = width // groups
    tok = pl.BlockSpec((1, rows, width), lambda c: (c, 0, 0))
    return pl.pallas_call(
        functools.partial(input_kernel, (clips, slots, rows), groups),
        grid=(clips,),
        in_specs=[pl.BlockSpec((1, rows, lanes), lambda c: (c, 0, 0))] * groups
        + [pl.BlockSpec((2, rows, lanes), lambda c: (0, c, 0))] * groups
        + [full(qkv_weight.shape), tok, tok, full((1, width)), full((1, width))],
        out_specs=[pl.BlockSpec((1, slots, width), lambda c: (c, 0, 0)), full((8, width))],
        out_shape=[
            jax.ShapeDtypeStruct((clips, slots, width), f32),
            jax.ShapeDtypeStruct((8, width), f32),
        ],
        compiler_params=params(),
        cost_estimate=pl.CostEstimate(
            flops=6 * clips * rows * width * width, bytes_accessed=16_000_000, transcendentals=0
        ),
        name="input_grads",
    )(*dqs, *dkvs, qkv_weight, tokens, gmid, gain, shift)


def swap_bit(array, axis, size, bit):
    return lax.ppermute(array, axis, [(i, i ^ (1 << bit)) for i in range(size)])


def add_low(left, right):
    return (left.astype(f32) + right.astype(f32)).astype(bf16)


def pick(array, index, dim):
    return lax.dynamic_index_in_dim(array, index, dim, keepdims=False)


def bit_of(axis, bit):
    return (lax.axis_index(axis) >> bit) & 1


def scatter_sum(split, clip_size, order):
    core = bit_of("freq", 0)
    vert = bit_of("freq", 1)
    bits = clip_size.bit_length() - 1
    lanes = split.shape[-1]
    value = add_low(pick(split, core, 0), swap_bit(pick(split, 1 - core, 0), "freq", 4, 0))
    rows = value.shape[0] // (2 * clip_size)
    value = value.reshape((2,) * bits + (2, rows, lanes))
    left = list(range(bits))[::-1]
    for bit in order:
        at = left.index(bit)
        mine = bit_of("clip", bit)
        value = add_low(
            pick(value, mine, at), swap_bit(pick(value, 1 - mine, at), "clip", clip_size, bit)
        )
        left.remove(bit)
    return add_low(pick(value, vert, 0), swap_bit(pick(value, 1 - vert, 0), "freq", 4, 1))


def gather_low(part):
    core = bit_of("freq", 0)
    vert = bit_of("freq", 1)
    other = swap_bit(part, "freq", 4, 1)
    tall = jnp.where(vert == 0, jnp.concatenate([part, other]), jnp.concatenate([other, part]))
    side = swap_bit(tall, "freq", 4, 0)
    return jnp.where(
        core == 0,
        jnp.concatenate([tall, side], axis=1),
        jnp.concatenate([side, tall], axis=1),
    ).astype(f32)


def total_sum(array, clip_size):
    for bit in range(2):
        array = array + swap_bit(array, "freq", 4, bit)
    for bit in range(clip_size.bit_length() - 1):
        array = array + swap_bit(array, "clip", clip_size, bit)
    return array


def on_device(
    clip_size, tokens, kept_counts, attn_gain, attn_shift, qkv_weight, query_bias, value_bias,
    proj_weight, proj_bias, mlp_gain, mlp_shift, fc1_weight, fc1_bias, fc2_weight, fc2_bias, cotangent,
):
    clips, slots, width = tokens.shape
    rows = -(-slots // 16) * 16
    total = clips * rows
    bits = clip_size.bit_length() - 1
    forward_order = list(range(bits))
    second_order = forward_order[1:2] + forward_order[:1] + forward_order[2:]
    pad = ((0, 0), (0, rows - slots), (0, 0))
    vec = lambda v: v.astype(f32)[None, :]
    slot_ids = jnp.arange(rows, dtype=jnp.int32)
    live = (slot_ids[None, :] < kept_counts).astype(f32).reshape(total, 1)
    kept = (kept_counts - slots // 2).astype(bf16)
    tok = jnp.concatenate(
        [tokens, jnp.broadcast_to(kept[:, :, None], (clips, rows - slots, width))], axis=1
    )
    vectors = [vec(v) for v in (query_bias, value_bias, attn_gain, attn_shift, proj_bias, mlp_gain, mlp_shift)]
    q, k, v, normed, mixed, lse, middle, normed2, mask = forward(
        tok, slots, qkv_weight, vectors, proj_weight
    )
    flat = lambda a: a.reshape(total, width)
    cot = jnp.pad(cotangent, pad)
    layer_out, dfc1, dfc2, dproj, db1, small2, gmid, gmixed = mlp(
        flat(normed2), flat(middle), flat(cot), live, flat(mixed), fc1_weight, vec(fc1_bias),
        fc2_weight, vec(fc2_bias), vectors[5], vectors[6], proj_weight, (clips, slots, rows),
    )
    early = total_sum(jnp.concatenate([small2[:4].reshape(-1), db1.reshape(-1)])[None, :], clip_size)[0]
    sum_fc1 = gather_low(scatter_sum(dfc1, clip_size, forward_order))
    sum_fc2 = gather_low(scatter_sum(dfc2, clip_size, second_order))
    sum_proj = gather_low(scatter_sum(dproj, clip_size, forward_order))

    groups = 3
    pairs = HEADS // 2 // groups
    lanes = pairs * 2 * DH
    gmixed = gmixed.reshape(clips, rows, width)
    dqs, dkvs, sums, sharded = [], [], [], []
    for group in range(groups):
        dq, keep, send = attend_back(q, k, v, mask, mixed, lse, gmixed, group * pairs, pairs)
        got = swap_bit(send, "freq", 4, 0)
        across = swap_bit(add_low(keep[:, :, rows:], got[:, :, rows:]), "freq", 4, 1)
        parts = [a.reshape(2, total, lanes) for a in (keep[:, :, :rows], got[:, :, :rows], across)]
        dw, dkv, colsum = weight_grads(flat(normed), dq.reshape(total, lanes), parts)
        half = lanes // 2
        split = jnp.stack(
            [
                jnp.concatenate([dw[i, :, s * half : (s + 1) * half] for i in range(3)], axis=1)
                for s in range(2)
            ]
        )
        order = forward_order if group % 2 == 0 else second_order
        summed = gather_low(scatter_sum(split, clip_size, order))
        sharded.append(summed.reshape(summed.shape[0], 2, 3, half))
        dqs.append(dq)
        dkvs.append(dkv)
        sums.append(colsum)
    grad_tokens, small1 = input_grads(
        dqs, dkvs, qkv_weight, tok, gmid.reshape(clips, rows, width), vectors[2], vectors[3], slots
    )
    qkv = jnp.stack(sharded, axis=1)
    sum_qkv = qkv.transpose(0, 3, 1, 2, 4).reshape(qkv.shape[0], 3 * width)
    bias = jnp.concatenate(sums, axis=2)
    late = total_sum(
        jnp.concatenate([small1[0:1], small1[1:2], bias[0], bias[2]], axis=1), clip_size
    )[0]
    cut = lambda a, i: a[i * width : (i + 1) * width]
    return (
        layer_out, grad_tokens, cut(late, 0), cut(late, 1), sum_qkv, cut(late, 2), cut(late, 3),
        sum_proj, cut(early, 3), cut(early, 0), cut(early, 1), sum_fc1, early[4 * width :],
        sum_fc2, cut(early, 2),
    )


def solution(mesh):
    rows = P("clip", "freq", None)
    shard = P("clip", None)
    return jax.shard_map(
        functools.partial(on_device, mesh.shape["clip"]),
        mesh=mesh,
        in_specs=(rows, P("clip", "freq")) + (P(),) * 13 + (rows,),
        out_specs=(rows, rows, P(), P(), shard, P(), P(), shard, P(), P(), P(), shard, P(), shard, P()),
        check_vma=False,
    )
```

```python
import functools
import math

import jax
import jax.numpy as jnp
from jax import lax
from jax.experimental import pallas as pl
from jax.experimental.pallas import tpu as pltpu
from jax.sharding import PartitionSpec as P

HEADS = 12
DH = 64
EPS = 1e-06
MASKED = -1000000000.0
VMEM_BYTES = 60 * 1024 * 1024

f32 = jnp.float32
bf16 = jnp.bfloat16
NN = (((1,), (0,)), ((), ()))
NT = (((1,), (1,)), ((), ()))
TN = (((0,), (0,)), ((), ()))


def dot(left, right, dims=NN):
    return lax.dot_general(left, right, dims, preferred_element_type=f32)


def center_scale(rows):
    center = rows - jnp.mean(rows, axis=-1, keepdims=True)
    inverse = lax.rsqrt(jnp.mean(center * center, axis=-1, keepdims=True) + EPS)
    return center * inverse, inverse


def norm_back(unit, inverse, gain, grad):
    scaled = grad * gain
    return inverse * (
        scaled
        - jnp.mean(scaled, axis=-1, keepdims=True)
        - unit * jnp.mean(scaled * unit, axis=-1, keepdims=True)
    )


def column_sums(rows):
    return jnp.sum(rows, axis=0, keepdims=True)


def own_lanes(shape, head):
    lane = lax.broadcasted_iota(jnp.int32, shape, len(shape) - 1)
    return lane < DH if head == 0 else lane >= DH


def only(rows, head):
    return jnp.where(own_lanes(rows.shape, head), rows, jnp.zeros_like(rows))


def full(shape):
    return pl.BlockSpec(shape, lambda *ids: (0,) * len(shape))


def params(**more):
    return pltpu.CompilerParams(vmem_limit_bytes=VMEM_BYTES, **more)


def partner(kind):
    index = lax.axis_index("freq")
    if kind == "vert":
        return {"freq": (index + 2) % 4}
    return {"freq": index + 1 - 2 * (index % 2)}


def forward_kernel(
    counts,
    tok_ref, qkv_ref, qb_ref, vb_ref, gain_ref, shift_ref, proj_ref, pb_ref, gain2_ref, shift2_ref,
    q_ref, k_ref, v_ref, normed_ref, mixed_ref, lse_ref, middle_ref, normed2_ref, mask_ref,
    held, send_sem, recv_sem,
):
    clips, slots, rows = counts
    clip = pl.program_id(0)
    pair = pl.program_id(1)
    width = tok_ref.shape[-1]

    def copy(kind, index):
        at = {"vert": 0, "core": 1, "diag": 2}[kind]
        return pltpu.make_async_remote_copy(
            src_ref=held.at[index, 0] if kind == "diag" else tok_ref.at[index],
            dst_ref=held.at[index, at],
            send_sem=send_sem.at[index, at],
            recv_sem=recv_sem.at[index, at],
            device_id=partner(kind),
            device_id_type=pl.DeviceIdType.MESH,
        )

    def project(slot, source):
        unit, _ = center_scale(source.astype(f32))
        normed = (unit * gain_ref[...] + shift_ref[...]).astype(bf16)
        if slot == 0:
            normed_ref[0] = normed
            query = (dot(normed, qkv_ref[:, :width]) + qb_ref[...]).astype(bf16)
            q_ref[0] = query * jnp.asarray(DH ** -0.5, bf16)
        both = dot(normed, qkv_ref[:, width:])
        k_ref[0, slot * rows : (slot + 1) * rows] = both[:, :width].astype(bf16)
        v_ref[0, slot * rows : (slot + 1) * rows] = (both[:, width:] + vb_ref[...]).astype(bf16)
        first = (slots // 16) * 16
        kept = source[first:].astype(f32)[slots - first : slots - first + 1, 0:1] + slots // 2
        lane = lax.broadcasted_iota(jnp.int32, (1, rows), 1).astype(f32)
        return (lane < kept).astype(f32)

    @pl.when((clip == 0) & (pair == 0))
    def enter():
        barrier = pltpu.get_barrier_semaphore()
        for kind in ("vert", "core"):
            pl.semaphore_signal(
                barrier, inc=1, device_id=partner(kind), device_id_type=pl.DeviceIdType.MESH
            )
        pl.semaphore_wait(barrier, 2)
        copy("vert", 0).start()
        for index in range(clips):
            copy("core", index).start()

    def pass_on(index):
        copy("vert", index).wait_recv()
        copy("diag", index).start()
        copy("vert", index).wait_send()

        @pl.when(index + 1 < clips)
        def more():
            copy("vert", index + 1).start()

    @pl.when(pair == 0)
    def project_all():
        live_own = project(0, tok_ref[clip])
        copy("core", clip).wait_recv()
        live_core = project(2, held[clip, 1])

        @pl.when(clip == 0)
        def first_pass():
            pass_on(clip)

        live_vert = project(1, held[clip, 0])
        copy("diag", clip).wait_recv()
        live_diag = project(3, held[clip, 2])
        mask_ref[0] = jnp.concatenate([live_own, live_vert, live_core, live_diag], axis=1)

    @pl.when((pair == 3) & (clip + 1 < clips))
    def next_pass():
        pass_on(clip + 1)

    lanes = pl.ds(pl.multiple_of(pair * 2 * DH, 2 * DH), 2 * DH)
    query = q_ref[0, :, lanes]
    keys = k_ref[0, :, lanes]
    values = v_ref[0, :, lanes]
    live = mask_ref[0] > 0.5
    outs, lses = [], []
    for head in range(2):
        scores = jnp.where(live, dot(only(query, head), keys, NT), MASKED)
        top = jnp.max(scores, axis=1, keepdims=True)
        exps = jnp.exp(scores - top)
        total = jnp.sum(exps, axis=1, keepdims=True)
        outs.append(dot(exps.astype(bf16), values) / total)
        lses.append(top + jnp.log(total))
    first = own_lanes(outs[0].shape, 0)
    mixed_ref[0, :, lanes] = jnp.where(first, outs[0], outs[1]).astype(bf16)
    lse_ref[0, :, lanes] = jnp.where(first, lses[0], lses[1])

    @pl.when(pair == pl.num_programs(1) - 1)
    def finish():
        middle = tok_ref[clip].astype(f32) + (dot(mixed_ref[0], proj_ref[...]) + pb_ref[...])
        middle_ref[0] = middle
        unit, _ = center_scale(middle)
        normed2_ref[0] = (unit * gain2_ref[...] + shift2_ref[...]).astype(bf16)
        copy("core", clip).wait_send()
        copy("diag", clip).wait_send()


def forward(tok, slots, qkv_weight, vectors, proj_weight):
    clips, rows, width = tok.shape
    keys = 4 * rows
    pairs = HEADS // 2
    query_bias, value_bias, gain, shift, proj_bias, gain2, shift2 = vectors
    one = pl.Buffered(buffer_count=1)
    row = full((1, width))
    block = lambda n: pl.BlockSpec((1, n, width), lambda c, p: (c, 0, 0))
    flops = 2 * clips * (10 * rows * width * width + 2 * rows * keys * width)
    weight = lambda w: pl.BlockSpec(w.shape, lambda c, p: (0, 0), pipeline_mode=one)
    return pl.pallas_call(
        functools.partial(forward_kernel, (clips, slots, rows)),
        grid=(clips, pairs),
        in_specs=[
            pl.BlockSpec(tok.shape, lambda c, p: (0, 0, 0), pipeline_mode=one),
            weight(qkv_weight), row, row, row, row, weight(proj_weight), row, row, row,
        ],
        out_specs=[block(rows), block(keys), block(keys)] + [block(rows)] * 5
        + [pl.BlockSpec((1, 1, keys), lambda c, p: (c, 0, 0))],
        out_shape=[
            jax.ShapeDtypeStruct((clips, rows, width), bf16),
            jax.ShapeDtypeStruct((clips, keys, width), bf16),
            jax.ShapeDtypeStruct((clips, keys, width), bf16),
            jax.ShapeDtypeStruct((clips, rows, width), bf16),
            jax.ShapeDtypeStruct((clips, rows, width), bf16),
            jax.ShapeDtypeStruct((clips, rows, width), f32),
            jax.ShapeDtypeStruct((clips, rows, width), f32),
            jax.ShapeDtypeStruct((clips, rows, width), bf16),
            jax.ShapeDtypeStruct((clips, 1, keys), f32),
        ],
        scratch_shapes=[
            pltpu.VMEM((clips, 3, rows, width), bf16),
            pltpu.SemaphoreType.DMA((clips, 3)),
            pltpu.SemaphoreType.DMA((clips, 3)),
        ],
        compiler_params=params(collective_id=0, has_side_effects=True),
        cost_estimate=pl.CostEstimate(
            flops=flops, bytes_accessed=40_000_000, transcendentals=clips * rows * keys * HEADS
        ),
        name="forward",
    )(tok, qkv_weight, query_bias, value_bias, gain, shift, proj_weight, proj_bias, gain2, shift2)


def mlp_kernel(
    counts,
    n2_ref, middle_ref, cot_ref, live_ref, mixed_ref, fc1_ref, b1_ref, fc2_ref, b2_ref,
    gain_ref, shift_ref, proj_ref,
    out_ref, dfc1_ref, dfc2_ref, dproj_ref, db1_ref, small_ref, gmid_ref, gmixed_ref,
    n2t_ref, grad_ref, out_acc, dn_acc, hidden_ref, dact_ref, active_ref, dhid_ref,
):
    clips, slots, rows, tile = counts
    step = pl.program_id(0)
    width = n2_ref.shape[-1]
    chunk = fc1_ref.shape[-1]
    total = clips * rows

    @pl.when(step == 0)
    def start():
        n2t_ref[...] = n2_ref[...].T
        grad_ref[...] = (cot_ref[...].astype(f32) * live_ref[...]).astype(bf16)
        out_acc[...] = jnp.zeros_like(out_acc)
        dn_acc[...] = jnp.zeros_like(dn_acc)

    hidden_ref[...] = dot(n2_ref[...], fc1_ref[...])
    dact_ref[...] = dot(grad_ref[...], fc2_ref[...], NT)
    bias = b1_ref[...]

    def gelu_tile(index, sums):
        at = pl.ds(pl.multiple_of(index * tile, tile), tile)
        hidden = hidden_ref[at, :] + bias
        cdf = 0.5 * (1.0 + lax.erf(hidden * (0.5 ** 0.5)))
        active_ref[at, :] = (hidden * cdf).astype(bf16)
        slope = cdf + hidden * (jnp.exp(-0.5 * hidden * hidden) * (1.0 / math.sqrt(2.0 * math.pi)))
        dhid = (dact_ref[at, :] * slope).astype(bf16)
        dhid_ref[at, :] = dhid
        return sums + dhid.astype(f32)

    sums = lax.fori_loop(0, total // tile, gelu_tile, jnp.zeros((tile, chunk), f32))
    db1_ref[...] = column_sums(sums)
    active = active_ref[...]
    dhid = dhid_ref[...]
    out_acc[...] += dot(active, fc2_ref[...])
    dn_acc[...] += dot(dhid, fc1_ref[...], NT)
    dfc1_ref[0] = dot(n2t_ref[...], dhid).astype(bf16)
    dfc2 = dot(active, grad_ref[...], TN).astype(bf16)
    half = width // 2
    dfc2_ref[0] = dfc2[:, :half]
    dfc2_ref[1] = dfc2[:, half:]

    @pl.when(step == pl.num_programs(0) - 1)
    def finish():
        gain = gain_ref[...]
        sum_gain = jnp.zeros((1, width), f32)
        sum_shift = jnp.zeros((1, width), f32)
        sum_grad = jnp.zeros((1, width), f32)
        sum_proj = jnp.zeros((1, width), f32)
        for clip in range(clips):
            at = slice(clip * rows, (clip + 1) * rows)
            middle = middle_ref[at]
            live = live_ref[at]
            layer = live * (middle + (out_acc[at] + b2_ref[...]))
            out_ref[clip] = layer[:slots].astype(bf16)
            unit, inverse = center_scale(middle)
            grad = dn_acc[at]
            out_grad = cot_ref[at].astype(f32) * live
            gmid = out_grad + norm_back(unit, inverse, gain, grad)
            gmid_ref[at] = gmid
            low = gmid.astype(bf16)
            dhid_ref[at, :width] = low
            gmixed_ref[at] = dot(low, proj_ref[...], NT).astype(bf16)
            sum_gain += column_sums(grad * unit)
            sum_shift += column_sums(grad)
            sum_grad += column_sums(grad_ref[at].astype(f32))
            sum_proj += column_sums(low.astype(f32))
        dproj = dot(mixed_ref[...], dhid_ref[:, :width], TN).astype(bf16)
        dproj_ref[0] = dproj[:, :half]
        dproj_ref[1] = dproj[:, half:]
        small_ref[0:1] = sum_gain
        small_ref[1:2] = sum_shift
        small_ref[2:3] = sum_grad
        small_ref[3:4] = sum_proj


def mlp(n2, middle, cot, live, mixed, fc1, b1, fc2, b2, gain, shift, proj, shape):
    clips, slots, rows = shape
    total, width = n2.shape
    hidden = fc1.shape[1]
    chunk = 768
    steps = hidden // chunk
    half = steps // 2
    tile = 16
    row = full((1, width))
    one = pl.Buffered(buffer_count=1)
    big = pl.BlockSpec((total, width), lambda j: (0, 0), pipeline_mode=one)
    return pl.pallas_call(
        functools.partial(mlp_kernel, (clips, slots, rows, tile)),
        grid=(steps,),
        in_specs=[
            big, big, big,
            pl.BlockSpec((total, 1), lambda j: (0, 0), pipeline_mode=one),
            big,
            pl.BlockSpec((width, chunk), lambda j: (0, j)),
            pl.BlockSpec((1, chunk), lambda j: (0, j)),
            pl.BlockSpec((chunk, width), lambda j: (j, 0)),
            row, row, row,
            pl.BlockSpec((width, width), lambda j: (0, 0), pipeline_mode=one),
        ],
        out_specs=[
            full((clips, slots, width)),
            pl.BlockSpec((1, width, chunk), lambda j: (j // half, 0, j % half)),
            pl.BlockSpec((2, chunk, width // 2), lambda j: (0, j, 0)),
            full((2, width, width // 2)),
            pl.BlockSpec((1, chunk), lambda j: (0, j)),
            full((8, width)),
            full((total, width)),
            full((total, width)),
        ],
        out_shape=[
            jax.ShapeDtypeStruct((clips, slots, width), bf16),
            jax.ShapeDtypeStruct((2, width, hidden // 2), bf16),
            jax.ShapeDtypeStruct((2, hidden, width // 2), bf16),
            jax.ShapeDtypeStruct((2, width, width // 2), bf16),
            jax.ShapeDtypeStruct((1, hidden), f32),
            jax.ShapeDtypeStruct((8, width), f32),
            jax.ShapeDtypeStruct((total, width), f32),
            jax.ShapeDtypeStruct((total, width), bf16),
        ],
        scratch_shapes=[
            pltpu.VMEM((width, total), bf16),
            pltpu.VMEM((total, width), bf16),
            pltpu.VMEM((total, width), f32),
            pltpu.VMEM((total, width), f32),
            pltpu.VMEM((total, chunk), f32),
            pltpu.VMEM((total, chunk), f32),
            pltpu.VMEM((total, chunk), bf16),
            pltpu.VMEM((total, chunk), bf16),
        ],
        compiler_params=params(),
        cost_estimate=pl.CostEstimate(
            flops=12 * total * width * hidden, bytes_accessed=40_000_000, transcendentals=2 * total * hidden
        ),
        name="mlp",
    )(n2, middle, cot, live, mixed, fc1, b1, fc2, b2, gain, shift, proj)


def sum_arrays(width, hidden, clip_size, chunks):
    rows = width // clip_size
    tall = hidden // clip_size
    last = 3 * 2 * chunks
    first, second = (0, 1, 2), (1, 0, 2)
    arrays = [
        ("fc1", 0, rows, hidden // 4, first, (1, 6, 9, 13, 15, 17, last + 2)),
        ("fc2", 0, tall // 2, width // 2, second, (2, 7, 10, 13, 15, 17, last + 2)),
        ("fc1", hidden // 4, rows, hidden // 4, first, (3, 11, 14, 17, last, last + 1, last + 2)),
        ("fc2", tall // 2, tall // 2, width // 2, second, (4, 12, 15, 17, last, last + 1, last + 2)),
        ("proj", 0, rows, width // 2, second, (5, 12, 15, last, last + 1, last + 2, last + 3)),
    ]
    after = [(last + 1, last + 2), (last + 2, last + 3), (last + 3, last + 4)]
    for chunk in range(chunks):
        begin = last + chunk + 1
        stages = tuple(min(begin + i, last + 6) for i in range(7))
        arrays.append(("qkv", chunk, rows, width // 2, second if chunk == 1 else first, stages))
    return arrays


def backward_kernel(
    meta,
    q_ref, k_ref, v_ref, mask_ref, mixed_ref, lse_ref, grad_ref,
    normed_ref, qkv_ref, tok_ref, gmid_ref, gain_ref, small_ref, db1_ref,
    dfc1_ref, dfc2_ref, dproj_ref,
    gtok_ref, fc1_out, fc2_out, proj_out, qkv_out, vec_out,
    *scratch,
):
    clips, slots, rows, bits, pairs, arrays = meta
    total = clips * rows
    width = qkv_ref.shape[0]
    lanes = 2 * DH
    step = pl.program_id(0)
    attention = pairs * clips
    chunks = pairs // 2
    mesh_id = pl.DeviceIdType.MESH
    count = len(arrays)

    scratch = list(scratch)
    take = lambda n: [scratch.pop(0) for _ in range(n)]
    dq_all, own_kv, far_kv, send_kv, got_kv, across_kv, weights, acc, vec_sum, vec_got = take(10)
    own_bufs = dict(zip(("fc1", "fc2", "proj"), take(3)))
    stage_bufs = [take(bits + 1) for _ in arrays]
    half_bufs = take(count)
    full_bufs = take(count)
    kv_send, kv_recv, sum_send, sum_recv, own_sem, vec_send, vec_recv = take(7)

    freq = lax.axis_index("freq")
    place = lax.axis_index("clip")
    core = freq % 2
    vert = freq // 2
    bit_at = [(place // 2 ** b) % 2 for b in range(bits)]
    core_dev = {"freq": freq + 1 - 2 * core}
    vert_dev = {"freq": (freq + 2) % 4}
    clip_dev = [{"clip": place + (1 - 2 * bit_at[b]) * 2 ** b} for b in range(bits)]

    def remote(src, dst, send, recv, device):
        return pltpu.make_async_remote_copy(
            src_ref=src, dst_ref=dst, send_sem=send, recv_sem=recv, device_id=device, device_id_type=mesh_id
        )

    def kv_core(p):
        return remote(send_kv.at[p % 2], got_kv.at[p % 2], kv_send.at[0, p], kv_recv.at[0, p], core_dev)

    def kv_vert(p):
        return remote(far_kv.at[p], across_kv.at[p], kv_send.at[1, p], kv_recv.at[1, p], vert_dev)

    def kv_pass(p):
        kv_core(p).wait_recv()

        def add_one(i, carry):
            part, clip = i // clips, i % clips
            own_kv[p, part, clip] = own_kv[p, part, clip] + got_kv[p % 2, 0, part, clip]
            far_kv[p, part, clip] = far_kv[p, part, clip] + got_kv[p % 2, 1, part, clip]
            return carry

        lax.fori_loop(0, 2 * clips, add_one, 0)
        kv_vert(p).start()

    every = (slice(None),) * bits

    def piece(a, who):
        name, at, r, width_a, _, _ = arrays[a]
        if name == "fc1":
            return dfc1_ref.at[(who,) + every + (slice(None), pl.ds(at, width_a))]
        if name == "fc2":
            return dfc2_ref.at[(who,) + every + (pl.ds(at, r), slice(None))]
        if name == "proj":
            return dproj_ref.at[who]
        return weights.at[at, who]

    def chosen(a, stage, index_of):
        order = arrays[a][4]
        left = [b for b in range(bits)[::-1] if b not in order[: stage - 1]]
        bit = order[stage - 1]
        at = (slice(None),) * left.index(bit) + (index_of(bit),)
        return stage_bufs[a][stage - 1].at[at]

    def stage_copy(a, stage):
        half = arrays[a][2] // 2
        sems = (sum_send.at[a, stage], sum_recv.at[a, stage])
        if stage == 0:
            return remote(piece(a, 1 - core), stage_bufs[a][0], *sems, core_dev)
        if stage <= bits:
            src = chosen(a, stage, lambda bit: 1 - bit_at[bit])
            return remote(src, stage_bufs[a][stage], *sems, clip_dev[arrays[a][4][stage - 1]])
        if stage == bits + 1:
            src = stage_bufs[a][bits].at[pl.ds((1 - vert) * half, half)]
            return remote(src, half_bufs[a], *sems, vert_dev)
        if stage == bits + 2:
            dst = full_bufs[a].at[core, pl.ds(vert * half, half)]
            return remote(half_bufs[a], dst, *sems, vert_dev)
        return remote(full_bufs[a].at[core], full_bufs[a].at[core], *sems, core_dev)

    def own_copy(a):
        return pltpu.make_async_copy(piece(a, core), own_bufs[arrays[a][0]], own_sem.at[a])

    def add_blocks(dst, src, lead):
        if lead == 0:
            dst[...] = dst[...] + src[...]
            return

        def add_one(i, carry):
            at = tuple((i // 2 ** (lead - 1 - j)) % 2 for j in range(lead))
            dst[at] = dst[at] + src[at]
            return carry

        lax.fori_loop(0, 2 ** lead, add_one, 0)

    def stage_end(a, stage):
        name, at, r, _, _, _ = arrays[a]
        stage_copy(a, stage).wait_recv()
        if stage == 0:
            if name == "qkv":
                add_blocks(stage_bufs[a][0], weights.at[at, core], bits)
            else:
                own_copy(a).wait()
                add_blocks(stage_bufs[a][0], own_bufs[name], bits)
                again = [b for b in range(a + 1, count) if arrays[b][0] == name]
                if again:
                    own_copy(again[0]).start()
        elif stage <= bits:
            add_blocks(stage_bufs[a][stage], chosen(a, stage, lambda bit: bit_at[bit]), bits - stage)
        elif stage == bits + 1:
            half = r // 2
            mine = pl.ds(pl.multiple_of(vert * half, half), half)
            value = half_bufs[a][...] + stage_bufs[a][bits][mine]
            half_bufs[a][...] = value
            full_bufs[a][core, mine] = value
        if stage == 0 and a in (2, 3):
            return
        if stage == 1 and a in (0, 1):
            stage_copy(a + 2, 1).start()
        if stage < bits + 3:
            stage_copy(a, stage + 1).start()

    def vec_copy(hop):
        device = core_dev if hop == 0 else vert_dev if hop == 1 else clip_dev[hop - 2]
        return remote(vec_sum.at[hop], vec_got.at[hop], vec_send.at[hop], vec_recv.at[hop], device)

    def vec_end(hop):
        vec_copy(hop).wait_recv()
        vec_sum[hop + 1] = vec_sum[hop] + vec_got[hop]
        if hop < bits + 1:
            vec_copy(hop + 1).start()

    final = attention + chunks + clips
    events = {}
    for a, entry in enumerate(arrays):
        for stage, at in enumerate(entry[5]):
            events.setdefault(at, []).append(functools.partial(stage_end, a, stage))
    for p in range(pairs):
        events.setdefault(clips * p + clips + 1, []).append(functools.partial(kv_pass, p))
        if p >= 2:
            events.setdefault(clips * p, []).append(lambda p=p: kv_core(p - 2).wait_send())

    @pl.when(step == 0)
    def enter():
        barrier = pltpu.get_barrier_semaphore()
        for device in [core_dev, vert_dev] + clip_dev:
            pl.semaphore_signal(barrier, inc=1, device_id=device, device_id_type=mesh_id)
        pl.semaphore_wait(barrier, 2 + bits)
        for a in (0, 1, 2, 3, 4):
            stage_copy(a, 0).start()
        for a in (0, 1, 4):
            own_copy(a).start()
        vec_sum[0] = jnp.zeros_like(vec_sum[0])
        vec_sum[0, 4:8] = small_ref[0:4]
        for i in range(db1_ref.shape[1] // width):
            vec_sum[0, 8 + i : 9 + i] = db1_ref[0:1, i * width : (i + 1) * width]
        acc[...] = jnp.zeros_like(acc)

    for at in sorted(events):
        if at < final:
            @pl.when(step == at)
            def run(at=at):
                for action in events[at]:
                    action()

    @pl.when(step < attention)
    def attend():
        p = step // clips
        clip = step % clips
        query = q_ref[0]
        keys = k_ref[0]
        values = v_ref[0]
        grad = grad_ref[0]
        live = mask_ref[0] > 0.5
        product = grad.astype(f32) * mixed_ref[0].astype(f32)
        dqs, dk, dv = [], None, None
        for head in range(2):
            own_query = only(query, head)
            own_grad = only(grad, head)
            scores = jnp.where(live, dot(own_query, keys, NT), MASKED)
            probs = jnp.exp(scores - lse_ref[0, :, head * DH : head * DH + 1])
            delta = jnp.sum(only(product, head), axis=1, keepdims=True)
            dscores = (probs * (dot(own_grad, values, NT) - delta)).astype(bf16)
            dqs.append(dot(dscores, keys))
            more_k = dot(dscores, own_query, TN)
            more_v = dot(probs.astype(bf16), own_grad, TN)
            dk = more_k if dk is None else dk + more_k
            dv = more_v if dv is None else dv + more_v
        first = own_lanes(dqs[0].shape, 0)
        dq = (jnp.where(first, dqs[0], dqs[1]) * DH ** -0.5).astype(bf16)
        dq_all[p, pl.ds(pl.multiple_of(clip * rows, rows), rows)] = dq
        for part, value in enumerate((dk, dv)):
            low = value.astype(bf16)
            own_kv[p, part, clip] = low[:rows]
            far_kv[p, part, clip] = low[rows : 2 * rows]
            send_kv[p % 2, 0, part, clip] = low[2 * rows : 3 * rows]
            send_kv[p % 2, 1, part, clip] = low[3 * rows :]

    for p in range(pairs):
        @pl.when(step == clips * p + clips - 1)
        def send_pair(p=p):
            kv_core(p).start()

    for j in range(chunks):
        @pl.when(step == attention + j)
        def weights_of(j=j):
            columns = []
            for p in (2 * j, 2 * j + 1):
                kv_vert(p).wait_recv()
                at = slice(p * lanes, (p + 1) * lanes)
                query = dq_all[p]
                key, value = [
                    (own_kv[p, part] + across_kv[p, part]).reshape(total, lanes) for part in range(2)
                ]
                vec_sum[0, 2:3, at] = column_sums(query.astype(f32))
                vec_sum[0, 3:4, at] = column_sums(value.astype(f32))
                columns += [query, key, value]
            wide = jnp.concatenate(columns, axis=1)
            grads = dot(normed_ref[...], wide, TN).astype(bf16)
            shape = weights.shape[2:]
            for half in range(2):
                weights[j, half] = grads[:, half * 3 * lanes : (half + 1) * 3 * lanes].reshape(shape)
            stage_copy(5 + j, 0).start()
            for part in range(3):
                low = jnp.concatenate([columns[part], columns[3 + part]], axis=1)
                at = part * width + 2 * j * lanes
                acc[...] += dot(low, qkv_ref[:, at : at + 2 * lanes], NT)

    @pl.when((step >= attention + chunks) & (step < final))
    def inputs():
        clip = step - (attention + chunks)
        at = pl.ds(pl.multiple_of(clip * rows, rows), rows)
        grad = acc[at]
        unit, inverse = center_scale(tok_ref[0].astype(f32))
        result = gmid_ref[0] + norm_back(unit, inverse, gain_ref[...], grad)
        gtok_ref[0] = result[:slots]
        vec_sum[0, 0:1] += column_sums(grad * unit)
        vec_sum[0, 1:2] += column_sums(grad)

    @pl.when(step == final)
    def finish():
        vec_copy(0).start()
        rest = [action for at in sorted(events) if at >= final for action in events[at]]
        hops = [functools.partial(vec_end, hop) for hop in range(bits + 2)]
        while rest or hops:
            if hops:
                hops.pop(0)()
            if rest:
                rest.pop(0)()
        for a, (name, at, r, width_a, _, _) in enumerate(arrays):
            for who in range(2):
                value = full_bufs[a][who]
                if name == "fc1":
                    start = who * fc1_out.shape[1] // 2 + at
                    fc1_out[:, start : start + width_a] = value
                elif name == "fc2":
                    fc2_out[at : at + r, who * width_a : (who + 1) * width_a] = value
                elif name == "proj":
                    proj_out[:, who * width_a : (who + 1) * width_a] = value
                else:
                    for part in range(3):
                        start = part * width + (2 * at + who) * lanes
                        qkv_out[:, start : start + lanes] = value[:, part * lanes : (part + 1) * lanes]
        vec_out[...] = vec_sum[bits + 2]
        for a in range(count):
            for stage in range(bits + 4):
                stage_copy(a, stage).wait_send()
        for p in range(pairs):
            if p >= pairs - 2:
                kv_core(p).wait_send()
            kv_vert(p).wait_send()
        for hop in range(bits + 2):
            vec_copy(hop).wait_send()


def backward(q, k, v, mask, mixed, lse, gmixed, normed, qkv_weight, tok, gmid, gain, small, db1,
             dfc1, dfc2, dproj, slots, clip_size):
    clips, rows, width = q.shape
    keys = k.shape[1]
    total = clips * rows
    pairs = HEADS // 2
    lanes = 2 * DH
    chunks = pairs // 2
    bits = clip_size.bit_length() - 1
    hidden = db1.shape[1]
    arrays = sum_arrays(width, hidden, clip_size, chunks)
    attention = pairs * clips
    steps = attention + chunks + clips + 1
    one = pl.Buffered(buffer_count=1)

    def of_pair(s):
        at = jnp.minimum(s, attention - 1)
        return at % clips, 0, at // clips

    def of_clip(s):
        return jnp.clip(s - attention - chunks, 0, clips - 1), 0, 0

    fixed = lambda shape: pl.BlockSpec(shape, lambda s: (0,) * len(shape), pipeline_mode=one)
    tok_pair = pl.BlockSpec((1, rows, lanes), of_pair)
    key_pair = pl.BlockSpec((1, keys, lanes), of_pair)
    tok_clip = pl.BlockSpec((1, rows, width), of_clip)
    anywhere = pl.BlockSpec(memory_space=pl.ANY)
    blocks = (2,) * bits
    r_fc1, r_fc2 = width // clip_size, hidden // clip_size
    dfc1 = dfc1.reshape((2,) + blocks + (r_fc1, hidden // 2))
    dfc2 = dfc2.reshape((2,) + blocks + (r_fc2, width // 2))
    dproj = dproj.reshape((2,) + blocks + (r_fc1, width // 2))
    vmem = lambda *shape: pltpu.VMEM(shape, bf16)
    scratch = [
        vmem(pairs, total, lanes),
        vmem(pairs, 2, clips, rows, lanes),
        vmem(pairs, 2, clips, rows, lanes),
        vmem(2, 2, 2, clips, rows, lanes),
        vmem(2, 2, 2, clips, rows, lanes),
        vmem(pairs, 2, clips, rows, lanes),
        vmem(chunks, 2, *blocks, r_fc1, 3 * lanes),
        pltpu.VMEM((total, width), f32),
        pltpu.VMEM((bits + 3, 16, width), f32),
        pltpu.VMEM((bits + 2, 16, width), f32),
        vmem(*blocks, r_fc1, hidden // 4),
        vmem(*blocks, r_fc2 // 2, width // 2),
        vmem(*blocks, r_fc1, width // 2),
    ]
    for _, _, r, width_a, _, _ in arrays:
        scratch += [vmem(*((2,) * (bits - stage)), r, width_a) for stage in range(bits + 1)]
    scratch += [vmem(r // 2, width_a) for _, _, r, width_a, _, _ in arrays]
    scratch += [vmem(2, r, width_a) for _, _, r, width_a, _, _ in arrays]
    dma = lambda *shape: pltpu.SemaphoreType.DMA(shape)
    scratch += [
        dma(2, pairs), dma(2, pairs), dma(len(arrays), bits + 4), dma(len(arrays), bits + 4),
        dma(len(arrays)), dma(bits + 2), dma(bits + 2),
    ]
    return pl.pallas_call(
        functools.partial(backward_kernel, (clips, slots, rows, bits, pairs, arrays)),
        grid=(steps,),
        in_specs=[
            tok_pair, key_pair, key_pair,
            pl.BlockSpec((1, 1, keys), lambda s: (of_pair(s)[0], 0, 0)),
            tok_pair, tok_pair, tok_pair,
            fixed((total, width)), fixed(qkv_weight.shape), tok_clip, tok_clip,
            fixed((1, width)), fixed((8, width)), fixed((1, hidden)),
            anywhere, anywhere, anywhere,
        ],
        out_specs=[
            pl.BlockSpec((1, slots, width), of_clip),
            fixed((r_fc1, hidden)), fixed((r_fc2, width)), fixed((r_fc1, width)),
            fixed((r_fc1, 3 * width)), fixed((16, width)),
        ],
        out_shape=[
            jax.ShapeDtypeStruct((clips, slots, width), f32),
            jax.ShapeDtypeStruct((r_fc1, hidden), bf16),
            jax.ShapeDtypeStruct((r_fc2, width), bf16),
            jax.ShapeDtypeStruct((r_fc1, width), bf16),
            jax.ShapeDtypeStruct((r_fc1, 3 * width), bf16),
            jax.ShapeDtypeStruct((16, width), f32),
        ],
        scratch_shapes=scratch,
        compiler_params=params(collective_id=1, has_side_effects=True),
        cost_estimate=pl.CostEstimate(
            flops=2 * total * (5 * keys * width + 6 * width * width),
            bytes_accessed=60_000_000,
            transcendentals=total * keys * HEADS,
        ),
        name="backward",
    )(q, k, v, mask, mixed, lse, gmixed, normed, qkv_weight, tok, gmid, gain, small, db1, dfc1, dfc2, dproj)


def attend_back_kernel(q_ref, k_ref, v_ref, mask_ref, mixed_ref, lse_ref, grad_ref,
                       dq_ref, dkeep_ref, dsend_ref):
    query = q_ref[0]
    keys = k_ref[0]
    values = v_ref[0]
    grad = grad_ref[0]
    live = mask_ref[0] > 0.5
    product = grad.astype(f32) * mixed_ref[0].astype(f32)
    dqs, dk, dv = [], None, None
    for head in range(2):
        own_query = only(query, head)
        own_grad = only(grad, head)
        scores = jnp.where(live, dot(own_query, keys, NT), MASKED)
        probs = jnp.exp(scores - lse_ref[0, :, head * DH : head * DH + 1])
        delta = jnp.sum(only(product, head), axis=1, keepdims=True)
        dscores = (probs * (dot(own_grad, values, NT) - delta)).astype(bf16)
        dqs.append(dot(dscores, keys))
        more_k = dot(dscores, own_query, TN)
        more_v = dot(probs.astype(bf16), own_grad, TN)
        dk = more_k if dk is None else dk + more_k
        dv = more_v if dv is None else dv + more_v
    first = own_lanes(dqs[0].shape, 0)
    dq_ref[0] = (jnp.where(first, dqs[0], dqs[1]) * DH ** -0.5).astype(bf16)
    half = dk.shape[0] // 2
    dkeep_ref[0, 0] = dk[:half].astype(bf16)
    dkeep_ref[1, 0] = dv[:half].astype(bf16)
    dsend_ref[0, 0] = dk[half:].astype(bf16)
    dsend_ref[1, 0] = dv[half:].astype(bf16)


def attend_back(q, k, v, mask, mixed, lse, grad, first_pair, pairs):
    clips, rows, _ = q.shape
    keys = k.shape[1]
    lanes = 2 * DH
    tok = pl.BlockSpec((1, rows, lanes), lambda c, p: (c, 0, first_pair + p))
    key = pl.BlockSpec((1, keys, lanes), lambda c, p: (c, 0, first_pair + p))
    part = pl.BlockSpec((2, 1, keys // 2, lanes), lambda c, p: (0, c, 0, p))
    return pl.pallas_call(
        attend_back_kernel,
        grid=(clips, pairs),
        in_specs=[tok, key, key, pl.BlockSpec((1, 1, keys), lambda c, p: (c, 0, 0)), tok, tok, tok],
        out_specs=[pl.BlockSpec((1, rows, lanes), lambda c, p: (c, 0, p)), part, part],
        out_shape=[
            jax.ShapeDtypeStruct((clips, rows, pairs * lanes), bf16),
            jax.ShapeDtypeStruct((2, clips, keys // 2, pairs * lanes), bf16),
            jax.ShapeDtypeStruct((2, clips, keys // 2, pairs * lanes), bf16),
        ],
        compiler_params=params(),
        cost_estimate=pl.CostEstimate(
            flops=4 * 10 * clips * rows * keys * pairs * lanes,
            bytes_accessed=clips * pairs * lanes * (keys * 10 + rows * 12),
            transcendentals=clips * rows * keys * 2 * pairs,
        ),
        name="attend_back",
    )(q, k, v, mask, mixed, lse, grad)


def weight_kernel(normed_ref, dq_ref, dk0_ref, dk1_ref, dk2_ref, out_ref, dkv_ref, sums_ref):
    part = pl.program_id(0)
    @pl.when(part == 0)
    def query():
        grad = dq_ref[...]
        out_ref[0] = dot(normed_ref[...], grad, TN).astype(bf16)
        sums_ref[0] = column_sums(grad.astype(f32))
        dkv_ref[0] = jnp.zeros_like(dkv_ref[0])

    @pl.when(part > 0)
    def other():
        grad = (dk0_ref[0].astype(f32) + dk1_ref[0].astype(f32) + dk2_ref[0].astype(f32)).astype(bf16)
        dkv_ref[0] = grad
        out_ref[0] = dot(normed_ref[...], grad, TN).astype(bf16)
        sums_ref[0] = column_sums(grad.astype(f32))


def weight_grads(normed, dq, parts):
    total, width = normed.shape
    lanes = dq.shape[1]
    before = lambda j: (jnp.maximum(j - 1, 0), 0, 0)
    part = pl.BlockSpec((1, total, lanes), before)
    return pl.pallas_call(
        weight_kernel,
        grid=(3,),
        in_specs=[full((total, width)), full((total, lanes)), part, part, part],
        out_specs=[
            pl.BlockSpec((1, width, lanes), lambda j: (j, 0, 0)),
            part,
            pl.BlockSpec((1, 1, lanes), lambda j: (j, 0, 0)),
        ],
        out_shape=[
            jax.ShapeDtypeStruct((3, width, lanes), bf16),
            jax.ShapeDtypeStruct((2, total, lanes), bf16),
            jax.ShapeDtypeStruct((3, 1, lanes), f32),
        ],
        compiler_params=params(),
        cost_estimate=pl.CostEstimate(
            flops=6 * total * width * lanes, bytes_accessed=8_000_000, transcendentals=0
        ),
        name="weight_grads",
    )(normed, dq, *parts)


def input_kernel(counts, groups, *refs):
    clips, slots, rows = counts
    dqs = refs[:groups]
    dkvs = refs[groups : 2 * groups]
    qkv_ref, tok_ref, gmid_ref, gain_ref, shift_ref, out_ref, small_ref = refs[2 * groups :]
    clip = pl.program_id(0)
    width = tok_ref.shape[-1]
    lanes = width // groups
    grad = None
    for group in range(groups):
        for part in range(3):
            rows_grad = dqs[group][0] if part == 0 else dkvs[group][part - 1]
            at = part * width + group * lanes
            more = dot(rows_grad, qkv_ref[:, at : at + lanes], NT)
            grad = more if grad is None else grad + more
    unit, inverse = center_scale(tok_ref[0].astype(f32))
    result = gmid_ref[0] + norm_back(unit, inverse, gain_ref[...], grad)
    out_ref[0] = result[:slots]

    @pl.when(clip == 0)
    def start():
        small_ref[...] = jnp.zeros_like(small_ref)

    small_ref[0:1] += column_sums(grad * unit)
    small_ref[1:2] += column_sums(grad)


def input_grads(dqs, dkvs, qkv_weight, tokens, gmid, gain, shift, slots):
    clips, rows, width = tokens.shape
    groups = len(dqs)
    lanes = width // groups
    tok = pl.BlockSpec((1, rows, width), lambda c: (c, 0, 0))
    return pl.pallas_call(
        functools.partial(input_kernel, (clips, slots, rows), groups),
        grid=(clips,),
        in_specs=[pl.BlockSpec((1, rows, lanes), lambda c: (c, 0, 0))] * groups
        + [pl.BlockSpec((2, rows, lanes), lambda c: (0, c, 0))] * groups
        + [full(qkv_weight.shape), tok, tok, full((1, width)), full((1, width))],
        out_specs=[pl.BlockSpec((1, slots, width), lambda c: (c, 0, 0)), full((8, width))],
        out_shape=[
            jax.ShapeDtypeStruct((clips, slots, width), f32),
            jax.ShapeDtypeStruct((8, width), f32),
        ],
        compiler_params=params(),
        cost_estimate=pl.CostEstimate(
            flops=6 * clips * rows * width * width, bytes_accessed=16_000_000, transcendentals=0
        ),
        name="input_grads",
    )(*dqs, *dkvs, qkv_weight, tokens, gmid, gain, shift)


def swap_bit(array, axis, size, bit):
    return lax.ppermute(array, axis, [(i, i ^ (1 << bit)) for i in range(size)])


def add_low(left, right):
    return (left.astype(f32) + right.astype(f32)).astype(bf16)


def pick(array, index, dim):
    return lax.dynamic_index_in_dim(array, index, dim, keepdims=False)


def bit_of(axis, bit):
    return (lax.axis_index(axis) >> bit) & 1


def scatter_sum(split, clip_size, order):
    core = bit_of("freq", 0)
    vert = bit_of("freq", 1)
    bits = clip_size.bit_length() - 1
    lanes = split.shape[-1]
    value = add_low(pick(split, core, 0), swap_bit(pick(split, 1 - core, 0), "freq", 4, 0))
    rows = value.shape[0] // (2 * clip_size)
    value = value.reshape((2,) * bits + (2, rows, lanes))
    left = list(range(bits))[::-1]
    for bit in order:
        at = left.index(bit)
        mine = bit_of("clip", bit)
        value = add_low(
            pick(value, mine, at), swap_bit(pick(value, 1 - mine, at), "clip", clip_size, bit)
        )
        left.remove(bit)
    return add_low(pick(value, vert, 0), swap_bit(pick(value, 1 - vert, 0), "freq", 4, 1))


def gather_low(part):
    core = bit_of("freq", 0)
    vert = bit_of("freq", 1)
    other = swap_bit(part, "freq", 4, 1)
    tall = jnp.where(vert == 0, jnp.concatenate([part, other]), jnp.concatenate([other, part]))
    side = swap_bit(tall, "freq", 4, 0)
    return jnp.where(
        core == 0,
        jnp.concatenate([tall, side], axis=1),
        jnp.concatenate([side, tall], axis=1),
    ).astype(f32)


def total_sum(array, clip_size):
    for bit in range(2):
        array = array + swap_bit(array, "freq", 4, bit)
    for bit in range(clip_size.bit_length() - 1):
        array = array + swap_bit(array, "clip", clip_size, bit)
    return array


def on_device(
    clip_size, tokens, kept_counts, attn_gain, attn_shift, qkv_weight, query_bias, value_bias,
    proj_weight, proj_bias, mlp_gain, mlp_shift, fc1_weight, fc1_bias, fc2_weight, fc2_bias, cotangent,
):
    clips, slots, width = tokens.shape
    rows = -(-slots // 16) * 16
    total = clips * rows
    bits = clip_size.bit_length() - 1
    forward_order = list(range(bits))
    second_order = forward_order[1:2] + forward_order[:1] + forward_order[2:]
    pad = ((0, 0), (0, rows - slots), (0, 0))
    vec = lambda v: v.astype(f32)[None, :]
    slot_ids = jnp.arange(rows, dtype=jnp.int32)
    live = (slot_ids[None, :] < kept_counts).astype(f32).reshape(total, 1)
    kept = (kept_counts - slots // 2).astype(bf16)
    tok = jnp.concatenate(
        [tokens, jnp.broadcast_to(kept[:, :, None], (clips, rows - slots, width))], axis=1
    )
    stacked = jnp.stack(
        [query_bias, value_bias, attn_gain, attn_shift, proj_bias, mlp_gain, mlp_shift, fc2_bias]
    ).astype(f32)
    vectors = [stacked[i : i + 1] for i in range(7)]
    q, k, v, normed, mixed, lse, middle, normed2, mask = forward(
        tok, slots, qkv_weight, vectors, proj_weight
    )
    flat = lambda a: a.reshape(total, width)
    cot = jnp.pad(cotangent, pad)
    layer_out, dfc1, dfc2, dproj, db1, small2, gmid, gmixed = mlp(
        flat(normed2), flat(middle), flat(cot), live, flat(mixed), fc1_weight, vec(fc1_bias),
        fc2_weight, vec(fc2_bias), vectors[5], vectors[6], proj_weight, (clips, slots, rows),
    )
    if clip_size == 8 and width % (32 * clip_size) == 0:
        grad_tokens, low_fc1, low_fc2, low_proj, low_qkv, summed = backward(
            q, k, v, mask, mixed, lse, gmixed.reshape(clips, rows, width), flat(normed), qkv_weight, tok,
            gmid.reshape(clips, rows, width), vectors[2], small2, db1, dfc1, dfc2, dproj, slots, clip_size,
        )
        return (
            layer_out, grad_tokens, summed[0], summed[1], low_qkv.astype(f32), summed[2], summed[3],
            low_proj.astype(f32), summed[7], summed[4], summed[5], low_fc1.astype(f32),
            summed[8:12].reshape(-1), low_fc2.astype(f32), summed[6],
        )
    early = total_sum(jnp.concatenate([small2[:4].reshape(-1), db1.reshape(-1)])[None, :], clip_size)[0]
    sum_fc1 = gather_low(scatter_sum(dfc1, clip_size, forward_order))
    sum_fc2 = gather_low(scatter_sum(dfc2, clip_size, second_order))
    sum_proj = gather_low(scatter_sum(dproj, clip_size, forward_order))

    groups = 3
    pairs = HEADS // 2 // groups
    lanes = pairs * 2 * DH
    gmixed = gmixed.reshape(clips, rows, width)
    dqs, dkvs, sums, sharded = [], [], [], []
    for group in range(groups):
        dq, keep, send = attend_back(q, k, v, mask, mixed, lse, gmixed, group * pairs, pairs)
        got = swap_bit(send, "freq", 4, 0)
        across = swap_bit(add_low(keep[:, :, rows:], got[:, :, rows:]), "freq", 4, 1)
        parts = [a.reshape(2, total, lanes) for a in (keep[:, :, :rows], got[:, :, :rows], across)]
        dw, dkv, colsum = weight_grads(flat(normed), dq.reshape(total, lanes), parts)
        half = lanes // 2
        split = jnp.stack(
            [
                jnp.concatenate([dw[i, :, s * half : (s + 1) * half] for i in range(3)], axis=1)
                for s in range(2)
            ]
        )
        order = forward_order if group % 2 == 0 else second_order
        summed = gather_low(scatter_sum(split, clip_size, order))
        sharded.append(summed.reshape(summed.shape[0], 2, 3, half))
        dqs.append(dq)
        dkvs.append(dkv)
        sums.append(colsum)
    grad_tokens, small1 = input_grads(
        dqs, dkvs, qkv_weight, tok, gmid.reshape(clips, rows, width), vectors[2], vectors[3], slots
    )
    qkv = jnp.stack(sharded, axis=1)
    sum_qkv = qkv.transpose(0, 3, 1, 2, 4).reshape(qkv.shape[0], 3 * width)
    bias = jnp.concatenate(sums, axis=2)
    late = total_sum(
        jnp.concatenate([small1[0:1], small1[1:2], bias[0], bias[2]], axis=1), clip_size
    )[0]
    cut = lambda a, i: a[i * width : (i + 1) * width]
    return (
        layer_out, grad_tokens, cut(late, 0), cut(late, 1), sum_qkv, cut(late, 2), cut(late, 3),
        sum_proj, cut(early, 3), cut(early, 0), cut(early, 1), sum_fc1, early[4 * width :],
        sum_fc2, cut(early, 2),
    )


def solution(mesh):
    rows = P("clip", "freq", None)
    shard = P("clip", None)
    return jax.shard_map(
        functools.partial(on_device, mesh.shape["clip"]),
        mesh=mesh,
        in_specs=(rows, P("clip", "freq")) + (P(),) * 13 + (rows,),
        out_specs=(rows, rows, P(), P(), shard, P(), P(), shard, P(), P(), P(), shard, P(), shard, P()),
        check_vma=False,
    )
```

```python
import functools
import math

import jax
import jax.numpy as jnp
from jax import lax
from jax.experimental import pallas as pl
from jax.experimental.pallas import tpu as pltpu
from jax.sharding import PartitionSpec as P

HEADS = 12
DH = 64
EPS = 1e-06
MASKED = -1000000000.0
VMEM_BYTES = 60 * 1024 * 1024

f32 = jnp.float32
bf16 = jnp.bfloat16
NN = (((1,), (0,)), ((), ()))
NT = (((1,), (1,)), ((), ()))
TN = (((0,), (0,)), ((), ()))


def dot(left, right, dims=NN):
    return lax.dot_general(left, right, dims, preferred_element_type=f32)


def center_scale(rows):
    center = rows - jnp.mean(rows, axis=-1, keepdims=True)
    inverse = lax.rsqrt(jnp.mean(center * center, axis=-1, keepdims=True) + EPS)
    return center * inverse, inverse


def norm_back(unit, inverse, gain, grad):
    scaled = grad * gain
    return inverse * (
        scaled
        - jnp.mean(scaled, axis=-1, keepdims=True)
        - unit * jnp.mean(scaled * unit, axis=-1, keepdims=True)
    )


def column_sums(rows):
    return jnp.sum(rows, axis=0, keepdims=True)


def own_lanes(shape, head):
    lane = lax.broadcasted_iota(jnp.int32, shape, len(shape) - 1)
    return lane < DH if head == 0 else lane >= DH


def only(rows, head):
    return jnp.where(own_lanes(rows.shape, head), rows, jnp.zeros_like(rows))


def full(shape):
    return pl.BlockSpec(shape, lambda *ids: (0,) * len(shape))


def params(**more):
    return pltpu.CompilerParams(vmem_limit_bytes=VMEM_BYTES, **more)


def freq_places():
    freq = lax.axis_index("freq")
    core, vert = freq % 2, freq // 2
    return core, vert, {"freq": freq + 1 - 2 * core}, {"freq": (freq + 2) % 4}


def lane_slice(start, size):
    return pl.ds(pl.multiple_of(start, 2 * DH), size)


def row_of(ref):
    return ref[...].astype(f32).reshape(1, ref.shape[0])


def forward_kernel(
    counts,
    kept_ref, tok_ref, qkv_ref, qb_ref, vb_ref, gain_ref, shift_ref, proj_ref, pb_ref, gain2_ref, shift2_ref,
    q_ref, k_ref, v_ref, normed_ref, part_ref, lse_ref, mask_ref, weight_ref, mixed_ref, middle_ref, normed2_ref,
    own, held, mix_send, mix_got, vecs, tok_send, tok_recv, part_send, part_recv,
):
    clips, slots, rows, pairs = counts
    clip = pl.program_id(0)
    pair = pl.program_id(1)
    width = tok_ref.shape[-1]
    half = width // 2
    lanes = 2 * DH
    core, vert, core_dev, vert_dev = freq_places()
    mesh_id = pl.DeviceIdType.MESH

    def copy(kind, index):
        at = {"vert": 0, "core": 1, "diag": 2}[kind]
        return pltpu.make_async_remote_copy(
            src_ref=held.at[index, 0] if kind == "diag" else own.at[index],
            dst_ref=held.at[index, at],
            send_sem=tok_send.at[index, at],
            recv_sem=tok_recv.at[index, at],
            device_id=vert_dev if kind == "vert" else core_dev,
            device_id_type=mesh_id,
        )

    def mix_copy(index, which):
        return pltpu.make_async_remote_copy(
            src_ref=mix_send.at[index, which],
            dst_ref=mix_got.at[index, which],
            send_sem=part_send.at[index, which],
            recv_sem=part_recv.at[index, which],
            device_id=vert_dev,
            device_id_type=mesh_id,
        )

    def project(slot, source):
        unit, _ = center_scale(source.astype(f32))
        normed = (unit * vecs[2:3] + vecs[3:4]).astype(bf16)
        at = slice(slot * rows, (slot + 1) * rows)
        if slot < 2:
            normed_ref[0, at] = normed
            query = (dot(normed, weight_ref[:, :half]) + vecs[0:1, lane_slice(vert * half, half)]).astype(bf16)
            q_ref[0, at] = query * jnp.asarray(DH ** -0.5, bf16)
        both = dot(normed, weight_ref[:, half:])
        k_ref[0, at] = both[:, :half].astype(bf16)
        v_ref[0, at] = (both[:, half:] + vecs[1:2, lane_slice(vert * half, half)]).astype(bf16)
        first = (slots // 16) * 16
        kept = source[first:].astype(f32)[slots - first : slots - first + 1, 0:1] + slots // 2
        lane = lax.broadcasted_iota(jnp.int32, (1, rows), 1).astype(f32)
        return (lane < kept).astype(f32)

    def pass_on(index):
        copy("vert", index).wait_recv()
        copy("diag", index).start()
        copy("vert", index).wait_send()

        @pl.when(index + 1 < clips)
        def more():
            copy("vert", index + 1).start()

    @pl.when((clip == 0) & (pair == 0))
    def enter():
        barrier = pltpu.get_barrier_semaphore()
        for device in (vert_dev, core_dev):
            pl.semaphore_signal(barrier, inc=1, device_id=device, device_id_type=mesh_id)
        first = (slots // 16) * 16
        for index in range(clips):
            kept = (kept_ref[index, 0] - slots // 2).astype(f32).astype(bf16)
            own[index, first:] = jnp.broadcast_to(kept, (rows - first, width))
            own[index, :slots] = tok_ref[index]
        pl.semaphore_wait(barrier, 2)
        copy("vert", 0).start()
        for index in range(clips):
            copy("core", index).start()
        for i, ref in enumerate((qb_ref, vb_ref, gain_ref, shift_ref, pb_ref, gain2_ref, shift2_ref)):
            vecs[i : i + 1] = row_of(ref)
        for part in range(3):
            weight_ref[:, part * half : (part + 1) * half] = qkv_ref[:, lane_slice(part * width + vert * half, half)]

    @pl.when(pair == 0)
    def project_all():
        live_own = project(0, own[clip])
        copy("core", clip).wait_recv()
        live_core = project(2, held[clip, 1])

        @pl.when(clip == 0)
        def first_pass():
            pass_on(clip)

        live_vert = project(1, held[clip, 0])
        copy("diag", clip).wait_recv()
        live_diag = project(3, held[clip, 2])
        mask_ref[0] = jnp.concatenate([live_own, live_vert, live_core, live_diag], axis=1)

    @pl.when((pair == 1) & (clip + 1 < clips))
    def next_pass():
        pass_on(clip + 1)

    def finish(index):
        at = lane_slice(vert * half, half)
        mixed_ref[0, :, at] = mix_own_of(index)
        for which in range(pairs):
            mix_copy(index, which).wait_recv()
            at = lane_slice((1 - vert) * half + which * lanes, lanes)
            mixed_ref[0, :, at] = mix_got[index, which]
        middle = own[index].astype(f32) + (dot(mixed_ref[0], proj_ref[...]) + vecs[4:5])
        middle_ref[0] = middle
        unit, _ = center_scale(middle)
        normed2_ref[0] = (unit * vecs[5:6] + vecs[6:7]).astype(bf16)
        copy("core", index).wait_send()
        copy("diag", index).wait_send()
        for which in range(pairs):
            mix_copy(index, which).wait_send()

    def mix_own_of(index):
        return jnp.concatenate([mix_send[index, pairs + which] for which in range(pairs)], axis=1)

    here = lane_slice(pair * lanes, lanes)
    keys = k_ref[0, :, here]
    values = v_ref[0, :, here]
    live = mask_ref[0] > 0.5
    for slot in (1, 0):
        at = slice(slot * rows, (slot + 1) * rows)
        query = q_ref[0, at, here]
        outs, lses = [], []
        for head in range(2):
            scores = jnp.where(live, dot(only(query, head), keys, NT), MASKED)
            top = jnp.max(scores, axis=1, keepdims=True)
            exps = jnp.exp(scores - top)
            total = jnp.sum(exps, axis=1, keepdims=True)
            outs.append(dot(exps.astype(bf16), values) / total)
            lses.append(top + jnp.log(total))
        first = own_lanes(outs[0].shape, 0)
        mixed = jnp.where(first, outs[0], outs[1]).astype(bf16)
        part_ref[0, at, here] = mixed
        lse_ref[0, at, here] = jnp.where(first, lses[0], lses[1])
        if slot == 1:
            mix_send[clip, pair] = mixed
            mix_copy(clip, pair).start()
        else:
            mix_send[clip, pairs + pair] = mixed

    last = pairs - 1
    for index in range(clips):
        when = (clip == index) & (pair == last) if index == clips - 1 else (clip == index + 1) & (pair == 1)

        @pl.when(when)
        def finish_clip(index=index):
            finish(index)


def forward(kept, tokens, rows, qkv_weight, query_bias, value_bias, gain, shift, proj_weight, proj_bias, gain2, shift2):
    clips, slots, width = tokens.shape
    keys = 4 * rows
    half = width // 2
    pairs = HEADS // 4
    lanes = 2 * DH
    one = pl.Buffered(buffer_count=1)
    block = lambda n, m: pl.BlockSpec((1, n, m), lambda c, p: (c, 0, 0))
    late = lambda n, m: pl.BlockSpec(
        (1, n, m),
        lambda c, p: (jnp.where((c == clips - 1) & (p == pairs - 1), c, jnp.maximum(c - 1, 0)), 0, 0),
    )
    whole = lambda a: pl.BlockSpec(a.shape, lambda c, p: (0,) * a.ndim, pipeline_mode=one)
    shape = jax.ShapeDtypeStruct
    flops = 2 * clips * (rows * width * width * 6 + 2 * rows * keys * width)
    vectors = (query_bias, value_bias, gain, shift)
    return pl.pallas_call(
        functools.partial(forward_kernel, (clips, slots, rows, pairs)),
        grid=(clips, pairs),
        in_specs=[pl.BlockSpec(memory_space=pltpu.SMEM), whole(tokens), whole(qkv_weight)]
        + [whole(v) for v in vectors]
        + [whole(proj_weight)]
        + [whole(v) for v in (proj_bias, gain2, shift2)],
        out_specs=[
            block(2 * rows, half), block(keys, half), block(keys, half), block(2 * rows, width),
            block(2 * rows, half), block(2 * rows, half), block(1, keys),
            pl.BlockSpec((width, 3 * half), lambda c, p: (0, 0), pipeline_mode=one),
            late(rows, width), late(rows, width), late(rows, width),
        ],
        out_shape=[
            shape((clips, 2 * rows, half), bf16),
            shape((clips, keys, half), bf16),
            shape((clips, keys, half), bf16),
            shape((clips, 2 * rows, width), bf16),
            shape((clips, 2 * rows, half), bf16),
            shape((clips, 2 * rows, half), f32),
            shape((clips, 1, keys), f32),
            shape((width, 3 * half), bf16),
            shape((clips, rows, width), bf16),
            shape((clips, rows, width), f32),
            shape((clips, rows, width), bf16),
        ],
        scratch_shapes=[
            pltpu.VMEM((clips, rows, width), bf16),
            pltpu.VMEM((clips, 3, rows, width), bf16),
            pltpu.VMEM((clips, 2 * pairs, rows, lanes), bf16),
            pltpu.VMEM((clips, pairs, rows, lanes), bf16),
            pltpu.VMEM((8, width), f32),
            pltpu.SemaphoreType.DMA((clips, 3)),
            pltpu.SemaphoreType.DMA((clips, 3)),
            pltpu.SemaphoreType.DMA((clips, pairs)),
            pltpu.SemaphoreType.DMA((clips, pairs)),
        ],
        compiler_params=params(collective_id=0, has_side_effects=True),
        cost_estimate=pl.CostEstimate(
            flops=flops, bytes_accessed=40_000_000, transcendentals=clips * rows * keys * HEADS
        ),
        name="forward",
    )(kept, tokens, qkv_weight, *vectors, proj_weight, proj_bias, gain2, shift2)


def mlp_kernel(
    counts,
    kept_ref, n2_ref, middle_ref, cot_ref, mixed_ref, fc1_ref, b1_ref, fc2_ref, b2_ref, gain_ref, proj_ref,
    out_ref, dfc1_ref, dfc2_ref, dproj_ref, db1_ref, small_ref, gmid_ref, gmixed_ref,
    n2t_ref, grad_ref, out_acc, dn_acc, hidden_ref, dact_ref, active_ref, dhid_ref, biases,
):
    clips, slots, rows, tile = counts
    step = pl.program_id(0)
    width = n2_ref.shape[-1]
    chunk = fc1_ref.shape[-1]
    total = clips * rows

    def live_rows(clip, size):
        slot = lax.broadcasted_iota(jnp.int32, (size, 1), 0)
        return (slot < kept_ref[clip, 0]).astype(f32)

    @pl.when(step == 0)
    def start():
        n2t_ref[...] = n2_ref[...].T
        first = (slots // 16) * 16
        for clip in range(clips):
            begin = clip * rows
            grad_ref[begin + first : begin + rows] = jnp.zeros((rows - first, width), bf16)
            grad_ref[begin : begin + slots] = cot_ref[clip] * live_rows(clip, slots).astype(bf16)
        all_biases = row_of(b1_ref)
        for i in range(all_biases.shape[1] // chunk):
            biases[i : i + 1] = all_biases[:, i * chunk : (i + 1) * chunk]
        out_acc[...] = jnp.zeros_like(out_acc)
        dn_acc[...] = jnp.zeros_like(dn_acc)

    hidden_ref[...] = dot(n2_ref[...], fc1_ref[...])
    dact_ref[...] = dot(grad_ref[...], fc2_ref[...], NT)
    bias = biases[pl.ds(step, 1), :]

    def gelu_tile(index, sums):
        at = pl.ds(pl.multiple_of(index * tile, tile), tile)
        hidden = hidden_ref[at, :] + bias
        cdf = 0.5 * (1.0 + lax.erf(hidden * (0.5 ** 0.5)))
        active_ref[at, :] = (hidden * cdf).astype(bf16)
        slope = cdf + hidden * (jnp.exp(-0.5 * hidden * hidden) * (1.0 / math.sqrt(2.0 * math.pi)))
        dhid = (dact_ref[at, :] * slope).astype(bf16)
        dhid_ref[at, :] = dhid
        return sums + dhid.astype(f32)

    sums = lax.fori_loop(0, total // tile, gelu_tile, jnp.zeros((tile, chunk), f32))
    db1_ref[...] = column_sums(sums)
    active = active_ref[...]
    dhid = dhid_ref[...]
    out_acc[...] += dot(active, fc2_ref[...])
    dn_acc[...] += dot(dhid, fc1_ref[...], NT)
    dfc1_ref[0] = dot(n2t_ref[...], dhid).astype(bf16)
    dfc2 = dot(active, grad_ref[...], TN).astype(bf16)
    half = width // 2
    dfc2_ref[0] = dfc2[:, :half]
    dfc2_ref[1] = dfc2[:, half:]

    @pl.when(step == pl.num_programs(0) - 1)
    def finish():
        gain = row_of(gain_ref)
        bias2 = row_of(b2_ref)
        sum_gain = jnp.zeros((1, width), f32)
        sum_shift = jnp.zeros((1, width), f32)
        sum_grad = jnp.zeros((1, width), f32)
        sum_proj = jnp.zeros((1, width), f32)
        for clip in range(clips):
            at = slice(clip * rows, (clip + 1) * rows)
            middle = middle_ref[at]
            layer = middle[:slots] + (out_acc[clip * rows : clip * rows + slots] + bias2)
            out_ref[clip] = (live_rows(clip, slots) * layer).astype(bf16)
            unit, inverse = center_scale(middle)
            grad = dn_acc[at]
            out_grad = grad_ref[at].astype(f32)
            gmid = out_grad + norm_back(unit, inverse, gain, grad)
            gmid_ref[at] = gmid
            low = gmid.astype(bf16)
            dhid_ref[at, :width] = low
            gmixed_ref[at] = dot(low, proj_ref[...], NT).astype(bf16)
            sum_gain += column_sums(grad * unit)
            sum_shift += column_sums(grad)
            sum_grad += column_sums(out_grad)
            sum_proj += column_sums(low.astype(f32))
        dproj = dot(mixed_ref[...], dhid_ref[:, :width], TN).astype(bf16)
        dproj_ref[0] = dproj[:, :half]
        dproj_ref[1] = dproj[:, half:]
        small_ref[0:1] = sum_gain
        small_ref[1:2] = sum_shift
        small_ref[2:3] = sum_grad
        small_ref[3:4] = sum_proj


def mlp(kept, n2, middle, cot, mixed, fc1, b1, fc2, b2, gain, proj, rows):
    clips, slots, _ = cot.shape
    total, width = n2.shape
    hidden = fc1.shape[1]
    chunk = 768
    steps = hidden // chunk
    half = steps // 2
    tile = 16
    whole = lambda a: pl.BlockSpec(a.shape, lambda j: (0,) * a.ndim, pipeline_mode=one)
    one = pl.Buffered(buffer_count=1)
    big = pl.BlockSpec((total, width), lambda j: (0, 0), pipeline_mode=one)
    return pl.pallas_call(
        functools.partial(mlp_kernel, (clips, slots, rows, tile)),
        grid=(steps,),
        in_specs=[
            pl.BlockSpec(memory_space=pltpu.SMEM),
            big, big, whole(cot), big,
            pl.BlockSpec((width, chunk), lambda j: (0, j)),
            whole(b1),
            pl.BlockSpec((chunk, width), lambda j: (j, 0)),
            whole(b2), whole(gain), whole(proj),
        ],
        out_specs=[
            full((clips, slots, width)),
            pl.BlockSpec((1, width, chunk), lambda j: (j // half, 0, j % half)),
            pl.BlockSpec((2, chunk, width // 2), lambda j: (0, j, 0)),
            full((2, width, width // 2)),
            pl.BlockSpec((1, chunk), lambda j: (0, j)),
            full((8, width)),
            full((total, width)),
            full((total, width)),
        ],
        out_shape=[
            jax.ShapeDtypeStruct((clips, slots, width), bf16),
            jax.ShapeDtypeStruct((2, width, hidden // 2), bf16),
            jax.ShapeDtypeStruct((2, hidden, width // 2), bf16),
            jax.ShapeDtypeStruct((2, width, width // 2), bf16),
            jax.ShapeDtypeStruct((1, hidden), f32),
            jax.ShapeDtypeStruct((8, width), f32),
            jax.ShapeDtypeStruct((total, width), f32),
            jax.ShapeDtypeStruct((total, width), bf16),
        ],
        scratch_shapes=[
            pltpu.VMEM((width, total), bf16),
            pltpu.VMEM((total, width), bf16),
            pltpu.VMEM((total, width), f32),
            pltpu.VMEM((total, width), f32),
            pltpu.VMEM((total, chunk), f32),
            pltpu.VMEM((total, chunk), f32),
            pltpu.VMEM((total, chunk), bf16),
            pltpu.VMEM((total, chunk), bf16),
            pltpu.VMEM((8, chunk), f32),
        ],
        compiler_params=params(),
        cost_estimate=pl.CostEstimate(
            flops=12 * total * width * hidden, bytes_accessed=40_000_000, transcendentals=2 * total * hidden
        ),
        name="mlp",
    )(kept, n2, middle, cot, mixed, fc1, b1, fc2, b2, gain, proj)


def sum_arrays(width, hidden, clip_size):
    rows = width // clip_size
    tall = hidden // clip_size
    first, second = (0, 1, 2), (1, 0, 2)
    cut = 5 * width // 6
    return [
        ("fc1", 0, rows, hidden // 4, first),
        ("fc2", 0, tall // 2, width // 2, second),
        ("fc1", hidden // 4, rows, hidden // 4, first),
        ("fc2", tall // 2, tall // 2, width // 2, second),
        ("proj", 0, rows, width // 2, PROJ_ORDER),
        ("qkv", 0, rows // 2, cut, QKV_ORDERS[0]),
        ("qkv", cut, rows // 2, 3 * width // 2 - cut, QKV_ORDERS[1]),
    ]


PROJ_ORDER = (1, 0, 2)
QKV_ORDERS = ((1, 0, 2), (0, 1, 2))
SUM_STEPS = {
    3: [("end", 4, 0), ("start", 4, 1)],
    4: [("end", 0, 0), ("start", 0, 1), ("end", 1, 0), ("end", 2, 0), ("end", 3, 0)],
    5: [("start", 1, 1)],
    6: [("end", 4, 1)],
    8: [("start", 2, 1)],
    9: [("end", 0, 1), ("start", 0, 2)],
    10: [("end", 1, 1)],
    11: [("start", 3, 1)],
    12: [("end", 0, 2), ("start", 0, 3), ("start", 1, 2)],
    13: [("end", 2, 1)],
    14: [("start", 4, 2)],
    15: [("end", 1, 2), ("start", 1, 3)],
    16: [("end", 0, 3), ("start", 0, 4), ("start", 2, 2), ("end", 4, 2)],
    17: [("start", 4, 3)],
    18: [("end", 3, 1), ("start", 3, 2)],
    19: [("end", 0, 4), ("start", 0, 5), ("end", 1, 3), ("start", 1, 4), ("end", 4, 3),
        ("start", 4, 4)],
    20: [("end", 0, 5), ("end", 2, 2), ("start", 2, 3)],
    21: [("end", 1, 4), ("start", 1, 5), ("end", 3, 2), ("start", 3, 3), ("end", 4, 4),
        ("start", 4, 5)],
    22: [("end", 1, 5), ("end", 4, 5)],
    23: [("end", 6, 0), ("start", 6, 1), ("end", 5, 0), ("start", 5, 1), ("end", 2, 3),
        ("start", 2, 4), ("end", 3, 3), ("start", 3, 4), ("input", 2, 0), ("end", 6, 1),
        ("start", 6, 2), ("end", 2, 4), ("start", 2, 5), ("vec", 0, 0), ("end", 5, 1),
        ("start", 5, 2), ("end", 2, 5), ("end", 3, 4), ("start", 3, 5), ("end", 6, 2),
        ("start", 6, 3), ("vec", 1, 0), ("end", 3, 5), ("end", 5, 2), ("start", 5, 3), ("vec", 2, 0),
        ("end", 6, 3), ("start", 6, 4), ("end", 5, 3), ("start", 5, 4), ("vec", 3, 0), ("end", 6, 4),
        ("start", 6, 5), ("end", 6, 5), ("end", 5, 4), ("start", 5, 5), ("vec", 4, 0), ("end", 5, 5)],
}


def backward_kernel(
    meta,
    q_ref, k_ref, v_ref, mask_ref, part_ref, lse_ref, normed_ref, weight_ref, tok_ref, gmid_ref, gain_ref,
    small_ref, db1_ref, gmixed_ref, dfc1_ref, dfc2_ref, dproj_ref,
    gtok_ref, fc1_out, fc2_out, proj_out, qkv_out, vec_out,
    *scratch,
):
    clips, slots, rows, bits, pairs, arrays = meta
    width = weight_ref.shape[0]
    half = width // 2
    lanes = 2 * DH
    step = pl.program_id(0)
    places = step_places(clips, pairs)
    mesh_id = pl.DeviceIdType.MESH
    count = len(arrays)

    scratch = list(scratch)
    take = lambda n: [scratch.pop(0) for _ in range(n)]
    (grad_all, packed, kv_acc, kv_send, kv_got, acc, dn_send, dn_got, dw_acc, bias_acc, vec_sum, vec_got) = take(12)
    own_bufs = dict(zip(("fc1", "fc2", "proj"), take(3)))
    dw_low = {5: scratch.pop(0), 6: scratch.pop(0)}
    stage_bufs = [take(bits + 1) for _ in arrays]
    vert_bufs = take(5)
    full_bufs = take(count)
    (grad_sem, grad_out, grad_in, kv_out, kv_in, dn_out, dn_in, sum_out, sum_in, own_sem, vec_out_sem, vec_in_sem) = take(12)

    core, vert, core_dev, vert_dev = freq_places()
    place = lax.axis_index("clip")
    bit_at = [(place // 2 ** b) % 2 for b in range(bits)]
    clip_dev = [{"clip": place + (1 - 2 * bit_at[b]) * 2 ** b} for b in range(bits)]

    def remote(src, dst, send, recv, device):
        return pltpu.make_async_remote_copy(
            src_ref=src, dst_ref=dst, send_sem=send, recv_sem=recv, device_id=device, device_id_type=mesh_id
        )

    def grad_own(clip):
        src = gmixed_ref.at[clip, :, lane_slice(vert * half, half)]
        return pltpu.make_async_copy(src, grad_all.at[0, clip], grad_sem.at[clip])

    def grad_vert(clip):
        src = gmixed_ref.at[clip, :, lane_slice((1 - vert) * half, half)]
        return remote(src, grad_all.at[1, clip], grad_out.at[clip], grad_in.at[clip], vert_dev)

    def kv_copy(clip, pair):
        return remote(
            kv_send.at[pair], kv_got.at[clip, pair], kv_out.at[clip, pair], kv_in.at[clip, pair], core_dev
        )

    def dn_copy(clip):
        return remote(dn_send.at[clip], dn_got.at[clip], dn_out.at[clip], dn_in.at[clip], vert_dev)

    every = (slice(None),) * bits

    def piece(a, who):
        name, at, r, width_a, _ = arrays[a]
        if name == "fc1":
            return dfc1_ref.at[(who,) + every + (slice(None), pl.ds(at, width_a))]
        if name == "fc2":
            return dfc2_ref.at[(who,) + every + (pl.ds(at, r), slice(None))]
        if name == "proj":
            return dproj_ref.at[who]
        return dw_low[a].at[who]

    def chosen(a, stage, index_of):
        order = arrays[a][4]
        left = [b for b in range(bits)[::-1] if b not in order[: stage - 1]]
        bit = order[stage - 1]
        at = (slice(None),) * left.index(bit) + (index_of(bit),)
        return stage_bufs[a][stage - 1].at[at]

    def stage_copy(a, stage):
        sems = (sum_out.at[a, stage], sum_in.at[a, stage])
        full, packed_array = full_bufs[a], arrays[a][0] == "qkv"
        if stage == 0:
            return remote(piece(a, 1 - core), stage_bufs[a][0], *sems, core_dev)
        if stage <= bits:
            src = chosen(a, stage, lambda bit: 1 - bit_at[bit])
            return remote(src, stage_bufs[a][stage], *sems, clip_dev[arrays[a][4][stage - 1]])
        if stage == bits + 1:
            dst = full.at[core, vert] if packed_array else vert_bufs[a]
            return remote(stage_bufs[a][bits], dst, *sems, vert_dev)
        return remote(full.at[core], full.at[core], *sems, core_dev)

    def own_copy(a):
        return pltpu.make_async_copy(piece(a, core), own_bufs[arrays[a][0]], own_sem.at[a])

    def add_blocks(dst, src, lead):
        if lead == 0:
            dst[...] = dst[...] + src[...]
            return

        def add_one(i, carry):
            at = tuple((i // 2 ** (lead - 1 - j)) % 2 for j in range(lead))
            dst[at] = dst[at] + src[at]
            return carry

        lax.fori_loop(0, 2 ** lead, add_one, 0)

    def stage_end(a, stage):
        name = arrays[a][0]
        stage_copy(a, stage).wait_recv()
        if stage == 0:
            if name == "qkv":
                add_blocks(stage_bufs[a][0], dw_low[a].at[core], bits)
            else:
                own_copy(a).wait()
                add_blocks(stage_bufs[a][0], own_bufs[name], bits)
                if a + 2 < 4:
                    own_copy(a + 2).start()
        elif stage <= bits:
            add_blocks(stage_bufs[a][stage], chosen(a, stage, lambda bit: bit_at[bit]), bits - stage)
            if stage == bits and name == "qkv":
                full_bufs[a][core, vert] = stage_bufs[a][bits][...]
        elif stage == bits + 1 and name != "qkv":
            full_bufs[a][core] = stage_bufs[a][bits][...] + vert_bufs[a][...]

    def vec_copy(hop):
        device = core_dev if hop == 0 else vert_dev if hop == 1 else clip_dev[hop - 2]
        return remote(vec_sum.at[hop], vec_got.at[hop], vec_out_sem.at[hop], vec_in_sem.at[hop], device)

    def vec_end(hop):
        vec_copy(hop).wait_recv()
        vec_sum[hop + 1] = vec_sum[hop] + vec_got[hop]
        if hop < bits + 1:
            vec_copy(hop + 1).start()

    def perform(action):
        kind, a, stage = action
        if kind == "vec":
            vec_end(a)
        elif kind == "start":
            stage_copy(a, stage).start()
        else:
            stage_end(a, stage)

    @pl.when(step == 0)
    def enter():
        barrier = pltpu.get_barrier_semaphore()
        for clip in range(clips):
            grad_own(clip).start()
        for device in [core_dev, vert_dev] + clip_dev:
            pl.semaphore_signal(barrier, inc=1, device_id=device, device_id_type=mesh_id)
        pl.semaphore_wait(barrier, 2 + bits)
        for clip in range(clips):
            grad_vert(clip).start()
        for a in range(5):
            stage_copy(a, 0).start()
        for a in (0, 1, 4):
            own_copy(a).start()
        vec_sum[0] = jnp.zeros_like(vec_sum[0])
        vec_sum[0, 4:8] = small_ref[0:4]
        for i in range(db1_ref.shape[1] // width):
            vec_sum[0, 8 + i : 9 + i] = db1_ref[0:1, i * width : (i + 1) * width]

    for at in sorted(SUM_STEPS):
        if at < places["end"]:
            @pl.when(step == at)
            def run(at=at):
                for action in SUM_STEPS[at]:
                    perform(action)

    def attend():
        index = attention_index(step, places)
        clip = index // (2 * pairs)
        slot = (index // pairs) % 2
        pair = index % pairs

        @pl.when((pair == 0) & (slot == 0))
        def own_grads():
            grad_own(clip).wait()

        @pl.when((pair == 0) & (slot == 1))
        def vert_grads():
            grad_vert(clip).wait_recv()

        query = q_ref[0]
        keys = k_ref[0]
        values = v_ref[0]
        grad = grad_all[slot, clip, :, lane_slice(pair * lanes, lanes)]
        live = mask_ref[0] > 0.5
        product = grad.astype(f32) * part_ref[0].astype(f32)
        dqs, dk, dv = [], None, None
        for head in range(2):
            own_query = only(query, head)
            own_grad = only(grad, head)
            scores = jnp.where(live, dot(own_query, keys, NT), MASKED)
            probs = jnp.exp(scores - lse_ref[0, :, head * DH : head * DH + 1])
            delta = jnp.sum(only(product, head), axis=1, keepdims=True)
            dscores = (probs * (dot(own_grad, values, NT) - delta)).astype(bf16)
            dqs.append(dot(dscores, keys))
            more_k = dot(dscores, own_query, TN)
            more_v = dot(probs.astype(bf16), own_grad, TN)
            dk = more_k if dk is None else dk + more_k
            dv = more_v if dv is None else dv + more_v
        first = own_lanes(dqs[0].shape, 0)
        dq = (jnp.where(first, dqs[0], dqs[1]) * DH ** -0.5).astype(bf16)
        at = pl.ds(pl.multiple_of(slot * rows, rows), rows)
        packed[clip, at, lane_slice(pair * lanes, lanes)] = dq

        @pl.when(slot == 0)
        def keep():
            kv_acc[pair, 0] = dk
            kv_acc[pair, 1] = dv

        @pl.when(slot == 1)
        def send():
            @pl.when(clip > 0)
            def free():
                kv_copy(clip - 1, pair).wait_send()

            for part, value in enumerate((dk, dv)):
                low = (kv_acc[pair, part] + value).astype(bf16)
                packed[clip, :, lane_slice((part + 1) * half + pair * lanes, lanes)] = low[: 2 * rows]
                kv_send[pair, part] = low[2 * rows :]
            kv_copy(clip, pair).start()

    is_attention = step < places["projections"][-1]
    for at in places["projections"][:-1]:
        is_attention = is_attention & (step != at)
    pl.when(is_attention)(attend)

    for clip in range(clips):
        @pl.when(step == places["projections"][clip])
        def projections(clip=clip):
            for pair in range(pairs):
                kv_copy(clip, pair).wait_recv()
                for part in range(2):
                    at = slice((part + 1) * half + pair * lanes, (part + 1) * half + (pair + 1) * lanes)
                    packed[clip, :, at] = packed[clip, :, at] + kv_got[clip, pair, part]
            grads = packed[clip]
            back = dot(grads, weight_ref[...], NT)
            acc[clip] = back[:rows]
            dn_send[clip] = back[rows:].astype(bf16)
            dn_copy(clip).start()
            more = dot(normed_ref[0], grads, TN)
            sum_q = column_sums(grads[:, :half].astype(f32))
            sum_v = column_sums(grads[:, 2 * half :].astype(f32))
            if clip == 0:
                dw_acc[...] = more
                bias_acc[0:1] = sum_q
                bias_acc[1:2] = sum_v
            elif clip < clips - 1:
                dw_acc[...] += more
                bias_acc[0:1] += sum_q
                bias_acc[1:2] += sum_v
            else:
                low = (dw_acc[...] + more).astype(bf16)
                for a, buf in dw_low.items():
                    _, at, r, width_a, _ = arrays[a]
                    for block in range(2 ** bits):
                        index = tuple((block >> b) & 1 for b in range(bits)[::-1])
                        for who in range(2):
                            start = (2 * block + who) * r
                            buf[(who,) + index] = low[start : start + r, at : at + width_a]
                    stage_copy(a, 0).start()
                mine = lane_slice(vert * half, half)
                vec_sum[0, 2:3, mine] = bias_acc[0:1] + sum_q
                vec_sum[0, 3:4, mine] = bias_acc[1:2] + sum_v

    def inputs(clip):
        dn_copy(clip).wait_recv()
        grad = acc[clip] + dn_got[clip].astype(f32)
        unit, inverse = center_scale(tok_ref[0].astype(f32))
        result = gmid_ref[0][:slots] + norm_back(unit, inverse, row_of(gain_ref), grad[:slots])
        gtok_ref[0] = result
        vec_sum[0, 0:1] += column_sums(grad[:slots] * unit)
        vec_sum[0, 1:2] += column_sums(grad[:slots])
        if clip == clips - 1:
            vec_copy(0).start()

    for clip in range(clips - 1):
        pl.when(step == places["inputs"] + clip)(functools.partial(inputs, clip))

    @pl.when(step == places["end"])
    def finish():
        for kind, a, stage in SUM_STEPS[places["end"]]:
            if kind == "input":
                inputs(clips - 1)
            else:
                perform((kind, a, stage))
        for a, (name, at, r, width_a, _) in enumerate(arrays):
            for who in range(2):
                full = full_bufs[a]
                if name == "fc1":
                    start = who * fc1_out.shape[1] // 2 + at
                    fc1_out[:, start : start + width_a] = full[who]
                elif name == "fc2":
                    fc2_out[at : at + r, who * width_a : (who + 1) * width_a] = full[who]
                elif name == "proj":
                    proj_out[:, who * width_a : (who + 1) * width_a] = full[who]
                else:
                    for side in range(2):
                        for start in range(0, width_a, lanes):
                            part, inside = divmod(at + start, half)
                            to = part * width + side * half + inside
                            qkv_out[who * r : (who + 1) * r, to : to + lanes] = full[who, side, :, start : start + lanes]
        vec_out[...] = vec_sum[bits + 2]
        for a in range(count):
            for stage in range(bits + 3):
                stage_copy(a, stage).wait_send()
        for clip in range(clips):
            grad_vert(clip).wait_send()
            dn_copy(clip).wait_send()
        for pair in range(pairs):
            kv_copy(clips - 1, pair).wait_send()
        for hop in range(bits + 2):
            vec_copy(hop).wait_send()


def step_places(clips, pairs):
    of_clip = 2 * pairs
    projections = [of_clip * (c + 1) + 2 + c for c in range(clips - 1)] + [of_clip * clips + clips - 1]
    inputs = projections[-1] + 1
    return {"projections": projections, "inputs": inputs, "end": inputs + clips - 1}


def attention_index(step, places):
    index = step
    for at in places["projections"][:-1]:
        index = index - (step > at).astype(jnp.int32)
    return index


def backward(q, k, v, mask, part, lse, normed, weight_half, tokens, gmid, gain, small, db1, gmixed,
             dfc1, dfc2, dproj, clip_size):
    clips, slots, width = tokens.shape
    rows = gmid.shape[1]
    half = width // 2
    keys = k.shape[1]
    pairs = HEADS // 4
    lanes = 2 * DH
    bits = clip_size.bit_length() - 1
    hidden = db1.shape[1]
    arrays = sum_arrays(width, hidden, clip_size)
    places = step_places(clips, pairs)
    one = pl.Buffered(buffer_count=1)

    def of_pair(s):
        at = jnp.minimum(attention_index(s, places), 2 * clips * pairs - 1)
        return at // (2 * pairs), (at // pairs) % 2, at % pairs

    def of_keys(s):
        clip, _, pair = of_pair(s)
        return clip, 0, pair

    def of_projection(s):
        index = s * 0
        for at in places["projections"][:-1]:
            index = index + (s > at).astype(jnp.int32)
        return index, 0, 0

    def of_clip(s):
        return jnp.clip(s - places["inputs"], 0, clips - 1), 0, 0

    fixed = lambda shape: pl.BlockSpec(shape, lambda s: (0,) * len(shape), pipeline_mode=one)
    tok_pair = pl.BlockSpec((1, rows, lanes), of_pair)
    key_pair = pl.BlockSpec((1, keys, lanes), of_keys)
    anywhere = pl.BlockSpec(memory_space=pl.ANY)
    blocks = (2,) * bits
    r_fc1, r_fc2 = width // clip_size, hidden // clip_size
    dfc1 = dfc1.reshape((2,) + blocks + (r_fc1, hidden // 2))
    dfc2 = dfc2.reshape((2,) + blocks + (r_fc2, half))
    dproj = dproj.reshape((2,) + blocks + (r_fc1, half))
    vmem = lambda *shape: pltpu.VMEM(shape, bf16)
    wide = lambda *shape: pltpu.VMEM(shape, f32)
    scratch = [
        vmem(2, clips, rows, half),
        vmem(clips, 2 * rows, 3 * half),
        wide(pairs, 2, keys, lanes),
        vmem(pairs, 2, 2 * rows, lanes),
        vmem(clips, pairs, 2, 2 * rows, lanes),
        wide(clips, rows, width),
        vmem(clips, rows, width),
        vmem(clips, rows, width),
        wide(width, 3 * half),
        wide(8, half),
        wide(bits + 3, 16, width),
        wide(bits + 2, 16, width),
        vmem(*blocks, r_fc1, hidden // 4),
        vmem(*blocks, r_fc2 // 2, half),
        vmem(*blocks, r_fc1, half),
    ]
    scratch += [vmem(2, *blocks, r, w) for name, _, r, w, _ in arrays if name == "qkv"]
    for _, _, r, w, _ in arrays:
        scratch += [vmem(*((2,) * (bits - stage)), r, w) for stage in range(bits + 1)]
    scratch += [vmem(r, w) for name, _, r, w, _ in arrays if name != "qkv"]
    scratch += [vmem(2, 2, r, w) if name == "qkv" else vmem(2, r, w) for name, _, r, w, _ in arrays]
    dma = lambda *shape: pltpu.SemaphoreType.DMA(shape)
    count = len(arrays)
    scratch += [
        dma(clips), dma(clips), dma(clips), dma(clips, pairs), dma(clips, pairs), dma(clips), dma(clips),
        dma(count, bits + 3), dma(count, bits + 3), dma(count), dma(bits + 2), dma(bits + 2),
    ]
    shape = jax.ShapeDtypeStruct
    return pl.pallas_call(
        functools.partial(backward_kernel, (clips, slots, rows, bits, pairs, arrays)),
        grid=(places["end"] + 1,),
        in_specs=[
            tok_pair, key_pair, key_pair,
            pl.BlockSpec((1, 1, keys), lambda s: (of_pair(s)[0], 0, 0)),
            tok_pair, tok_pair,
            pl.BlockSpec((1, 2 * rows, width), of_projection),
            fixed(weight_half.shape),
            pl.BlockSpec((1, slots, width), of_clip),
            pl.BlockSpec((1, rows, width), of_clip),
            fixed((width,)), fixed((8, width)), fixed((1, hidden)),
            anywhere, anywhere, anywhere, anywhere,
        ],
        out_specs=[
            pl.BlockSpec((1, slots, width), of_clip),
            fixed((r_fc1, hidden)), fixed((r_fc2, width)), fixed((r_fc1, width)),
            fixed((r_fc1, 3 * width)), fixed((16, width)),
        ],
        out_shape=[
            shape((clips, slots, width), f32),
            shape((r_fc1, hidden), bf16),
            shape((r_fc2, width), bf16),
            shape((r_fc1, width), bf16),
            shape((r_fc1, 3 * width), bf16),
            shape((16, width), f32),
        ],
        scratch_shapes=scratch,
        compiler_params=params(collective_id=1, has_side_effects=True),
        cost_estimate=pl.CostEstimate(
            flops=2 * clips * rows * (5 * keys * width + 6 * width * width),
            bytes_accessed=60_000_000,
            transcendentals=clips * rows * keys * HEADS,
        ),
        name="backward",
    )(q, k, v, mask, part, lse, normed, weight_half, tokens, gmid, gain, small, db1, gmixed, dfc1, dfc2, dproj)


def outputs_kernel(fc1, fc2, proj, qkv, vec, gtok, fc1_out, fc2_out, proj_out, qkv_out, gtok_out, db1_out, *rest):
    outs, sem = rest[:-1], rest[-1]
    copy = pltpu.make_async_copy(gtok, gtok_out, sem)
    copy.start()
    for src, dst in ((fc1, fc1_out), (fc2, fc2_out), (proj, proj_out), (qkv, qkv_out)):
        dst[...] = src[...].astype(f32)
    width = vec.shape[1]
    for i, dst in enumerate(outs):
        dst[...] = vec[i : i + 1].reshape(width)
    tall = db1_out.shape[0] // width
    db1_out[...] = jnp.concatenate([vec[8 + i : 9 + i] for i in range(tall)], axis=1).reshape(db1_out.shape[0])
    copy.wait()


def final_outputs(low_fc1, low_fc2, low_proj, low_qkv, summed, gtok, hidden):
    width = summed.shape[1]
    vmem = pl.BlockSpec(memory_space=pltpu.VMEM)
    anywhere = pl.BlockSpec(memory_space=pl.ANY)
    shape = jax.ShapeDtypeStruct
    return pl.pallas_call(
        outputs_kernel,
        in_specs=[vmem] * 5 + [anywhere],
        out_specs=[vmem] * 4 + [anywhere] + [vmem] * 9,
        out_shape=[shape(a.shape, f32) for a in (low_fc1, low_fc2, low_proj, low_qkv)]
        + [shape(gtok.shape, f32), shape((hidden,), f32)]
        + [shape((width,), f32)] * 8,
        scratch_shapes=[pltpu.SemaphoreType.DMA(())],
        compiler_params=params(),
        name="final_outputs",
    )(low_fc1, low_fc2, low_proj, low_qkv, summed, gtok)


def partner(kind):
    index = lax.axis_index("freq")
    if kind == "vert":
        return {"freq": (index + 2) % 4}
    return {"freq": index + 1 - 2 * (index % 2)}


def whole_forward_kernel(
    counts,
    tok_ref, qkv_ref, qb_ref, vb_ref, gain_ref, shift_ref, proj_ref, pb_ref, gain2_ref, shift2_ref,
    q_ref, k_ref, v_ref, normed_ref, mixed_ref, lse_ref, middle_ref, normed2_ref, mask_ref,
    held, send_sem, recv_sem,
):
    clips, slots, rows = counts
    clip = pl.program_id(0)
    pair = pl.program_id(1)
    width = tok_ref.shape[-1]

    def copy(kind, index):
        at = {"vert": 0, "core": 1, "diag": 2}[kind]
        return pltpu.make_async_remote_copy(
            src_ref=held.at[index, 0] if kind == "diag" else tok_ref.at[index],
            dst_ref=held.at[index, at],
            send_sem=send_sem.at[index, at],
            recv_sem=recv_sem.at[index, at],
            device_id=partner(kind),
            device_id_type=pl.DeviceIdType.MESH,
        )

    def project(slot, source):
        unit, _ = center_scale(source.astype(f32))
        normed = (unit * gain_ref[...] + shift_ref[...]).astype(bf16)
        if slot == 0:
            normed_ref[0] = normed
            query = (dot(normed, qkv_ref[:, :width]) + qb_ref[...]).astype(bf16)
            q_ref[0] = query * jnp.asarray(DH ** -0.5, bf16)
        both = dot(normed, qkv_ref[:, width:])
        k_ref[0, slot * rows : (slot + 1) * rows] = both[:, :width].astype(bf16)
        v_ref[0, slot * rows : (slot + 1) * rows] = (both[:, width:] + vb_ref[...]).astype(bf16)
        first = (slots // 16) * 16
        kept = source[first:].astype(f32)[slots - first : slots - first + 1, 0:1] + slots // 2
        lane = lax.broadcasted_iota(jnp.int32, (1, rows), 1).astype(f32)
        return (lane < kept).astype(f32)

    @pl.when((clip == 0) & (pair == 0))
    def enter():
        barrier = pltpu.get_barrier_semaphore()
        for kind in ("vert", "core"):
            pl.semaphore_signal(
                barrier, inc=1, device_id=partner(kind), device_id_type=pl.DeviceIdType.MESH
            )
        pl.semaphore_wait(barrier, 2)
        copy("vert", 0).start()
        for index in range(clips):
            copy("core", index).start()

    def pass_on(index):
        copy("vert", index).wait_recv()
        copy("diag", index).start()
        copy("vert", index).wait_send()

        @pl.when(index + 1 < clips)
        def more():
            copy("vert", index + 1).start()

    @pl.when(pair == 0)
    def project_all():
        live_own = project(0, tok_ref[clip])
        copy("core", clip).wait_recv()
        live_core = project(2, held[clip, 1])

        @pl.when(clip == 0)
        def first_pass():
            pass_on(clip)

        live_vert = project(1, held[clip, 0])
        copy("diag", clip).wait_recv()
        live_diag = project(3, held[clip, 2])
        mask_ref[0] = jnp.concatenate([live_own, live_vert, live_core, live_diag], axis=1)

    @pl.when((pair == 3) & (clip + 1 < clips))
    def next_pass():
        pass_on(clip + 1)

    lanes = pl.ds(pl.multiple_of(pair * 2 * DH, 2 * DH), 2 * DH)
    query = q_ref[0, :, lanes]
    keys = k_ref[0, :, lanes]
    values = v_ref[0, :, lanes]
    live = mask_ref[0] > 0.5
    outs, lses = [], []
    for head in range(2):
        scores = jnp.where(live, dot(only(query, head), keys, NT), MASKED)
        top = jnp.max(scores, axis=1, keepdims=True)
        exps = jnp.exp(scores - top)
        total = jnp.sum(exps, axis=1, keepdims=True)
        outs.append(dot(exps.astype(bf16), values) / total)
        lses.append(top + jnp.log(total))
    first = own_lanes(outs[0].shape, 0)
    mixed_ref[0, :, lanes] = jnp.where(first, outs[0], outs[1]).astype(bf16)
    lse_ref[0, :, lanes] = jnp.where(first, lses[0], lses[1])

    @pl.when(pair == pl.num_programs(1) - 1)
    def finish():
        middle = tok_ref[clip].astype(f32) + (dot(mixed_ref[0], proj_ref[...]) + pb_ref[...])
        middle_ref[0] = middle
        unit, _ = center_scale(middle)
        normed2_ref[0] = (unit * gain2_ref[...] + shift2_ref[...]).astype(bf16)
        copy("core", clip).wait_send()
        copy("diag", clip).wait_send()


def whole_forward(tok, slots, qkv_weight, vectors, proj_weight):
    clips, rows, width = tok.shape
    keys = 4 * rows
    pairs = HEADS // 2
    query_bias, value_bias, gain, shift, proj_bias, gain2, shift2 = vectors
    one = pl.Buffered(buffer_count=1)
    row = full((1, width))
    block = lambda n: pl.BlockSpec((1, n, width), lambda c, p: (c, 0, 0))
    flops = 2 * clips * (10 * rows * width * width + 2 * rows * keys * width)
    weight = lambda w: pl.BlockSpec(w.shape, lambda c, p: (0, 0), pipeline_mode=one)
    return pl.pallas_call(
        functools.partial(whole_forward_kernel, (clips, slots, rows)),
        grid=(clips, pairs),
        in_specs=[
            pl.BlockSpec(tok.shape, lambda c, p: (0, 0, 0), pipeline_mode=one),
            weight(qkv_weight), row, row, row, row, weight(proj_weight), row, row, row,
        ],
        out_specs=[block(rows), block(keys), block(keys)] + [block(rows)] * 5
        + [pl.BlockSpec((1, 1, keys), lambda c, p: (c, 0, 0))],
        out_shape=[
            jax.ShapeDtypeStruct((clips, rows, width), bf16),
            jax.ShapeDtypeStruct((clips, keys, width), bf16),
            jax.ShapeDtypeStruct((clips, keys, width), bf16),
            jax.ShapeDtypeStruct((clips, rows, width), bf16),
            jax.ShapeDtypeStruct((clips, rows, width), bf16),
            jax.ShapeDtypeStruct((clips, rows, width), f32),
            jax.ShapeDtypeStruct((clips, rows, width), f32),
            jax.ShapeDtypeStruct((clips, rows, width), bf16),
            jax.ShapeDtypeStruct((clips, 1, keys), f32),
        ],
        scratch_shapes=[
            pltpu.VMEM((clips, 3, rows, width), bf16),
            pltpu.SemaphoreType.DMA((clips, 3)),
            pltpu.SemaphoreType.DMA((clips, 3)),
        ],
        compiler_params=params(collective_id=0, has_side_effects=True),
        cost_estimate=pl.CostEstimate(
            flops=flops, bytes_accessed=40_000_000, transcendentals=clips * rows * keys * HEADS
        ),
        name="whole_forward",
    )(tok, qkv_weight, query_bias, value_bias, gain, shift, proj_weight, proj_bias, gain2, shift2)


def attend_back_kernel(q_ref, k_ref, v_ref, mask_ref, mixed_ref, lse_ref, grad_ref,
                       dq_ref, dkeep_ref, dsend_ref):
    query = q_ref[0]
    keys = k_ref[0]
    values = v_ref[0]
    grad = grad_ref[0]
    live = mask_ref[0] > 0.5
    product = grad.astype(f32) * mixed_ref[0].astype(f32)
    dqs, dk, dv = [], None, None
    for head in range(2):
        own_query = only(query, head)
        own_grad = only(grad, head)
        scores = jnp.where(live, dot(own_query, keys, NT), MASKED)
        probs = jnp.exp(scores - lse_ref[0, :, head * DH : head * DH + 1])
        delta = jnp.sum(only(product, head), axis=1, keepdims=True)
        dscores = (probs * (dot(own_grad, values, NT) - delta)).astype(bf16)
        dqs.append(dot(dscores, keys))
        more_k = dot(dscores, own_query, TN)
        more_v = dot(probs.astype(bf16), own_grad, TN)
        dk = more_k if dk is None else dk + more_k
        dv = more_v if dv is None else dv + more_v
    first = own_lanes(dqs[0].shape, 0)
    dq_ref[0] = (jnp.where(first, dqs[0], dqs[1]) * DH ** -0.5).astype(bf16)
    half = dk.shape[0] // 2
    dkeep_ref[0, 0] = dk[:half].astype(bf16)
    dkeep_ref[1, 0] = dv[:half].astype(bf16)
    dsend_ref[0, 0] = dk[half:].astype(bf16)
    dsend_ref[1, 0] = dv[half:].astype(bf16)


def attend_back(q, k, v, mask, mixed, lse, grad, first_pair, pairs):
    clips, rows, _ = q.shape
    keys = k.shape[1]
    lanes = 2 * DH
    tok = pl.BlockSpec((1, rows, lanes), lambda c, p: (c, 0, first_pair + p))
    key = pl.BlockSpec((1, keys, lanes), lambda c, p: (c, 0, first_pair + p))
    part = pl.BlockSpec((2, 1, keys // 2, lanes), lambda c, p: (0, c, 0, p))
    return pl.pallas_call(
        attend_back_kernel,
        grid=(clips, pairs),
        in_specs=[tok, key, key, pl.BlockSpec((1, 1, keys), lambda c, p: (c, 0, 0)), tok, tok, tok],
        out_specs=[pl.BlockSpec((1, rows, lanes), lambda c, p: (c, 0, p)), part, part],
        out_shape=[
            jax.ShapeDtypeStruct((clips, rows, pairs * lanes), bf16),
            jax.ShapeDtypeStruct((2, clips, keys // 2, pairs * lanes), bf16),
            jax.ShapeDtypeStruct((2, clips, keys // 2, pairs * lanes), bf16),
        ],
        compiler_params=params(),
        cost_estimate=pl.CostEstimate(
            flops=4 * 10 * clips * rows * keys * pairs * lanes,
            bytes_accessed=clips * pairs * lanes * (keys * 10 + rows * 12),
            transcendentals=clips * rows * keys * 2 * pairs,
        ),
        name="attend_back",
    )(q, k, v, mask, mixed, lse, grad)


def weight_kernel(normed_ref, dq_ref, dk0_ref, dk1_ref, dk2_ref, out_ref, dkv_ref, sums_ref):
    part = pl.program_id(0)
    @pl.when(part == 0)
    def query():
        grad = dq_ref[...]
        out_ref[0] = dot(normed_ref[...], grad, TN).astype(bf16)
        sums_ref[0] = column_sums(grad.astype(f32))
        dkv_ref[0] = jnp.zeros_like(dkv_ref[0])

    @pl.when(part > 0)
    def other():
        grad = (dk0_ref[0].astype(f32) + dk1_ref[0].astype(f32) + dk2_ref[0].astype(f32)).astype(bf16)
        dkv_ref[0] = grad
        out_ref[0] = dot(normed_ref[...], grad, TN).astype(bf16)
        sums_ref[0] = column_sums(grad.astype(f32))


def weight_grads(normed, dq, parts):
    total, width = normed.shape
    lanes = dq.shape[1]
    before = lambda j: (jnp.maximum(j - 1, 0), 0, 0)
    part = pl.BlockSpec((1, total, lanes), before)
    return pl.pallas_call(
        weight_kernel,
        grid=(3,),
        in_specs=[full((total, width)), full((total, lanes)), part, part, part],
        out_specs=[
            pl.BlockSpec((1, width, lanes), lambda j: (j, 0, 0)),
            part,
            pl.BlockSpec((1, 1, lanes), lambda j: (j, 0, 0)),
        ],
        out_shape=[
            jax.ShapeDtypeStruct((3, width, lanes), bf16),
            jax.ShapeDtypeStruct((2, total, lanes), bf16),
            jax.ShapeDtypeStruct((3, 1, lanes), f32),
        ],
        compiler_params=params(),
        cost_estimate=pl.CostEstimate(
            flops=6 * total * width * lanes, bytes_accessed=8_000_000, transcendentals=0
        ),
        name="weight_grads",
    )(normed, dq, *parts)


def input_kernel(counts, groups, *refs):
    clips, slots, rows = counts
    dqs = refs[:groups]
    dkvs = refs[groups : 2 * groups]
    qkv_ref, tok_ref, gmid_ref, gain_ref, shift_ref, out_ref, small_ref = refs[2 * groups :]
    clip = pl.program_id(0)
    width = tok_ref.shape[-1]
    lanes = width // groups
    grad = None
    for group in range(groups):
        for part in range(3):
            rows_grad = dqs[group][0] if part == 0 else dkvs[group][part - 1]
            at = part * width + group * lanes
            more = dot(rows_grad, qkv_ref[:, at : at + lanes], NT)
            grad = more if grad is None else grad + more
    unit, inverse = center_scale(tok_ref[0].astype(f32))
    result = gmid_ref[0] + norm_back(unit, inverse, gain_ref[...], grad)
    out_ref[0] = result[:slots]

    @pl.when(clip == 0)
    def start():
        small_ref[...] = jnp.zeros_like(small_ref)

    small_ref[0:1] += column_sums(grad * unit)
    small_ref[1:2] += column_sums(grad)


def input_grads(dqs, dkvs, qkv_weight, tokens, gmid, gain, shift, slots):
    clips, rows, width = tokens.shape
    groups = len(dqs)
    lanes = width // groups
    tok = pl.BlockSpec((1, rows, width), lambda c: (c, 0, 0))
    return pl.pallas_call(
        functools.partial(input_kernel, (clips, slots, rows), groups),
        grid=(clips,),
        in_specs=[pl.BlockSpec((1, rows, lanes), lambda c: (c, 0, 0))] * groups
        + [pl.BlockSpec((2, rows, lanes), lambda c: (0, c, 0))] * groups
        + [full(qkv_weight.shape), tok, tok, full((1, width)), full((1, width))],
        out_specs=[pl.BlockSpec((1, slots, width), lambda c: (c, 0, 0)), full((8, width))],
        out_shape=[
            jax.ShapeDtypeStruct((clips, slots, width), f32),
            jax.ShapeDtypeStruct((8, width), f32),
        ],
        compiler_params=params(),
        cost_estimate=pl.CostEstimate(
            flops=6 * clips * rows * width * width, bytes_accessed=16_000_000, transcendentals=0
        ),
        name="input_grads",
    )(*dqs, *dkvs, qkv_weight, tokens, gmid, gain, shift)


def swap_bit(array, axis, size, bit):
    return lax.ppermute(array, axis, [(i, i ^ (1 << bit)) for i in range(size)])


def add_low(left, right):
    return (left.astype(f32) + right.astype(f32)).astype(bf16)


def pick(array, index, dim):
    return lax.dynamic_index_in_dim(array, index, dim, keepdims=False)


def bit_of(axis, bit):
    return (lax.axis_index(axis) >> bit) & 1


def scatter_sum(split, clip_size, order):
    core = bit_of("freq", 0)
    vert = bit_of("freq", 1)
    bits = clip_size.bit_length() - 1
    lanes = split.shape[-1]
    value = add_low(pick(split, core, 0), swap_bit(pick(split, 1 - core, 0), "freq", 4, 0))
    rows = value.shape[0] // (2 * clip_size)
    value = value.reshape((2,) * bits + (2, rows, lanes))
    left = list(range(bits))[::-1]
    for bit in order:
        at = left.index(bit)
        mine = bit_of("clip", bit)
        value = add_low(
            pick(value, mine, at), swap_bit(pick(value, 1 - mine, at), "clip", clip_size, bit)
        )
        left.remove(bit)
    return add_low(pick(value, vert, 0), swap_bit(pick(value, 1 - vert, 0), "freq", 4, 1))


def gather_low(part):
    core = bit_of("freq", 0)
    vert = bit_of("freq", 1)
    other = swap_bit(part, "freq", 4, 1)
    tall = jnp.where(vert == 0, jnp.concatenate([part, other]), jnp.concatenate([other, part]))
    side = swap_bit(tall, "freq", 4, 0)
    return jnp.where(
        core == 0,
        jnp.concatenate([tall, side], axis=1),
        jnp.concatenate([side, tall], axis=1),
    ).astype(f32)


def total_sum(array, clip_size):
    for bit in range(2):
        array = array + swap_bit(array, "freq", 4, bit)
    for bit in range(clip_size.bit_length() - 1):
        array = array + swap_bit(array, "clip", clip_size, bit)
    return array


def on_device_plain(
    clip_size, tokens, kept_counts, attn_gain, attn_shift, qkv_weight, query_bias, value_bias,
    proj_weight, proj_bias, mlp_gain, mlp_shift, fc1_weight, fc1_bias, fc2_weight, fc2_bias, cotangent,
):
    clips, slots, width = tokens.shape
    rows = -(-slots // 16) * 16
    total = clips * rows
    bits = clip_size.bit_length() - 1
    forward_order = list(range(bits))
    second_order = forward_order[1:2] + forward_order[:1] + forward_order[2:]
    vec = lambda v: v.astype(f32)[None, :]
    kept = (kept_counts - slots // 2).astype(bf16)
    tok = jnp.concatenate(
        [tokens, jnp.broadcast_to(kept[:, :, None], (clips, rows - slots, width))], axis=1
    )
    vectors = [vec(v) for v in (query_bias, value_bias, attn_gain, attn_shift, proj_bias, mlp_gain, mlp_shift)]
    q, k, v, normed, mixed, lse, middle, normed2, mask = whole_forward(
        tok, slots, qkv_weight, vectors, proj_weight
    )
    flat = lambda a: a.reshape(total, width)
    layer_out, dfc1, dfc2, dproj, db1, small2, gmid, gmixed = mlp(
        kept_counts, flat(normed2), flat(middle), cotangent, flat(mixed), fc1_weight, fc1_bias,
        fc2_weight, fc2_bias, mlp_gain, proj_weight, rows,
    )
    early = total_sum(jnp.concatenate([small2[:4].reshape(-1), db1.reshape(-1)])[None, :], clip_size)[0]
    sum_fc1 = gather_low(scatter_sum(dfc1, clip_size, forward_order))
    sum_fc2 = gather_low(scatter_sum(dfc2, clip_size, second_order))
    sum_proj = gather_low(scatter_sum(dproj, clip_size, forward_order))

    groups = 3
    pairs = HEADS // 2 // groups
    lanes = pairs * 2 * DH
    gmixed = gmixed.reshape(clips, rows, width)
    dqs, dkvs, sums, sharded = [], [], [], []
    for group in range(groups):
        dq, keep, send = attend_back(q, k, v, mask, mixed, lse, gmixed, group * pairs, pairs)
        got = swap_bit(send, "freq", 4, 0)
        across = swap_bit(add_low(keep[:, :, rows:], got[:, :, rows:]), "freq", 4, 1)
        parts = [a.reshape(2, total, lanes) for a in (keep[:, :, :rows], got[:, :, :rows], across)]
        dw, dkv, colsum = weight_grads(flat(normed), dq.reshape(total, lanes), parts)
        half = lanes // 2
        split = jnp.stack(
            [
                jnp.concatenate([dw[i, :, s * half : (s + 1) * half] for i in range(3)], axis=1)
                for s in range(2)
            ]
        )
        order = forward_order if group % 2 == 0 else second_order
        summed = gather_low(scatter_sum(split, clip_size, order))
        sharded.append(summed.reshape(summed.shape[0], 2, 3, half))
        dqs.append(dq)
        dkvs.append(dkv)
        sums.append(colsum)
    grad_tokens, small1 = input_grads(
        dqs, dkvs, qkv_weight, tok, gmid.reshape(clips, rows, width), vectors[2], vectors[3], slots
    )
    qkv = jnp.stack(sharded, axis=1)
    sum_qkv = qkv.transpose(0, 3, 1, 2, 4).reshape(qkv.shape[0], 3 * width)
    bias = jnp.concatenate(sums, axis=2)
    late = total_sum(
        jnp.concatenate([small1[0:1], small1[1:2], bias[0], bias[2]], axis=1), clip_size
    )[0]
    cut = lambda a, i: a[i * width : (i + 1) * width]
    return (
        layer_out, grad_tokens, cut(late, 0), cut(late, 1), sum_qkv, cut(late, 2), cut(late, 3),
        sum_proj, cut(early, 3), cut(early, 0), cut(early, 1), sum_fc1, early[4 * width :],
        sum_fc2, cut(early, 2),
    )


def on_device(
    clip_size, tokens, kept_counts, attn_gain, attn_shift, qkv_weight, query_bias, value_bias,
    proj_weight, proj_bias, mlp_gain, mlp_shift, fc1_weight, fc1_bias, fc2_weight, fc2_bias, cotangent,
):
    clips, slots, width = tokens.shape
    rows = -(-slots // 16) * 16
    if clip_size != 8 or width % (32 * clip_size):
        return on_device_plain(
            clip_size, tokens, kept_counts, attn_gain, attn_shift, qkv_weight, query_bias, value_bias,
            proj_weight, proj_bias, mlp_gain, mlp_shift, fc1_weight, fc1_bias, fc2_weight, fc2_bias, cotangent,
        )
    q, k, v, normed, part, lse, mask, weight_half, mixed, middle, normed2 = forward(
        kept_counts, tokens, rows, qkv_weight, query_bias, value_bias, attn_gain, attn_shift,
        proj_weight, proj_bias, mlp_gain, mlp_shift,
    )
    flat = lambda a: a.reshape(clips * rows, width)
    layer_out, dfc1, dfc2, dproj, db1, small, gmid, gmixed = mlp(
        kept_counts, flat(normed2), flat(middle), cotangent, flat(mixed), fc1_weight, fc1_bias,
        fc2_weight, fc2_bias, mlp_gain, proj_weight, rows,
    )
    by_clip = lambda a: a.reshape(clips, rows, width)
    gtok, low_fc1, low_fc2, low_proj, low_qkv, summed = backward(
        q, k, v, mask, part, lse, normed, weight_half, tokens, by_clip(gmid), attn_gain, small, db1,
        by_clip(gmixed), dfc1, dfc2, dproj, clip_size,
    )
    fc1, fc2, proj, qkv, grad_tokens, fc1_b, *rows_out = final_outputs(
        low_fc1, low_fc2, low_proj, low_qkv, summed, gtok, fc1_bias.shape[0]
    )
    return (
        layer_out, grad_tokens, rows_out[0], rows_out[1], qkv, rows_out[2], rows_out[3], proj, rows_out[7],
        rows_out[4], rows_out[5], fc1, fc1_b, fc2, rows_out[6],
    )


def solution(mesh):
    rows = P("clip", "freq", None)
    shard = P("clip", None)
    return jax.shard_map(
        functools.partial(on_device, mesh.shape["clip"]),
        mesh=mesh,
        in_specs=(rows, P("clip", "freq")) + (P(),) * 13 + (rows,),
        out_specs=(rows, rows, P(), P(), shard, P(), P(), shard, P(), P(), P(), shard, P(), shard, P()),
        check_vma=False,
    )
```

```python
import functools
import math

import jax
import jax.numpy as jnp
from jax import lax
from jax.experimental import pallas as pl
from jax.experimental.pallas import tpu as pltpu
from jax.sharding import PartitionSpec as P

HEADS = 12
DH = 64
EPS = 1e-06
MASKED = -1000000000.0
VMEM_BYTES = 60 * 1024 * 1024

f32 = jnp.float32
bf16 = jnp.bfloat16
NN = (((1,), (0,)), ((), ()))
NT = (((1,), (1,)), ((), ()))
TN = (((0,), (0,)), ((), ()))


def dot(left, right, dims=NN):
    return lax.dot_general(left, right, dims, preferred_element_type=f32)


def center_scale(rows):
    center = rows - jnp.mean(rows, axis=-1, keepdims=True)
    inverse = lax.rsqrt(jnp.mean(center * center, axis=-1, keepdims=True) + EPS)
    return center * inverse, inverse


def norm_back(unit, inverse, gain, grad):
    scaled = grad * gain
    return inverse * (
        scaled
        - jnp.mean(scaled, axis=-1, keepdims=True)
        - unit * jnp.mean(scaled * unit, axis=-1, keepdims=True)
    )


def column_sums(rows):
    return jnp.sum(rows, axis=0, keepdims=True)


def own_lanes(shape, head):
    lane = lax.broadcasted_iota(jnp.int32, shape, len(shape) - 1)
    return lane < DH if head == 0 else lane >= DH


def only(rows, head):
    return jnp.where(own_lanes(rows.shape, head), rows, jnp.zeros_like(rows))


def full(shape):
    return pl.BlockSpec(shape, lambda *ids: (0,) * len(shape))


def params(**more):
    return pltpu.CompilerParams(vmem_limit_bytes=VMEM_BYTES, **more)


def freq_places():
    freq = lax.axis_index("freq")
    core, vert = freq % 2, freq // 2
    return core, vert, {"freq": freq + 1 - 2 * core}, {"freq": (freq + 2) % 4}


def lane_slice(start, size):
    return pl.ds(pl.multiple_of(start, 2 * DH), size)


def row_of(ref):
    return ref[...].astype(f32).reshape(1, ref.shape[0])


def forward_kernel(
    counts,
    kept_ref, tok_ref, qkv_ref, qb_ref, vb_ref, gain_ref, shift_ref, proj_ref, pb_ref, gain2_ref, shift2_ref,
    q_ref, k_ref, v_ref, normed_ref, part_ref, lse_ref, mask_ref, weight_ref, mixed_ref, middle_ref, normed2_ref,
    own, held, mix_send, mix_got, vecs, tok_send, tok_recv, part_send, part_recv,
):
    clips, slots, rows, pairs = counts
    clip = pl.program_id(0)
    pair = pl.program_id(1)
    width = tok_ref.shape[-1]
    half = width // 2
    lanes = 2 * DH
    core, vert, core_dev, vert_dev = freq_places()
    mesh_id = pl.DeviceIdType.MESH

    def copy(kind, index):
        at = {"vert": 0, "core": 1, "diag": 2}[kind]
        return pltpu.make_async_remote_copy(
            src_ref=held.at[index, 0] if kind == "diag" else own.at[index],
            dst_ref=held.at[index, at],
            send_sem=tok_send.at[index, at],
            recv_sem=tok_recv.at[index, at],
            device_id=vert_dev if kind == "vert" else core_dev,
            device_id_type=mesh_id,
        )

    def mix_copy(index, which):
        return pltpu.make_async_remote_copy(
            src_ref=mix_send.at[index, which],
            dst_ref=mix_got.at[index, which],
            send_sem=part_send.at[index, which],
            recv_sem=part_recv.at[index, which],
            device_id=vert_dev,
            device_id_type=mesh_id,
        )

    def project(slot, source):
        unit, _ = center_scale(source.astype(f32))
        normed = (unit * vecs[2:3] + vecs[3:4]).astype(bf16)
        at = slice(slot * rows, (slot + 1) * rows)
        if slot < 2:
            normed_ref[0, at] = normed
            query = (dot(normed, weight_ref[:, :half]) + vecs[0:1, lane_slice(vert * half, half)]).astype(bf16)
            q_ref[0, at] = query * jnp.asarray(DH ** -0.5, bf16)
        both = dot(normed, weight_ref[:, half:])
        k_ref[0, at] = both[:, :half].astype(bf16)
        v_ref[0, at] = (both[:, half:] + vecs[1:2, lane_slice(vert * half, half)]).astype(bf16)
        first = (slots // 16) * 16
        kept = source[first:].astype(f32)[slots - first : slots - first + 1, 0:1] + slots // 2
        lane = lax.broadcasted_iota(jnp.int32, (1, rows), 1).astype(f32)
        return (lane < kept).astype(f32)

    def pass_on(index):
        copy("vert", index).wait_recv()
        copy("diag", index).start()
        copy("vert", index).wait_send()

        @pl.when(index + 1 < clips)
        def more():
            copy("vert", index + 1).start()

    @pl.when((clip == 0) & (pair == 0))
    def enter():
        barrier = pltpu.get_barrier_semaphore()
        for device in (vert_dev, core_dev):
            pl.semaphore_signal(barrier, inc=1, device_id=device, device_id_type=mesh_id)
        first = (slots // 16) * 16
        for index in range(clips):
            kept = (kept_ref[index, 0] - slots // 2).astype(f32).astype(bf16)
            own[index, first:] = jnp.broadcast_to(kept, (rows - first, width))
            own[index, :slots] = tok_ref[index]
        pl.semaphore_wait(barrier, 2)
        copy("vert", 0).start()
        for index in range(clips):
            copy("core", index).start()
        for i, ref in enumerate((qb_ref, vb_ref, gain_ref, shift_ref, pb_ref, gain2_ref, shift2_ref)):
            vecs[i : i + 1] = row_of(ref)
        for part in range(3):
            weight_ref[:, part * half : (part + 1) * half] = qkv_ref[:, lane_slice(part * width + vert * half, half)]

    @pl.when(pair == 0)
    def project_all():
        live_own = project(0, own[clip])
        copy("core", clip).wait_recv()
        live_core = project(2, held[clip, 1])

        @pl.when(clip == 0)
        def first_pass():
            pass_on(clip)

        live_vert = project(1, held[clip, 0])
        copy("diag", clip).wait_recv()
        live_diag = project(3, held[clip, 2])
        mask_ref[0] = jnp.concatenate([live_own, live_vert, live_core, live_diag], axis=1)

    @pl.when((pair == 1) & (clip + 1 < clips))
    def next_pass():
        pass_on(clip + 1)

    def finish(index):
        at = lane_slice(vert * half, half)
        mixed_ref[0, :, at] = mix_own_of(index)
        for which in range(pairs):
            mix_copy(index, which).wait_recv()
            at = lane_slice((1 - vert) * half + which * lanes, lanes)
            mixed_ref[0, :, at] = mix_got[index, which]
        middle = own[index].astype(f32) + (dot(mixed_ref[0], proj_ref[...]) + vecs[4:5])
        middle_ref[0] = middle
        unit, _ = center_scale(middle)
        normed2_ref[0] = (unit * vecs[5:6] + vecs[6:7]).astype(bf16)
        copy("core", index).wait_send()
        copy("diag", index).wait_send()
        for which in range(pairs):
            mix_copy(index, which).wait_send()

    def mix_own_of(index):
        return jnp.concatenate([mix_send[index, pairs + which] for which in range(pairs)], axis=1)

    here = lane_slice(pair * lanes, lanes)
    keys = k_ref[0, :, here]
    values = v_ref[0, :, here]
    live = mask_ref[0] > 0.5
    for slot in (1, 0):
        at = slice(slot * rows, (slot + 1) * rows)
        query = q_ref[0, at, here]
        outs, lses = [], []
        for head in range(2):
            scores = jnp.where(live, dot(only(query, head), keys, NT), MASKED)
            top = jnp.max(scores, axis=1, keepdims=True)
            exps = jnp.exp(scores - top)
            total = jnp.sum(exps, axis=1, keepdims=True)
            outs.append(dot(exps.astype(bf16), values) / total)
            lses.append(top + jnp.log(total))
        first = own_lanes(outs[0].shape, 0)
        mixed = jnp.where(first, outs[0], outs[1]).astype(bf16)
        part_ref[0, at, here] = mixed
        lse_ref[0, at, here] = jnp.where(first, lses[0], lses[1])
        if slot == 1:
            mix_send[clip, pair] = mixed
            mix_copy(clip, pair).start()
        else:
            mix_send[clip, pairs + pair] = mixed

    last = pairs - 1
    for index in range(clips):
        when = (clip == index) & (pair == last) if index == clips - 1 else (clip == index + 1) & (pair == 1)

        @pl.when(when)
        def finish_clip(index=index):
            finish(index)


def forward(kept, tokens, rows, qkv_weight, query_bias, value_bias, gain, shift, proj_weight, proj_bias, gain2, shift2):
    clips, slots, width = tokens.shape
    keys = 4 * rows
    half = width // 2
    pairs = HEADS // 4
    lanes = 2 * DH
    one = pl.Buffered(buffer_count=1)
    block = lambda n, m: pl.BlockSpec((1, n, m), lambda c, p: (c, 0, 0))
    late = lambda n, m: pl.BlockSpec(
        (1, n, m),
        lambda c, p: (jnp.where((c == clips - 1) & (p == pairs - 1), c, jnp.maximum(c - 1, 0)), 0, 0),
    )
    whole = lambda a: pl.BlockSpec(a.shape, lambda c, p: (0,) * a.ndim, pipeline_mode=one)
    shape = jax.ShapeDtypeStruct
    flops = 2 * clips * (rows * width * width * 6 + 2 * rows * keys * width)
    vectors = (query_bias, value_bias, gain, shift)
    return pl.pallas_call(
        functools.partial(forward_kernel, (clips, slots, rows, pairs)),
        grid=(clips, pairs),
        in_specs=[pl.BlockSpec(memory_space=pltpu.SMEM), whole(tokens), whole(qkv_weight)]
        + [whole(v) for v in vectors]
        + [whole(proj_weight)]
        + [whole(v) for v in (proj_bias, gain2, shift2)],
        out_specs=[
            block(2 * rows, half), block(keys, half), block(keys, half), block(2 * rows, width),
            block(2 * rows, half), block(2 * rows, half), block(1, keys),
            pl.BlockSpec((width, 3 * half), lambda c, p: (0, 0), pipeline_mode=one),
            late(rows, width), late(rows, width), late(rows, width),
        ],
        out_shape=[
            shape((clips, 2 * rows, half), bf16),
            shape((clips, keys, half), bf16),
            shape((clips, keys, half), bf16),
            shape((clips, 2 * rows, width), bf16),
            shape((clips, 2 * rows, half), bf16),
            shape((clips, 2 * rows, half), f32),
            shape((clips, 1, keys), f32),
            shape((width, 3 * half), bf16),
            shape((clips, rows, width), bf16),
            shape((clips, rows, width), f32),
            shape((clips, rows, width), bf16),
        ],
        scratch_shapes=[
            pltpu.VMEM((clips, rows, width), bf16),
            pltpu.VMEM((clips, 3, rows, width), bf16),
            pltpu.VMEM((clips, 2 * pairs, rows, lanes), bf16),
            pltpu.VMEM((clips, pairs, rows, lanes), bf16),
            pltpu.VMEM((8, width), f32),
            pltpu.SemaphoreType.DMA((clips, 3)),
            pltpu.SemaphoreType.DMA((clips, 3)),
            pltpu.SemaphoreType.DMA((clips, pairs)),
            pltpu.SemaphoreType.DMA((clips, pairs)),
        ],
        compiler_params=params(collective_id=0, has_side_effects=True),
        cost_estimate=pl.CostEstimate(
            flops=flops, bytes_accessed=40_000_000, transcendentals=clips * rows * keys * HEADS
        ),
        name="forward",
    )(kept, tokens, qkv_weight, *vectors, proj_weight, proj_bias, gain2, shift2)


def mlp_kernel(
    counts,
    kept_ref, n2_ref, middle_ref, cot_ref, mixed_ref, fc1_ref, b1_ref, fc2_ref, b2_ref, gain_ref, proj_ref,
    out_ref, dfc1_ref, dfc2_ref, dproj_ref, db1_ref, small_ref, gmid_ref, gmixed_ref,
    n2t_ref, grad_ref, out_acc, dn_acc, hidden_ref, dact_ref, active_ref, dhid_ref, biases,
):
    clips, slots, rows, tile = counts
    step = pl.program_id(0)
    width = n2_ref.shape[-1]
    chunk = fc1_ref.shape[-1]
    total = clips * rows

    def live_rows(clip, size):
        slot = lax.broadcasted_iota(jnp.int32, (size, 1), 0)
        return (slot < kept_ref[clip, 0]).astype(f32)

    @pl.when(step == 0)
    def start():
        n2t_ref[...] = n2_ref[...].T
        first = (slots // 16) * 16
        for clip in range(clips):
            begin = clip * rows
            grad_ref[begin + first : begin + rows] = jnp.zeros((rows - first, width), bf16)
            grad_ref[begin : begin + slots] = cot_ref[clip] * live_rows(clip, slots).astype(bf16)
        all_biases = row_of(b1_ref)
        for i in range(all_biases.shape[1] // chunk):
            biases[i : i + 1] = all_biases[:, i * chunk : (i + 1) * chunk]
        out_acc[...] = jnp.zeros_like(out_acc)
        dn_acc[...] = jnp.zeros_like(dn_acc)

    hidden_ref[...] = dot(n2_ref[...], fc1_ref[...])
    dact_ref[...] = dot(grad_ref[...], fc2_ref[...], NT)
    bias = biases[pl.ds(step, 1), :]

    def gelu_tile(index, sums):
        at = pl.ds(pl.multiple_of(index * tile, tile), tile)
        hidden = hidden_ref[at, :] + bias
        cdf = 0.5 * (1.0 + lax.erf(hidden * (0.5 ** 0.5)))
        active_ref[at, :] = (hidden * cdf).astype(bf16)
        slope = cdf + hidden * (jnp.exp(-0.5 * hidden * hidden) * (1.0 / math.sqrt(2.0 * math.pi)))
        dhid = (dact_ref[at, :] * slope).astype(bf16)
        dhid_ref[at, :] = dhid
        return sums + dhid.astype(f32)

    sums = lax.fori_loop(0, total // tile, gelu_tile, jnp.zeros((tile, chunk), f32))
    db1_ref[...] = column_sums(sums)
    active = active_ref[...]
    dhid = dhid_ref[...]
    out_acc[...] += dot(active, fc2_ref[...])
    dn_acc[...] += dot(dhid, fc1_ref[...], NT)
    dfc1_ref[0] = dot(n2t_ref[...], dhid).astype(bf16)
    dfc2 = dot(active, grad_ref[...], TN).astype(bf16)
    half = width // 2
    dfc2_ref[0] = dfc2[:, :half]
    dfc2_ref[1] = dfc2[:, half:]

    @pl.when(step == pl.num_programs(0) - 1)
    def finish():
        gain = row_of(gain_ref)
        bias2 = row_of(b2_ref)
        sum_gain = jnp.zeros((1, width), f32)
        sum_shift = jnp.zeros((1, width), f32)
        sum_grad = jnp.zeros((1, width), f32)
        sum_proj = jnp.zeros((1, width), f32)
        for clip in range(clips):
            at = slice(clip * rows, (clip + 1) * rows)
            middle = middle_ref[at]
            layer = middle[:slots] + (out_acc[clip * rows : clip * rows + slots] + bias2)
            out_ref[clip] = (live_rows(clip, slots) * layer).astype(bf16)
            unit, inverse = center_scale(middle)
            grad = dn_acc[at]
            out_grad = grad_ref[at].astype(f32)
            gmid = out_grad + norm_back(unit, inverse, gain, grad)
            gmid_ref[at] = gmid
            low = gmid.astype(bf16)
            dhid_ref[at, :width] = low
            gmixed_ref[at] = dot(low, proj_ref[...], NT).astype(bf16)
            sum_gain += column_sums(grad * unit)
            sum_shift += column_sums(grad)
            sum_grad += column_sums(out_grad)
            sum_proj += column_sums(low.astype(f32))
        dproj = dot(mixed_ref[...], dhid_ref[:, :width], TN).astype(bf16)
        dproj_ref[0] = dproj[:, :half]
        dproj_ref[1] = dproj[:, half:]
        small_ref[0:1] = sum_gain
        small_ref[1:2] = sum_shift
        small_ref[2:3] = sum_grad
        small_ref[3:4] = sum_proj


def mlp(kept, n2, middle, cot, mixed, fc1, b1, fc2, b2, gain, proj, rows):
    clips, slots, _ = cot.shape
    total, width = n2.shape
    hidden = fc1.shape[1]
    chunk = 768
    steps = hidden // chunk
    half = steps // 2
    tile = 16
    whole = lambda a: pl.BlockSpec(a.shape, lambda j: (0,) * a.ndim, pipeline_mode=one)
    one = pl.Buffered(buffer_count=1)
    big = pl.BlockSpec((total, width), lambda j: (0, 0), pipeline_mode=one)
    return pl.pallas_call(
        functools.partial(mlp_kernel, (clips, slots, rows, tile)),
        grid=(steps,),
        in_specs=[
            pl.BlockSpec(memory_space=pltpu.SMEM),
            big, big, whole(cot), big,
            pl.BlockSpec((width, chunk), lambda j: (0, j)),
            whole(b1),
            pl.BlockSpec((chunk, width), lambda j: (j, 0)),
            whole(b2), whole(gain), whole(proj),
        ],
        out_specs=[
            full((clips, slots, width)),
            pl.BlockSpec((1, width, chunk), lambda j: (j // half, 0, j % half)),
            pl.BlockSpec((2, chunk, width // 2), lambda j: (0, j, 0)),
            full((2, width, width // 2)),
            pl.BlockSpec((1, chunk), lambda j: (0, j)),
            full((8, width)),
            full((total, width)),
            full((total, width)),
        ],
        out_shape=[
            jax.ShapeDtypeStruct((clips, slots, width), bf16),
            jax.ShapeDtypeStruct((2, width, hidden // 2), bf16),
            jax.ShapeDtypeStruct((2, hidden, width // 2), bf16),
            jax.ShapeDtypeStruct((2, width, width // 2), bf16),
            jax.ShapeDtypeStruct((1, hidden), f32),
            jax.ShapeDtypeStruct((8, width), f32),
            jax.ShapeDtypeStruct((total, width), f32),
            jax.ShapeDtypeStruct((total, width), bf16),
        ],
        scratch_shapes=[
            pltpu.VMEM((width, total), bf16),
            pltpu.VMEM((total, width), bf16),
            pltpu.VMEM((total, width), f32),
            pltpu.VMEM((total, width), f32),
            pltpu.VMEM((total, chunk), f32),
            pltpu.VMEM((total, chunk), f32),
            pltpu.VMEM((total, chunk), bf16),
            pltpu.VMEM((total, chunk), bf16),
            pltpu.VMEM((8, chunk), f32),
        ],
        compiler_params=params(),
        cost_estimate=pl.CostEstimate(
            flops=12 * total * width * hidden, bytes_accessed=40_000_000, transcendentals=2 * total * hidden
        ),
        name="mlp",
    )(kept, n2, middle, cot, mixed, fc1, b1, fc2, b2, gain, proj)


def sum_arrays(width, hidden, clip_size):
    rows = width // clip_size
    tall = hidden // clip_size
    first, second = (0, 1, 2), (1, 0, 2)
    cut = 5 * width // 6
    return [
        ("fc1", 0, rows, hidden // 4, first),
        ("fc2", 0, tall // 2, width // 2, second),
        ("fc1", hidden // 4, rows, hidden // 4, first),
        ("fc2", tall // 2, tall // 2, width // 2, second),
        ("proj", 0, rows, width // 2, PROJ_ORDER),
        ("qkv", 0, rows // 2, cut, QKV_ORDERS[0]),
        ("qkv", cut, rows // 2, 3 * width // 2 - cut, QKV_ORDERS[1]),
    ]


PROJ_ORDER = (1, 0, 2)
QKV_ORDERS = ((1, 0, 2), (0, 1, 2))
SUM_STEPS = {
    3: [("end", 4, 0), ("start", 4, 1)],
    4: [("end", 0, 0), ("start", 0, 1), ("end", 1, 0), ("end", 2, 0), ("end", 3, 0)],
    5: [("start", 1, 1)],
    6: [("end", 4, 1)],
    8: [("start", 2, 1)],
    9: [("end", 0, 1), ("start", 0, 2)],
    10: [("end", 1, 1)],
    11: [("start", 3, 1)],
    12: [("end", 0, 2), ("start", 0, 3), ("start", 1, 2)],
    13: [("end", 2, 1)],
    14: [("start", 4, 2)],
    15: [("end", 1, 2), ("start", 1, 3)],
    16: [("end", 0, 3), ("start", 0, 4), ("start", 2, 2), ("end", 4, 2)],
    17: [("start", 4, 3)],
    18: [("end", 3, 1), ("start", 3, 2)],
    19: [("end", 0, 4), ("start", 0, 5), ("end", 1, 3), ("start", 1, 4), ("end", 4, 3),
        ("start", 4, 4)],
    20: [("end", 0, 5), ("end", 2, 2), ("start", 2, 3)],
    21: [("end", 1, 4), ("start", 1, 5), ("end", 3, 2), ("start", 3, 3), ("end", 4, 4),
        ("start", 4, 5)],
    22: [("end", 1, 5), ("end", 4, 5)],
    23: [("end", 6, 0), ("start", 6, 1), ("end", 5, 0), ("start", 5, 1), ("end", 2, 3),
        ("start", 2, 4), ("end", 3, 3), ("start", 3, 4), ("input", 2, 0), ("end", 6, 1),
        ("start", 6, 2), ("end", 2, 4), ("start", 2, 5), ("vec", 0, 0), ("end", 5, 1),
        ("start", 5, 2), ("end", 2, 5), ("end", 3, 4), ("start", 3, 5), ("end", 6, 2),
        ("start", 6, 3), ("vec", 1, 0), ("end", 3, 5), ("end", 5, 2), ("start", 5, 3), ("vec", 2, 0),
        ("end", 6, 3), ("start", 6, 4), ("end", 5, 3), ("start", 5, 4), ("vec", 3, 0), ("end", 6, 4),
        ("start", 6, 5), ("end", 6, 5), ("end", 5, 4), ("start", 5, 5), ("vec", 4, 0), ("end", 5, 5)],
}


def backward_kernel(
    meta,
    q_ref, k_ref, v_ref, mask_ref, part_ref, lse_ref, normed_ref, weight_ref, tok_ref, gmid_ref, gain_ref,
    small_ref, db1_ref, gmixed_ref, dfc1_ref, dfc2_ref, dproj_ref,
    gtok_ref, fc1_out, fc2_out, proj_out, qkv_out, vec_out,
    *scratch,
):
    clips, slots, rows, bits, pairs, arrays = meta
    width = weight_ref.shape[0]
    half = width // 2
    lanes = 2 * DH
    step = pl.program_id(0)
    places = step_places(clips, pairs)
    mesh_id = pl.DeviceIdType.MESH
    count = len(arrays)

    scratch = list(scratch)
    take = lambda n: [scratch.pop(0) for _ in range(n)]
    (grad_all, packed, kv_acc, kv_send, kv_got, acc, dn_send, dn_got, dw_acc, bias_acc, vec_sum, vec_got) = take(12)
    own_bufs = dict(zip(("fc1", "fc2", "proj"), take(3)))
    dw_low = {5: scratch.pop(0), 6: scratch.pop(0)}
    stage_bufs = [take(bits + 1) for _ in arrays]
    vert_bufs = take(5)
    full_bufs = take(count)
    (grad_sem, grad_out, grad_in, kv_out, kv_in, dn_out, dn_in, sum_out, sum_in, own_sem, vec_out_sem, vec_in_sem) = take(12)

    core, vert, core_dev, vert_dev = freq_places()
    place = lax.axis_index("clip")
    bit_at = [(place // 2 ** b) % 2 for b in range(bits)]
    clip_dev = [{"clip": place + (1 - 2 * bit_at[b]) * 2 ** b} for b in range(bits)]

    def remote(src, dst, send, recv, device):
        return pltpu.make_async_remote_copy(
            src_ref=src, dst_ref=dst, send_sem=send, recv_sem=recv, device_id=device, device_id_type=mesh_id
        )

    def grad_own(clip):
        src = gmixed_ref.at[clip, :, lane_slice(vert * half, half)]
        return pltpu.make_async_copy(src, grad_all.at[0, clip], grad_sem.at[clip])

    def grad_vert(clip):
        src = gmixed_ref.at[clip, :, lane_slice((1 - vert) * half, half)]
        return remote(src, grad_all.at[1, clip], grad_out.at[clip], grad_in.at[clip], vert_dev)

    def kv_copy(clip, pair):
        return remote(
            kv_send.at[pair], kv_got.at[clip, pair], kv_out.at[clip, pair], kv_in.at[clip, pair], core_dev
        )

    def dn_copy(clip):
        return remote(dn_send.at[clip], dn_got.at[clip], dn_out.at[clip], dn_in.at[clip], vert_dev)

    every = (slice(None),) * bits

    def piece(a, who):
        name, at, r, width_a, _ = arrays[a]
        if name == "fc1":
            return dfc1_ref.at[(who,) + every + (slice(None), pl.ds(at, width_a))]
        if name == "fc2":
            return dfc2_ref.at[(who,) + every + (pl.ds(at, r), slice(None))]
        if name == "proj":
            return dproj_ref.at[who]
        return dw_low[a].at[who]

    def chosen(a, stage, index_of):
        order = arrays[a][4]
        left = [b for b in range(bits)[::-1] if b not in order[: stage - 1]]
        bit = order[stage - 1]
        at = (slice(None),) * left.index(bit) + (index_of(bit),)
        return stage_bufs[a][stage - 1].at[at]

    def stage_copy(a, stage):
        sems = (sum_out.at[a, stage], sum_in.at[a, stage])
        full, packed_array = full_bufs[a], arrays[a][0] == "qkv"
        if stage == 0:
            return remote(piece(a, 1 - core), stage_bufs[a][0], *sems, core_dev)
        if stage <= bits:
            src = chosen(a, stage, lambda bit: 1 - bit_at[bit])
            return remote(src, stage_bufs[a][stage], *sems, clip_dev[arrays[a][4][stage - 1]])
        if stage == bits + 1:
            dst = full.at[core, vert] if packed_array else vert_bufs[a]
            return remote(stage_bufs[a][bits], dst, *sems, vert_dev)
        return remote(full.at[core], full.at[core], *sems, core_dev)

    def own_copy(a):
        return pltpu.make_async_copy(piece(a, core), own_bufs[arrays[a][0]], own_sem.at[a])

    def add_blocks(dst, src, lead):
        if lead == 0:
            dst[...] = dst[...] + src[...]
            return

        def add_one(i, carry):
            at = tuple((i // 2 ** (lead - 1 - j)) % 2 for j in range(lead))
            dst[at] = dst[at] + src[at]
            return carry

        lax.fori_loop(0, 2 ** lead, add_one, 0)

    def stage_end(a, stage):
        name = arrays[a][0]
        stage_copy(a, stage).wait_recv()
        if stage == 0:
            if name == "qkv":
                add_blocks(stage_bufs[a][0], dw_low[a].at[core], bits)
            else:
                own_copy(a).wait()
                add_blocks(stage_bufs[a][0], own_bufs[name], bits)
                if a + 2 < 4:
                    own_copy(a + 2).start()
        elif stage <= bits:
            add_blocks(stage_bufs[a][stage], chosen(a, stage, lambda bit: bit_at[bit]), bits - stage)
            if stage == bits and name == "qkv":
                full_bufs[a][core, vert] = stage_bufs[a][bits][...]
        elif stage == bits + 1 and name != "qkv":
            full_bufs[a][core] = stage_bufs[a][bits][...] + vert_bufs[a][...]

    def vec_copy(hop):
        device = core_dev if hop == 0 else vert_dev if hop == 1 else clip_dev[hop - 2]
        return remote(vec_sum.at[hop], vec_got.at[hop], vec_out_sem.at[hop], vec_in_sem.at[hop], device)

    def vec_end(hop):
        vec_copy(hop).wait_recv()
        vec_sum[hop + 1] = vec_sum[hop] + vec_got[hop]
        if hop < bits + 1:
            vec_copy(hop + 1).start()

    def perform(action):
        kind, a, stage = action
        if kind == "vec":
            vec_end(a)
        elif kind == "start":
            stage_copy(a, stage).start()
        else:
            stage_end(a, stage)

    @pl.when(step == 0)
    def enter():
        barrier = pltpu.get_barrier_semaphore()
        for clip in range(clips):
            grad_own(clip).start()
        for device in [core_dev, vert_dev] + clip_dev:
            pl.semaphore_signal(barrier, inc=1, device_id=device, device_id_type=mesh_id)
        pl.semaphore_wait(barrier, 2 + bits)
        for clip in range(clips):
            grad_vert(clip).start()
        for a in range(5):
            stage_copy(a, 0).start()
        for a in (0, 1, 4):
            own_copy(a).start()
        vec_sum[0] = jnp.zeros_like(vec_sum[0])
        vec_sum[0, 4:8] = small_ref[0:4]
        for i in range(db1_ref.shape[1] // width):
            vec_sum[0, 8 + i : 9 + i] = db1_ref[0:1, i * width : (i + 1) * width]

    for at in sorted(SUM_STEPS):
        if at < places["end"]:
            @pl.when(step == at)
            def run(at=at):
                for action in SUM_STEPS[at]:
                    perform(action)

    def attend():
        index = attention_index(step, places)
        clip = index // (2 * pairs)
        slot = (index // pairs) % 2
        pair = index % pairs

        @pl.when((pair == 0) & (slot == 0))
        def own_grads():
            grad_own(clip).wait()

        @pl.when((pair == 0) & (slot == 1))
        def vert_grads():
            grad_vert(clip).wait_recv()

        query = q_ref[0]
        keys = k_ref[0]
        values = v_ref[0]
        grad = grad_all[slot, clip, :, lane_slice(pair * lanes, lanes)]
        live = mask_ref[0] > 0.5
        product = grad.astype(f32) * part_ref[0].astype(f32)
        dqs, dk, dv = [], None, None
        for head in range(2):
            own_query = only(query, head)
            own_grad = only(grad, head)
            scores = jnp.where(live, dot(own_query, keys, NT), MASKED)
            probs = jnp.exp(scores - lse_ref[0, :, head * DH : head * DH + 1])
            delta = jnp.sum(only(product, head), axis=1, keepdims=True)
            dscores = (probs * (dot(own_grad, values, NT) - delta)).astype(bf16)
            dqs.append(dot(dscores, keys))
            more_k = dot(dscores, own_query, TN)
            more_v = dot(probs.astype(bf16), own_grad, TN)
            dk = more_k if dk is None else dk + more_k
            dv = more_v if dv is None else dv + more_v
        first = own_lanes(dqs[0].shape, 0)
        dq = (jnp.where(first, dqs[0], dqs[1]) * DH ** -0.5).astype(bf16)
        at = pl.ds(pl.multiple_of(slot * rows, rows), rows)
        packed[clip, at, lane_slice(pair * lanes, lanes)] = dq

        @pl.when(slot == 0)
        def keep():
            kv_acc[pair, 0] = dk
            kv_acc[pair, 1] = dv

        @pl.when(slot == 1)
        def send():
            @pl.when(clip > 0)
            def free():
                kv_copy(clip - 1, pair).wait_send()

            for part, value in enumerate((dk, dv)):
                low = (kv_acc[pair, part] + value).astype(bf16)
                packed[clip, :, lane_slice((part + 1) * half + pair * lanes, lanes)] = low[: 2 * rows]
                kv_send[pair, part] = low[2 * rows :]
            kv_copy(clip, pair).start()

    is_attention = step < places["projections"][-1]
    for at in places["projections"][:-1]:
        is_attention = is_attention & (step != at)
    pl.when(is_attention)(attend)

    for clip in range(clips):
        @pl.when(step == places["projections"][clip])
        def projections(clip=clip):
            for pair in range(pairs):
                kv_copy(clip, pair).wait_recv()
                for part in range(2):
                    at = slice((part + 1) * half + pair * lanes, (part + 1) * half + (pair + 1) * lanes)
                    packed[clip, :, at] = packed[clip, :, at] + kv_got[clip, pair, part]
            grads = packed[clip]
            back = dot(grads, weight_ref[...], NT)
            acc[clip] = back[:rows]
            dn_send[clip] = back[rows:].astype(bf16)
            dn_copy(clip).start()
            more = dot(normed_ref[0], grads, TN)
            sum_q = column_sums(grads[:, :half].astype(f32))
            sum_v = column_sums(grads[:, 2 * half :].astype(f32))
            if clip == 0:
                dw_acc[...] = more
                bias_acc[0:1] = sum_q
                bias_acc[1:2] = sum_v
            elif clip < clips - 1:
                dw_acc[...] += more
                bias_acc[0:1] += sum_q
                bias_acc[1:2] += sum_v
            else:
                low = (dw_acc[...] + more).astype(bf16)
                for a, buf in dw_low.items():
                    _, at, r, width_a, _ = arrays[a]
                    for block in range(2 ** bits):
                        index = tuple((block >> b) & 1 for b in range(bits)[::-1])
                        for who in range(2):
                            start = (2 * block + who) * r
                            buf[(who,) + index] = low[start : start + r, at : at + width_a]
                    stage_copy(a, 0).start()
                mine = lane_slice(vert * half, half)
                vec_sum[0, 2:3, mine] = bias_acc[0:1] + sum_q
                vec_sum[0, 3:4, mine] = bias_acc[1:2] + sum_v

    def inputs(clip):
        dn_copy(clip).wait_recv()
        grad = acc[clip] + dn_got[clip].astype(f32)
        unit, inverse = center_scale(tok_ref[0].astype(f32))
        result = gmid_ref[0][:slots] + norm_back(unit, inverse, row_of(gain_ref), grad[:slots])
        gtok_ref[0] = result
        vec_sum[0, 0:1] += column_sums(grad[:slots] * unit)
        vec_sum[0, 1:2] += column_sums(grad[:slots])
        if clip == clips - 1:
            vec_copy(0).start()

    for clip in range(clips - 1):
        pl.when(step == places["inputs"] + clip)(functools.partial(inputs, clip))

    @pl.when(step == places["end"])
    def finish():
        for kind, a, stage in SUM_STEPS[places["end"]]:
            if kind == "input":
                inputs(clips - 1)
            else:
                perform((kind, a, stage))
        for a, (name, at, r, width_a, _) in enumerate(arrays):
            for who in range(2):
                full = full_bufs[a]
                if name == "fc1":
                    start = who * fc1_out.shape[1] // 2 + at
                    fc1_out[:, start : start + width_a] = full[who]
                elif name == "fc2":
                    fc2_out[at : at + r, who * width_a : (who + 1) * width_a] = full[who]
                elif name == "proj":
                    proj_out[:, who * width_a : (who + 1) * width_a] = full[who]
                else:
                    for side in range(2):
                        for start in range(0, width_a, lanes):
                            part, inside = divmod(at + start, half)
                            to = part * width + side * half + inside
                            qkv_out[who * r : (who + 1) * r, to : to + lanes] = full[who, side, :, start : start + lanes]
        vec_out[...] = vec_sum[bits + 2]
        for a in range(count):
            for stage in range(bits + 3):
                stage_copy(a, stage).wait_send()
        for clip in range(clips):
            grad_vert(clip).wait_send()
            dn_copy(clip).wait_send()
        for pair in range(pairs):
            kv_copy(clips - 1, pair).wait_send()
        for hop in range(bits + 2):
            vec_copy(hop).wait_send()


def step_places(clips, pairs):
    of_clip = 2 * pairs
    projections = [of_clip * (c + 1) + 2 + c for c in range(clips - 1)] + [of_clip * clips + clips - 1]
    inputs = projections[-1] + 1
    return {"projections": projections, "inputs": inputs, "end": inputs + clips - 1}


def attention_index(step, places):
    index = step
    for at in places["projections"][:-1]:
        index = index - (step > at).astype(jnp.int32)
    return index


def backward(q, k, v, mask, part, lse, normed, weight_half, tokens, gmid, gain, small, db1, gmixed,
             dfc1, dfc2, dproj, clip_size):
    clips, slots, width = tokens.shape
    rows = gmid.shape[1]
    half = width // 2
    keys = k.shape[1]
    pairs = HEADS // 4
    lanes = 2 * DH
    bits = clip_size.bit_length() - 1
    hidden = db1.shape[1]
    arrays = sum_arrays(width, hidden, clip_size)
    places = step_places(clips, pairs)
    one = pl.Buffered(buffer_count=1)

    def of_pair(s):
        at = jnp.minimum(attention_index(s, places), 2 * clips * pairs - 1)
        return at // (2 * pairs), (at // pairs) % 2, at % pairs

    def of_keys(s):
        clip, _, pair = of_pair(s)
        return clip, 0, pair

    def of_projection(s):
        index = s * 0
        for at in places["projections"][:-1]:
            index = index + (s > at).astype(jnp.int32)
        return index, 0, 0

    def of_clip(s):
        return jnp.clip(s - places["inputs"], 0, clips - 1), 0, 0

    fixed = lambda shape: pl.BlockSpec(shape, lambda s: (0,) * len(shape), pipeline_mode=one)
    tok_pair = pl.BlockSpec((1, rows, lanes), of_pair)
    key_pair = pl.BlockSpec((1, keys, lanes), of_keys)
    anywhere = pl.BlockSpec(memory_space=pl.ANY)
    blocks = (2,) * bits
    r_fc1, r_fc2 = width // clip_size, hidden // clip_size
    dfc1 = dfc1.reshape((2,) + blocks + (r_fc1, hidden // 2))
    dfc2 = dfc2.reshape((2,) + blocks + (r_fc2, half))
    dproj = dproj.reshape((2,) + blocks + (r_fc1, half))
    vmem = lambda *shape: pltpu.VMEM(shape, bf16)
    wide = lambda *shape: pltpu.VMEM(shape, f32)
    scratch = [
        vmem(2, clips, rows, half),
        vmem(clips, 2 * rows, 3 * half),
        wide(pairs, 2, keys, lanes),
        vmem(pairs, 2, 2 * rows, lanes),
        vmem(clips, pairs, 2, 2 * rows, lanes),
        wide(clips, rows, width),
        vmem(clips, rows, width),
        vmem(clips, rows, width),
        wide(width, 3 * half),
        wide(8, half),
        wide(bits + 3, 16, width),
        wide(bits + 2, 16, width),
        vmem(*blocks, r_fc1, hidden // 4),
        vmem(*blocks, r_fc2 // 2, half),
        vmem(*blocks, r_fc1, half),
    ]
    scratch += [vmem(2, *blocks, r, w) for name, _, r, w, _ in arrays if name == "qkv"]
    for _, _, r, w, _ in arrays:
        scratch += [vmem(*((2,) * (bits - stage)), r, w) for stage in range(bits + 1)]
    scratch += [vmem(r, w) for name, _, r, w, _ in arrays if name != "qkv"]
    scratch += [vmem(2, 2, r, w) if name == "qkv" else vmem(2, r, w) for name, _, r, w, _ in arrays]
    dma = lambda *shape: pltpu.SemaphoreType.DMA(shape)
    count = len(arrays)
    scratch += [
        dma(clips), dma(clips), dma(clips), dma(clips, pairs), dma(clips, pairs), dma(clips), dma(clips),
        dma(count, bits + 3), dma(count, bits + 3), dma(count), dma(bits + 2), dma(bits + 2),
    ]
    shape = jax.ShapeDtypeStruct
    return pl.pallas_call(
        functools.partial(backward_kernel, (clips, slots, rows, bits, pairs, arrays)),
        grid=(places["end"] + 1,),
        in_specs=[
            tok_pair, key_pair, key_pair,
            pl.BlockSpec((1, 1, keys), lambda s: (of_pair(s)[0], 0, 0)),
            tok_pair, tok_pair,
            pl.BlockSpec((1, 2 * rows, width), of_projection),
            fixed(weight_half.shape),
            pl.BlockSpec((1, slots, width), of_clip),
            pl.BlockSpec((1, rows, width), of_clip),
            fixed((width,)), fixed((8, width)), fixed((1, hidden)),
            anywhere, anywhere, anywhere, anywhere,
        ],
        out_specs=[
            pl.BlockSpec((1, slots, width), of_clip),
            fixed((r_fc1, hidden)), fixed((r_fc2, width)), fixed((r_fc1, width)),
            fixed((r_fc1, 3 * width)), fixed((16, width)),
        ],
        out_shape=[
            shape((clips, slots, width), f32),
            shape((r_fc1, hidden), bf16),
            shape((r_fc2, width), bf16),
            shape((r_fc1, width), bf16),
            shape((r_fc1, 3 * width), bf16),
            shape((16, width), f32),
        ],
        scratch_shapes=scratch,
        compiler_params=params(collective_id=1, has_side_effects=True),
        cost_estimate=pl.CostEstimate(
            flops=2 * clips * rows * (5 * keys * width + 6 * width * width),
            bytes_accessed=60_000_000,
            transcendentals=clips * rows * keys * HEADS,
        ),
        name="backward",
    )(q, k, v, mask, part, lse, normed, weight_half, tokens, gmid, gain, small, db1, gmixed, dfc1, dfc2, dproj)


def outputs_kernel(fc1, fc2, proj, qkv, vec, gtok, fc1_out, fc2_out, proj_out, qkv_out, gtok_out, db1_out, *outs):
    gtok_out[...] = gtok[...]

    @pl.when(pl.program_id(0) == 0)
    def others():
        for src, dst in ((fc1, fc1_out), (fc2, fc2_out), (proj, proj_out), (qkv, qkv_out)):
            dst[...] = src[...].astype(f32)
        width = vec.shape[1]
        for i, dst in enumerate(outs):
            dst[...] = vec[i : i + 1].reshape(width)
        tall = db1_out.shape[0] // width
        db1_out[...] = jnp.concatenate([vec[8 + i : 9 + i] for i in range(tall)], axis=1).reshape(db1_out.shape[0])


def final_outputs(low_fc1, low_fc2, low_proj, low_qkv, summed, gtok, hidden):
    width = summed.shape[1]
    one = pl.Buffered(buffer_count=1)
    fixed = lambda shape: pl.BlockSpec(shape, lambda c: (0,) * len(shape), pipeline_mode=one)
    by_clip = pl.BlockSpec((1,) + gtok.shape[1:], lambda c: (c, 0, 0))
    shape = jax.ShapeDtypeStruct
    lows = (low_fc1, low_fc2, low_proj, low_qkv)
    return pl.pallas_call(
        outputs_kernel,
        grid=(gtok.shape[0],),
        in_specs=[fixed(a.shape) for a in lows] + [fixed(summed.shape), by_clip],
        out_specs=[fixed(a.shape) for a in lows] + [by_clip, fixed((hidden,))] + [fixed((width,))] * 8,
        out_shape=[shape(a.shape, f32) for a in lows]
        + [shape(gtok.shape, f32), shape((hidden,), f32)]
        + [shape((width,), f32)] * 8,
        compiler_params=params(),
        name="final_outputs",
    )(*lows, summed, gtok)


def partner(kind):
    index = lax.axis_index("freq")
    if kind == "vert":
        return {"freq": (index + 2) % 4}
    return {"freq": index + 1 - 2 * (index % 2)}


def whole_forward_kernel(
    counts,
    tok_ref, qkv_ref, qb_ref, vb_ref, gain_ref, shift_ref, proj_ref, pb_ref, gain2_ref, shift2_ref,
    q_ref, k_ref, v_ref, normed_ref, mixed_ref, lse_ref, middle_ref, normed2_ref, mask_ref,
    held, send_sem, recv_sem,
):
    clips, slots, rows = counts
    clip = pl.program_id(0)
    pair = pl.program_id(1)
    width = tok_ref.shape[-1]

    def copy(kind, index):
        at = {"vert": 0, "core": 1, "diag": 2}[kind]
        return pltpu.make_async_remote_copy(
            src_ref=held.at[index, 0] if kind == "diag" else tok_ref.at[index],
            dst_ref=held.at[index, at],
            send_sem=send_sem.at[index, at],
            recv_sem=recv_sem.at[index, at],
            device_id=partner(kind),
            device_id_type=pl.DeviceIdType.MESH,
        )

    def project(slot, source):
        unit, _ = center_scale(source.astype(f32))
        normed = (unit * gain_ref[...] + shift_ref[...]).astype(bf16)
        if slot == 0:
            normed_ref[0] = normed
            query = (dot(normed, qkv_ref[:, :width]) + qb_ref[...]).astype(bf16)
            q_ref[0] = query * jnp.asarray(DH ** -0.5, bf16)
        both = dot(normed, qkv_ref[:, width:])
        k_ref[0, slot * rows : (slot + 1) * rows] = both[:, :width].astype(bf16)
        v_ref[0, slot * rows : (slot + 1) * rows] = (both[:, width:] + vb_ref[...]).astype(bf16)
        first = (slots // 16) * 16
        kept = source[first:].astype(f32)[slots - first : slots - first + 1, 0:1] + slots // 2
        lane = lax.broadcasted_iota(jnp.int32, (1, rows), 1).astype(f32)
        return (lane < kept).astype(f32)

    @pl.when((clip == 0) & (pair == 0))
    def enter():
        barrier = pltpu.get_barrier_semaphore()
        for kind in ("vert", "core"):
            pl.semaphore_signal(
                barrier, inc=1, device_id=partner(kind), device_id_type=pl.DeviceIdType.MESH
            )
        pl.semaphore_wait(barrier, 2)
        copy("vert", 0).start()
        for index in range(clips):
            copy("core", index).start()

    def pass_on(index):
        copy("vert", index).wait_recv()
        copy("diag", index).start()
        copy("vert", index).wait_send()

        @pl.when(index + 1 < clips)
        def more():
            copy("vert", index + 1).start()

    @pl.when(pair == 0)
    def project_all():
        live_own = project(0, tok_ref[clip])
        copy("core", clip).wait_recv()
        live_core = project(2, held[clip, 1])

        @pl.when(clip == 0)
        def first_pass():
            pass_on(clip)

        live_vert = project(1, held[clip, 0])
        copy("diag", clip).wait_recv()
        live_diag = project(3, held[clip, 2])
        mask_ref[0] = jnp.concatenate([live_own, live_vert, live_core, live_diag], axis=1)

    @pl.when((pair == 3) & (clip + 1 < clips))
    def next_pass():
        pass_on(clip + 1)

    lanes = pl.ds(pl.multiple_of(pair * 2 * DH, 2 * DH), 2 * DH)
    query = q_ref[0, :, lanes]
    keys = k_ref[0, :, lanes]
    values = v_ref[0, :, lanes]
    live = mask_ref[0] > 0.5
    outs, lses = [], []
    for head in range(2):
        scores = jnp.where(live, dot(only(query, head), keys, NT), MASKED)
        top = jnp.max(scores, axis=1, keepdims=True)
        exps = jnp.exp(scores - top)
        total = jnp.sum(exps, axis=1, keepdims=True)
        outs.append(dot(exps.astype(bf16), values) / total)
        lses.append(top + jnp.log(total))
    first = own_lanes(outs[0].shape, 0)
    mixed_ref[0, :, lanes] = jnp.where(first, outs[0], outs[1]).astype(bf16)
    lse_ref[0, :, lanes] = jnp.where(first, lses[0], lses[1])

    @pl.when(pair == pl.num_programs(1) - 1)
    def finish():
        middle = tok_ref[clip].astype(f32) + (dot(mixed_ref[0], proj_ref[...]) + pb_ref[...])
        middle_ref[0] = middle
        unit, _ = center_scale(middle)
        normed2_ref[0] = (unit * gain2_ref[...] + shift2_ref[...]).astype(bf16)
        copy("core", clip).wait_send()
        copy("diag", clip).wait_send()


def whole_forward(tok, slots, qkv_weight, vectors, proj_weight):
    clips, rows, width = tok.shape
    keys = 4 * rows
    pairs = HEADS // 2
    query_bias, value_bias, gain, shift, proj_bias, gain2, shift2 = vectors
    one = pl.Buffered(buffer_count=1)
    row = full((1, width))
    block = lambda n: pl.BlockSpec((1, n, width), lambda c, p: (c, 0, 0))
    flops = 2 * clips * (10 * rows * width * width + 2 * rows * keys * width)
    weight = lambda w: pl.BlockSpec(w.shape, lambda c, p: (0, 0), pipeline_mode=one)
    return pl.pallas_call(
        functools.partial(whole_forward_kernel, (clips, slots, rows)),
        grid=(clips, pairs),
        in_specs=[
            pl.BlockSpec(tok.shape, lambda c, p: (0, 0, 0), pipeline_mode=one),
            weight(qkv_weight), row, row, row, row, weight(proj_weight), row, row, row,
        ],
        out_specs=[block(rows), block(keys), block(keys)] + [block(rows)] * 5
        + [pl.BlockSpec((1, 1, keys), lambda c, p: (c, 0, 0))],
        out_shape=[
            jax.ShapeDtypeStruct((clips, rows, width), bf16),
            jax.ShapeDtypeStruct((clips, keys, width), bf16),
            jax.ShapeDtypeStruct((clips, keys, width), bf16),
            jax.ShapeDtypeStruct((clips, rows, width), bf16),
            jax.ShapeDtypeStruct((clips, rows, width), bf16),
            jax.ShapeDtypeStruct((clips, rows, width), f32),
            jax.ShapeDtypeStruct((clips, rows, width), f32),
            jax.ShapeDtypeStruct((clips, rows, width), bf16),
            jax.ShapeDtypeStruct((clips, 1, keys), f32),
        ],
        scratch_shapes=[
            pltpu.VMEM((clips, 3, rows, width), bf16),
            pltpu.SemaphoreType.DMA((clips, 3)),
            pltpu.SemaphoreType.DMA((clips, 3)),
        ],
        compiler_params=params(collective_id=0, has_side_effects=True),
        cost_estimate=pl.CostEstimate(
            flops=flops, bytes_accessed=40_000_000, transcendentals=clips * rows * keys * HEADS
        ),
        name="whole_forward",
    )(tok, qkv_weight, query_bias, value_bias, gain, shift, proj_weight, proj_bias, gain2, shift2)


def attend_back_kernel(q_ref, k_ref, v_ref, mask_ref, mixed_ref, lse_ref, grad_ref,
                       dq_ref, dkeep_ref, dsend_ref):
    query = q_ref[0]
    keys = k_ref[0]
    values = v_ref[0]
    grad = grad_ref[0]
    live = mask_ref[0] > 0.5
    product = grad.astype(f32) * mixed_ref[0].astype(f32)
    dqs, dk, dv = [], None, None
    for head in range(2):
        own_query = only(query, head)
        own_grad = only(grad, head)
        scores = jnp.where(live, dot(own_query, keys, NT), MASKED)
        probs = jnp.exp(scores - lse_ref[0, :, head * DH : head * DH + 1])
        delta = jnp.sum(only(product, head), axis=1, keepdims=True)
        dscores = (probs * (dot(own_grad, values, NT) - delta)).astype(bf16)
        dqs.append(dot(dscores, keys))
        more_k = dot(dscores, own_query, TN)
        more_v = dot(probs.astype(bf16), own_grad, TN)
        dk = more_k if dk is None else dk + more_k
        dv = more_v if dv is None else dv + more_v
    first = own_lanes(dqs[0].shape, 0)
    dq_ref[0] = (jnp.where(first, dqs[0], dqs[1]) * DH ** -0.5).astype(bf16)
    half = dk.shape[0] // 2
    dkeep_ref[0, 0] = dk[:half].astype(bf16)
    dkeep_ref[1, 0] = dv[:half].astype(bf16)
    dsend_ref[0, 0] = dk[half:].astype(bf16)
    dsend_ref[1, 0] = dv[half:].astype(bf16)


def attend_back(q, k, v, mask, mixed, lse, grad, first_pair, pairs):
    clips, rows, _ = q.shape
    keys = k.shape[1]
    lanes = 2 * DH
    tok = pl.BlockSpec((1, rows, lanes), lambda c, p: (c, 0, first_pair + p))
    key = pl.BlockSpec((1, keys, lanes), lambda c, p: (c, 0, first_pair + p))
    part = pl.BlockSpec((2, 1, keys // 2, lanes), lambda c, p: (0, c, 0, p))
    return pl.pallas_call(
        attend_back_kernel,
        grid=(clips, pairs),
        in_specs=[tok, key, key, pl.BlockSpec((1, 1, keys), lambda c, p: (c, 0, 0)), tok, tok, tok],
        out_specs=[pl.BlockSpec((1, rows, lanes), lambda c, p: (c, 0, p)), part, part],
        out_shape=[
            jax.ShapeDtypeStruct((clips, rows, pairs * lanes), bf16),
            jax.ShapeDtypeStruct((2, clips, keys // 2, pairs * lanes), bf16),
            jax.ShapeDtypeStruct((2, clips, keys // 2, pairs * lanes), bf16),
        ],
        compiler_params=params(),
        cost_estimate=pl.CostEstimate(
            flops=4 * 10 * clips * rows * keys * pairs * lanes,
            bytes_accessed=clips * pairs * lanes * (keys * 10 + rows * 12),
            transcendentals=clips * rows * keys * 2 * pairs,
        ),
        name="attend_back",
    )(q, k, v, mask, mixed, lse, grad)


def weight_kernel(normed_ref, dq_ref, dk0_ref, dk1_ref, dk2_ref, out_ref, dkv_ref, sums_ref):
    part = pl.program_id(0)
    @pl.when(part == 0)
    def query():
        grad = dq_ref[...]
        out_ref[0] = dot(normed_ref[...], grad, TN).astype(bf16)
        sums_ref[0] = column_sums(grad.astype(f32))
        dkv_ref[0] = jnp.zeros_like(dkv_ref[0])

    @pl.when(part > 0)
    def other():
        grad = (dk0_ref[0].astype(f32) + dk1_ref[0].astype(f32) + dk2_ref[0].astype(f32)).astype(bf16)
        dkv_ref[0] = grad
        out_ref[0] = dot(normed_ref[...], grad, TN).astype(bf16)
        sums_ref[0] = column_sums(grad.astype(f32))


def weight_grads(normed, dq, parts):
    total, width = normed.shape
    lanes = dq.shape[1]
    before = lambda j: (jnp.maximum(j - 1, 0), 0, 0)
    part = pl.BlockSpec((1, total, lanes), before)
    return pl.pallas_call(
        weight_kernel,
        grid=(3,),
        in_specs=[full((total, width)), full((total, lanes)), part, part, part],
        out_specs=[
            pl.BlockSpec((1, width, lanes), lambda j: (j, 0, 0)),
            part,
            pl.BlockSpec((1, 1, lanes), lambda j: (j, 0, 0)),
        ],
        out_shape=[
            jax.ShapeDtypeStruct((3, width, lanes), bf16),
            jax.ShapeDtypeStruct((2, total, lanes), bf16),
            jax.ShapeDtypeStruct((3, 1, lanes), f32),
        ],
        compiler_params=params(),
        cost_estimate=pl.CostEstimate(
            flops=6 * total * width * lanes, bytes_accessed=8_000_000, transcendentals=0
        ),
        name="weight_grads",
    )(normed, dq, *parts)


def input_kernel(counts, groups, *refs):
    clips, slots, rows = counts
    dqs = refs[:groups]
    dkvs = refs[groups : 2 * groups]
    qkv_ref, tok_ref, gmid_ref, gain_ref, shift_ref, out_ref, small_ref = refs[2 * groups :]
    clip = pl.program_id(0)
    width = tok_ref.shape[-1]
    lanes = width // groups
    grad = None
    for group in range(groups):
        for part in range(3):
            rows_grad = dqs[group][0] if part == 0 else dkvs[group][part - 1]
            at = part * width + group * lanes
            more = dot(rows_grad, qkv_ref[:, at : at + lanes], NT)
            grad = more if grad is None else grad + more
    unit, inverse = center_scale(tok_ref[0].astype(f32))
    result = gmid_ref[0] + norm_back(unit, inverse, gain_ref[...], grad)
    out_ref[0] = result[:slots]

    @pl.when(clip == 0)
    def start():
        small_ref[...] = jnp.zeros_like(small_ref)

    small_ref[0:1] += column_sums(grad * unit)
    small_ref[1:2] += column_sums(grad)


def input_grads(dqs, dkvs, qkv_weight, tokens, gmid, gain, shift, slots):
    clips, rows, width = tokens.shape
    groups = len(dqs)
    lanes = width // groups
    tok = pl.BlockSpec((1, rows, width), lambda c: (c, 0, 0))
    return pl.pallas_call(
        functools.partial(input_kernel, (clips, slots, rows), groups),
        grid=(clips,),
        in_specs=[pl.BlockSpec((1, rows, lanes), lambda c: (c, 0, 0))] * groups
        + [pl.BlockSpec((2, rows, lanes), lambda c: (0, c, 0))] * groups
        + [full(qkv_weight.shape), tok, tok, full((1, width)), full((1, width))],
        out_specs=[pl.BlockSpec((1, slots, width), lambda c: (c, 0, 0)), full((8, width))],
        out_shape=[
            jax.ShapeDtypeStruct((clips, slots, width), f32),
            jax.ShapeDtypeStruct((8, width), f32),
        ],
        compiler_params=params(),
        cost_estimate=pl.CostEstimate(
            flops=6 * clips * rows * width * width, bytes_accessed=16_000_000, transcendentals=0
        ),
        name="input_grads",
    )(*dqs, *dkvs, qkv_weight, tokens, gmid, gain, shift)


def swap_bit(array, axis, size, bit):
    return lax.ppermute(array, axis, [(i, i ^ (1 << bit)) for i in range(size)])


def add_low(left, right):
    return (left.astype(f32) + right.astype(f32)).astype(bf16)


def pick(array, index, dim):
    return lax.dynamic_index_in_dim(array, index, dim, keepdims=False)


def bit_of(axis, bit):
    return (lax.axis_index(axis) >> bit) & 1


def scatter_sum(split, clip_size, order):
    core = bit_of("freq", 0)
    vert = bit_of("freq", 1)
    bits = clip_size.bit_length() - 1
    lanes = split.shape[-1]
    value = add_low(pick(split, core, 0), swap_bit(pick(split, 1 - core, 0), "freq", 4, 0))
    rows = value.shape[0] // (2 * clip_size)
    value = value.reshape((2,) * bits + (2, rows, lanes))
    left = list(range(bits))[::-1]
    for bit in order:
        at = left.index(bit)
        mine = bit_of("clip", bit)
        value = add_low(
            pick(value, mine, at), swap_bit(pick(value, 1 - mine, at), "clip", clip_size, bit)
        )
        left.remove(bit)
    return add_low(pick(value, vert, 0), swap_bit(pick(value, 1 - vert, 0), "freq", 4, 1))


def gather_low(part):
    core = bit_of("freq", 0)
    vert = bit_of("freq", 1)
    other = swap_bit(part, "freq", 4, 1)
    tall = jnp.where(vert == 0, jnp.concatenate([part, other]), jnp.concatenate([other, part]))
    side = swap_bit(tall, "freq", 4, 0)
    return jnp.where(
        core == 0,
        jnp.concatenate([tall, side], axis=1),
        jnp.concatenate([side, tall], axis=1),
    ).astype(f32)


def total_sum(array, clip_size):
    for bit in range(2):
        array = array + swap_bit(array, "freq", 4, bit)
    for bit in range(clip_size.bit_length() - 1):
        array = array + swap_bit(array, "clip", clip_size, bit)
    return array


def on_device_plain(
    clip_size, tokens, kept_counts, attn_gain, attn_shift, qkv_weight, query_bias, value_bias,
    proj_weight, proj_bias, mlp_gain, mlp_shift, fc1_weight, fc1_bias, fc2_weight, fc2_bias, cotangent,
):
    clips, slots, width = tokens.shape
    rows = -(-slots // 16) * 16
    total = clips * rows
    bits = clip_size.bit_length() - 1
    forward_order = list(range(bits))
    second_order = forward_order[1:2] + forward_order[:1] + forward_order[2:]
    vec = lambda v: v.astype(f32)[None, :]
    kept = (kept_counts - slots // 2).astype(bf16)
    tok = jnp.concatenate(
        [tokens, jnp.broadcast_to(kept[:, :, None], (clips, rows - slots, width))], axis=1
    )
    vectors = [vec(v) for v in (query_bias, value_bias, attn_gain, attn_shift, proj_bias, mlp_gain, mlp_shift)]
    q, k, v, normed, mixed, lse, middle, normed2, mask = whole_forward(
        tok, slots, qkv_weight, vectors, proj_weight
    )
    flat = lambda a: a.reshape(total, width)
    layer_out, dfc1, dfc2, dproj, db1, small2, gmid, gmixed = mlp(
        kept_counts, flat(normed2), flat(middle), cotangent, flat(mixed), fc1_weight, fc1_bias,
        fc2_weight, fc2_bias, mlp_gain, proj_weight, rows,
    )
    early = total_sum(jnp.concatenate([small2[:4].reshape(-1), db1.reshape(-1)])[None, :], clip_size)[0]
    sum_fc1 = gather_low(scatter_sum(dfc1, clip_size, forward_order))
    sum_fc2 = gather_low(scatter_sum(dfc2, clip_size, second_order))
    sum_proj = gather_low(scatter_sum(dproj, clip_size, forward_order))

    groups = 3
    pairs = HEADS // 2 // groups
    lanes = pairs * 2 * DH
    gmixed = gmixed.reshape(clips, rows, width)
    dqs, dkvs, sums, sharded = [], [], [], []
    for group in range(groups):
        dq, keep, send = attend_back(q, k, v, mask, mixed, lse, gmixed, group * pairs, pairs)
        got = swap_bit(send, "freq", 4, 0)
        across = swap_bit(add_low(keep[:, :, rows:], got[:, :, rows:]), "freq", 4, 1)
        parts = [a.reshape(2, total, lanes) for a in (keep[:, :, :rows], got[:, :, :rows], across)]
        dw, dkv, colsum = weight_grads(flat(normed), dq.reshape(total, lanes), parts)
        half = lanes // 2
        split = jnp.stack(
            [
                jnp.concatenate([dw[i, :, s * half : (s + 1) * half] for i in range(3)], axis=1)
                for s in range(2)
            ]
        )
        order = forward_order if group % 2 == 0 else second_order
        summed = gather_low(scatter_sum(split, clip_size, order))
        sharded.append(summed.reshape(summed.shape[0], 2, 3, half))
        dqs.append(dq)
        dkvs.append(dkv)
        sums.append(colsum)
    grad_tokens, small1 = input_grads(
        dqs, dkvs, qkv_weight, tok, gmid.reshape(clips, rows, width), vectors[2], vectors[3], slots
    )
    qkv = jnp.stack(sharded, axis=1)
    sum_qkv = qkv.transpose(0, 3, 1, 2, 4).reshape(qkv.shape[0], 3 * width)
    bias = jnp.concatenate(sums, axis=2)
    late = total_sum(
        jnp.concatenate([small1[0:1], small1[1:2], bias[0], bias[2]], axis=1), clip_size
    )[0]
    cut = lambda a, i: a[i * width : (i + 1) * width]
    return (
        layer_out, grad_tokens, cut(late, 0), cut(late, 1), sum_qkv, cut(late, 2), cut(late, 3),
        sum_proj, cut(early, 3), cut(early, 0), cut(early, 1), sum_fc1, early[4 * width :],
        sum_fc2, cut(early, 2),
    )


def on_device(
    clip_size, tokens, kept_counts, attn_gain, attn_shift, qkv_weight, query_bias, value_bias,
    proj_weight, proj_bias, mlp_gain, mlp_shift, fc1_weight, fc1_bias, fc2_weight, fc2_bias, cotangent,
):
    clips, slots, width = tokens.shape
    rows = -(-slots // 16) * 16
    if clip_size != 8 or width % (32 * clip_size):
        return on_device_plain(
            clip_size, tokens, kept_counts, attn_gain, attn_shift, qkv_weight, query_bias, value_bias,
            proj_weight, proj_bias, mlp_gain, mlp_shift, fc1_weight, fc1_bias, fc2_weight, fc2_bias, cotangent,
        )
    q, k, v, normed, part, lse, mask, weight_half, mixed, middle, normed2 = forward(
        kept_counts, tokens, rows, qkv_weight, query_bias, value_bias, attn_gain, attn_shift,
        proj_weight, proj_bias, mlp_gain, mlp_shift,
    )
    flat = lambda a: a.reshape(clips * rows, width)
    layer_out, dfc1, dfc2, dproj, db1, small, gmid, gmixed = mlp(
        kept_counts, flat(normed2), flat(middle), cotangent, flat(mixed), fc1_weight, fc1_bias,
        fc2_weight, fc2_bias, mlp_gain, proj_weight, rows,
    )
    by_clip = lambda a: a.reshape(clips, rows, width)
    gtok, low_fc1, low_fc2, low_proj, low_qkv, summed = backward(
        q, k, v, mask, part, lse, normed, weight_half, tokens, by_clip(gmid), attn_gain, small, db1,
        by_clip(gmixed), dfc1, dfc2, dproj, clip_size,
    )
    fc1, fc2, proj, qkv, grad_tokens, fc1_b, *rows_out = final_outputs(
        low_fc1, low_fc2, low_proj, low_qkv, summed, gtok, fc1_bias.shape[0]
    )
    return (
        layer_out, grad_tokens, rows_out[0], rows_out[1], qkv, rows_out[2], rows_out[3], proj, rows_out[7],
        rows_out[4], rows_out[5], fc1, fc1_b, fc2, rows_out[6],
    )


def solution(mesh):
    rows = P("clip", "freq", None)
    shard = P("clip", None)
    return jax.shard_map(
        functools.partial(on_device, mesh.shape["clip"]),
        mesh=mesh,
        in_specs=(rows, P("clip", "freq")) + (P(),) * 13 + (rows,),
        out_specs=(rows, rows, P(), P(), shard, P(), P(), shard, P(), P(), P(), shard, P(), shard, P()),
        check_vma=False,
    )
```

```python
import functools
import math

import jax
import jax.numpy as jnp
from jax import lax
from jax.experimental import pallas as pl
from jax.experimental.pallas import tpu as pltpu
from jax.sharding import PartitionSpec as P

HEADS = 12
DH = 64
EPS = 1e-06
MASKED = -1000000000.0
VMEM_BYTES = 60 * 1024 * 1024

f32 = jnp.float32
bf16 = jnp.bfloat16
NN = (((1,), (0,)), ((), ()))
NT = (((1,), (1,)), ((), ()))
TN = (((0,), (0,)), ((), ()))


def dot(left, right, dims=NN):
    return lax.dot_general(left, right, dims, preferred_element_type=f32)


def center_scale(rows):
    center = rows - jnp.mean(rows, axis=-1, keepdims=True)
    inverse = lax.rsqrt(jnp.mean(center * center, axis=-1, keepdims=True) + EPS)
    return center * inverse, inverse


def norm_back(unit, inverse, gain, grad):
    scaled = grad * gain
    return inverse * (
        scaled
        - jnp.mean(scaled, axis=-1, keepdims=True)
        - unit * jnp.mean(scaled * unit, axis=-1, keepdims=True)
    )


def column_sums(rows):
    return jnp.sum(rows, axis=0, keepdims=True)


def own_lanes(shape, head):
    lane = lax.broadcasted_iota(jnp.int32, shape, len(shape) - 1)
    return lane < DH if head == 0 else lane >= DH


def only(rows, head):
    return jnp.where(own_lanes(rows.shape, head), rows, jnp.zeros_like(rows))


def full(shape):
    return pl.BlockSpec(shape, lambda *ids: (0,) * len(shape))


def params(**more):
    return pltpu.CompilerParams(vmem_limit_bytes=VMEM_BYTES, **more)


def freq_places():
    freq = lax.axis_index("freq")
    core, vert = freq % 2, freq // 2
    return core, vert, {"freq": freq + 1 - 2 * core}, {"freq": (freq + 2) % 4}


def lane_slice(start, size):
    return pl.ds(pl.multiple_of(start, 2 * DH), size)


def row_of(ref):
    return ref[...].astype(f32).reshape(1, ref.shape[0])


def forward_kernel(
    counts,
    kept_ref, tok_ref, qkv_ref, qb_ref, vb_ref, gain_ref, shift_ref, proj_ref, pb_ref, gain2_ref, shift2_ref,
    q_out, k_out, v_out, normed_out, weight_out, part_ref, lse_ref, mask_ref, mixed_ref, middle_ref, normed2_ref,
    q_all, k_all, v_all, normed_all, weight, live_all, own, held, mix_send, mix_got, own_mix, vecs,
    tok_send, tok_recv, part_send, part_recv, out_sem, weight_sem,
):
    clips, slots, rows, pairs = counts
    clip = pl.program_id(0)
    turn = pl.program_id(1)
    slot = 1 - turn
    width = tok_ref.shape[-1]
    half = width // 2
    lanes = 2 * DH
    core, vert, core_dev, vert_dev = freq_places()
    mesh_id = pl.DeviceIdType.MESH

    def copy(kind, index):
        at = {"vert": 0, "core": 1, "diag": 2}[kind]
        return pltpu.make_async_remote_copy(
            src_ref=held.at[index, 0] if kind == "diag" else own.at[index],
            dst_ref=held.at[index, at],
            send_sem=tok_send.at[index, at],
            recv_sem=tok_recv.at[index, at],
            device_id=vert_dev if kind == "vert" else core_dev,
            device_id_type=mesh_id,
        )

    def mix_copy(index, which):
        return pltpu.make_async_remote_copy(
            src_ref=mix_send.at[index, which],
            dst_ref=mix_got.at[index, which],
            send_sem=part_send.at[index, which],
            recv_sem=part_recv.at[index, which],
            device_id=vert_dev,
            device_id_type=mesh_id,
        )

    def project(index, slot, source):
        unit, _ = center_scale(source.astype(f32))
        normed = (unit * vecs[2:3] + vecs[3:4]).astype(bf16)
        at = slice(slot * rows, (slot + 1) * rows)
        if slot < 2:
            normed_all[index, at] = normed
            query = (dot(normed, weight[:, :half]) + vecs[0:1, lane_slice(vert * half, half)]).astype(bf16)
            q_all[index, at] = query * jnp.asarray(DH ** -0.5, bf16)
        both = dot(normed, weight[:, half:])
        k_all[index, at] = both[:, :half].astype(bf16)
        v_all[index, at] = (both[:, half:] + vecs[1:2, lane_slice(vert * half, half)]).astype(bf16)
        first = (slots // 16) * 16
        kept = source[first:].astype(f32)[slots - first : slots - first + 1, 0:1] + slots // 2
        lane = lax.broadcasted_iota(jnp.int32, (1, rows), 1).astype(f32)
        live_all[index, slot] = (lane < kept).astype(f32)

    def out_copies(index):
        return [
            pltpu.make_async_copy(src.at[index], dst.at[index], out_sem.at[index, i])
            for i, (src, dst) in enumerate(
                ((q_all, q_out), (k_all, k_out), (v_all, v_out), (normed_all, normed_out))
            )
        ]

    def weight_copy():
        return pltpu.make_async_copy(weight, weight_out, weight_sem)

    @pl.when((clip == 0) & (turn == 0))
    def enter():
        barrier = pltpu.get_barrier_semaphore()
        for device in (vert_dev, core_dev):
            pl.semaphore_signal(barrier, inc=1, device_id=device, device_id_type=mesh_id)
        first = (slots // 16) * 16
        for index in range(clips):
            kept = (kept_ref[index, 0] - slots // 2).astype(f32).astype(bf16)
            own[index, first:] = jnp.broadcast_to(kept, (rows - first, width))
            own[index, :slots] = tok_ref[index]
        pl.semaphore_wait(barrier, 2)
        copy("vert", 0).start()
        for index in range(clips):
            copy("core", index).start()
        for i, ref in enumerate((qb_ref, vb_ref, gain_ref, shift_ref, pb_ref, gain2_ref, shift2_ref)):
            vecs[i : i + 1] = row_of(ref)
        for part in range(3):
            weight[:, part * half : (part + 1) * half] = qkv_ref[:, lane_slice(part * width + vert * half, half)]
        weight_copy().start()

        def own_slots(index, carry):
            project(index, 0, own[index])
            return carry

        def core_slots(index, carry):
            copy("core", index).wait_recv()
            project(index, 2, held[index, 1])
            return carry

        lax.fori_loop(0, clips, own_slots, 0)
        lax.fori_loop(0, clips, core_slots, 0)
        copy("vert", 0).wait_recv()
        copy("diag", 0).start()
        copy("vert", 0).wait_send()
        if clips > 1:
            copy("vert", 1).start()

    @pl.when(turn == 0)
    def project_rest():
        project(clip, 1, held[clip, 0])
        copy("diag", clip).wait_recv()
        project(clip, 3, held[clip, 2])
        for i in range(4):
            mask_ref[0, :, i * rows : (i + 1) * rows] = live_all[clip, i]
        for move in out_copies(clip):
            move.start()

    for index in range(2, clips):
        @pl.when((turn == 1) & (clip == index - 2))
        def send_ahead(index=index):
            copy("vert", index - 1).wait_send()
            copy("vert", index).start()

    def finish(index):
        at = lane_slice(vert * half, half)
        mixed_ref[0, :, at] = own_mix[...]
        for which in range(pairs):
            mix_copy(index, which).wait_recv()
            at = lane_slice((1 - vert) * half + which * lanes, lanes)
            mixed_ref[0, :, at] = mix_got[index, which]
        middle = own[index].astype(f32) + (dot(mixed_ref[0], proj_ref[...]) + vecs[4:5])
        middle_ref[0] = middle
        unit, _ = center_scale(middle)
        normed2_ref[0] = (unit * vecs[5:6] + vecs[6:7]).astype(bf16)
        copy("core", index).wait_send()
        copy("diag", index).wait_send()
        for which in range(pairs):
            mix_copy(index, which).wait_send()

    at = pl.ds(pl.multiple_of(slot * rows, rows), rows)
    live = mask_ref[0] > 0.5
    for pair in range(pairs):
        here = slice(pair * lanes, (pair + 1) * lanes)
        keys = k_all[clip, :, here]
        values = v_all[clip, :, here]
        query = q_all[clip, at, here]
        outs, lses = [], []
        for head in range(2):
            scores = jnp.where(live, dot(only(query, head), keys, NT), MASKED)
            top = jnp.max(scores, axis=1, keepdims=True)
            exps = jnp.exp(scores - top)
            total = jnp.sum(exps, axis=1, keepdims=True)
            outs.append(dot(exps.astype(bf16), values) / total)
            lses.append(top + jnp.log(total))
        first = own_lanes(outs[0].shape, 0)
        mixed = jnp.where(first, outs[0], outs[1]).astype(bf16)
        part_ref[0, at, here] = mixed
        lse_ref[0, at, here] = jnp.where(first, lses[0], lses[1])

    @pl.when(slot == 1)
    def give():
        for pair in range(pairs):
            mix_send[clip, pair] = part_ref[0, rows:, pair * lanes : (pair + 1) * lanes]
            mix_copy(clip, pair).start()

    @pl.when((turn == 0) & (clip > 0))
    def finish_before():
        finish(clip - 1)

    @pl.when(turn == 1)
    def keep_own():
        own_mix[...] = part_ref[0, :rows]

    @pl.when((turn == 1) & (clip + 1 < clips))
    def pass_on():
        copy("vert", clip + 1).wait_recv()
        copy("diag", clip + 1).start()

    @pl.when((turn == 1) & (clip == clips - 1))
    def finish_last():
        finish(clip)
        copy("vert", clips - 1).wait_send()

    @pl.when((turn == 1) & (clip == clips - 1))
    def leave():
        weight_copy().wait()
        for index in range(clips):
            for move in out_copies(index):
                move.wait()


def forward(kept, tokens, rows, qkv_weight, query_bias, value_bias, gain, shift, proj_weight, proj_bias, gain2, shift2):
    clips, slots, width = tokens.shape
    keys = 4 * rows
    half = width // 2
    pairs = HEADS // 4
    lanes = 2 * DH
    one = pl.Buffered(buffer_count=1)
    block = lambda n, m: pl.BlockSpec((1, n, m), lambda c, p: (c, 0, 0))
    late = pl.BlockSpec((1, rows, width), lambda c, t: (jnp.maximum(c - 1 + t, 0), 0, 0))
    anywhere = pl.BlockSpec(memory_space=pl.ANY)
    whole = lambda a: pl.BlockSpec(a.shape, lambda c, p: (0,) * a.ndim, pipeline_mode=one)
    shape = jax.ShapeDtypeStruct
    flops = 2 * clips * (rows * width * width * 6 + 2 * rows * keys * width)
    vectors = (query_bias, value_bias, gain, shift)
    return pl.pallas_call(
        functools.partial(forward_kernel, (clips, slots, rows, pairs)),
        grid=(clips, 2),
        in_specs=[pl.BlockSpec(memory_space=pltpu.SMEM), whole(tokens), whole(qkv_weight)]
        + [whole(v) for v in vectors]
        + [whole(proj_weight)]
        + [whole(v) for v in (proj_bias, gain2, shift2)],
        out_specs=[
            anywhere, anywhere, anywhere, anywhere, anywhere,
            block(2 * rows, half), block(2 * rows, half), block(1, keys),
            late, late, late,
        ],
        out_shape=[
            shape((clips, 2 * rows, half), bf16),
            shape((clips, keys, half), bf16),
            shape((clips, keys, half), bf16),
            shape((clips, 2 * rows, width), bf16),
            shape((width, 3 * half), bf16),
            shape((clips, 2 * rows, half), bf16),
            shape((clips, 2 * rows, half), f32),
            shape((clips, 1, keys), f32),
            shape((clips, rows, width), bf16),
            shape((clips, rows, width), f32),
            shape((clips, rows, width), bf16),
        ],
        scratch_shapes=[
            pltpu.VMEM((clips, 2 * rows, half), bf16),
            pltpu.VMEM((clips, keys, half), bf16),
            pltpu.VMEM((clips, keys, half), bf16),
            pltpu.VMEM((clips, 2 * rows, width), bf16),
            pltpu.VMEM((width, 3 * half), bf16),
            pltpu.VMEM((clips, 4, 1, rows), f32),
            pltpu.VMEM((clips, rows, width), bf16),
            pltpu.VMEM((clips, 3, rows, width), bf16),
            pltpu.VMEM((clips, pairs, rows, lanes), bf16),
            pltpu.VMEM((clips, pairs, rows, lanes), bf16),
            pltpu.VMEM((rows, half), bf16),
            pltpu.VMEM((8, width), f32),
            pltpu.SemaphoreType.DMA((clips, 3)),
            pltpu.SemaphoreType.DMA((clips, 3)),
            pltpu.SemaphoreType.DMA((clips, pairs)),
            pltpu.SemaphoreType.DMA((clips, pairs)),
            pltpu.SemaphoreType.DMA((clips, 4)),
            pltpu.SemaphoreType.DMA(()),
        ],
        compiler_params=params(collective_id=0, has_side_effects=True),
        cost_estimate=pl.CostEstimate(
            flops=flops, bytes_accessed=40_000_000, transcendentals=clips * rows * keys * HEADS
        ),
        name="forward",
    )(kept, tokens, qkv_weight, *vectors, proj_weight, proj_bias, gain2, shift2)


def mlp_kernel(
    counts,
    kept_ref, n2_ref, middle_ref, cot_ref, mixed_ref, fc1_ref, b1_ref, fc2_ref, b2_ref, gain_ref, proj_ref,
    out_ref, dfc1_ref, dfc2_ref, dproj_ref, db1_ref, small_ref, gmid_ref, gmixed_ref,
    n2t_ref, grad_ref, out_acc, dn_acc, hidden_ref, dact_ref, active_ref, dhid_ref, biases,
):
    clips, slots, rows, tile = counts
    step = pl.program_id(0)
    width = n2_ref.shape[-1]
    chunk = fc1_ref.shape[-1]
    total = clips * rows

    def live_rows(clip, size):
        slot = lax.broadcasted_iota(jnp.int32, (size, 1), 0)
        return (slot < kept_ref[clip, 0]).astype(f32)

    @pl.when(step == 0)
    def start():
        n2t_ref[...] = n2_ref[...].T
        first = (slots // 16) * 16
        for clip in range(clips):
            begin = clip * rows
            grad_ref[begin + first : begin + rows] = jnp.zeros((rows - first, width), bf16)
            grad_ref[begin : begin + slots] = cot_ref[clip] * live_rows(clip, slots).astype(bf16)
        all_biases = row_of(b1_ref)
        for i in range(all_biases.shape[1] // chunk):
            biases[i : i + 1] = all_biases[:, i * chunk : (i + 1) * chunk]
        out_acc[...] = jnp.zeros_like(out_acc)
        dn_acc[...] = jnp.zeros_like(dn_acc)

    hidden_ref[...] = dot(n2_ref[...], fc1_ref[...])
    dact_ref[...] = dot(grad_ref[...], fc2_ref[...], NT)
    bias = biases[pl.ds(step, 1), :]

    def gelu_tile(index, sums):
        at = pl.ds(pl.multiple_of(index * tile, tile), tile)
        hidden = hidden_ref[at, :] + bias
        cdf = 0.5 * (1.0 + lax.erf(hidden * (0.5 ** 0.5)))
        active_ref[at, :] = (hidden * cdf).astype(bf16)
        slope = cdf + hidden * (jnp.exp(-0.5 * hidden * hidden) * (1.0 / math.sqrt(2.0 * math.pi)))
        dhid = (dact_ref[at, :] * slope).astype(bf16)
        dhid_ref[at, :] = dhid
        return sums + dhid.astype(f32)

    sums = lax.fori_loop(0, total // tile, gelu_tile, jnp.zeros((tile, chunk), f32))
    db1_ref[...] = column_sums(sums)
    active = active_ref[...]
    dhid = dhid_ref[...]
    out_acc[...] += dot(active, fc2_ref[...])
    dn_acc[...] += dot(dhid, fc1_ref[...], NT)
    dfc1_ref[0] = dot(n2t_ref[...], dhid).astype(bf16)
    dfc2 = dot(active, grad_ref[...], TN).astype(bf16)
    half = width // 2
    dfc2_ref[0] = dfc2[:, :half]
    dfc2_ref[1] = dfc2[:, half:]

    @pl.when(step == pl.num_programs(0) - 1)
    def finish():
        gain = row_of(gain_ref)
        bias2 = row_of(b2_ref)
        sum_gain = jnp.zeros((1, width), f32)
        sum_shift = jnp.zeros((1, width), f32)
        sum_grad = jnp.zeros((1, width), f32)
        sum_proj = jnp.zeros((1, width), f32)
        for clip in range(clips):
            at = slice(clip * rows, (clip + 1) * rows)
            middle = middle_ref[at]
            layer = middle[:slots] + (out_acc[clip * rows : clip * rows + slots] + bias2)
            out_ref[clip] = (live_rows(clip, slots) * layer).astype(bf16)
            unit, inverse = center_scale(middle)
            grad = dn_acc[at]
            out_grad = grad_ref[at].astype(f32)
            gmid = out_grad + norm_back(unit, inverse, gain, grad)
            gmid_ref[at] = gmid
            low = gmid.astype(bf16)
            dhid_ref[at, :width] = low
            gmixed_ref[at] = dot(low, proj_ref[...], NT).astype(bf16)
            sum_gain += column_sums(grad * unit)
            sum_shift += column_sums(grad)
            sum_grad += column_sums(out_grad)
            sum_proj += column_sums(low.astype(f32))
        dproj = dot(mixed_ref[...], dhid_ref[:, :width], TN).astype(bf16)
        dproj_ref[0] = dproj[:, :half]
        dproj_ref[1] = dproj[:, half:]
        small_ref[0:1] = sum_gain
        small_ref[1:2] = sum_shift
        small_ref[2:3] = sum_grad
        small_ref[3:4] = sum_proj


def mlp(kept, n2, middle, cot, mixed, fc1, b1, fc2, b2, gain, proj, rows):
    clips, slots, _ = cot.shape
    total, width = n2.shape
    hidden = fc1.shape[1]
    chunk = 768
    steps = hidden // chunk
    half = steps // 2
    tile = 16
    whole = lambda a: pl.BlockSpec(a.shape, lambda j: (0,) * a.ndim, pipeline_mode=one)
    one = pl.Buffered(buffer_count=1)
    big = pl.BlockSpec((total, width), lambda j: (0, 0), pipeline_mode=one)
    return pl.pallas_call(
        functools.partial(mlp_kernel, (clips, slots, rows, tile)),
        grid=(steps,),
        in_specs=[
            pl.BlockSpec(memory_space=pltpu.SMEM),
            big, big, whole(cot), big,
            pl.BlockSpec((width, chunk), lambda j: (0, j)),
            whole(b1),
            pl.BlockSpec((chunk, width), lambda j: (j, 0)),
            whole(b2), whole(gain), whole(proj),
        ],
        out_specs=[
            full((clips, slots, width)),
            pl.BlockSpec((1, width, chunk), lambda j: (j // half, 0, j % half)),
            pl.BlockSpec((2, chunk, width // 2), lambda j: (0, j, 0)),
            full((2, width, width // 2)),
            pl.BlockSpec((1, chunk), lambda j: (0, j)),
            full((8, width)),
            full((total, width)),
            full((total, width)),
        ],
        out_shape=[
            jax.ShapeDtypeStruct((clips, slots, width), bf16),
            jax.ShapeDtypeStruct((2, width, hidden // 2), bf16),
            jax.ShapeDtypeStruct((2, hidden, width // 2), bf16),
            jax.ShapeDtypeStruct((2, width, width // 2), bf16),
            jax.ShapeDtypeStruct((1, hidden), f32),
            jax.ShapeDtypeStruct((8, width), f32),
            jax.ShapeDtypeStruct((total, width), f32),
            jax.ShapeDtypeStruct((total, width), bf16),
        ],
        scratch_shapes=[
            pltpu.VMEM((width, total), bf16),
            pltpu.VMEM((total, width), bf16),
            pltpu.VMEM((total, width), f32),
            pltpu.VMEM((total, width), f32),
            pltpu.VMEM((total, chunk), f32),
            pltpu.VMEM((total, chunk), f32),
            pltpu.VMEM((total, chunk), bf16),
            pltpu.VMEM((total, chunk), bf16),
            pltpu.VMEM((8, chunk), f32),
        ],
        compiler_params=params(),
        cost_estimate=pl.CostEstimate(
            flops=12 * total * width * hidden, bytes_accessed=40_000_000, transcendentals=2 * total * hidden
        ),
        name="mlp",
    )(kept, n2, middle, cot, mixed, fc1, b1, fc2, b2, gain, proj)


def sum_arrays(width, hidden, clip_size):
    rows = width // clip_size
    tall = hidden // clip_size
    first, second = (0, 1, 2), (1, 0, 2)
    cut = 5 * width // 6
    return [
        ("fc1", 0, rows, hidden // 4, first),
        ("fc2", 0, tall // 2, width // 2, second),
        ("fc1", hidden // 4, rows, hidden // 4, first),
        ("fc2", tall // 2, tall // 2, width // 2, second),
        ("proj", 0, rows, width // 2, PROJ_ORDER),
        ("qkv", 0, rows // 2, cut, QKV_ORDERS[0]),
        ("qkv", cut, rows // 2, 3 * width // 2 - cut, QKV_ORDERS[1]),
    ]


PROJ_ORDER = (1, 0, 2)
QKV_ORDERS = ((1, 0, 2), (0, 1, 2))
SUM_STEPS = {
    3: [("end", 4, 0), ("start", 4, 1)],
    4: [("end", 0, 0), ("start", 0, 1), ("end", 1, 0), ("end", 2, 0), ("end", 3, 0)],
    5: [("start", 1, 1)],
    6: [("end", 4, 1)],
    8: [("start", 2, 1)],
    9: [("end", 0, 1), ("start", 0, 2)],
    10: [("end", 1, 1)],
    11: [("start", 3, 1)],
    12: [("end", 0, 2), ("start", 0, 3), ("start", 1, 2)],
    13: [("end", 2, 1)],
    14: [("start", 4, 2)],
    15: [("end", 1, 2), ("start", 1, 3)],
    16: [("end", 0, 3), ("start", 0, 4), ("start", 2, 2), ("end", 4, 2)],
    17: [("start", 4, 3)],
    18: [("end", 3, 1), ("start", 3, 2)],
    19: [("end", 0, 4), ("start", 0, 5), ("end", 1, 3), ("start", 1, 4), ("end", 4, 3),
        ("start", 4, 4)],
    20: [("end", 0, 5), ("end", 2, 2), ("start", 2, 3)],
    21: [("end", 1, 4), ("start", 1, 5), ("end", 3, 2), ("start", 3, 3), ("end", 4, 4),
        ("start", 4, 5)],
    22: [("end", 1, 5), ("end", 4, 5)],
    23: [("end", 6, 0), ("start", 6, 1), ("end", 5, 0), ("start", 5, 1), ("end", 2, 3),
        ("start", 2, 4), ("end", 3, 3), ("start", 3, 4), ("input", 2, 0), ("end", 6, 1),
        ("start", 6, 2), ("end", 2, 4), ("start", 2, 5), ("vec", 0, 0), ("end", 5, 1),
        ("start", 5, 2), ("end", 2, 5), ("end", 3, 4), ("start", 3, 5), ("end", 6, 2),
        ("start", 6, 3), ("vec", 1, 0), ("end", 3, 5), ("end", 5, 2), ("start", 5, 3), ("vec", 2, 0),
        ("end", 6, 3), ("start", 6, 4), ("end", 5, 3), ("start", 5, 4), ("vec", 3, 0), ("end", 6, 4),
        ("start", 6, 5), ("end", 6, 5), ("end", 5, 4), ("start", 5, 5), ("vec", 4, 0), ("end", 5, 5)],
}


def backward_kernel(
    meta,
    q_ref, k_ref, v_ref, mask_ref, part_ref, lse_ref, normed_ref, weight_ref, tok_ref, gmid_ref, gain_ref,
    small_ref, db1_ref, gmixed_ref, dfc1_ref, dfc2_ref, dproj_ref,
    gtok_ref, fc1_out, fc2_out, proj_out, qkv_out, vec_out,
    *scratch,
):
    clips, slots, rows, bits, pairs, arrays = meta
    width = weight_ref.shape[0]
    half = width // 2
    lanes = 2 * DH
    step = pl.program_id(0)
    places = step_places(clips, pairs)
    mesh_id = pl.DeviceIdType.MESH
    count = len(arrays)

    scratch = list(scratch)
    take = lambda n: [scratch.pop(0) for _ in range(n)]
    (grad_all, packed, kv_acc, kv_send, kv_got, acc, dn_send, dn_got, dw_acc, bias_acc, vec_sum, vec_got) = take(12)
    own_bufs = dict(zip(("fc1", "fc2", "proj"), take(3)))
    dw_low = {5: scratch.pop(0), 6: scratch.pop(0)}
    stage_bufs = [take(bits + 1) for _ in arrays]
    vert_bufs = take(5)
    full_bufs = take(count)
    (grad_sem, grad_out, grad_in, kv_out, kv_in, dn_out, dn_in, sum_out, sum_in, own_sem, vec_out_sem, vec_in_sem) = take(12)

    core, vert, core_dev, vert_dev = freq_places()
    place = lax.axis_index("clip")
    bit_at = [(place // 2 ** b) % 2 for b in range(bits)]
    clip_dev = [{"clip": place + (1 - 2 * bit_at[b]) * 2 ** b} for b in range(bits)]

    def remote(src, dst, send, recv, device):
        return pltpu.make_async_remote_copy(
            src_ref=src, dst_ref=dst, send_sem=send, recv_sem=recv, device_id=device, device_id_type=mesh_id
        )

    def grad_own(clip):
        src = gmixed_ref.at[clip, :, lane_slice(vert * half, half)]
        return pltpu.make_async_copy(src, grad_all.at[0, clip], grad_sem.at[clip])

    def grad_vert(clip):
        src = gmixed_ref.at[clip, :, lane_slice((1 - vert) * half, half)]
        return remote(src, grad_all.at[1, clip], grad_out.at[clip], grad_in.at[clip], vert_dev)

    def kv_copy(clip, pair):
        return remote(
            kv_send.at[pair], kv_got.at[clip, pair], kv_out.at[clip, pair], kv_in.at[clip, pair], core_dev
        )

    def dn_copy(clip):
        return remote(dn_send.at[clip], dn_got.at[clip], dn_out.at[clip], dn_in.at[clip], vert_dev)

    every = (slice(None),) * bits

    def piece(a, who):
        name, at, r, width_a, _ = arrays[a]
        if name == "fc1":
            return dfc1_ref.at[(who,) + every + (slice(None), pl.ds(at, width_a))]
        if name == "fc2":
            return dfc2_ref.at[(who,) + every + (pl.ds(at, r), slice(None))]
        if name == "proj":
            return dproj_ref.at[who]
        return dw_low[a].at[who]

    def chosen(a, stage, index_of):
        order = arrays[a][4]
        left = [b for b in range(bits)[::-1] if b not in order[: stage - 1]]
        bit = order[stage - 1]
        at = (slice(None),) * left.index(bit) + (index_of(bit),)
        return stage_bufs[a][stage - 1].at[at]

    def stage_copy(a, stage):
        sems = (sum_out.at[a, stage], sum_in.at[a, stage])
        full, packed_array = full_bufs[a], arrays[a][0] == "qkv"
        if stage == 0:
            return remote(piece(a, 1 - core), stage_bufs[a][0], *sems, core_dev)
        if stage <= bits:
            src = chosen(a, stage, lambda bit: 1 - bit_at[bit])
            return remote(src, stage_bufs[a][stage], *sems, clip_dev[arrays[a][4][stage - 1]])
        if stage == bits + 1:
            dst = full.at[core, vert] if packed_array else vert_bufs[a]
            return remote(stage_bufs[a][bits], dst, *sems, vert_dev)
        return remote(full.at[core], full.at[core], *sems, core_dev)

    def own_copy(a):
        return pltpu.make_async_copy(piece(a, core), own_bufs[arrays[a][0]], own_sem.at[a])

    def add_blocks(dst, src, lead):
        if lead == 0:
            dst[...] = dst[...] + src[...]
            return

        def add_one(i, carry):
            at = tuple((i // 2 ** (lead - 1 - j)) % 2 for j in range(lead))
            dst[at] = dst[at] + src[at]
            return carry

        lax.fori_loop(0, 2 ** lead, add_one, 0)

    def stage_end(a, stage):
        name = arrays[a][0]
        stage_copy(a, stage).wait_recv()
        if stage == 0:
            if name == "qkv":
                add_blocks(stage_bufs[a][0], dw_low[a].at[core], bits)
            else:
                own_copy(a).wait()
                add_blocks(stage_bufs[a][0], own_bufs[name], bits)
                if a + 2 < 4:
                    own_copy(a + 2).start()
        elif stage <= bits:
            add_blocks(stage_bufs[a][stage], chosen(a, stage, lambda bit: bit_at[bit]), bits - stage)
            if stage == bits and name == "qkv":
                full_bufs[a][core, vert] = stage_bufs[a][bits][...]
        elif stage == bits + 1 and name != "qkv":
            full_bufs[a][core] = stage_bufs[a][bits][...] + vert_bufs[a][...]

    def vec_copy(hop):
        device = core_dev if hop == 0 else vert_dev if hop == 1 else clip_dev[hop - 2]
        return remote(vec_sum.at[hop], vec_got.at[hop], vec_out_sem.at[hop], vec_in_sem.at[hop], device)

    def vec_end(hop):
        vec_copy(hop).wait_recv()
        vec_sum[hop + 1] = vec_sum[hop] + vec_got[hop]
        if hop < bits + 1:
            vec_copy(hop + 1).start()

    def perform(action):
        kind, a, stage = action
        if kind == "vec":
            vec_end(a)
        elif kind == "start":
            stage_copy(a, stage).start()
        else:
            stage_end(a, stage)

    @pl.when(step == 0)
    def enter():
        barrier = pltpu.get_barrier_semaphore()
        for clip in range(clips):
            grad_own(clip).start()
        for device in [core_dev, vert_dev] + clip_dev:
            pl.semaphore_signal(barrier, inc=1, device_id=device, device_id_type=mesh_id)
        pl.semaphore_wait(barrier, 2 + bits)
        for clip in range(clips):
            grad_vert(clip).start()
        for a in range(5):
            stage_copy(a, 0).start()
        for a in (0, 1, 4):
            own_copy(a).start()
        vec_sum[0] = jnp.zeros_like(vec_sum[0])
        vec_sum[0, 4:8] = small_ref[0:4]
        for i in range(db1_ref.shape[1] // width):
            vec_sum[0, 8 + i : 9 + i] = db1_ref[0:1, i * width : (i + 1) * width]

    for at in sorted(SUM_STEPS):
        if at < places["end"]:
            @pl.when(step == at)
            def run(at=at):
                for action in SUM_STEPS[at]:
                    perform(action)

    def attend():
        index = attention_index(step, places)
        clip = index // (2 * pairs)
        slot = (index // pairs) % 2
        pair = index % pairs

        @pl.when((pair == 0) & (slot == 0))
        def own_grads():
            grad_own(clip).wait()

        @pl.when((pair == 0) & (slot == 1))
        def vert_grads():
            grad_vert(clip).wait_recv()

        query = q_ref[0]
        keys = k_ref[0]
        values = v_ref[0]
        grad = grad_all[slot, clip, :, lane_slice(pair * lanes, lanes)]
        live = mask_ref[0] > 0.5
        product = grad.astype(f32) * part_ref[0].astype(f32)
        dqs, dk, dv = [], None, None
        for head in range(2):
            own_query = only(query, head)
            own_grad = only(grad, head)
            scores = jnp.where(live, dot(own_query, keys, NT), MASKED)
            probs = jnp.exp(scores - lse_ref[0, :, head * DH : head * DH + 1])
            delta = jnp.sum(only(product, head), axis=1, keepdims=True)
            dscores = (probs * (dot(own_grad, values, NT) - delta)).astype(bf16)
            dqs.append(dot(dscores, keys))
            more_k = dot(dscores, own_query, TN)
            more_v = dot(probs.astype(bf16), own_grad, TN)
            dk = more_k if dk is None else dk + more_k
            dv = more_v if dv is None else dv + more_v
        first = own_lanes(dqs[0].shape, 0)
        dq = (jnp.where(first, dqs[0], dqs[1]) * DH ** -0.5).astype(bf16)
        at = pl.ds(pl.multiple_of(slot * rows, rows), rows)
        packed[clip, at, lane_slice(pair * lanes, lanes)] = dq

        @pl.when(slot == 0)
        def keep():
            kv_acc[pair, 0] = dk
            kv_acc[pair, 1] = dv

        @pl.when(slot == 1)
        def send():
            @pl.when(clip > 0)
            def free():
                kv_copy(clip - 1, pair).wait_send()

            for part, value in enumerate((dk, dv)):
                low = (kv_acc[pair, part] + value).astype(bf16)
                packed[clip, :, lane_slice((part + 1) * half + pair * lanes, lanes)] = low[: 2 * rows]
                kv_send[pair, part] = low[2 * rows :]
            kv_copy(clip, pair).start()

    is_attention = step < places["projections"][-1]
    for at in places["projections"][:-1]:
        is_attention = is_attention & (step != at)
    pl.when(is_attention)(attend)

    for clip in range(clips):
        @pl.when(step == places["projections"][clip])
        def projections(clip=clip):
            for pair in range(pairs):
                kv_copy(clip, pair).wait_recv()
                for part in range(2):
                    at = slice((part + 1) * half + pair * lanes, (part + 1) * half + (pair + 1) * lanes)
                    packed[clip, :, at] = packed[clip, :, at] + kv_got[clip, pair, part]
            grads = packed[clip]
            back = dot(grads, weight_ref[...], NT)
            acc[clip] = back[:rows]
            dn_send[clip] = back[rows:].astype(bf16)
            dn_copy(clip).start()
            more = dot(normed_ref[0], grads, TN)
            sum_q = column_sums(grads[:, :half].astype(f32))
            sum_v = column_sums(grads[:, 2 * half :].astype(f32))
            if clip == 0:
                dw_acc[...] = more
                bias_acc[0:1] = sum_q
                bias_acc[1:2] = sum_v
            elif clip < clips - 1:
                dw_acc[...] += more
                bias_acc[0:1] += sum_q
                bias_acc[1:2] += sum_v
            else:
                low = (dw_acc[...] + more).astype(bf16)
                for a, buf in dw_low.items():
                    _, at, r, width_a, _ = arrays[a]
                    for block in range(2 ** bits):
                        index = tuple((block >> b) & 1 for b in range(bits)[::-1])
                        for who in range(2):
                            start = (2 * block + who) * r
                            buf[(who,) + index] = low[start : start + r, at : at + width_a]
                    stage_copy(a, 0).start()
                mine = lane_slice(vert * half, half)
                vec_sum[0, 2:3, mine] = bias_acc[0:1] + sum_q
                vec_sum[0, 3:4, mine] = bias_acc[1:2] + sum_v

    def inputs(clip):
        dn_copy(clip).wait_recv()
        grad = acc[clip] + dn_got[clip].astype(f32)
        unit, inverse = center_scale(tok_ref[0].astype(f32))
        result = gmid_ref[0][:slots] + norm_back(unit, inverse, row_of(gain_ref), grad[:slots])
        gtok_ref[0] = result
        vec_sum[0, 0:1] += column_sums(grad[:slots] * unit)
        vec_sum[0, 1:2] += column_sums(grad[:slots])
        if clip == clips - 1:
            vec_copy(0).start()

    for clip in range(clips - 1):
        pl.when(step == places["inputs"] + clip)(functools.partial(inputs, clip))

    @pl.when(step == places["end"])
    def finish():
        for kind, a, stage in SUM_STEPS[places["end"]]:
            if kind == "input":
                inputs(clips - 1)
            else:
                perform((kind, a, stage))
        for a, (name, at, r, width_a, _) in enumerate(arrays):
            for who in range(2):
                full = full_bufs[a]
                if name == "fc1":
                    start = who * fc1_out.shape[1] // 2 + at
                    fc1_out[:, start : start + width_a] = full[who]
                elif name == "fc2":
                    fc2_out[at : at + r, who * width_a : (who + 1) * width_a] = full[who]
                elif name == "proj":
                    proj_out[:, who * width_a : (who + 1) * width_a] = full[who]
                else:
                    for side in range(2):
                        for start in range(0, width_a, lanes):
                            part, inside = divmod(at + start, half)
                            to = part * width + side * half + inside
                            qkv_out[who * r : (who + 1) * r, to : to + lanes] = full[who, side, :, start : start + lanes]
        vec_out[...] = vec_sum[bits + 2]
        for a in range(count):
            for stage in range(bits + 3):
                stage_copy(a, stage).wait_send()
        for clip in range(clips):
            grad_vert(clip).wait_send()
            dn_copy(clip).wait_send()
        for pair in range(pairs):
            kv_copy(clips - 1, pair).wait_send()
        for hop in range(bits + 2):
            vec_copy(hop).wait_send()


def step_places(clips, pairs):
    of_clip = 2 * pairs
    projections = [of_clip * (c + 1) + 2 + c for c in range(clips - 1)] + [of_clip * clips + clips - 1]
    inputs = projections[-1] + 1
    return {"projections": projections, "inputs": inputs, "end": inputs + clips - 1}


def attention_index(step, places):
    index = step
    for at in places["projections"][:-1]:
        index = index - (step > at).astype(jnp.int32)
    return index


def backward(q, k, v, mask, part, lse, normed, weight_half, tokens, gmid, gain, small, db1, gmixed,
             dfc1, dfc2, dproj, clip_size):
    clips, slots, width = tokens.shape
    rows = gmid.shape[1]
    half = width // 2
    keys = k.shape[1]
    pairs = HEADS // 4
    lanes = 2 * DH
    bits = clip_size.bit_length() - 1
    hidden = db1.shape[1]
    arrays = sum_arrays(width, hidden, clip_size)
    places = step_places(clips, pairs)
    one = pl.Buffered(buffer_count=1)

    def of_pair(s):
        at = jnp.minimum(attention_index(s, places), 2 * clips * pairs - 1)
        return at // (2 * pairs), (at // pairs) % 2, at % pairs

    def of_keys(s):
        clip, _, pair = of_pair(s)
        return clip, 0, pair

    def of_projection(s):
        index = s * 0
        for at in places["projections"][:-1]:
            index = index + (s > at).astype(jnp.int32)
        return index, 0, 0

    def of_clip(s):
        return jnp.clip(s - places["inputs"], 0, clips - 1), 0, 0

    fixed = lambda shape: pl.BlockSpec(shape, lambda s: (0,) * len(shape), pipeline_mode=one)
    tok_pair = pl.BlockSpec((1, rows, lanes), of_pair)
    key_pair = pl.BlockSpec((1, keys, lanes), of_keys)
    anywhere = pl.BlockSpec(memory_space=pl.ANY)
    blocks = (2,) * bits
    r_fc1, r_fc2 = width // clip_size, hidden // clip_size
    dfc1 = dfc1.reshape((2,) + blocks + (r_fc1, hidden // 2))
    dfc2 = dfc2.reshape((2,) + blocks + (r_fc2, half))
    dproj = dproj.reshape((2,) + blocks + (r_fc1, half))
    vmem = lambda *shape: pltpu.VMEM(shape, bf16)
    wide = lambda *shape: pltpu.VMEM(shape, f32)
    scratch = [
        vmem(2, clips, rows, half),
        vmem(clips, 2 * rows, 3 * half),
        wide(pairs, 2, keys, lanes),
        vmem(pairs, 2, 2 * rows, lanes),
        vmem(clips, pairs, 2, 2 * rows, lanes),
        wide(clips, rows, width),
        vmem(clips, rows, width),
        vmem(clips, rows, width),
        wide(width, 3 * half),
        wide(8, half),
        wide(bits + 3, 16, width),
        wide(bits + 2, 16, width),
        vmem(*blocks, r_fc1, hidden // 4),
        vmem(*blocks, r_fc2 // 2, half),
        vmem(*blocks, r_fc1, half),
    ]
    scratch += [vmem(2, *blocks, r, w) for name, _, r, w, _ in arrays if name == "qkv"]
    for _, _, r, w, _ in arrays:
        scratch += [vmem(*((2,) * (bits - stage)), r, w) for stage in range(bits + 1)]
    scratch += [vmem(r, w) for name, _, r, w, _ in arrays if name != "qkv"]
    scratch += [vmem(2, 2, r, w) if name == "qkv" else vmem(2, r, w) for name, _, r, w, _ in arrays]
    dma = lambda *shape: pltpu.SemaphoreType.DMA(shape)
    count = len(arrays)
    scratch += [
        dma(clips), dma(clips), dma(clips), dma(clips, pairs), dma(clips, pairs), dma(clips), dma(clips),
        dma(count, bits + 3), dma(count, bits + 3), dma(count), dma(bits + 2), dma(bits + 2),
    ]
    shape = jax.ShapeDtypeStruct
    return pl.pallas_call(
        functools.partial(backward_kernel, (clips, slots, rows, bits, pairs, arrays)),
        grid=(places["end"] + 1,),
        in_specs=[
            tok_pair, key_pair, key_pair,
            pl.BlockSpec((1, 1, keys), lambda s: (of_pair(s)[0], 0, 0)),
            tok_pair, tok_pair,
            pl.BlockSpec((1, 2 * rows, width), of_projection),
            fixed(weight_half.shape),
            pl.BlockSpec((1, slots, width), of_clip),
            pl.BlockSpec((1, rows, width), of_clip),
            fixed((width,)), fixed((8, width)), fixed((1, hidden)),
            anywhere, anywhere, anywhere, anywhere,
        ],
        out_specs=[
            pl.BlockSpec((1, slots, width), of_clip),
            fixed((r_fc1, hidden)), fixed((r_fc2, width)), fixed((r_fc1, width)),
            fixed((r_fc1, 3 * width)), fixed((16, width)),
        ],
        out_shape=[
            shape((clips, slots, width), f32),
            shape((r_fc1, hidden), bf16),
            shape((r_fc2, width), bf16),
            shape((r_fc1, width), bf16),
            shape((r_fc1, 3 * width), bf16),
            shape((16, width), f32),
        ],
        scratch_shapes=scratch,
        compiler_params=params(collective_id=1, has_side_effects=True),
        cost_estimate=pl.CostEstimate(
            flops=2 * clips * rows * (5 * keys * width + 6 * width * width),
            bytes_accessed=60_000_000,
            transcendentals=clips * rows * keys * HEADS,
        ),
        name="backward",
    )(q, k, v, mask, part, lse, normed, weight_half, tokens, gmid, gain, small, db1, gmixed, dfc1, dfc2, dproj)


def outputs_kernel(fc1, fc2, proj, qkv, vec, gtok, fc1_out, fc2_out, proj_out, qkv_out, gtok_out, db1_out, *outs):
    gtok_out[...] = gtok[...]

    @pl.when(pl.program_id(0) == 0)
    def others():
        for src, dst in ((fc1, fc1_out), (fc2, fc2_out), (proj, proj_out), (qkv, qkv_out)):
            dst[...] = src[...].astype(f32)
        width = vec.shape[1]
        for i, dst in enumerate(outs):
            dst[...] = vec[i : i + 1].reshape(width)
        tall = db1_out.shape[0] // width
        db1_out[...] = jnp.concatenate([vec[8 + i : 9 + i] for i in range(tall)], axis=1).reshape(db1_out.shape[0])


def final_outputs(low_fc1, low_fc2, low_proj, low_qkv, summed, gtok, hidden):
    width = summed.shape[1]
    one = pl.Buffered(buffer_count=1)
    fixed = lambda shape: pl.BlockSpec(shape, lambda c: (0,) * len(shape), pipeline_mode=one)
    by_clip = pl.BlockSpec((1,) + gtok.shape[1:], lambda c: (c, 0, 0))
    shape = jax.ShapeDtypeStruct
    lows = (low_fc1, low_fc2, low_proj, low_qkv)
    return pl.pallas_call(
        outputs_kernel,
        grid=(gtok.shape[0],),
        in_specs=[fixed(a.shape) for a in lows] + [fixed(summed.shape), by_clip],
        out_specs=[fixed(a.shape) for a in lows] + [by_clip, fixed((hidden,))] + [fixed((width,))] * 8,
        out_shape=[shape(a.shape, f32) for a in lows]
        + [shape(gtok.shape, f32), shape((hidden,), f32)]
        + [shape((width,), f32)] * 8,
        compiler_params=params(),
        name="final_outputs",
    )(*lows, summed, gtok)


def partner(kind):
    index = lax.axis_index("freq")
    if kind == "vert":
        return {"freq": (index + 2) % 4}
    return {"freq": index + 1 - 2 * (index % 2)}


def whole_forward_kernel(
    counts,
    tok_ref, qkv_ref, qb_ref, vb_ref, gain_ref, shift_ref, proj_ref, pb_ref, gain2_ref, shift2_ref,
    q_ref, k_ref, v_ref, normed_ref, mixed_ref, lse_ref, middle_ref, normed2_ref, mask_ref,
    held, send_sem, recv_sem,
):
    clips, slots, rows = counts
    clip = pl.program_id(0)
    pair = pl.program_id(1)
    width = tok_ref.shape[-1]

    def copy(kind, index):
        at = {"vert": 0, "core": 1, "diag": 2}[kind]
        return pltpu.make_async_remote_copy(
            src_ref=held.at[index, 0] if kind == "diag" else tok_ref.at[index],
            dst_ref=held.at[index, at],
            send_sem=send_sem.at[index, at],
            recv_sem=recv_sem.at[index, at],
            device_id=partner(kind),
            device_id_type=pl.DeviceIdType.MESH,
        )

    def project(slot, source):
        unit, _ = center_scale(source.astype(f32))
        normed = (unit * gain_ref[...] + shift_ref[...]).astype(bf16)
        if slot == 0:
            normed_ref[0] = normed
            query = (dot(normed, qkv_ref[:, :width]) + qb_ref[...]).astype(bf16)
            q_ref[0] = query * jnp.asarray(DH ** -0.5, bf16)
        both = dot(normed, qkv_ref[:, width:])
        k_ref[0, slot * rows : (slot + 1) * rows] = both[:, :width].astype(bf16)
        v_ref[0, slot * rows : (slot + 1) * rows] = (both[:, width:] + vb_ref[...]).astype(bf16)
        first = (slots // 16) * 16
        kept = source[first:].astype(f32)[slots - first : slots - first + 1, 0:1] + slots // 2
        lane = lax.broadcasted_iota(jnp.int32, (1, rows), 1).astype(f32)
        return (lane < kept).astype(f32)

    @pl.when((clip == 0) & (pair == 0))
    def enter():
        barrier = pltpu.get_barrier_semaphore()
        for kind in ("vert", "core"):
            pl.semaphore_signal(
                barrier, inc=1, device_id=partner(kind), device_id_type=pl.DeviceIdType.MESH
            )
        pl.semaphore_wait(barrier, 2)
        copy("vert", 0).start()
        for index in range(clips):
            copy("core", index).start()

    def pass_on(index):
        copy("vert", index).wait_recv()
        copy("diag", index).start()
        copy("vert", index).wait_send()

        @pl.when(index + 1 < clips)
        def more():
            copy("vert", index + 1).start()

    @pl.when(pair == 0)
    def project_all():
        live_own = project(0, tok_ref[clip])
        copy("core", clip).wait_recv()
        live_core = project(2, held[clip, 1])

        @pl.when(clip == 0)
        def first_pass():
            pass_on(clip)

        live_vert = project(1, held[clip, 0])
        copy("diag", clip).wait_recv()
        live_diag = project(3, held[clip, 2])
        mask_ref[0] = jnp.concatenate([live_own, live_vert, live_core, live_diag], axis=1)

    @pl.when((pair == 3) & (clip + 1 < clips))
    def next_pass():
        pass_on(clip + 1)

    lanes = pl.ds(pl.multiple_of(pair * 2 * DH, 2 * DH), 2 * DH)
    query = q_ref[0, :, lanes]
    keys = k_ref[0, :, lanes]
    values = v_ref[0, :, lanes]
    live = mask_ref[0] > 0.5
    outs, lses = [], []
    for head in range(2):
        scores = jnp.where(live, dot(only(query, head), keys, NT), MASKED)
        top = jnp.max(scores, axis=1, keepdims=True)
        exps = jnp.exp(scores - top)
        total = jnp.sum(exps, axis=1, keepdims=True)
        outs.append(dot(exps.astype(bf16), values) / total)
        lses.append(top + jnp.log(total))
    first = own_lanes(outs[0].shape, 0)
    mixed_ref[0, :, lanes] = jnp.where(first, outs[0], outs[1]).astype(bf16)
    lse_ref[0, :, lanes] = jnp.where(first, lses[0], lses[1])

    @pl.when(pair == pl.num_programs(1) - 1)
    def finish():
        middle = tok_ref[clip].astype(f32) + (dot(mixed_ref[0], proj_ref[...]) + pb_ref[...])
        middle_ref[0] = middle
        unit, _ = center_scale(middle)
        normed2_ref[0] = (unit * gain2_ref[...] + shift2_ref[...]).astype(bf16)
        copy("core", clip).wait_send()
        copy("diag", clip).wait_send()


def whole_forward(tok, slots, qkv_weight, vectors, proj_weight):
    clips, rows, width = tok.shape
    keys = 4 * rows
    pairs = HEADS // 2
    query_bias, value_bias, gain, shift, proj_bias, gain2, shift2 = vectors
    one = pl.Buffered(buffer_count=1)
    row = full((1, width))
    block = lambda n: pl.BlockSpec((1, n, width), lambda c, p: (c, 0, 0))
    flops = 2 * clips * (10 * rows * width * width + 2 * rows * keys * width)
    weight = lambda w: pl.BlockSpec(w.shape, lambda c, p: (0, 0), pipeline_mode=one)
    return pl.pallas_call(
        functools.partial(whole_forward_kernel, (clips, slots, rows)),
        grid=(clips, pairs),
        in_specs=[
            pl.BlockSpec(tok.shape, lambda c, p: (0, 0, 0), pipeline_mode=one),
            weight(qkv_weight), row, row, row, row, weight(proj_weight), row, row, row,
        ],
        out_specs=[block(rows), block(keys), block(keys)] + [block(rows)] * 5
        + [pl.BlockSpec((1, 1, keys), lambda c, p: (c, 0, 0))],
        out_shape=[
            jax.ShapeDtypeStruct((clips, rows, width), bf16),
            jax.ShapeDtypeStruct((clips, keys, width), bf16),
            jax.ShapeDtypeStruct((clips, keys, width), bf16),
            jax.ShapeDtypeStruct((clips, rows, width), bf16),
            jax.ShapeDtypeStruct((clips, rows, width), bf16),
            jax.ShapeDtypeStruct((clips, rows, width), f32),
            jax.ShapeDtypeStruct((clips, rows, width), f32),
            jax.ShapeDtypeStruct((clips, rows, width), bf16),
            jax.ShapeDtypeStruct((clips, 1, keys), f32),
        ],
        scratch_shapes=[
            pltpu.VMEM((clips, 3, rows, width), bf16),
            pltpu.SemaphoreType.DMA((clips, 3)),
            pltpu.SemaphoreType.DMA((clips, 3)),
        ],
        compiler_params=params(collective_id=0, has_side_effects=True),
        cost_estimate=pl.CostEstimate(
            flops=flops, bytes_accessed=40_000_000, transcendentals=clips * rows * keys * HEADS
        ),
        name="whole_forward",
    )(tok, qkv_weight, query_bias, value_bias, gain, shift, proj_weight, proj_bias, gain2, shift2)


def attend_back_kernel(q_ref, k_ref, v_ref, mask_ref, mixed_ref, lse_ref, grad_ref,
                       dq_ref, dkeep_ref, dsend_ref):
    query = q_ref[0]
    keys = k_ref[0]
    values = v_ref[0]
    grad = grad_ref[0]
    live = mask_ref[0] > 0.5
    product = grad.astype(f32) * mixed_ref[0].astype(f32)
    dqs, dk, dv = [], None, None
    for head in range(2):
        own_query = only(query, head)
        own_grad = only(grad, head)
        scores = jnp.where(live, dot(own_query, keys, NT), MASKED)
        probs = jnp.exp(scores - lse_ref[0, :, head * DH : head * DH + 1])
        delta = jnp.sum(only(product, head), axis=1, keepdims=True)
        dscores = (probs * (dot(own_grad, values, NT) - delta)).astype(bf16)
        dqs.append(dot(dscores, keys))
        more_k = dot(dscores, own_query, TN)
        more_v = dot(probs.astype(bf16), own_grad, TN)
        dk = more_k if dk is None else dk + more_k
        dv = more_v if dv is None else dv + more_v
    first = own_lanes(dqs[0].shape, 0)
    dq_ref[0] = (jnp.where(first, dqs[0], dqs[1]) * DH ** -0.5).astype(bf16)
    half = dk.shape[0] // 2
    dkeep_ref[0, 0] = dk[:half].astype(bf16)
    dkeep_ref[1, 0] = dv[:half].astype(bf16)
    dsend_ref[0, 0] = dk[half:].astype(bf16)
    dsend_ref[1, 0] = dv[half:].astype(bf16)


def attend_back(q, k, v, mask, mixed, lse, grad, first_pair, pairs):
    clips, rows, _ = q.shape
    keys = k.shape[1]
    lanes = 2 * DH
    tok = pl.BlockSpec((1, rows, lanes), lambda c, p: (c, 0, first_pair + p))
    key = pl.BlockSpec((1, keys, lanes), lambda c, p: (c, 0, first_pair + p))
    part = pl.BlockSpec((2, 1, keys // 2, lanes), lambda c, p: (0, c, 0, p))
    return pl.pallas_call(
        attend_back_kernel,
        grid=(clips, pairs),
        in_specs=[tok, key, key, pl.BlockSpec((1, 1, keys), lambda c, p: (c, 0, 0)), tok, tok, tok],
        out_specs=[pl.BlockSpec((1, rows, lanes), lambda c, p: (c, 0, p)), part, part],
        out_shape=[
            jax.ShapeDtypeStruct((clips, rows, pairs * lanes), bf16),
            jax.ShapeDtypeStruct((2, clips, keys // 2, pairs * lanes), bf16),
            jax.ShapeDtypeStruct((2, clips, keys // 2, pairs * lanes), bf16),
        ],
        compiler_params=params(),
        cost_estimate=pl.CostEstimate(
            flops=4 * 10 * clips * rows * keys * pairs * lanes,
            bytes_accessed=clips * pairs * lanes * (keys * 10 + rows * 12),
            transcendentals=clips * rows * keys * 2 * pairs,
        ),
        name="attend_back",
    )(q, k, v, mask, mixed, lse, grad)


def weight_kernel(normed_ref, dq_ref, dk0_ref, dk1_ref, dk2_ref, out_ref, dkv_ref, sums_ref):
    part = pl.program_id(0)
    @pl.when(part == 0)
    def query():
        grad = dq_ref[...]
        out_ref[0] = dot(normed_ref[...], grad, TN).astype(bf16)
        sums_ref[0] = column_sums(grad.astype(f32))
        dkv_ref[0] = jnp.zeros_like(dkv_ref[0])

    @pl.when(part > 0)
    def other():
        grad = (dk0_ref[0].astype(f32) + dk1_ref[0].astype(f32) + dk2_ref[0].astype(f32)).astype(bf16)
        dkv_ref[0] = grad
        out_ref[0] = dot(normed_ref[...], grad, TN).astype(bf16)
        sums_ref[0] = column_sums(grad.astype(f32))


def weight_grads(normed, dq, parts):
    total, width = normed.shape
    lanes = dq.shape[1]
    before = lambda j: (jnp.maximum(j - 1, 0), 0, 0)
    part = pl.BlockSpec((1, total, lanes), before)
    return pl.pallas_call(
        weight_kernel,
        grid=(3,),
        in_specs=[full((total, width)), full((total, lanes)), part, part, part],
        out_specs=[
            pl.BlockSpec((1, width, lanes), lambda j: (j, 0, 0)),
            part,
            pl.BlockSpec((1, 1, lanes), lambda j: (j, 0, 0)),
        ],
        out_shape=[
            jax.ShapeDtypeStruct((3, width, lanes), bf16),
            jax.ShapeDtypeStruct((2, total, lanes), bf16),
            jax.ShapeDtypeStruct((3, 1, lanes), f32),
        ],
        compiler_params=params(),
        cost_estimate=pl.CostEstimate(
            flops=6 * total * width * lanes, bytes_accessed=8_000_000, transcendentals=0
        ),
        name="weight_grads",
    )(normed, dq, *parts)


def input_kernel(counts, groups, *refs):
    clips, slots, rows = counts
    dqs = refs[:groups]
    dkvs = refs[groups : 2 * groups]
    qkv_ref, tok_ref, gmid_ref, gain_ref, shift_ref, out_ref, small_ref = refs[2 * groups :]
    clip = pl.program_id(0)
    width = tok_ref.shape[-1]
    lanes = width // groups
    grad = None
    for group in range(groups):
        for part in range(3):
            rows_grad = dqs[group][0] if part == 0 else dkvs[group][part - 1]
            at = part * width + group * lanes
            more = dot(rows_grad, qkv_ref[:, at : at + lanes], NT)
            grad = more if grad is None else grad + more
    unit, inverse = center_scale(tok_ref[0].astype(f32))
    result = gmid_ref[0] + norm_back(unit, inverse, gain_ref[...], grad)
    out_ref[0] = result[:slots]

    @pl.when(clip == 0)
    def start():
        small_ref[...] = jnp.zeros_like(small_ref)

    small_ref[0:1] += column_sums(grad * unit)
    small_ref[1:2] += column_sums(grad)


def input_grads(dqs, dkvs, qkv_weight, tokens, gmid, gain, shift, slots):
    clips, rows, width = tokens.shape
    groups = len(dqs)
    lanes = width // groups
    tok = pl.BlockSpec((1, rows, width), lambda c: (c, 0, 0))
    return pl.pallas_call(
        functools.partial(input_kernel, (clips, slots, rows), groups),
        grid=(clips,),
        in_specs=[pl.BlockSpec((1, rows, lanes), lambda c: (c, 0, 0))] * groups
        + [pl.BlockSpec((2, rows, lanes), lambda c: (0, c, 0))] * groups
        + [full(qkv_weight.shape), tok, tok, full((1, width)), full((1, width))],
        out_specs=[pl.BlockSpec((1, slots, width), lambda c: (c, 0, 0)), full((8, width))],
        out_shape=[
            jax.ShapeDtypeStruct((clips, slots, width), f32),
            jax.ShapeDtypeStruct((8, width), f32),
        ],
        compiler_params=params(),
        cost_estimate=pl.CostEstimate(
            flops=6 * clips * rows * width * width, bytes_accessed=16_000_000, transcendentals=0
        ),
        name="input_grads",
    )(*dqs, *dkvs, qkv_weight, tokens, gmid, gain, shift)


def swap_bit(array, axis, size, bit):
    return lax.ppermute(array, axis, [(i, i ^ (1 << bit)) for i in range(size)])


def add_low(left, right):
    return (left.astype(f32) + right.astype(f32)).astype(bf16)


def pick(array, index, dim):
    return lax.dynamic_index_in_dim(array, index, dim, keepdims=False)


def bit_of(axis, bit):
    return (lax.axis_index(axis) >> bit) & 1


def scatter_sum(split, clip_size, order):
    core = bit_of("freq", 0)
    vert = bit_of("freq", 1)
    bits = clip_size.bit_length() - 1
    lanes = split.shape[-1]
    value = add_low(pick(split, core, 0), swap_bit(pick(split, 1 - core, 0), "freq", 4, 0))
    rows = value.shape[0] // (2 * clip_size)
    value = value.reshape((2,) * bits + (2, rows, lanes))
    left = list(range(bits))[::-1]
    for bit in order:
        at = left.index(bit)
        mine = bit_of("clip", bit)
        value = add_low(
            pick(value, mine, at), swap_bit(pick(value, 1 - mine, at), "clip", clip_size, bit)
        )
        left.remove(bit)
    return add_low(pick(value, vert, 0), swap_bit(pick(value, 1 - vert, 0), "freq", 4, 1))


def gather_low(part):
    core = bit_of("freq", 0)
    vert = bit_of("freq", 1)
    other = swap_bit(part, "freq", 4, 1)
    tall = jnp.where(vert == 0, jnp.concatenate([part, other]), jnp.concatenate([other, part]))
    side = swap_bit(tall, "freq", 4, 0)
    return jnp.where(
        core == 0,
        jnp.concatenate([tall, side], axis=1),
        jnp.concatenate([side, tall], axis=1),
    ).astype(f32)


def total_sum(array, clip_size):
    for bit in range(2):
        array = array + swap_bit(array, "freq", 4, bit)
    for bit in range(clip_size.bit_length() - 1):
        array = array + swap_bit(array, "clip", clip_size, bit)
    return array


def on_device_plain(
    clip_size, tokens, kept_counts, attn_gain, attn_shift, qkv_weight, query_bias, value_bias,
    proj_weight, proj_bias, mlp_gain, mlp_shift, fc1_weight, fc1_bias, fc2_weight, fc2_bias, cotangent,
):
    clips, slots, width = tokens.shape
    rows = -(-slots // 16) * 16
    total = clips * rows
    bits = clip_size.bit_length() - 1
    forward_order = list(range(bits))
    second_order = forward_order[1:2] + forward_order[:1] + forward_order[2:]
    vec = lambda v: v.astype(f32)[None, :]
    kept = (kept_counts - slots // 2).astype(bf16)
    tok = jnp.concatenate(
        [tokens, jnp.broadcast_to(kept[:, :, None], (clips, rows - slots, width))], axis=1
    )
    vectors = [vec(v) for v in (query_bias, value_bias, attn_gain, attn_shift, proj_bias, mlp_gain, mlp_shift)]
    q, k, v, normed, mixed, lse, middle, normed2, mask = whole_forward(
        tok, slots, qkv_weight, vectors, proj_weight
    )
    flat = lambda a: a.reshape(total, width)
    layer_out, dfc1, dfc2, dproj, db1, small2, gmid, gmixed = mlp(
        kept_counts, flat(normed2), flat(middle), cotangent, flat(mixed), fc1_weight, fc1_bias,
        fc2_weight, fc2_bias, mlp_gain, proj_weight, rows,
    )
    early = total_sum(jnp.concatenate([small2[:4].reshape(-1), db1.reshape(-1)])[None, :], clip_size)[0]
    sum_fc1 = gather_low(scatter_sum(dfc1, clip_size, forward_order))
    sum_fc2 = gather_low(scatter_sum(dfc2, clip_size, second_order))
    sum_proj = gather_low(scatter_sum(dproj, clip_size, forward_order))

    groups = 3
    pairs = HEADS // 2 // groups
    lanes = pairs * 2 * DH
    gmixed = gmixed.reshape(clips, rows, width)
    dqs, dkvs, sums, sharded = [], [], [], []
    for group in range(groups):
        dq, keep, send = attend_back(q, k, v, mask, mixed, lse, gmixed, group * pairs, pairs)
        got = swap_bit(send, "freq", 4, 0)
        across = swap_bit(add_low(keep[:, :, rows:], got[:, :, rows:]), "freq", 4, 1)
        parts = [a.reshape(2, total, lanes) for a in (keep[:, :, :rows], got[:, :, :rows], across)]
        dw, dkv, colsum = weight_grads(flat(normed), dq.reshape(total, lanes), parts)
        half = lanes // 2
        split = jnp.stack(
            [
                jnp.concatenate([dw[i, :, s * half : (s + 1) * half] for i in range(3)], axis=1)
                for s in range(2)
            ]
        )
        order = forward_order if group % 2 == 0 else second_order
        summed = gather_low(scatter_sum(split, clip_size, order))
        sharded.append(summed.reshape(summed.shape[0], 2, 3, half))
        dqs.append(dq)
        dkvs.append(dkv)
        sums.append(colsum)
    grad_tokens, small1 = input_grads(
        dqs, dkvs, qkv_weight, tok, gmid.reshape(clips, rows, width), vectors[2], vectors[3], slots
    )
    qkv = jnp.stack(sharded, axis=1)
    sum_qkv = qkv.transpose(0, 3, 1, 2, 4).reshape(qkv.shape[0], 3 * width)
    bias = jnp.concatenate(sums, axis=2)
    late = total_sum(
        jnp.concatenate([small1[0:1], small1[1:2], bias[0], bias[2]], axis=1), clip_size
    )[0]
    cut = lambda a, i: a[i * width : (i + 1) * width]
    return (
        layer_out, grad_tokens, cut(late, 0), cut(late, 1), sum_qkv, cut(late, 2), cut(late, 3),
        sum_proj, cut(early, 3), cut(early, 0), cut(early, 1), sum_fc1, early[4 * width :],
        sum_fc2, cut(early, 2),
    )


def on_device(
    clip_size, tokens, kept_counts, attn_gain, attn_shift, qkv_weight, query_bias, value_bias,
    proj_weight, proj_bias, mlp_gain, mlp_shift, fc1_weight, fc1_bias, fc2_weight, fc2_bias, cotangent,
):
    clips, slots, width = tokens.shape
    rows = -(-slots // 16) * 16
    if clip_size != 8 or width % (32 * clip_size):
        return on_device_plain(
            clip_size, tokens, kept_counts, attn_gain, attn_shift, qkv_weight, query_bias, value_bias,
            proj_weight, proj_bias, mlp_gain, mlp_shift, fc1_weight, fc1_bias, fc2_weight, fc2_bias, cotangent,
        )
    q, k, v, normed, weight_half, part, lse, mask, mixed, middle, normed2 = forward(
        kept_counts, tokens, rows, qkv_weight, query_bias, value_bias, attn_gain, attn_shift,
        proj_weight, proj_bias, mlp_gain, mlp_shift,
    )
    flat = lambda a: a.reshape(clips * rows, width)
    layer_out, dfc1, dfc2, dproj, db1, small, gmid, gmixed = mlp(
        kept_counts, flat(normed2), flat(middle), cotangent, flat(mixed), fc1_weight, fc1_bias,
        fc2_weight, fc2_bias, mlp_gain, proj_weight, rows,
    )
    by_clip = lambda a: a.reshape(clips, rows, width)
    gtok, low_fc1, low_fc2, low_proj, low_qkv, summed = backward(
        q, k, v, mask, part, lse, normed, weight_half, tokens, by_clip(gmid), attn_gain, small, db1,
        by_clip(gmixed), dfc1, dfc2, dproj, clip_size,
    )
    fc1, fc2, proj, qkv, grad_tokens, fc1_b, *rows_out = final_outputs(
        low_fc1, low_fc2, low_proj, low_qkv, summed, gtok, fc1_bias.shape[0]
    )
    return (
        layer_out, grad_tokens, rows_out[0], rows_out[1], qkv, rows_out[2], rows_out[3], proj, rows_out[7],
        rows_out[4], rows_out[5], fc1, fc1_b, fc2, rows_out[6],
    )


def solution(mesh):
    rows = P("clip", "freq", None)
    shard = P("clip", None)
    return jax.shard_map(
        functools.partial(on_device, mesh.shape["clip"]),
        mesh=mesh,
        in_specs=(rows, P("clip", "freq")) + (P(),) * 13 + (rows,),
        out_specs=(rows, rows, P(), P(), shard, P(), P(), shard, P(), P(), P(), shard, P(), shard, P()),
        check_vma=False,
    )
```

```python
import functools
import math

import jax
import jax.numpy as jnp
from jax import lax
from jax.experimental import pallas as pl
from jax.experimental.pallas import tpu as pltpu
from jax.sharding import PartitionSpec as P

HEADS = 12
DH = 64
EPS = 1e-06
MASKED = -1000000000.0
VMEM_BYTES = 60 * 1024 * 1024

f32 = jnp.float32
bf16 = jnp.bfloat16
NN = (((1,), (0,)), ((), ()))
NT = (((1,), (1,)), ((), ()))
TN = (((0,), (0,)), ((), ()))


def dot(left, right, dims=NN):
    return lax.dot_general(left, right, dims, preferred_element_type=f32)


def center_scale(rows):
    center = rows - jnp.mean(rows, axis=-1, keepdims=True)
    inverse = lax.rsqrt(jnp.mean(center * center, axis=-1, keepdims=True) + EPS)
    return center * inverse, inverse


def norm_back(unit, inverse, gain, grad):
    scaled = grad * gain
    return inverse * (
        scaled
        - jnp.mean(scaled, axis=-1, keepdims=True)
        - unit * jnp.mean(scaled * unit, axis=-1, keepdims=True)
    )


def column_sums(rows):
    return jnp.sum(rows, axis=0, keepdims=True)


def own_lanes(shape, head):
    lane = lax.broadcasted_iota(jnp.int32, shape, len(shape) - 1)
    return lane < DH if head == 0 else lane >= DH


def only(rows, head):
    return jnp.where(own_lanes(rows.shape, head), rows, jnp.zeros_like(rows))


def full(shape):
    return pl.BlockSpec(shape, lambda *ids: (0,) * len(shape))


def params(**more):
    return pltpu.CompilerParams(vmem_limit_bytes=VMEM_BYTES, **more)


def freq_places():
    freq = lax.axis_index("freq")
    core, vert = freq % 2, freq // 2
    return core, vert, {"freq": freq + 1 - 2 * core}, {"freq": (freq + 2) % 4}


def lane_slice(start, size):
    return pl.ds(pl.multiple_of(start, 2 * DH), size)


def row_of(ref):
    return ref[...].astype(f32).reshape(1, ref.shape[0])


def forward_kernel(
    counts,
    kept_ref, tok_ref, qkv_ref, qb_ref, vb_ref, gain_ref, shift_ref, proj_ref, pb_ref, gain2_ref, shift2_ref,
    q_out, k_out, v_out, normed_out, far_out, weight_out, part_ref, lse_ref, mask_ref, mixed_ref, middle_ref, normed2_ref,
    q_all, k_all, v_all, normed_all, weight, live_all, own, held, mix_send, mix_got, own_mix, vecs,
    tok_send, tok_recv, part_send, part_recv, out_sem, weight_sem,
):
    clips, slots, rows, pairs = counts
    clip = pl.program_id(0)
    turn = pl.program_id(1)
    slot = 1 - turn
    width = tok_ref.shape[-1]
    half = width // 2
    lanes = 2 * DH
    core, vert, core_dev, vert_dev = freq_places()
    mesh_id = pl.DeviceIdType.MESH

    def copy(kind, index):
        at = {"vert": 0, "core": 1, "diag": 2}[kind]
        return pltpu.make_async_remote_copy(
            src_ref=held.at[index, 0] if kind == "diag" else own.at[index],
            dst_ref=held.at[index, at],
            send_sem=tok_send.at[index, at],
            recv_sem=tok_recv.at[index, at],
            device_id=vert_dev if kind == "vert" else core_dev,
            device_id_type=mesh_id,
        )

    def mix_copy(index, which):
        return pltpu.make_async_remote_copy(
            src_ref=mix_send.at[index, which],
            dst_ref=mix_got.at[index, which],
            send_sem=part_send.at[index, which],
            recv_sem=part_recv.at[index, which],
            device_id=vert_dev,
            device_id_type=mesh_id,
        )

    def project(index, slot, source):
        unit, _ = center_scale(source.astype(f32))
        normed = (unit * vecs[2:3] + vecs[3:4]).astype(bf16)
        at = slice(slot * rows, (slot + 1) * rows)
        if slot < 2:
            normed_all[index, at] = normed
            query = (dot(normed, weight[:, :half]) + vecs[0:1, lane_slice(vert * half, half)]).astype(bf16)
            q_all[index, at] = query * jnp.asarray(DH ** -0.5, bf16)
        both = dot(normed, weight[:, half:])
        k_all[index, at] = both[:, :half].astype(bf16)
        v_all[index, at] = (both[:, half:] + vecs[1:2, lane_slice(vert * half, half)]).astype(bf16)
        first = (slots // 16) * 16
        kept = source[first:].astype(f32)[slots - first : slots - first + 1, 0:1] + slots // 2
        lane = lax.broadcasted_iota(jnp.int32, (1, rows), 1).astype(f32)
        live_all[index, slot] = (lane < kept).astype(f32)

    def out_copies(index):
        return [
            pltpu.make_async_copy(src.at[index], dst.at[index], out_sem.at[index, i])
            for i, (src, dst) in enumerate(
                ((q_all, q_out), (k_all, k_out), (v_all, v_out), (normed_all, normed_out))
            )
        ] + [pltpu.make_async_copy(held.at[index, 0], far_out.at[index], out_sem.at[index, 4])]

    def weight_copies():
        moves = []
        for pair in range(pairs):
            for part in range(3):
                src = weight.at[:, pl.ds(part * half + pair * lanes, lanes)]
                dst = weight_out.at[:, pl.ds((3 * pair + part) * lanes, lanes)]
                moves.append(pltpu.make_async_copy(src, dst, weight_sem.at[3 * pair + part]))
        return moves

    @pl.when((clip == 0) & (turn == 0))
    def enter():
        barrier = pltpu.get_barrier_semaphore()
        for device in (vert_dev, core_dev):
            pl.semaphore_signal(barrier, inc=1, device_id=device, device_id_type=mesh_id)
        first = (slots // 16) * 16
        for index in range(clips):
            kept = (kept_ref[index, 0] - slots // 2).astype(f32).astype(bf16)
            own[index, first:] = jnp.broadcast_to(kept, (rows - first, width))
            own[index, :slots] = tok_ref[index]
        pl.semaphore_wait(barrier, 2)
        copy("vert", 0).start()
        for index in range(clips):
            copy("core", index).start()
        for i, ref in enumerate((qb_ref, vb_ref, gain_ref, shift_ref, pb_ref, gain2_ref, shift2_ref)):
            vecs[i : i + 1] = row_of(ref)
        for part in range(3):
            weight[:, part * half : (part + 1) * half] = qkv_ref[:, lane_slice(part * width + vert * half, half)]
        for move in weight_copies():
            move.start()

        def own_slots(index, carry):
            project(index, 0, own[index])
            return carry

        def core_slots(index, carry):
            copy("core", index).wait_recv()
            project(index, 2, held[index, 1])
            return carry

        lax.fori_loop(0, clips, own_slots, 0)
        lax.fori_loop(0, clips, core_slots, 0)
        copy("vert", 0).wait_recv()
        copy("diag", 0).start()
        copy("vert", 0).wait_send()
        if clips > 1:
            copy("vert", 1).start()

    @pl.when(turn == 0)
    def project_rest():
        project(clip, 1, held[clip, 0])
        copy("diag", clip).wait_recv()
        project(clip, 3, held[clip, 2])
        for i in range(4):
            mask_ref[0, :, i * rows : (i + 1) * rows] = live_all[clip, i]
        for move in out_copies(clip):
            move.start()

    for index in range(2, clips):
        @pl.when((turn == 1) & (clip == index - 2))
        def send_ahead(index=index):
            copy("vert", index - 1).wait_send()
            copy("vert", index).start()

    def finish(index):
        at = lane_slice(vert * half, half)
        mixed_ref[0, :, at] = own_mix[...]
        for which in range(pairs):
            mix_copy(index, which).wait_recv()
            at = lane_slice((1 - vert) * half + which * lanes, lanes)
            mixed_ref[0, :, at] = mix_got[index, which]
        middle = own[index].astype(f32) + (dot(mixed_ref[0], proj_ref[...]) + vecs[4:5])
        middle_ref[0] = middle
        unit, _ = center_scale(middle)
        normed2_ref[0] = (unit * vecs[5:6] + vecs[6:7]).astype(bf16)
        copy("core", index).wait_send()
        copy("diag", index).wait_send()
        for which in range(pairs):
            mix_copy(index, which).wait_send()

    at = pl.ds(pl.multiple_of(slot * rows, rows), rows)
    live = mask_ref[0] > 0.5
    for pair in range(pairs):
        here = slice(pair * lanes, (pair + 1) * lanes)
        keys = k_all[clip, :, here]
        values = v_all[clip, :, here]
        query = q_all[clip, at, here]
        outs, lses = [], []
        for head in range(2):
            scores = jnp.where(live, dot(only(query, head), keys, NT), MASKED)
            top = jnp.max(scores, axis=1, keepdims=True)
            exps = jnp.exp(scores - top)
            total = jnp.sum(exps, axis=1, keepdims=True)
            outs.append(dot(exps.astype(bf16), values) / total)
            lses.append(top + jnp.log(total))
        first = own_lanes(outs[0].shape, 0)
        mixed = jnp.where(first, outs[0], outs[1]).astype(bf16)
        part_ref[0, at, here] = mixed
        lse_ref[0, at, here] = jnp.where(first, lses[0], lses[1])

    @pl.when(slot == 1)
    def give():
        for pair in range(pairs):
            mix_send[clip, pair] = part_ref[0, rows:, pair * lanes : (pair + 1) * lanes]
            mix_copy(clip, pair).start()

    @pl.when((turn == 0) & (clip > 0))
    def finish_before():
        finish(clip - 1)

    @pl.when(turn == 1)
    def keep_own():
        own_mix[...] = part_ref[0, :rows]

    @pl.when((turn == 1) & (clip + 1 < clips))
    def pass_on():
        copy("vert", clip + 1).wait_recv()
        copy("diag", clip + 1).start()

    @pl.when((turn == 1) & (clip == clips - 1))
    def finish_last():
        finish(clip)
        copy("vert", clips - 1).wait_send()

    @pl.when((turn == 1) & (clip == clips - 1))
    def leave():
        for move in weight_copies():
            move.wait()
        for index in range(clips):
            for move in out_copies(index):
                move.wait()


def forward(kept, tokens, rows, qkv_weight, query_bias, value_bias, gain, shift, proj_weight, proj_bias, gain2, shift2):
    clips, slots, width = tokens.shape
    keys = 4 * rows
    half = width // 2
    pairs = HEADS // 4
    lanes = 2 * DH
    one = pl.Buffered(buffer_count=1)
    block = lambda n, m: pl.BlockSpec((1, n, m), lambda c, p: (c, 0, 0))
    late = pl.BlockSpec((1, rows, width), lambda c, t: (jnp.maximum(c - 1 + t, 0), 0, 0))
    anywhere = pl.BlockSpec(memory_space=pl.ANY)
    whole = lambda a: pl.BlockSpec(a.shape, lambda c, p: (0,) * a.ndim, pipeline_mode=one)
    shape = jax.ShapeDtypeStruct
    flops = 2 * clips * (rows * width * width * 6 + 2 * rows * keys * width)
    vectors = (query_bias, value_bias, gain, shift)
    return pl.pallas_call(
        functools.partial(forward_kernel, (clips, slots, rows, pairs)),
        grid=(clips, 2),
        in_specs=[pl.BlockSpec(memory_space=pltpu.SMEM), whole(tokens), whole(qkv_weight)]
        + [whole(v) for v in vectors]
        + [whole(proj_weight)]
        + [whole(v) for v in (proj_bias, gain2, shift2)],
        out_specs=[
            anywhere, anywhere, anywhere, anywhere, anywhere, anywhere,
            block(2 * rows, half), block(2 * rows, half), block(1, keys),
            late, late, late,
        ],
        out_shape=[
            shape((clips, 2 * rows, half), bf16),
            shape((clips, keys, half), bf16),
            shape((clips, keys, half), bf16),
            shape((clips, 2 * rows, width), bf16),
            shape((clips, rows, width), bf16),
            shape((width, 3 * half), bf16),
            shape((clips, 2 * rows, half), bf16),
            shape((clips, 2 * rows, half), f32),
            shape((clips, 1, keys), f32),
            shape((clips, rows, width), bf16),
            shape((clips, rows, width), f32),
            shape((clips, rows, width), bf16),
        ],
        scratch_shapes=[
            pltpu.VMEM((clips, 2 * rows, half), bf16),
            pltpu.VMEM((clips, keys, half), bf16),
            pltpu.VMEM((clips, keys, half), bf16),
            pltpu.VMEM((clips, 2 * rows, width), bf16),
            pltpu.VMEM((width, 3 * half), bf16),
            pltpu.VMEM((clips, 4, 1, rows), f32),
            pltpu.VMEM((clips, rows, width), bf16),
            pltpu.VMEM((clips, 3, rows, width), bf16),
            pltpu.VMEM((clips, pairs, rows, lanes), bf16),
            pltpu.VMEM((clips, pairs, rows, lanes), bf16),
            pltpu.VMEM((rows, half), bf16),
            pltpu.VMEM((8, width), f32),
            pltpu.SemaphoreType.DMA((clips, 3)),
            pltpu.SemaphoreType.DMA((clips, 3)),
            pltpu.SemaphoreType.DMA((clips, pairs)),
            pltpu.SemaphoreType.DMA((clips, pairs)),
            pltpu.SemaphoreType.DMA((clips, 5)),
            pltpu.SemaphoreType.DMA((3 * pairs,)),
        ],
        compiler_params=params(collective_id=0, has_side_effects=True),
        cost_estimate=pl.CostEstimate(
            flops=flops, bytes_accessed=40_000_000, transcendentals=clips * rows * keys * HEADS
        ),
        name="forward",
    )(kept, tokens, qkv_weight, *vectors, proj_weight, proj_bias, gain2, shift2)


def mlp_kernel(
    counts,
    kept_ref, n2_ref, middle_ref, cot_ref, mixed_ref, fc1_ref, b1_ref, fc2_ref, b2_ref, gain_ref, proj_ref,
    out_ref, dfc1_ref, dfc2_ref, dproj_ref, db1_ref, small_ref, gmid_ref, gmixed_ref,
    n2t_ref, grad_ref, out_acc, dn_acc, hidden_ref, dact_ref, active_ref, dhid_ref, biases,
):
    clips, slots, rows, tile = counts
    step = pl.program_id(0)
    width = n2_ref.shape[-1]
    chunk = fc1_ref.shape[-1]
    total = clips * rows

    def live_rows(clip, size):
        slot = lax.broadcasted_iota(jnp.int32, (size, 1), 0)
        return (slot < kept_ref[clip, 0]).astype(f32)

    @pl.when(step == 0)
    def start():
        n2t_ref[...] = n2_ref[...].T
        first = (slots // 16) * 16
        for clip in range(clips):
            begin = clip * rows
            grad_ref[begin + first : begin + rows] = jnp.zeros((rows - first, width), bf16)
            grad_ref[begin : begin + slots] = cot_ref[clip] * live_rows(clip, slots).astype(bf16)
        all_biases = row_of(b1_ref)
        for i in range(all_biases.shape[1] // chunk):
            biases[i : i + 1] = all_biases[:, i * chunk : (i + 1) * chunk]
        out_acc[...] = jnp.zeros_like(out_acc)
        dn_acc[...] = jnp.zeros_like(dn_acc)

    bias = biases[pl.ds(step, 1), :]
    hidden_ref[...] = dot(n2_ref[...], fc1_ref[...])
    dact_ref[...] = dot(grad_ref[...], fc2_ref[...], NT)
    sums = jnp.zeros((tile, chunk), f32)
    for begin in range(0, total, tile):
        at = slice(begin, begin + tile)
        hidden = hidden_ref[at] + bias
        cdf = 0.5 * (1.0 + lax.erf(hidden * (0.5 ** 0.5)))
        active_ref[at] = (hidden * cdf).astype(bf16)
        slope = cdf + hidden * (jnp.exp(-0.5 * hidden * hidden) * (1.0 / math.sqrt(2.0 * math.pi)))
        dhid = (dact_ref[at] * slope).astype(bf16)
        dhid_ref[at] = dhid
        sums = sums + dhid.astype(f32)
    db1_ref[...] = column_sums(sums)
    active = active_ref[...]
    dhid = dhid_ref[...]
    out_acc[...] += dot(active, fc2_ref[...])
    dn_acc[...] += dot(dhid, fc1_ref[...], NT)
    dfc1_ref[0] = dot(n2t_ref[...], dhid).astype(bf16)
    dfc2 = dot(active, grad_ref[...], TN).astype(bf16)
    half = width // 2
    dfc2_ref[0] = dfc2[:, :half]
    dfc2_ref[1] = dfc2[:, half:]

    @pl.when(step == pl.num_programs(0) - 1)
    def finish():
        gain = row_of(gain_ref)
        bias2 = row_of(b2_ref)
        small_ref[...] = jnp.zeros_like(small_ref)

        def finish_clip(clip, carry):
            at = pl.ds(pl.multiple_of(clip * rows, rows), rows)
            middle = middle_ref[at]
            layer = middle + (out_acc[at] + bias2)
            out_ref[clip] = (live_rows(clip, slots) * layer[:slots]).astype(bf16)
            unit, inverse = center_scale(middle)
            grad = dn_acc[at]
            out_grad = grad_ref[at].astype(f32)
            gmid = out_grad + norm_back(unit, inverse, gain, grad)
            gmid_ref[at] = gmid
            low = gmid.astype(bf16)
            dhid_ref[at, :width] = low
            gmixed_ref[at] = dot(low, proj_ref[...], NT).astype(bf16)
            small_ref[0:1] += column_sums(grad * unit)
            small_ref[1:2] += column_sums(grad)
            small_ref[2:3] += column_sums(out_grad)
            small_ref[3:4] += column_sums(low.astype(f32))
            return carry

        lax.fori_loop(0, clips, finish_clip, 0)
        dproj = dot(mixed_ref[...], dhid_ref[:, :width], TN).astype(bf16)
        dproj_ref[0] = dproj[:, :half]
        dproj_ref[1] = dproj[:, half:]


def mlp(kept, n2, middle, cot, mixed, fc1, b1, fc2, b2, gain, proj, rows):
    clips, slots, _ = cot.shape
    total, width = n2.shape
    hidden = fc1.shape[1]
    chunk = 768
    steps = hidden // chunk
    half = steps // 2
    tile = 16
    whole = lambda a: pl.BlockSpec(a.shape, lambda j: (0,) * a.ndim, pipeline_mode=one)
    one = pl.Buffered(buffer_count=1)
    big = pl.BlockSpec((total, width), lambda j: (0, 0), pipeline_mode=one)
    return pl.pallas_call(
        functools.partial(mlp_kernel, (clips, slots, rows, tile)),
        grid=(steps,),
        in_specs=[
            pl.BlockSpec(memory_space=pltpu.SMEM),
            big, big, whole(cot), big,
            pl.BlockSpec((width, chunk), lambda j: (0, j)),
            whole(b1),
            pl.BlockSpec((chunk, width), lambda j: (j, 0)),
            whole(b2), whole(gain), whole(proj),
        ],
        out_specs=[
            full((clips, slots, width)),
            pl.BlockSpec((1, width, chunk), lambda j: (j // half, 0, j % half)),
            pl.BlockSpec((2, chunk, width // 2), lambda j: (0, j, 0)),
            full((2, width, width // 2)),
            pl.BlockSpec((1, chunk), lambda j: (0, j)),
            full((8, width)),
            full((total, width)),
            full((total, width)),
        ],
        out_shape=[
            jax.ShapeDtypeStruct((clips, slots, width), bf16),
            jax.ShapeDtypeStruct((2, width, hidden // 2), bf16),
            jax.ShapeDtypeStruct((2, hidden, width // 2), bf16),
            jax.ShapeDtypeStruct((2, width, width // 2), bf16),
            jax.ShapeDtypeStruct((1, hidden), f32),
            jax.ShapeDtypeStruct((8, width), f32),
            jax.ShapeDtypeStruct((total, width), f32),
            jax.ShapeDtypeStruct((total, width), bf16),
        ],
        scratch_shapes=[
            pltpu.VMEM((width, total), bf16),
            pltpu.VMEM((total, width), bf16),
            pltpu.VMEM((total, width), f32),
            pltpu.VMEM((total, width), f32),
            pltpu.VMEM((total, chunk), f32),
            pltpu.VMEM((total, chunk), f32),
            pltpu.VMEM((total, chunk), bf16),
            pltpu.VMEM((total, chunk), bf16),
            pltpu.VMEM((8, chunk), f32),
        ],
        compiler_params=params(),
        cost_estimate=pl.CostEstimate(
            flops=12 * total * width * hidden, bytes_accessed=40_000_000, transcendentals=2 * total * hidden
        ),
        name="mlp",
    )(kept, n2, middle, cot, mixed, fc1, b1, fc2, b2, gain, proj)


def sum_arrays(width, hidden, clip_size):
    rows = width // clip_size
    tall = hidden // clip_size
    first, second = (0, 1, 2), (1, 0, 2)
    chunks = [("qkv", i, rows // 2, width // 2, order) for i, order in enumerate(QKV_ORDERS)]
    return [
        ("fc1", 0, rows, hidden // 4, first),
        ("fc2", 0, tall // 2, width // 2, second),
        ("fc1", hidden // 4, rows, hidden // 4, first),
        ("fc2", tall // 2, tall // 2, width // 2, second),
        ("proj", 0, rows, width // 2, PROJ_ORDER),
    ] + chunks


PROJ_ORDER = (1, 0, 2)
QKV_ORDERS = ((1, 0, 2), (1, 0, 2), (1, 0, 2))
SUM_STEPS = {
    2: [("end", 0, 0), ("start", 0, 1), ("end", 1, 0), ("start", 1, 1)],
    3: [("end", 2, 0)],
    4: [("end", 3, 0), ("end", 4, 0)],
    5: [("start", 2, 1), ("start", 3, 1)],
    7: [("end", 0, 1), ("end", 1, 1)],
    9: [("start", 0, 2), ("start", 1, 2)],
    10: [("start", 4, 1)],
    11: [("end", 2, 1), ("end", 3, 1), ("start", 3, 2)],
    12: [("start", 2, 2)],
    13: [("end", 0, 2), ("start", 0, 3), ("end", 1, 2)],
    15: [("end", 3, 2), ("start", 1, 3), ("end", 4, 1), ("start", 4, 2)],
    16: [("end", 2, 2), ("start", 2, 3)],
    17: [("end", 0, 3), ("start", 0, 4), ("end", 4, 2)],
    18: [("start", 3, 3)],
    19: [("end", 5, 0), ("start", 5, 1), ("end", 1, 3), ("start", 1, 4)],
    20: [("end", 0, 4), ("start", 0, 5), ("start", 4, 3)],
    21: [("end", 0, 5), ("end", 2, 3), ("start", 2, 4)],
    22: [("end", 6, 0), ("start", 6, 1), ("end", 1, 4), ("start", 1, 5)],
    23: [("end", 5, 1), ("start", 5, 2), ("end", 6, 1), ("start", 6, 2), ("end", 7, 0),
        ("start", 7, 1), ("end", 1, 5), ("end", 2, 4), ("start", 2, 5), ("end", 3, 3),
        ("start", 3, 4), ("end", 4, 3), ("start", 4, 4)],
    24: [("end", 2, 5)],
    25: [("end", 5, 2), ("start", 5, 3), ("vec", 0, 0), ("end", 6, 2), ("start", 6, 3), ("end", 7, 1),
        ("start", 7, 2), ("vec", 1, 0), ("input", 2, 0), ("end", 7, 2), ("start", 7, 3),
        ("end", 6, 3), ("start", 6, 4), ("end", 5, 3), ("start", 5, 4), ("end", 3, 4),
        ("start", 3, 5), ("vec", 2, 0), ("end", 4, 4), ("start", 4, 5), ("end", 3, 5), ("end", 6, 4),
        ("start", 6, 5), ("end", 4, 5), ("end", 5, 4), ("start", 5, 5), ("end", 7, 3),
        ("start", 7, 4), ("end", 6, 5), ("end", 5, 5), ("vec", 3, 0), ("end", 7, 4), ("start", 7, 5),
        ("end", 7, 5), ("vec", 4, 0)],
}


def backward_kernel(
    meta,
    q_ref, k_ref, v_ref, mask_ref, part_ref, lse_ref, normed_ref, weight_ref, near_ref, far_ref,
    tok_ref, gmid_ref, gain_ref,
    small_ref, db1_ref, gmixed_ref, dfc1_ref, dfc2_ref, dproj_ref,
    gtok_ref, fc1_out, fc2_out, proj_out, qkv_out, vec_out,
    *scratch,
):
    clips, slots, rows, bits, pairs, arrays = meta
    width = weight_ref.shape[0]
    half = width // 2
    lanes = 2 * DH
    step = pl.program_id(0)
    places = step_places(clips, pairs)
    mesh_id = pl.DeviceIdType.MESH
    count = len(arrays)

    scratch = list(scratch)
    take = lambda n: [scratch.pop(0) for _ in range(n)]
    (grad_all, packed, kv_acc, kv_send, kv_got, acc, dn_send, dn_got, dw_acc, bias_acc, vec_sum, vec_got) = take(12)
    own_bufs = dict(zip(("fc1", "fc2", "proj"), take(3)))
    dw_low = scratch.pop(0)
    stage_bufs = [take(bits + 1) for _ in arrays]
    vert_bufs = take(5)
    full_bufs = take(count)
    (grad_sem, grad_out, grad_in, kv_out, kv_in, dn_out, dn_in, sum_out, sum_in, own_sem, vec_out_sem, vec_in_sem) = take(12)

    core, vert, core_dev, vert_dev = freq_places()
    place = lax.axis_index("clip")
    bit_at = [(place // 2 ** b) % 2 for b in range(bits)]
    clip_dev = [{"clip": place + (1 - 2 * bit_at[b]) * 2 ** b} for b in range(bits)]

    def remote(src, dst, send, recv, device):
        return pltpu.make_async_remote_copy(
            src_ref=src, dst_ref=dst, send_sem=send, recv_sem=recv, device_id=device, device_id_type=mesh_id
        )

    def grad_own(clip):
        src = gmixed_ref.at[clip, :, lane_slice(vert * half, half)]
        return pltpu.make_async_copy(src, grad_all.at[0, clip], grad_sem.at[clip])

    def grad_vert(clip):
        src = gmixed_ref.at[clip, :, lane_slice((1 - vert) * half, half)]
        return remote(src, grad_all.at[1, clip], grad_out.at[clip], grad_in.at[clip], vert_dev)

    def kv_copy(clip, pair):
        return remote(
            kv_send.at[pair], kv_got.at[clip, pair], kv_out.at[clip, pair], kv_in.at[clip, pair], core_dev
        )

    def dn_copy(clip):
        return remote(dn_send.at[clip], dn_got.at[clip], dn_out.at[clip], dn_in.at[clip], vert_dev)

    every = (slice(None),) * bits

    def piece(a, who):
        name, at, r, width_a, _ = arrays[a]
        if name == "fc1":
            return dfc1_ref.at[(who,) + every + (slice(None), pl.ds(at, width_a))]
        if name == "fc2":
            return dfc2_ref.at[(who,) + every + (pl.ds(at, r), slice(None))]
        if name == "proj":
            return dproj_ref.at[who]
        return dw_low.at[at, who]

    def chosen(a, stage, index_of):
        order = arrays[a][4]
        left = [b for b in range(bits)[::-1] if b not in order[: stage - 1]]
        bit = order[stage - 1]
        at = (slice(None),) * left.index(bit) + (index_of(bit),)
        return stage_bufs[a][stage - 1].at[at]

    def stage_copy(a, stage):
        sems = (sum_out.at[a, stage], sum_in.at[a, stage])
        full, packed_array = full_bufs[a], arrays[a][0] == "qkv"
        if stage == 0:
            return remote(piece(a, 1 - core), stage_bufs[a][0], *sems, core_dev)
        if stage <= bits:
            src = chosen(a, stage, lambda bit: 1 - bit_at[bit])
            return remote(src, stage_bufs[a][stage], *sems, clip_dev[arrays[a][4][stage - 1]])
        if stage == bits + 1:
            dst = full.at[core, vert] if packed_array else vert_bufs[a]
            return remote(stage_bufs[a][bits], dst, *sems, vert_dev)
        return remote(full.at[core], full.at[core], *sems, core_dev)

    def own_copy(a):
        return pltpu.make_async_copy(piece(a, core), own_bufs[arrays[a][0]], own_sem.at[a])

    def add_blocks(dst, src, lead):
        if lead == 0:
            dst[...] = dst[...] + src[...]
            return

        def add_one(i, carry):
            at = tuple((i // 2 ** (lead - 1 - j)) % 2 for j in range(lead))
            dst[at] = dst[at] + src[at]
            return carry

        lax.fori_loop(0, 2 ** lead, add_one, 0)

    def stage_end(a, stage):
        name = arrays[a][0]
        stage_copy(a, stage).wait_recv()
        if stage == 0:
            if name == "qkv":
                add_blocks(stage_bufs[a][0], dw_low.at[arrays[a][1], core], bits)
            else:
                own_copy(a).wait()
                add_blocks(stage_bufs[a][0], own_bufs[name], bits)
                if a + 2 < 4:
                    own_copy(a + 2).start()
        elif stage <= bits:
            add_blocks(stage_bufs[a][stage], chosen(a, stage, lambda bit: bit_at[bit]), bits - stage)
            if stage == bits and name == "qkv":
                full_bufs[a][core, vert] = stage_bufs[a][bits][...]
        elif stage == bits + 1 and name != "qkv":
            full_bufs[a][core] = stage_bufs[a][bits][...] + vert_bufs[a][...]

    def vec_copy(hop):
        device = ([core_dev] + clip_dev + [vert_dev])[hop]
        return remote(vec_sum.at[hop], vec_got.at[hop], vec_out_sem.at[hop], vec_in_sem.at[hop], device)

    def vec_end(hop):
        vec_copy(hop).wait_recv()
        vec_sum[hop + 1] = vec_sum[hop] + vec_got[hop]
        if hop < bits + 1:
            vec_copy(hop + 1).start()

    def perform(action):
        kind, a, stage = action
        if kind == "vec":
            vec_end(a)
        elif kind == "start":
            stage_copy(a, stage).start()
        else:
            stage_end(a, stage)

    @pl.when(step == 0)
    def enter():
        barrier = pltpu.get_barrier_semaphore()
        for clip in range(clips):
            grad_own(clip).start()
        for device in [core_dev, vert_dev] + clip_dev:
            pl.semaphore_signal(barrier, inc=1, device_id=device, device_id_type=mesh_id)
        pl.semaphore_wait(barrier, 2 + bits)
        for clip in range(clips):
            grad_vert(clip).start()
        for a in range(5):
            stage_copy(a, 0).start()
        for a in (0, 1, 4):
            own_copy(a).start()
        vec_sum[0] = jnp.zeros_like(vec_sum[0])
        bias_acc[...] = jnp.zeros_like(bias_acc)
        dw_acc[...] = jnp.zeros_like(dw_acc)
        vec_sum[0, 4:8] = small_ref[0:4]
        for i in range(db1_ref.shape[1] // width):
            vec_sum[0, 8 + i : 9 + i] = db1_ref[0:1, i * width : (i + 1) * width]

    for at in sorted(SUM_STEPS):
        if at < places["end"]:
            @pl.when(step == at)
            def run(at=at):
                for action in SUM_STEPS[at]:
                    perform(action)

    def attend():
        clip, slot, pair = attention_unit(step, places, clips, pairs)

        @pl.when((pair == 0) & (slot == 0))
        def own_grads():
            grad_own(clip).wait()

        @pl.when((pair == 0) & (slot == 1))
        def vert_grads():
            grad_vert(clip).wait_recv()

        query = q_ref[0]
        keys = k_ref[0]
        values = v_ref[0]
        grad = grad_all[slot, clip, :, lane_slice(pair * lanes, lanes)]
        live = mask_ref[0] > 0.5
        product = grad.astype(f32) * part_ref[0].astype(f32)
        dqs, dk, dv = [], None, None
        for head in range(2):
            own_query = only(query, head)
            own_grad = only(grad, head)
            scores = jnp.where(live, dot(own_query, keys, NT), MASKED)
            probs = jnp.exp(scores - lse_ref[0, :, head * DH : head * DH + 1])
            delta = jnp.sum(only(product, head), axis=1, keepdims=True)
            dscores = (probs * (dot(own_grad, values, NT) - delta)).astype(bf16)
            dqs.append(dot(dscores, keys))
            more_k = dot(dscores, own_query, TN)
            more_v = dot(probs.astype(bf16), own_grad, TN)
            dk = more_k if dk is None else dk + more_k
            dv = more_v if dv is None else dv + more_v
        first = own_lanes(dqs[0].shape, 0)
        dq = (jnp.where(first, dqs[0], dqs[1]) * DH ** -0.5).astype(bf16)
        at = pl.ds(pl.multiple_of(slot * rows, rows), rows)
        packed[clip, at, lane_slice(3 * pair * lanes, lanes)] = dq

        @pl.when(slot == 0)
        def keep():
            kv_acc[pair, 0] = dk
            kv_acc[pair, 1] = dv

        @pl.when(slot == 1)
        def send():
            @pl.when(clip > 0)
            def free():
                kv_copy(clip - 1, pair).wait_send()

            for part, value in enumerate((dk, dv)):
                low = (kv_acc[pair, part] + value).astype(bf16)
                packed[clip, :, lane_slice((3 * pair + part + 1) * lanes, lanes)] = low[: 2 * rows]
                kv_send[pair, part] = low[2 * rows :]
            kv_copy(clip, pair).start()

    is_attention = step < places["projections"][-1]
    for at in places["pauses"]:
        is_attention = is_attention & (step != at)
    pl.when(is_attention)(attend)

    def take_pair(clip, pair):
        kv_copy(clip, pair).wait_recv()
        for part in range(2):
            at = lane_slice((3 * pair + part + 1) * lanes, lanes)
            packed[clip, :, at] = packed[clip, :, at] + kv_got[clip, pair, part]
        at = lane_slice(pair * lanes, lanes)
        for row, part in ((0, 0), (1, 2)):
            value = packed[clip, :, lane_slice((3 * pair + part) * lanes, lanes)]
            bias_acc[row : row + 1, at] += column_sums(value.astype(f32))

    def norm_sums(clip, back):
        near, _ = center_scale(near_ref[0].astype(f32))
        far, _ = center_scale(far_ref[0].astype(f32))
        vec_sum[0, 0:1] += column_sums(back[:slots] * near) + column_sums(back[rows:] * far)
        vec_sum[0, 1:2] += column_sums(back)

    def give_back(clip, back):
        acc[clip] = back[:rows]
        dn_send[clip] = back[rows:].astype(bf16)
        dn_copy(clip).start()

    def last_chunk(pair):
        at = lane_slice(3 * pair * lanes, 3 * lanes)
        more = dot(normed_ref[0], packed[clips - 1, :, at], TN)
        low = (dw_acc[:, at] + more).astype(bf16)
        r = arrays[5][2]
        for block in range(2 ** bits):
            index = tuple((block >> b) & 1 for b in range(bits)[::-1])
            for who in range(2):
                start = (2 * block + who) * r
                dw_low[(pair, who) + index] = low[start : start + r]

    early_steps = places["projections"][:-1]
    early = functools.reduce(jnp.logical_or, [step == at for at in early_steps])

    @pl.when(early)
    def projections():
        clip = sum((step > at).astype(jnp.int32) for at in early_steps)

        def take_one(pair, carry):
            take_pair(clip, pair)
            return carry

        lax.fori_loop(0, pairs, take_one, 0)
        grads = packed[clip]
        back = dot(grads, weight_ref[...], NT)
        give_back(clip, back)
        dw_acc[...] += dot(normed_ref[0], grads, TN)
        norm_sums(clip, back)

    chunk_steps = places["chunks"]

    @pl.when(functools.reduce(jnp.logical_or, [step == at for at in chunk_steps]))
    def chunk():
        pair = sum((step > at).astype(jnp.int32) for at in chunk_steps)
        take_pair(clips - 1, pair)
        last_chunk(pair)

    for pair in range(pairs - 1):
        @pl.when(step == chunk_steps[pair])
        def send_chunk(pair=pair):
            stage_copy(5 + pair, 0).start()

    @pl.when(step == places["projections"][-1])
    def last_projections():
        clip = clips - 1
        before = 3 * (pairs - 1) * lanes
        back = dot(packed[clip, :, :before], weight_ref[:, :before], NT)
        take_pair(clip, pairs - 1)
        last_chunk(pairs - 1)
        stage_copy(4 + pairs, 0).start()
        back = back + dot(packed[clip, :, before:], weight_ref[:, before:], NT)
        give_back(clip, back)
        norm_sums(clip, back)
        mine = lane_slice(vert * half, half)
        vec_sum[0, 2:3, mine] = bias_acc[0:1]
        vec_sum[0, 3:4, mine] = bias_acc[1:2]
        vec_copy(0).start()

    def inputs(clip):
        dn_copy(clip).wait_recv()
        grad = acc[clip] + dn_got[clip].astype(f32)
        unit, inverse = center_scale(tok_ref[0].astype(f32))
        result = gmid_ref[0][:slots] + norm_back(unit, inverse, row_of(gain_ref), grad[:slots])
        gtok_ref[0] = result

    @pl.when((step >= places["inputs"]) & (step < places["end"]))
    def early_inputs():
        inputs(step - places["inputs"])

    @pl.when(step == places["end"])
    def finish():
        for kind, a, stage in SUM_STEPS[places["end"]]:
            if kind == "input":
                inputs(clips - 1)
            else:
                perform((kind, a, stage))
        for a, (name, at, r, width_a, _) in enumerate(arrays):
            for who in range(2):
                full = full_bufs[a]
                if name == "fc1":
                    start = who * fc1_out.shape[1] // 2 + at
                    fc1_out[:, start : start + width_a] = full[who]
                elif name == "fc2":
                    fc2_out[at : at + r, who * width_a : (who + 1) * width_a] = full[who]
                elif name == "proj":
                    proj_out[:, who * width_a : (who + 1) * width_a] = full[who]
                else:
                    for side in range(2):
                        for part in range(3):
                            to = part * width + side * half + at * lanes
                            value = full[who, side, :, part * lanes : (part + 1) * lanes]
                            qkv_out[who * r : (who + 1) * r, to : to + lanes] = value
        vec_out[...] = vec_sum[bits + 2]
        for a in range(count):
            for stage in range(bits + 3):
                stage_copy(a, stage).wait_send()
        for clip in range(clips):
            grad_vert(clip).wait_send()
            dn_copy(clip).wait_send()
        for pair in range(pairs):
            kv_copy(clips - 1, pair).wait_send()
        for hop in range(bits + 2):
            vec_copy(hop).wait_send()


def step_places(clips, pairs):
    of_clip = 2 * pairs
    projections = [of_clip * (c + 1) + 2 + c for c in range(clips - 1)]
    begin = of_clip * (clips - 1) + clips - 1
    chunks = [begin + 2 * (pair + 1) + 1 + pair for pair in range(pairs - 1)]
    projections.append(begin + of_clip + pairs - 1)
    inputs = projections[-1] + 1
    pauses = projections[:-1] + chunks
    return {"projections": projections, "chunks": chunks, "pauses": pauses, "inputs": inputs, "end": inputs + clips - 1}


def attention_unit(step, places, clips, pairs):
    index = step
    for at in places["pauses"]:
        index = index - (step > at).astype(jnp.int32)
    index = jnp.minimum(index, 2 * clips * pairs - 1)
    clip = index // (2 * pairs)
    inside = index % (2 * pairs)
    last = clip == clips - 1
    return clip, jnp.where(last, inside % 2, inside // pairs), jnp.where(last, inside // 2, inside % pairs)


def backward(q, k, v, mask, part, lse, normed, weight_half, tokens, far, gmid, gain, small, db1, gmixed,
             dfc1, dfc2, dproj, clip_size):
    clips, slots, width = tokens.shape
    rows = gmid.shape[1]
    half = width // 2
    keys = k.shape[1]
    pairs = HEADS // 4
    lanes = 2 * DH
    bits = clip_size.bit_length() - 1
    hidden = db1.shape[1]
    arrays = sum_arrays(width, hidden, clip_size)
    places = step_places(clips, pairs)
    one = pl.Buffered(buffer_count=1)

    def of_pair(s):
        return attention_unit(s, places, clips, pairs)

    def of_keys(s):
        clip, _, pair = of_pair(s)
        return clip, 0, pair

    def of_projection(s):
        index = s * 0
        for at in places["projections"][:-1]:
            index = index + (s > at).astype(jnp.int32)
        return index, 0, 0

    def of_clip(s):
        return jnp.clip(s - places["inputs"], 0, clips - 1), 0, 0

    fixed = lambda shape: pl.BlockSpec(shape, lambda s: (0,) * len(shape), pipeline_mode=one)
    tok_pair = pl.BlockSpec((1, rows, lanes), of_pair)
    key_pair = pl.BlockSpec((1, keys, lanes), of_keys)
    anywhere = pl.BlockSpec(memory_space=pl.ANY)
    blocks = (2,) * bits
    r_fc1, r_fc2 = width // clip_size, hidden // clip_size
    dfc1 = dfc1.reshape((2,) + blocks + (r_fc1, hidden // 2))
    dfc2 = dfc2.reshape((2,) + blocks + (r_fc2, half))
    dproj = dproj.reshape((2,) + blocks + (r_fc1, half))
    vmem = lambda *shape: pltpu.VMEM(shape, bf16)
    wide = lambda *shape: pltpu.VMEM(shape, f32)
    scratch = [
        vmem(2, clips, rows, half),
        vmem(clips, 2 * rows, 3 * half),
        wide(pairs, 2, keys, lanes),
        vmem(pairs, 2, 2 * rows, lanes),
        vmem(clips, pairs, 2, 2 * rows, lanes),
        wide(clips, rows, width),
        vmem(clips, rows, width),
        vmem(clips, rows, width),
        wide(width, 3 * half),
        wide(8, half),
        wide(bits + 3, 16, width),
        wide(bits + 2, 16, width),
        vmem(*blocks, r_fc1, hidden // 4),
        vmem(*blocks, r_fc2 // 2, half),
        vmem(*blocks, r_fc1, half),
    ]
    scratch.append(vmem(pairs, 2, *blocks, r_fc1 // 2, half))
    for _, _, r, w, _ in arrays:
        scratch += [vmem(*((2,) * (bits - stage)), r, w) for stage in range(bits + 1)]
    scratch += [vmem(r, w) for name, _, r, w, _ in arrays if name != "qkv"]
    scratch += [vmem(2, 2, r, w) if name == "qkv" else vmem(2, r, w) for name, _, r, w, _ in arrays]
    dma = lambda *shape: pltpu.SemaphoreType.DMA(shape)
    count = len(arrays)
    scratch += [
        dma(clips), dma(clips), dma(clips), dma(clips, pairs), dma(clips, pairs), dma(clips), dma(clips),
        dma(count, bits + 3), dma(count, bits + 3), dma(count), dma(bits + 2), dma(bits + 2),
    ]
    shape = jax.ShapeDtypeStruct
    return pl.pallas_call(
        functools.partial(backward_kernel, (clips, slots, rows, bits, pairs, arrays)),
        grid=(places["end"] + 1,),
        in_specs=[
            tok_pair, key_pair, key_pair,
            pl.BlockSpec((1, 1, keys), lambda s: (of_pair(s)[0], 0, 0)),
            tok_pair, tok_pair,
            pl.BlockSpec((1, 2 * rows, width), of_projection),
            fixed(weight_half.shape),
            pl.BlockSpec((1, slots, width), of_projection),
            pl.BlockSpec((1, rows, width), of_projection),
            pl.BlockSpec((1, slots, width), of_clip),
            pl.BlockSpec((1, rows, width), of_clip),
            fixed((width,)), fixed((8, width)), fixed((1, hidden)),
            anywhere, anywhere, anywhere, anywhere,
        ],
        out_specs=[
            pl.BlockSpec((1, slots, width), of_clip),
            fixed((r_fc1, hidden)), fixed((r_fc2, width)), fixed((r_fc1, width)),
            fixed((r_fc1, 3 * width)), fixed((16, width)),
        ],
        out_shape=[
            shape((clips, slots, width), f32),
            shape((r_fc1, hidden), bf16),
            shape((r_fc2, width), bf16),
            shape((r_fc1, width), bf16),
            shape((r_fc1, 3 * width), bf16),
            shape((16, width), f32),
        ],
        scratch_shapes=scratch,
        compiler_params=params(collective_id=1, has_side_effects=True),
        cost_estimate=pl.CostEstimate(
            flops=2 * clips * rows * (5 * keys * width + 6 * width * width),
            bytes_accessed=60_000_000,
            transcendentals=clips * rows * keys * HEADS,
        ),
        name="backward",
    )(q, k, v, mask, part, lse, normed, weight_half, tokens, far, tokens, gmid, gain, small, db1, gmixed, dfc1, dfc2, dproj)


def outputs_kernel(fc1, fc2, proj, qkv, vec, gtok, fc1_out, fc2_out, proj_out, qkv_out, gtok_out, db1_out, *outs):
    gtok_out[...] = gtok[...]

    @pl.when(pl.program_id(0) == 0)
    def others():
        for src, dst in ((fc1, fc1_out), (fc2, fc2_out), (proj, proj_out), (qkv, qkv_out)):
            dst[...] = src[...].astype(f32)
        width = vec.shape[1]
        for i, dst in enumerate(outs):
            dst[...] = vec[i : i + 1].reshape(width)
        tall = db1_out.shape[0] // width
        db1_out[...] = jnp.concatenate([vec[8 + i : 9 + i] for i in range(tall)], axis=1).reshape(db1_out.shape[0])


def final_outputs(low_fc1, low_fc2, low_proj, low_qkv, summed, gtok, hidden):
    width = summed.shape[1]
    one = pl.Buffered(buffer_count=1)
    fixed = lambda shape: pl.BlockSpec(shape, lambda c: (0,) * len(shape), pipeline_mode=one)
    by_clip = pl.BlockSpec((1,) + gtok.shape[1:], lambda c: (c, 0, 0))
    shape = jax.ShapeDtypeStruct
    lows = (low_fc1, low_fc2, low_proj, low_qkv)
    return pl.pallas_call(
        outputs_kernel,
        grid=(gtok.shape[0],),
        in_specs=[fixed(a.shape) for a in lows] + [fixed(summed.shape), by_clip],
        out_specs=[fixed(a.shape) for a in lows] + [by_clip, fixed((hidden,))] + [fixed((width,))] * 8,
        out_shape=[shape(a.shape, f32) for a in lows]
        + [shape(gtok.shape, f32), shape((hidden,), f32)]
        + [shape((width,), f32)] * 8,
        compiler_params=params(),
        name="final_outputs",
    )(*lows, summed, gtok)


def partner(kind):
    index = lax.axis_index("freq")
    if kind == "vert":
        return {"freq": (index + 2) % 4}
    return {"freq": index + 1 - 2 * (index % 2)}


def whole_forward_kernel(
    counts,
    tok_ref, qkv_ref, qb_ref, vb_ref, gain_ref, shift_ref, proj_ref, pb_ref, gain2_ref, shift2_ref,
    q_ref, k_ref, v_ref, normed_ref, mixed_ref, lse_ref, middle_ref, normed2_ref, mask_ref,
    held, send_sem, recv_sem,
):
    clips, slots, rows = counts
    clip = pl.program_id(0)
    pair = pl.program_id(1)
    width = tok_ref.shape[-1]

    def copy(kind, index):
        at = {"vert": 0, "core": 1, "diag": 2}[kind]
        return pltpu.make_async_remote_copy(
            src_ref=held.at[index, 0] if kind == "diag" else tok_ref.at[index],
            dst_ref=held.at[index, at],
            send_sem=send_sem.at[index, at],
            recv_sem=recv_sem.at[index, at],
            device_id=partner(kind),
            device_id_type=pl.DeviceIdType.MESH,
        )

    def project(slot, source):
        unit, _ = center_scale(source.astype(f32))
        normed = (unit * gain_ref[...] + shift_ref[...]).astype(bf16)
        if slot == 0:
            normed_ref[0] = normed
            query = (dot(normed, qkv_ref[:, :width]) + qb_ref[...]).astype(bf16)
            q_ref[0] = query * jnp.asarray(DH ** -0.5, bf16)
        both = dot(normed, qkv_ref[:, width:])
        k_ref[0, slot * rows : (slot + 1) * rows] = both[:, :width].astype(bf16)
        v_ref[0, slot * rows : (slot + 1) * rows] = (both[:, width:] + vb_ref[...]).astype(bf16)
        first = (slots // 16) * 16
        kept = source[first:].astype(f32)[slots - first : slots - first + 1, 0:1] + slots // 2
        lane = lax.broadcasted_iota(jnp.int32, (1, rows), 1).astype(f32)
        return (lane < kept).astype(f32)

    @pl.when((clip == 0) & (pair == 0))
    def enter():
        barrier = pltpu.get_barrier_semaphore()
        for kind in ("vert", "core"):
            pl.semaphore_signal(
                barrier, inc=1, device_id=partner(kind), device_id_type=pl.DeviceIdType.MESH
            )
        pl.semaphore_wait(barrier, 2)
        copy("vert", 0).start()
        for index in range(clips):
            copy("core", index).start()

    def pass_on(index):
        copy("vert", index).wait_recv()
        copy("diag", index).start()
        copy("vert", index).wait_send()

        @pl.when(index + 1 < clips)
        def more():
            copy("vert", index + 1).start()

    @pl.when(pair == 0)
    def project_all():
        live_own = project(0, tok_ref[clip])
        copy("core", clip).wait_recv()
        live_core = project(2, held[clip, 1])

        @pl.when(clip == 0)
        def first_pass():
            pass_on(clip)

        live_vert = project(1, held[clip, 0])
        copy("diag", clip).wait_recv()
        live_diag = project(3, held[clip, 2])
        mask_ref[0] = jnp.concatenate([live_own, live_vert, live_core, live_diag], axis=1)

    @pl.when((pair == 3) & (clip + 1 < clips))
    def next_pass():
        pass_on(clip + 1)

    lanes = pl.ds(pl.multiple_of(pair * 2 * DH, 2 * DH), 2 * DH)
    query = q_ref[0, :, lanes]
    keys = k_ref[0, :, lanes]
    values = v_ref[0, :, lanes]
    live = mask_ref[0] > 0.5
    outs, lses = [], []
    for head in range(2):
        scores = jnp.where(live, dot(only(query, head), keys, NT), MASKED)
        top = jnp.max(scores, axis=1, keepdims=True)
        exps = jnp.exp(scores - top)
        total = jnp.sum(exps, axis=1, keepdims=True)
        outs.append(dot(exps.astype(bf16), values) / total)
        lses.append(top + jnp.log(total))
    first = own_lanes(outs[0].shape, 0)
    mixed_ref[0, :, lanes] = jnp.where(first, outs[0], outs[1]).astype(bf16)
    lse_ref[0, :, lanes] = jnp.where(first, lses[0], lses[1])

    @pl.when(pair == pl.num_programs(1) - 1)
    def finish():
        middle = tok_ref[clip].astype(f32) + (dot(mixed_ref[0], proj_ref[...]) + pb_ref[...])
        middle_ref[0] = middle
        unit, _ = center_scale(middle)
        normed2_ref[0] = (unit * gain2_ref[...] + shift2_ref[...]).astype(bf16)
        copy("core", clip).wait_send()
        copy("diag", clip).wait_send()


def whole_forward(tok, slots, qkv_weight, vectors, proj_weight):
    clips, rows, width = tok.shape
    keys = 4 * rows
    pairs = HEADS // 2
    query_bias, value_bias, gain, shift, proj_bias, gain2, shift2 = vectors
    one = pl.Buffered(buffer_count=1)
    row = full((1, width))
    block = lambda n: pl.BlockSpec((1, n, width), lambda c, p: (c, 0, 0))
    flops = 2 * clips * (10 * rows * width * width + 2 * rows * keys * width)
    weight = lambda w: pl.BlockSpec(w.shape, lambda c, p: (0, 0), pipeline_mode=one)
    return pl.pallas_call(
        functools.partial(whole_forward_kernel, (clips, slots, rows)),
        grid=(clips, pairs),
        in_specs=[
            pl.BlockSpec(tok.shape, lambda c, p: (0, 0, 0), pipeline_mode=one),
            weight(qkv_weight), row, row, row, row, weight(proj_weight), row, row, row,
        ],
        out_specs=[block(rows), block(keys), block(keys)] + [block(rows)] * 5
        + [pl.BlockSpec((1, 1, keys), lambda c, p: (c, 0, 0))],
        out_shape=[
            jax.ShapeDtypeStruct((clips, rows, width), bf16),
            jax.ShapeDtypeStruct((clips, keys, width), bf16),
            jax.ShapeDtypeStruct((clips, keys, width), bf16),
            jax.ShapeDtypeStruct((clips, rows, width), bf16),
            jax.ShapeDtypeStruct((clips, rows, width), bf16),
            jax.ShapeDtypeStruct((clips, rows, width), f32),
            jax.ShapeDtypeStruct((clips, rows, width), f32),
            jax.ShapeDtypeStruct((clips, rows, width), bf16),
            jax.ShapeDtypeStruct((clips, 1, keys), f32),
        ],
        scratch_shapes=[
            pltpu.VMEM((clips, 3, rows, width), bf16),
            pltpu.SemaphoreType.DMA((clips, 3)),
            pltpu.SemaphoreType.DMA((clips, 3)),
        ],
        compiler_params=params(collective_id=0, has_side_effects=True),
        cost_estimate=pl.CostEstimate(
            flops=flops, bytes_accessed=40_000_000, transcendentals=clips * rows * keys * HEADS
        ),
        name="whole_forward",
    )(tok, qkv_weight, query_bias, value_bias, gain, shift, proj_weight, proj_bias, gain2, shift2)


def attend_back_kernel(q_ref, k_ref, v_ref, mask_ref, mixed_ref, lse_ref, grad_ref,
                       dq_ref, dkeep_ref, dsend_ref):
    query = q_ref[0]
    keys = k_ref[0]
    values = v_ref[0]
    grad = grad_ref[0]
    live = mask_ref[0] > 0.5
    product = grad.astype(f32) * mixed_ref[0].astype(f32)
    dqs, dk, dv = [], None, None
    for head in range(2):
        own_query = only(query, head)
        own_grad = only(grad, head)
        scores = jnp.where(live, dot(own_query, keys, NT), MASKED)
        probs = jnp.exp(scores - lse_ref[0, :, head * DH : head * DH + 1])
        delta = jnp.sum(only(product, head), axis=1, keepdims=True)
        dscores = (probs * (dot(own_grad, values, NT) - delta)).astype(bf16)
        dqs.append(dot(dscores, keys))
        more_k = dot(dscores, own_query, TN)
        more_v = dot(probs.astype(bf16), own_grad, TN)
        dk = more_k if dk is None else dk + more_k
        dv = more_v if dv is None else dv + more_v
    first = own_lanes(dqs[0].shape, 0)
    dq_ref[0] = (jnp.where(first, dqs[0], dqs[1]) * DH ** -0.5).astype(bf16)
    half = dk.shape[0] // 2
    dkeep_ref[0, 0] = dk[:half].astype(bf16)
    dkeep_ref[1, 0] = dv[:half].astype(bf16)
    dsend_ref[0, 0] = dk[half:].astype(bf16)
    dsend_ref[1, 0] = dv[half:].astype(bf16)


def attend_back(q, k, v, mask, mixed, lse, grad, first_pair, pairs):
    clips, rows, _ = q.shape
    keys = k.shape[1]
    lanes = 2 * DH
    tok = pl.BlockSpec((1, rows, lanes), lambda c, p: (c, 0, first_pair + p))
    key = pl.BlockSpec((1, keys, lanes), lambda c, p: (c, 0, first_pair + p))
    part = pl.BlockSpec((2, 1, keys // 2, lanes), lambda c, p: (0, c, 0, p))
    return pl.pallas_call(
        attend_back_kernel,
        grid=(clips, pairs),
        in_specs=[tok, key, key, pl.BlockSpec((1, 1, keys), lambda c, p: (c, 0, 0)), tok, tok, tok],
        out_specs=[pl.BlockSpec((1, rows, lanes), lambda c, p: (c, 0, p)), part, part],
        out_shape=[
            jax.ShapeDtypeStruct((clips, rows, pairs * lanes), bf16),
            jax.ShapeDtypeStruct((2, clips, keys // 2, pairs * lanes), bf16),
            jax.ShapeDtypeStruct((2, clips, keys // 2, pairs * lanes), bf16),
        ],
        compiler_params=params(),
        cost_estimate=pl.CostEstimate(
            flops=4 * 10 * clips * rows * keys * pairs * lanes,
            bytes_accessed=clips * pairs * lanes * (keys * 10 + rows * 12),
            transcendentals=clips * rows * keys * 2 * pairs,
        ),
        name="attend_back",
    )(q, k, v, mask, mixed, lse, grad)


def weight_kernel(normed_ref, dq_ref, dk0_ref, dk1_ref, dk2_ref, out_ref, dkv_ref, sums_ref):
    part = pl.program_id(0)
    @pl.when(part == 0)
    def query():
        grad = dq_ref[...]
        out_ref[0] = dot(normed_ref[...], grad, TN).astype(bf16)
        sums_ref[0] = column_sums(grad.astype(f32))
        dkv_ref[0] = jnp.zeros_like(dkv_ref[0])

    @pl.when(part > 0)
    def other():
        grad = (dk0_ref[0].astype(f32) + dk1_ref[0].astype(f32) + dk2_ref[0].astype(f32)).astype(bf16)
        dkv_ref[0] = grad
        out_ref[0] = dot(normed_ref[...], grad, TN).astype(bf16)
        sums_ref[0] = column_sums(grad.astype(f32))


def weight_grads(normed, dq, parts):
    total, width = normed.shape
    lanes = dq.shape[1]
    before = lambda j: (jnp.maximum(j - 1, 0), 0, 0)
    part = pl.BlockSpec((1, total, lanes), before)
    return pl.pallas_call(
        weight_kernel,
        grid=(3,),
        in_specs=[full((total, width)), full((total, lanes)), part, part, part],
        out_specs=[
            pl.BlockSpec((1, width, lanes), lambda j: (j, 0, 0)),
            part,
            pl.BlockSpec((1, 1, lanes), lambda j: (j, 0, 0)),
        ],
        out_shape=[
            jax.ShapeDtypeStruct((3, width, lanes), bf16),
            jax.ShapeDtypeStruct((2, total, lanes), bf16),
            jax.ShapeDtypeStruct((3, 1, lanes), f32),
        ],
        compiler_params=params(),
        cost_estimate=pl.CostEstimate(
            flops=6 * total * width * lanes, bytes_accessed=8_000_000, transcendentals=0
        ),
        name="weight_grads",
    )(normed, dq, *parts)


def input_kernel(counts, groups, *refs):
    clips, slots, rows = counts
    dqs = refs[:groups]
    dkvs = refs[groups : 2 * groups]
    qkv_ref, tok_ref, gmid_ref, gain_ref, shift_ref, out_ref, small_ref = refs[2 * groups :]
    clip = pl.program_id(0)
    width = tok_ref.shape[-1]
    lanes = width // groups
    grad = None
    for group in range(groups):
        for part in range(3):
            rows_grad = dqs[group][0] if part == 0 else dkvs[group][part - 1]
            at = part * width + group * lanes
            more = dot(rows_grad, qkv_ref[:, at : at + lanes], NT)
            grad = more if grad is None else grad + more
    unit, inverse = center_scale(tok_ref[0].astype(f32))
    result = gmid_ref[0] + norm_back(unit, inverse, gain_ref[...], grad)
    out_ref[0] = result[:slots]

    @pl.when(clip == 0)
    def start():
        small_ref[...] = jnp.zeros_like(small_ref)

    small_ref[0:1] += column_sums(grad * unit)
    small_ref[1:2] += column_sums(grad)


def input_grads(dqs, dkvs, qkv_weight, tokens, gmid, gain, shift, slots):
    clips, rows, width = tokens.shape
    groups = len(dqs)
    lanes = width // groups
    tok = pl.BlockSpec((1, rows, width), lambda c: (c, 0, 0))
    return pl.pallas_call(
        functools.partial(input_kernel, (clips, slots, rows), groups),
        grid=(clips,),
        in_specs=[pl.BlockSpec((1, rows, lanes), lambda c: (c, 0, 0))] * groups
        + [pl.BlockSpec((2, rows, lanes), lambda c: (0, c, 0))] * groups
        + [full(qkv_weight.shape), tok, tok, full((1, width)), full((1, width))],
        out_specs=[pl.BlockSpec((1, slots, width), lambda c: (c, 0, 0)), full((8, width))],
        out_shape=[
            jax.ShapeDtypeStruct((clips, slots, width), f32),
            jax.ShapeDtypeStruct((8, width), f32),
        ],
        compiler_params=params(),
        cost_estimate=pl.CostEstimate(
            flops=6 * clips * rows * width * width, bytes_accessed=16_000_000, transcendentals=0
        ),
        name="input_grads",
    )(*dqs, *dkvs, qkv_weight, tokens, gmid, gain, shift)


def swap_bit(array, axis, size, bit):
    return lax.ppermute(array, axis, [(i, i ^ (1 << bit)) for i in range(size)])


def add_low(left, right):
    return (left.astype(f32) + right.astype(f32)).astype(bf16)


def pick(array, index, dim):
    return lax.dynamic_index_in_dim(array, index, dim, keepdims=False)


def bit_of(axis, bit):
    return (lax.axis_index(axis) >> bit) & 1


def scatter_sum(split, clip_size, order):
    core = bit_of("freq", 0)
    vert = bit_of("freq", 1)
    bits = clip_size.bit_length() - 1
    lanes = split.shape[-1]
    value = add_low(pick(split, core, 0), swap_bit(pick(split, 1 - core, 0), "freq", 4, 0))
    rows = value.shape[0] // (2 * clip_size)
    value = value.reshape((2,) * bits + (2, rows, lanes))
    left = list(range(bits))[::-1]
    for bit in order:
        at = left.index(bit)
        mine = bit_of("clip", bit)
        value = add_low(
            pick(value, mine, at), swap_bit(pick(value, 1 - mine, at), "clip", clip_size, bit)
        )
        left.remove(bit)
    return add_low(pick(value, vert, 0), swap_bit(pick(value, 1 - vert, 0), "freq", 4, 1))


def gather_low(part):
    core = bit_of("freq", 0)
    vert = bit_of("freq", 1)
    other = swap_bit(part, "freq", 4, 1)
    tall = jnp.where(vert == 0, jnp.concatenate([part, other]), jnp.concatenate([other, part]))
    side = swap_bit(tall, "freq", 4, 0)
    return jnp.where(
        core == 0,
        jnp.concatenate([tall, side], axis=1),
        jnp.concatenate([side, tall], axis=1),
    ).astype(f32)


def total_sum(array, clip_size):
    for bit in range(2):
        array = array + swap_bit(array, "freq", 4, bit)
    for bit in range(clip_size.bit_length() - 1):
        array = array + swap_bit(array, "clip", clip_size, bit)
    return array


def on_device_plain(
    clip_size, tokens, kept_counts, attn_gain, attn_shift, qkv_weight, query_bias, value_bias,
    proj_weight, proj_bias, mlp_gain, mlp_shift, fc1_weight, fc1_bias, fc2_weight, fc2_bias, cotangent,
):
    clips, slots, width = tokens.shape
    rows = -(-slots // 16) * 16
    total = clips * rows
    bits = clip_size.bit_length() - 1
    forward_order = list(range(bits))
    second_order = forward_order[1:2] + forward_order[:1] + forward_order[2:]
    vec = lambda v: v.astype(f32)[None, :]
    kept = (kept_counts - slots // 2).astype(bf16)
    tok = jnp.concatenate(
        [tokens, jnp.broadcast_to(kept[:, :, None], (clips, rows - slots, width))], axis=1
    )
    vectors = [vec(v) for v in (query_bias, value_bias, attn_gain, attn_shift, proj_bias, mlp_gain, mlp_shift)]
    q, k, v, normed, mixed, lse, middle, normed2, mask = whole_forward(
        tok, slots, qkv_weight, vectors, proj_weight
    )
    flat = lambda a: a.reshape(total, width)
    layer_out, dfc1, dfc2, dproj, db1, small2, gmid, gmixed = mlp(
        kept_counts, flat(normed2), flat(middle), cotangent, flat(mixed), fc1_weight, fc1_bias,
        fc2_weight, fc2_bias, mlp_gain, proj_weight, rows,
    )
    early = total_sum(jnp.concatenate([small2[:4].reshape(-1), db1.reshape(-1)])[None, :], clip_size)[0]
    sum_fc1 = gather_low(scatter_sum(dfc1, clip_size, forward_order))
    sum_fc2 = gather_low(scatter_sum(dfc2, clip_size, second_order))
    sum_proj = gather_low(scatter_sum(dproj, clip_size, forward_order))

    groups = 3
    pairs = HEADS // 2 // groups
    lanes = pairs * 2 * DH
    gmixed = gmixed.reshape(clips, rows, width)
    dqs, dkvs, sums, sharded = [], [], [], []
    for group in range(groups):
        dq, keep, send = attend_back(q, k, v, mask, mixed, lse, gmixed, group * pairs, pairs)
        got = swap_bit(send, "freq", 4, 0)
        across = swap_bit(add_low(keep[:, :, rows:], got[:, :, rows:]), "freq", 4, 1)
        parts = [a.reshape(2, total, lanes) for a in (keep[:, :, :rows], got[:, :, :rows], across)]
        dw, dkv, colsum = weight_grads(flat(normed), dq.reshape(total, lanes), parts)
        half = lanes // 2
        split = jnp.stack(
            [
                jnp.concatenate([dw[i, :, s * half : (s + 1) * half] for i in range(3)], axis=1)
                for s in range(2)
            ]
        )
        order = forward_order if group % 2 == 0 else second_order
        summed = gather_low(scatter_sum(split, clip_size, order))
        sharded.append(summed.reshape(summed.shape[0], 2, 3, half))
        dqs.append(dq)
        dkvs.append(dkv)
        sums.append(colsum)
    grad_tokens, small1 = input_grads(
        dqs, dkvs, qkv_weight, tok, gmid.reshape(clips, rows, width), vectors[2], vectors[3], slots
    )
    qkv = jnp.stack(sharded, axis=1)
    sum_qkv = qkv.transpose(0, 3, 1, 2, 4).reshape(qkv.shape[0], 3 * width)
    bias = jnp.concatenate(sums, axis=2)
    late = total_sum(
        jnp.concatenate([small1[0:1], small1[1:2], bias[0], bias[2]], axis=1), clip_size
    )[0]
    cut = lambda a, i: a[i * width : (i + 1) * width]
    return (
        layer_out, grad_tokens, cut(late, 0), cut(late, 1), sum_qkv, cut(late, 2), cut(late, 3),
        sum_proj, cut(early, 3), cut(early, 0), cut(early, 1), sum_fc1, early[4 * width :],
        sum_fc2, cut(early, 2),
    )


def on_device(
    clip_size, tokens, kept_counts, attn_gain, attn_shift, qkv_weight, query_bias, value_bias,
    proj_weight, proj_bias, mlp_gain, mlp_shift, fc1_weight, fc1_bias, fc2_weight, fc2_bias, cotangent,
):
    clips, slots, width = tokens.shape
    rows = -(-slots // 16) * 16
    if clip_size != 8 or width % (32 * clip_size):
        return on_device_plain(
            clip_size, tokens, kept_counts, attn_gain, attn_shift, qkv_weight, query_bias, value_bias,
            proj_weight, proj_bias, mlp_gain, mlp_shift, fc1_weight, fc1_bias, fc2_weight, fc2_bias, cotangent,
        )
    q, k, v, normed, far, weight_half, part, lse, mask, mixed, middle, normed2 = forward(
        kept_counts, tokens, rows, qkv_weight, query_bias, value_bias, attn_gain, attn_shift,
        proj_weight, proj_bias, mlp_gain, mlp_shift,
    )
    flat = lambda a: a.reshape(clips * rows, width)
    layer_out, dfc1, dfc2, dproj, db1, small, gmid, gmixed = mlp(
        kept_counts, flat(normed2), flat(middle), cotangent, flat(mixed), fc1_weight, fc1_bias,
        fc2_weight, fc2_bias, mlp_gain, proj_weight, rows,
    )
    by_clip = lambda a: a.reshape(clips, rows, width)
    gtok, low_fc1, low_fc2, low_proj, low_qkv, summed = backward(
        q, k, v, mask, part, lse, normed, weight_half, tokens, far, by_clip(gmid), attn_gain, small, db1,
        by_clip(gmixed), dfc1, dfc2, dproj, clip_size,
    )
    fc1, fc2, proj, qkv, grad_tokens, fc1_b, *rows_out = final_outputs(
        low_fc1, low_fc2, low_proj, low_qkv, summed, gtok, fc1_bias.shape[0]
    )
    return (
        layer_out, grad_tokens, rows_out[0], rows_out[1], qkv, rows_out[2], rows_out[3], proj, rows_out[7],
        rows_out[4], rows_out[5], fc1, fc1_b, fc2, rows_out[6],
    )


def solution(mesh):
    rows = P("clip", "freq", None)
    shard = P("clip", None)
    return jax.shard_map(
        functools.partial(on_device, mesh.shape["clip"]),
        mesh=mesh,
        in_specs=(rows, P("clip", "freq")) + (P(),) * 13 + (rows,),
        out_specs=(rows, rows, P(), P(), shard, P(), P(), shard, P(), P(), P(), shard, P(), shard, P()),
        check_vma=False,
    )
```

```python
import functools
import math

import jax
import jax.numpy as jnp
from jax import lax
from jax.experimental import pallas as pl
from jax.experimental.pallas import tpu as pltpu
from jax.sharding import PartitionSpec as P

HEADS = 12
DH = 64
EPS = 1e-06
MASKED = -1000000000.0
VMEM_BYTES = 60 * 1024 * 1024

f32 = jnp.float32
bf16 = jnp.bfloat16
NN = (((1,), (0,)), ((), ()))
NT = (((1,), (1,)), ((), ()))
TN = (((0,), (0,)), ((), ()))


def dot(left, right, dims=NN):
    return lax.dot_general(left, right, dims, preferred_element_type=f32)


def center_scale(rows):
    center = rows - jnp.mean(rows, axis=-1, keepdims=True)
    inverse = lax.rsqrt(jnp.mean(center * center, axis=-1, keepdims=True) + EPS)
    return center * inverse, inverse


def norm_back(unit, inverse, gain, grad):
    scaled = grad * gain
    return inverse * (
        scaled
        - jnp.mean(scaled, axis=-1, keepdims=True)
        - unit * jnp.mean(scaled * unit, axis=-1, keepdims=True)
    )


def column_sums(rows):
    return jnp.sum(rows, axis=0, keepdims=True)


def own_lanes(shape, head):
    lane = lax.broadcasted_iota(jnp.int32, shape, len(shape) - 1)
    return lane < DH if head == 0 else lane >= DH


def only(rows, head):
    return jnp.where(own_lanes(rows.shape, head), rows, jnp.zeros_like(rows))


def full(shape):
    return pl.BlockSpec(shape, lambda *ids: (0,) * len(shape))


def params(**more):
    return pltpu.CompilerParams(vmem_limit_bytes=VMEM_BYTES, **more)


def freq_places():
    freq = lax.axis_index("freq")
    core, vert = freq % 2, freq // 2
    return core, vert, {"freq": freq + 1 - 2 * core}, {"freq": (freq + 2) % 4}


def lane_slice(start, size):
    return pl.ds(pl.multiple_of(start, 2 * DH), size)


def row_of(ref):
    return ref[...].astype(f32).reshape(1, ref.shape[0])


def forward_kernel(
    counts,
    kept_ref, tok_ref, qkv_ref, qb_ref, vb_ref, gain_ref, shift_ref, proj_ref, pb_ref, gain2_ref, shift2_ref,
    q_out, k_out, v_out, normed_out, far_out, weight_out, part_ref, lse_ref, mask_ref, mixed_ref, middle_ref, normed2_ref,
    q_all, k_all, v_all, normed_all, weight, live_all, own, held, mix_send, mix_got, own_mix, vecs,
    tok_send, tok_recv, part_send, part_recv, out_sem, weight_sem,
):
    clips, slots, rows, pairs = counts
    clip = pl.program_id(0)
    turn = pl.program_id(1)
    slot = 1 - turn
    width = tok_ref.shape[-1]
    half = width // 2
    lanes = 2 * DH
    core, vert, core_dev, vert_dev = freq_places()
    mesh_id = pl.DeviceIdType.MESH

    def copy(kind, index):
        at = {"vert": 0, "core": 1, "diag": 2}[kind]
        return pltpu.make_async_remote_copy(
            src_ref=held.at[index, 0] if kind == "diag" else own.at[index],
            dst_ref=held.at[index, at],
            send_sem=tok_send.at[index, at],
            recv_sem=tok_recv.at[index, at],
            device_id=vert_dev if kind == "vert" else core_dev,
            device_id_type=mesh_id,
        )

    def mix_copy(index, which):
        return pltpu.make_async_remote_copy(
            src_ref=mix_send.at[index, which],
            dst_ref=mix_got.at[index, which],
            send_sem=part_send.at[index, which],
            recv_sem=part_recv.at[index, which],
            device_id=vert_dev,
            device_id_type=mesh_id,
        )

    def project(index, slot, source):
        unit, _ = center_scale(source.astype(f32))
        normed = (unit * vecs[2:3] + vecs[3:4]).astype(bf16)
        at = slice(slot * rows, (slot + 1) * rows)
        if slot < 2:
            normed_all[index, at] = normed
            query = (dot(normed, weight[:, :half]) + vecs[0:1, lane_slice(vert * half, half)]).astype(bf16)
            q_all[index, at] = query * jnp.asarray(DH ** -0.5, bf16)
        both = dot(normed, weight[:, half:])
        k_all[index, at] = both[:, :half].astype(bf16)
        v_all[index, at] = (both[:, half:] + vecs[1:2, lane_slice(vert * half, half)]).astype(bf16)
        first = (slots // 16) * 16
        kept = source[first:].astype(f32)[slots - first : slots - first + 1, 0:1] + slots // 2
        lane = lax.broadcasted_iota(jnp.int32, (1, rows), 1).astype(f32)
        live_all[index, slot] = (lane < kept).astype(f32)

    def out_copies(index):
        return [
            pltpu.make_async_copy(src.at[index], dst.at[index], out_sem.at[index, i])
            for i, (src, dst) in enumerate(
                ((q_all, q_out), (k_all, k_out), (v_all, v_out), (normed_all, normed_out))
            )
        ] + [pltpu.make_async_copy(held.at[index, 0], far_out.at[index], out_sem.at[index, 4])]

    def weight_copies():
        moves = []
        for pair in range(pairs):
            for part in range(3):
                src = weight.at[:, pl.ds(part * half + pair * lanes, lanes)]
                dst = weight_out.at[:, pl.ds((3 * pair + part) * lanes, lanes)]
                moves.append(pltpu.make_async_copy(src, dst, weight_sem.at[3 * pair + part]))
        return moves

    @pl.when((clip == 0) & (turn == 0))
    def enter():
        barrier = pltpu.get_barrier_semaphore()
        for device in (vert_dev, core_dev):
            pl.semaphore_signal(barrier, inc=1, device_id=device, device_id_type=mesh_id)
        first = (slots // 16) * 16
        for index in range(clips):
            kept = (kept_ref[index] - slots // 2).astype(f32).astype(bf16)
            own[index, first:] = jnp.broadcast_to(kept, (rows - first, width))
            own[index, :slots] = tok_ref[index]
        pl.semaphore_wait(barrier, 2)
        copy("vert", 0).start()
        for index in range(clips):
            copy("core", index).start()
        for i, ref in enumerate((qb_ref, vb_ref, gain_ref, shift_ref, pb_ref, gain2_ref, shift2_ref)):
            vecs[i : i + 1] = row_of(ref)
        for part in range(3):
            weight[:, part * half : (part + 1) * half] = qkv_ref[:, lane_slice(part * width + vert * half, half)]
        for move in weight_copies():
            move.start()

        def own_slots(index, carry):
            project(index, 0, own[index])
            return carry

        def core_slots(index, carry):
            copy("core", index).wait_recv()
            project(index, 2, held[index, 1])
            return carry

        lax.fori_loop(0, clips, own_slots, 0)
        lax.fori_loop(0, clips, core_slots, 0)
        copy("vert", 0).wait_recv()
        copy("diag", 0).start()
        copy("vert", 0).wait_send()
        if clips > 1:
            copy("vert", 1).start()

    @pl.when(turn == 0)
    def project_rest():
        project(clip, 1, held[clip, 0])
        copy("diag", clip).wait_recv()
        project(clip, 3, held[clip, 2])
        for i in range(4):
            mask_ref[0, :, i * rows : (i + 1) * rows] = live_all[clip, i]
        for move in out_copies(clip):
            move.start()

    for index in range(2, clips):
        @pl.when((turn == 1) & (clip == index - 2))
        def send_ahead(index=index):
            copy("vert", index - 1).wait_send()
            copy("vert", index).start()

    def finish(index):
        at = lane_slice(vert * half, half)
        mixed_ref[0, :, at] = own_mix[...]
        for which in range(pairs):
            mix_copy(index, which).wait_recv()
            at = lane_slice((1 - vert) * half + which * lanes, lanes)
            mixed_ref[0, :, at] = mix_got[index, which]
        middle = own[index].astype(f32) + (dot(mixed_ref[0], proj_ref[...]) + vecs[4:5])
        middle_ref[0] = middle
        unit, _ = center_scale(middle)
        normed2_ref[0] = (unit * vecs[5:6] + vecs[6:7]).astype(bf16)
        copy("core", index).wait_send()
        copy("diag", index).wait_send()
        for which in range(pairs):
            mix_copy(index, which).wait_send()

    at = pl.ds(pl.multiple_of(slot * rows, rows), rows)
    live = mask_ref[0] > 0.5
    ones = jnp.ones((4 * rows, lanes), bf16)
    for pair in range(pairs):
        here = slice(pair * lanes, (pair + 1) * lanes)
        keys = k_all[clip, :, here]
        values = jnp.concatenate([v_all[clip, :, here], ones], axis=1)
        query = q_all[clip, at, here]
        outs, lses = [], []
        for head in range(2):
            scores = jnp.where(live, dot(only(query, head), keys, NT), MASKED)
            top = jnp.max(scores, axis=1, keepdims=True)
            exps = jnp.exp(scores - top)
            both = dot(exps.astype(bf16), values)
            total = both[:, lanes:]
            outs.append(both[:, :lanes] / total)
            lses.append(top + jnp.log(total))
        first = own_lanes(outs[0].shape, 0)
        mixed = jnp.where(first, outs[0], outs[1]).astype(bf16)
        part_ref[0, at, here] = mixed
        lse_ref[0, at, here] = jnp.where(first, lses[0], lses[1])

    @pl.when(slot == 1)
    def give():
        for pair in range(pairs):
            mix_send[clip, pair] = part_ref[0, rows:, pair * lanes : (pair + 1) * lanes]
            mix_copy(clip, pair).start()

    @pl.when((turn == 0) & (clip > 0))
    def finish_before():
        finish(clip - 1)

    @pl.when(turn == 1)
    def keep_own():
        own_mix[...] = part_ref[0, :rows]

    @pl.when((turn == 1) & (clip + 1 < clips))
    def pass_on():
        copy("vert", clip + 1).wait_recv()
        copy("diag", clip + 1).start()

    @pl.when((turn == 1) & (clip == clips - 1))
    def finish_last():
        finish(clip)
        copy("vert", clips - 1).wait_send()

    @pl.when((turn == 1) & (clip == clips - 1))
    def leave():
        for move in weight_copies():
            move.wait()
        for index in range(clips):
            for move in out_copies(index):
                move.wait()


def forward(kept, tokens, rows, qkv_weight, query_bias, value_bias, gain, shift, proj_weight, proj_bias, gain2, shift2):
    clips, slots, width = tokens.shape
    keys = 4 * rows
    half = width // 2
    pairs = HEADS // 4
    lanes = 2 * DH
    one = pl.Buffered(buffer_count=1)
    block = lambda n, m: pl.BlockSpec((1, n, m), lambda c, p: (c, 0, 0))
    late = pl.BlockSpec((1, rows, width), lambda c, t: (jnp.maximum(c - 1 + t, 0), 0, 0))
    anywhere = pl.BlockSpec(memory_space=pl.ANY)
    whole = lambda a: pl.BlockSpec(a.shape, lambda c, p: (0,) * a.ndim, pipeline_mode=one)
    shape = jax.ShapeDtypeStruct
    flops = 2 * clips * (rows * width * width * 6 + 2 * rows * keys * width)
    vectors = (query_bias, value_bias, gain, shift)
    return pl.pallas_call(
        functools.partial(forward_kernel, (clips, slots, rows, pairs)),
        grid=(clips, 2),
        in_specs=[pl.BlockSpec(memory_space=pltpu.SMEM), whole(tokens), whole(qkv_weight)]
        + [whole(v) for v in vectors]
        + [whole(proj_weight)]
        + [whole(v) for v in (proj_bias, gain2, shift2)],
        out_specs=[
            anywhere, anywhere, anywhere, anywhere, anywhere, anywhere,
            block(2 * rows, half), block(2 * rows, half), block(1, keys),
            late, late, late,
        ],
        out_shape=[
            shape((clips, 2 * rows, half), bf16),
            shape((clips, keys, half), bf16),
            shape((clips, keys, half), bf16),
            shape((clips, 2 * rows, width), bf16),
            shape((clips, rows, width), bf16),
            shape((width, 3 * half), bf16),
            shape((clips, 2 * rows, half), bf16),
            shape((clips, 2 * rows, half), f32),
            shape((clips, 1, keys), f32),
            shape((clips, rows, width), bf16),
            shape((clips, rows, width), f32),
            shape((clips, rows, width), bf16),
        ],
        scratch_shapes=[
            pltpu.VMEM((clips, 2 * rows, half), bf16),
            pltpu.VMEM((clips, keys, half), bf16),
            pltpu.VMEM((clips, keys, half), bf16),
            pltpu.VMEM((clips, 2 * rows, width), bf16),
            pltpu.VMEM((width, 3 * half), bf16),
            pltpu.VMEM((clips, 4, 1, rows), f32),
            pltpu.VMEM((clips, rows, width), bf16),
            pltpu.VMEM((clips, 3, rows, width), bf16),
            pltpu.VMEM((clips, pairs, rows, lanes), bf16),
            pltpu.VMEM((clips, pairs, rows, lanes), bf16),
            pltpu.VMEM((rows, half), bf16),
            pltpu.VMEM((8, width), f32),
            pltpu.SemaphoreType.DMA((clips, 3)),
            pltpu.SemaphoreType.DMA((clips, 3)),
            pltpu.SemaphoreType.DMA((clips, pairs)),
            pltpu.SemaphoreType.DMA((clips, pairs)),
            pltpu.SemaphoreType.DMA((clips, 5)),
            pltpu.SemaphoreType.DMA((3 * pairs,)),
        ],
        compiler_params=params(collective_id=0, has_side_effects=True),
        cost_estimate=pl.CostEstimate(
            flops=flops, bytes_accessed=40_000_000, transcendentals=clips * rows * keys * HEADS
        ),
        name="forward",
    )(kept, tokens, qkv_weight, *vectors, proj_weight, proj_bias, gain2, shift2)


def mlp_kernel(
    counts,
    kept_ref, n2_ref, middle_hbm, cot_ref, mixed_hbm, fc1_ref, b1_ref, fc2_ref, b2_ref, gain_ref, proj_hbm,
    out_ref, dfc1_ref, dfc2_ref, dproj_ref, db1_ref, small_ref, gmid_hbm, gmixed_hbm,
    middle_ref, mixed_ref, proj_ref, gmixed_ref, in_sems, out_sems,
    n2t_ref, grad_ref, out_acc, dn_acc, hidden_ref, dact_ref, active_ref, dhid_ref, biases,
):
    clips, slots, rows, tile = counts
    step = pl.program_id(0)
    width = n2_ref.shape[-1]
    chunk = fc1_ref.shape[-1]
    total = clips * rows

    def live_rows(clip, size):
        slot = lax.broadcasted_iota(jnp.int32, (size, 1), 0)
        return (slot < kept_ref[clip]).astype(f32)

    def loads():
        pairs = ((middle_hbm, middle_ref), (mixed_hbm, mixed_ref), (proj_hbm, proj_ref))
        return [pltpu.make_async_copy(src, dst, in_sems.at[i]) for i, (src, dst) in enumerate(pairs)]

    def stores(clip):
        at = pl.ds(pl.multiple_of(clip * rows, rows), rows)
        pairs = ((middle_ref, gmid_hbm), (gmixed_ref, gmixed_hbm))
        return [
            pltpu.make_async_copy(src.at[at], dst.at[at], out_sems.at[clip, i]) for i, (src, dst) in enumerate(pairs)
        ]

    @pl.when(step == 0)
    def start():
        for load in loads():
            load.start()
        n2t_ref[...] = n2_ref[...].T
        first = (slots // 16) * 16
        for clip in range(clips):
            begin = clip * rows
            grad_ref[begin + first : begin + rows] = jnp.zeros((rows - first, width), bf16)
            grad_ref[begin : begin + slots] = cot_ref[clip] * live_rows(clip, slots).astype(bf16)
        all_biases = row_of(b1_ref)
        for i in range(all_biases.shape[1] // chunk):
            biases[i : i + 1] = all_biases[:, i * chunk : (i + 1) * chunk]
        out_acc[...] = jnp.zeros_like(out_acc)
        dn_acc[...] = jnp.zeros_like(dn_acc)

    bias = biases[pl.ds(step, 1), :]
    hidden_ref[...] = dot(n2_ref[...], fc1_ref[...])
    dact_ref[...] = dot(grad_ref[...], fc2_ref[...], NT)
    sums = jnp.zeros((tile, chunk), f32)
    for begin in range(0, total, tile):
        at = slice(begin, begin + tile)
        hidden = hidden_ref[at] + bias
        cdf = 0.5 * (1.0 + lax.erf(hidden * (0.5 ** 0.5)))
        active_ref[at] = (hidden * cdf).astype(bf16)
        slope = cdf + hidden * (jnp.exp(-0.5 * hidden * hidden) * (1.0 / math.sqrt(2.0 * math.pi)))
        dhid = (dact_ref[at] * slope).astype(bf16)
        dhid_ref[at] = dhid
        sums = sums + dhid.astype(f32)
    db1_ref[...] = column_sums(sums)
    active = active_ref[...]
    dhid = dhid_ref[...]
    out_acc[...] += dot(active, fc2_ref[...])
    dn_acc[...] += dot(dhid, fc1_ref[...], NT)
    dfc1_ref[0] = dot(n2t_ref[...], dhid).astype(bf16)
    dfc2 = dot(active, grad_ref[...], TN).astype(bf16)
    half = width // 2
    dfc2_ref[0] = dfc2[:, :half]
    dfc2_ref[1] = dfc2[:, half:]

    @pl.when(step == pl.num_programs(0) - 1)
    def finish():
        for load in loads():
            load.wait()
        gain = row_of(gain_ref)
        bias2 = row_of(b2_ref)
        small_ref[...] = jnp.zeros_like(small_ref)

        def finish_clip(clip, carry):
            at = pl.ds(pl.multiple_of(clip * rows, rows), rows)
            middle = middle_ref[at]
            layer = middle + (out_acc[at] + bias2)
            out_ref[clip] = (live_rows(clip, slots) * layer[:slots]).astype(bf16)
            unit, inverse = center_scale(middle)
            grad = dn_acc[at]
            out_grad = grad_ref[at].astype(f32)
            gmid = out_grad + norm_back(unit, inverse, gain, grad)
            middle_ref[at] = gmid
            low = gmid.astype(bf16)
            dhid_ref[at, :width] = low
            gmixed_ref[at] = dot(low, proj_ref[...], NT).astype(bf16)
            small_ref[0:1] += column_sums(grad * unit)
            small_ref[1:2] += column_sums(grad)
            small_ref[2:3] += column_sums(out_grad)
            small_ref[3:4] += column_sums(low.astype(f32))
            for store in stores(clip):
                store.start()
            return carry

        lax.fori_loop(0, clips, finish_clip, 0)
        dproj = dot(mixed_ref[...], dhid_ref[:, :width], TN).astype(bf16)
        dproj_ref[0] = dproj[:, :half]
        dproj_ref[1] = dproj[:, half:]
        for clip in range(clips):
            for store in stores(clip):
                store.wait()


def mlp(kept, n2, middle, cot, mixed, fc1, b1, fc2, b2, gain, proj, rows):
    clips, slots, _ = cot.shape
    total, width = n2.shape
    hidden = fc1.shape[1]
    chunk = 768
    steps = hidden // chunk
    half = steps // 2
    tile = 16
    whole = lambda a: pl.BlockSpec(a.shape, lambda j: (0,) * a.ndim, pipeline_mode=one)
    anywhere = pl.BlockSpec(memory_space=pl.ANY)
    one = pl.Buffered(buffer_count=1)
    big = pl.BlockSpec((total, width), lambda j: (0, 0), pipeline_mode=one)
    return pl.pallas_call(
        functools.partial(mlp_kernel, (clips, slots, rows, tile)),
        grid=(steps,),
        in_specs=[
            pl.BlockSpec(memory_space=pltpu.SMEM),
            big, anywhere, whole(cot), anywhere,
            pl.BlockSpec((width, chunk), lambda j: (0, j)),
            whole(b1),
            pl.BlockSpec((chunk, width), lambda j: (j, 0)),
            whole(b2), whole(gain), anywhere,
        ],
        out_specs=[
            full((clips, slots, width)),
            pl.BlockSpec((1, width, chunk), lambda j: (j // half, 0, j % half)),
            pl.BlockSpec((2, chunk, width // 2), lambda j: (0, j, 0)),
            full((2, width, width // 2)),
            pl.BlockSpec((1, chunk), lambda j: (0, j)),
            full((8, width)),
            anywhere,
            anywhere,
        ],
        out_shape=[
            jax.ShapeDtypeStruct((clips, slots, width), bf16),
            jax.ShapeDtypeStruct((2, width, hidden // 2), bf16),
            jax.ShapeDtypeStruct((2, hidden, width // 2), bf16),
            jax.ShapeDtypeStruct((2, width, width // 2), bf16),
            jax.ShapeDtypeStruct((1, hidden), f32),
            jax.ShapeDtypeStruct((8, width), f32),
            jax.ShapeDtypeStruct((total, width), f32),
            jax.ShapeDtypeStruct((total, width), bf16),
        ],
        scratch_shapes=[
            pltpu.VMEM((total, width), f32),
            pltpu.VMEM((total, width), bf16),
            pltpu.VMEM((width, width), bf16),
            pltpu.VMEM((total, width), bf16),
            pltpu.SemaphoreType.DMA((3,)),
            pltpu.SemaphoreType.DMA((clips, 2)),
            pltpu.VMEM((width, total), bf16),
            pltpu.VMEM((total, width), bf16),
            pltpu.VMEM((total, width), f32),
            pltpu.VMEM((total, width), f32),
            pltpu.VMEM((total, chunk), f32),
            pltpu.VMEM((total, chunk), f32),
            pltpu.VMEM((total, chunk), bf16),
            pltpu.VMEM((total, chunk), bf16),
            pltpu.VMEM((8, chunk), f32),
        ],
        compiler_params=params(),
        cost_estimate=pl.CostEstimate(
            flops=12 * total * width * hidden, bytes_accessed=40_000_000, transcendentals=2 * total * hidden
        ),
        name="mlp",
    )(kept, n2, middle, cot, mixed, fc1, b1, fc2, b2, gain, proj)


def sum_arrays(width, hidden, clip_size):
    rows = width // clip_size
    tall = hidden // clip_size
    first, second = (0, 1, 2), (1, 0, 2)
    chunks = [("qkv", i, rows // 2, width // 2, order) for i, order in enumerate(QKV_ORDERS)]
    return [
        ("fc1", 0, rows, hidden // 4, first),
        ("fc2", 0, tall // 2, width // 2, second),
        ("fc1", hidden // 4, rows, hidden // 4, first),
        ("fc2", tall // 2, tall // 2, width // 2, second),
        ("proj", 0, rows, width // 2, PROJ_ORDER),
    ] + chunks


PROJ_ORDER = (1, 0, 2)
QKV_ORDERS = ((1, 0, 2), (1, 0, 2), (1, 0, 2))
SUM_STEPS = {
    2: [("end", 0, 0), ("start", 0, 1), ("end", 1, 0), ("start", 1, 1)],
    3: [("end", 2, 0)],
    4: [("end", 3, 0), ("end", 4, 0)],
    5: [("start", 2, 1), ("start", 3, 1)],
    7: [("end", 0, 1), ("end", 1, 1)],
    9: [("start", 0, 2), ("start", 1, 2)],
    10: [("start", 4, 1)],
    11: [("end", 2, 1), ("end", 3, 1), ("start", 3, 2)],
    12: [("start", 2, 2)],
    13: [("end", 0, 2), ("start", 0, 3), ("end", 1, 2)],
    15: [("end", 3, 2), ("start", 1, 3), ("end", 4, 1), ("start", 4, 2)],
    16: [("end", 2, 2), ("start", 2, 3)],
    17: [("end", 0, 3), ("start", 0, 4), ("end", 4, 2)],
    18: [("start", 3, 3)],
    19: [("end", 5, 0), ("start", 5, 1), ("end", 1, 3), ("start", 1, 4)],
    20: [("end", 0, 4), ("start", 0, 5), ("start", 4, 3)],
    21: [("end", 0, 5), ("end", 2, 3), ("start", 2, 4)],
    22: [("end", 6, 0), ("start", 6, 1), ("end", 1, 4), ("start", 1, 5)],
    23: [("end", 5, 1), ("start", 5, 2), ("end", 6, 1), ("start", 6, 2), ("end", 7, 0),
        ("start", 7, 1), ("end", 1, 5), ("end", 2, 4), ("start", 2, 5), ("end", 3, 3),
        ("start", 3, 4), ("end", 4, 3), ("start", 4, 4)],
    24: [("end", 2, 5)],
    25: [("end", 5, 2), ("start", 5, 3), ("vec", 0, 0), ("end", 6, 2), ("start", 6, 3), ("end", 7, 1),
        ("start", 7, 2), ("vec", 1, 0), ("input", 2, 0), ("end", 7, 2), ("start", 7, 3),
        ("end", 6, 3), ("start", 6, 4), ("end", 5, 3), ("start", 5, 4), ("end", 3, 4),
        ("start", 3, 5), ("vec", 2, 0), ("end", 4, 4), ("start", 4, 5), ("end", 3, 5), ("end", 6, 4),
        ("start", 6, 5), ("end", 4, 5), ("end", 5, 4), ("start", 5, 5), ("end", 7, 3),
        ("start", 7, 4), ("end", 6, 5), ("end", 5, 5), ("vec", 3, 0), ("end", 7, 4), ("start", 7, 5),
        ("end", 7, 5), ("vec", 4, 0)],
}


def backward_kernel(
    meta,
    q_ref, k_ref, v_ref, mask_ref, part_ref, lse_ref, normed_ref, weight_ref, near_ref, far_ref,
    tok_ref, gmid_ref, gain_ref,
    small_ref, db1_ref, gmixed_ref, dfc1_ref, dfc2_ref, dproj_ref,
    gtok_ref, fc1_out, fc2_out, proj_out, qkv_out, vec_out,
    *scratch,
):
    clips, slots, rows, bits, pairs, arrays = meta
    width = weight_ref.shape[0]
    half = width // 2
    lanes = 2 * DH
    step = pl.program_id(0)
    places = step_places(clips, pairs)
    mesh_id = pl.DeviceIdType.MESH
    count = len(arrays)

    scratch = list(scratch)
    take = lambda n: [scratch.pop(0) for _ in range(n)]
    (grad_all, packed, kv_acc, kv_send, kv_got, acc, dn_send, dn_got, dw_acc, bias_acc, vec_sum, vec_got) = take(12)
    own_bufs = dict(zip(("fc1", "fc2", "proj"), take(3)))
    dw_low = scratch.pop(0)
    stage_bufs = [take(bits + 1) for _ in arrays]
    vert_bufs = take(5)
    full_bufs = take(count)
    (grad_sem, grad_out, grad_in, kv_out, kv_in, dn_out, dn_in, sum_out, sum_in, own_sem, vec_out_sem, vec_in_sem) = take(12)

    core, vert, core_dev, vert_dev = freq_places()
    place = lax.axis_index("clip")
    bit_at = [(place // 2 ** b) % 2 for b in range(bits)]
    clip_dev = [{"clip": place + (1 - 2 * bit_at[b]) * 2 ** b} for b in range(bits)]

    def remote(src, dst, send, recv, device):
        return pltpu.make_async_remote_copy(
            src_ref=src, dst_ref=dst, send_sem=send, recv_sem=recv, device_id=device, device_id_type=mesh_id
        )

    def grad_own(clip):
        src = gmixed_ref.at[clip, :, lane_slice(vert * half, half)]
        return pltpu.make_async_copy(src, grad_all.at[0, clip], grad_sem.at[clip])

    def grad_vert(clip):
        src = gmixed_ref.at[clip, :, lane_slice((1 - vert) * half, half)]
        return remote(src, grad_all.at[1, clip], grad_out.at[clip], grad_in.at[clip], vert_dev)

    def kv_copy(clip, pair):
        return remote(
            kv_send.at[pair], kv_got.at[clip, pair], kv_out.at[clip, pair], kv_in.at[clip, pair], core_dev
        )

    def dn_copy(clip):
        return remote(dn_send.at[clip], dn_got.at[clip], dn_out.at[clip], dn_in.at[clip], vert_dev)

    every = (slice(None),) * bits

    def piece(a, who):
        name, at, r, width_a, _ = arrays[a]
        if name == "fc1":
            return dfc1_ref.at[(who,) + every + (slice(None), pl.ds(at, width_a))]
        if name == "fc2":
            return dfc2_ref.at[(who,) + every + (pl.ds(at, r), slice(None))]
        if name == "proj":
            return dproj_ref.at[who]
        return dw_low.at[at, who]

    def chosen(a, stage, index_of):
        order = arrays[a][4]
        left = [b for b in range(bits)[::-1] if b not in order[: stage - 1]]
        bit = order[stage - 1]
        at = (slice(None),) * left.index(bit) + (index_of(bit),)
        return stage_bufs[a][stage - 1].at[at]

    def stage_copy(a, stage):
        sems = (sum_out.at[a, stage], sum_in.at[a, stage])
        full, packed_array = full_bufs[a], arrays[a][0] == "qkv"
        if stage == 0:
            return remote(piece(a, 1 - core), stage_bufs[a][0], *sems, core_dev)
        if stage <= bits:
            src = chosen(a, stage, lambda bit: 1 - bit_at[bit])
            return remote(src, stage_bufs[a][stage], *sems, clip_dev[arrays[a][4][stage - 1]])
        if stage == bits + 1:
            dst = full.at[core, vert] if packed_array else vert_bufs[a]
            return remote(stage_bufs[a][bits], dst, *sems, vert_dev)
        return remote(full.at[core], full.at[core], *sems, core_dev)

    def own_copy(a):
        return pltpu.make_async_copy(piece(a, core), own_bufs[arrays[a][0]], own_sem.at[a])

    def add_blocks(dst, src, lead):
        if lead == 0:
            dst[...] = dst[...] + src[...]
            return

        def add_one(i, carry):
            at = tuple((i // 2 ** (lead - 1 - j)) % 2 for j in range(lead))
            dst[at] = dst[at] + src[at]
            return carry

        lax.fori_loop(0, 2 ** lead, add_one, 0)

    def stage_end(a, stage):
        name = arrays[a][0]
        stage_copy(a, stage).wait_recv()
        if stage == 0:
            if name == "qkv":
                add_blocks(stage_bufs[a][0], dw_low.at[arrays[a][1], core], bits)
            else:
                own_copy(a).wait()
                add_blocks(stage_bufs[a][0], own_bufs[name], bits)
                if a + 2 < 4:
                    own_copy(a + 2).start()
        elif stage <= bits:
            add_blocks(stage_bufs[a][stage], chosen(a, stage, lambda bit: bit_at[bit]), bits - stage)
            if stage == bits and name == "qkv":
                full_bufs[a][core, vert] = stage_bufs[a][bits][...]
        elif stage == bits + 1 and name != "qkv":
            full_bufs[a][core] = stage_bufs[a][bits][...] + vert_bufs[a][...]

    def vec_copy(hop):
        device = ([core_dev] + clip_dev + [vert_dev])[hop]
        return remote(vec_sum.at[hop], vec_got.at[hop], vec_out_sem.at[hop], vec_in_sem.at[hop], device)

    def vec_end(hop):
        vec_copy(hop).wait_recv()
        vec_sum[hop + 1] = vec_sum[hop] + vec_got[hop]
        if hop < bits + 1:
            vec_copy(hop + 1).start()

    def perform(action):
        kind, a, stage = action
        if kind == "vec":
            vec_end(a)
        elif kind == "start":
            stage_copy(a, stage).start()
        else:
            stage_end(a, stage)

    @pl.when(step == 0)
    def enter():
        barrier = pltpu.get_barrier_semaphore()
        for clip in range(clips):
            grad_own(clip).start()
        for device in [core_dev, vert_dev] + clip_dev:
            pl.semaphore_signal(barrier, inc=1, device_id=device, device_id_type=mesh_id)
        pl.semaphore_wait(barrier, 2 + bits)
        for clip in range(clips):
            grad_vert(clip).start()
        for a in range(5):
            stage_copy(a, 0).start()
        for a in (0, 1, 4):
            own_copy(a).start()
        vec_sum[0] = jnp.zeros_like(vec_sum[0])
        bias_acc[...] = jnp.zeros_like(bias_acc)
        dw_acc[...] = jnp.zeros_like(dw_acc)
        vec_sum[0, 4:8] = small_ref[0:4]
        for i in range(db1_ref.shape[1] // width):
            vec_sum[0, 8 + i : 9 + i] = db1_ref[0:1, i * width : (i + 1) * width]

    for at in sorted(SUM_STEPS):
        if at < places["end"]:
            @pl.when(step == at)
            def run(at=at):
                for action in SUM_STEPS[at]:
                    perform(action)

    def attend():
        clip, slot, pair = attention_unit(step, places, clips, pairs)

        @pl.when((pair == 0) & (slot == 0))
        def own_grads():
            grad_own(clip).wait()

        @pl.when((pair == 0) & (slot == 1))
        def vert_grads():
            grad_vert(clip).wait_recv()

        query = q_ref[0]
        keys = k_ref[0]
        values = v_ref[0]
        grad = grad_all[slot, clip, :, lane_slice(pair * lanes, lanes)]
        live = mask_ref[0] > 0.5
        product = grad.astype(f32) * part_ref[0].astype(f32)
        dqs, dk, dv = [], None, None
        for head in range(2):
            own_query = only(query, head)
            own_grad = only(grad, head)
            scores = jnp.where(live, dot(own_query, keys, NT), MASKED)
            probs = jnp.exp(scores - lse_ref[0, :, head * DH : head * DH + 1])
            delta = jnp.sum(only(product, head), axis=1, keepdims=True)
            dscores = (probs * (dot(own_grad, values, NT) - delta)).astype(bf16)
            dqs.append(dot(dscores, keys))
            more_k = dot(dscores, own_query, TN)
            more_v = dot(probs.astype(bf16), own_grad, TN)
            dk = more_k if dk is None else dk + more_k
            dv = more_v if dv is None else dv + more_v
        first = own_lanes(dqs[0].shape, 0)
        dq = (jnp.where(first, dqs[0], dqs[1]) * DH ** -0.5).astype(bf16)
        at = pl.ds(pl.multiple_of(slot * rows, rows), rows)
        packed[clip, at, lane_slice(3 * pair * lanes, lanes)] = dq

        @pl.when(slot == 0)
        def keep():
            kv_acc[pair, 0] = dk
            kv_acc[pair, 1] = dv

        @pl.when(slot == 1)
        def send():
            @pl.when(clip > 0)
            def free():
                kv_copy(clip - 1, pair).wait_send()

            for part, value in enumerate((dk, dv)):
                low = (kv_acc[pair, part] + value).astype(bf16)
                packed[clip, :, lane_slice((3 * pair + part + 1) * lanes, lanes)] = low[: 2 * rows]
                kv_send[pair, part] = low[2 * rows :]
            kv_copy(clip, pair).start()

    is_attention = step < places["projections"][-1]
    for at in places["pauses"]:
        is_attention = is_attention & (step != at)
    pl.when(is_attention)(attend)

    def take_pair(clip, pair):
        kv_copy(clip, pair).wait_recv()
        for part in range(2):
            at = lane_slice((3 * pair + part + 1) * lanes, lanes)
            packed[clip, :, at] = packed[clip, :, at] + kv_got[clip, pair, part]
        at = lane_slice(pair * lanes, lanes)
        for row, part in ((0, 0), (1, 2)):
            value = packed[clip, :, lane_slice((3 * pair + part) * lanes, lanes)]
            bias_acc[row : row + 1, at] += column_sums(value.astype(f32))

    def norm_sums(clip, back):
        near, _ = center_scale(near_ref[0].astype(f32))
        far, _ = center_scale(far_ref[0].astype(f32))
        vec_sum[0, 0:1] += column_sums(back[:slots] * near) + column_sums(back[rows:] * far)
        vec_sum[0, 1:2] += column_sums(back)

    def give_back(clip, back):
        acc[clip] = back[:rows]
        dn_send[clip] = back[rows:].astype(bf16)
        dn_copy(clip).start()

    def last_chunk(pair):
        at = lane_slice(3 * pair * lanes, 3 * lanes)
        more = dot(normed_ref[0], packed[clips - 1, :, at], TN)
        low = (dw_acc[:, at] + more).astype(bf16)
        r = arrays[5][2]
        for block in range(2 ** bits):
            index = tuple((block >> b) & 1 for b in range(bits)[::-1])
            for who in range(2):
                start = (2 * block + who) * r
                dw_low[(pair, who) + index] = low[start : start + r]

    early_steps = places["projections"][:-1]
    early = functools.reduce(jnp.logical_or, [step == at for at in early_steps])

    @pl.when(early)
    def projections():
        clip = sum((step > at).astype(jnp.int32) for at in early_steps)

        def take_one(pair, carry):
            take_pair(clip, pair)
            return carry

        lax.fori_loop(0, pairs, take_one, 0)
        grads = packed[clip]
        back = dot(grads, weight_ref[...], NT)
        give_back(clip, back)
        dw_acc[...] += dot(normed_ref[0], grads, TN)
        norm_sums(clip, back)

    chunk_steps = places["chunks"]

    @pl.when(functools.reduce(jnp.logical_or, [step == at for at in chunk_steps]))
    def chunk():
        pair = sum((step > at).astype(jnp.int32) for at in chunk_steps)
        take_pair(clips - 1, pair)
        last_chunk(pair)

    for pair in range(pairs - 1):
        @pl.when(step == chunk_steps[pair])
        def send_chunk(pair=pair):
            stage_copy(5 + pair, 0).start()

    @pl.when(step == places["projections"][-1])
    def last_projections():
        clip = clips - 1
        before = 3 * (pairs - 1) * lanes
        back = dot(packed[clip, :, :before], weight_ref[:, :before], NT)
        take_pair(clip, pairs - 1)
        last_chunk(pairs - 1)
        stage_copy(4 + pairs, 0).start()
        back = back + dot(packed[clip, :, before:], weight_ref[:, before:], NT)
        give_back(clip, back)
        norm_sums(clip, back)
        mine = lane_slice(vert * half, half)
        vec_sum[0, 2:3, mine] = bias_acc[0:1]
        vec_sum[0, 3:4, mine] = bias_acc[1:2]
        vec_copy(0).start()

    def inputs(clip):
        dn_copy(clip).wait_recv()
        grad = acc[clip] + dn_got[clip].astype(f32)
        unit, inverse = center_scale(tok_ref[0].astype(f32))
        result = gmid_ref[0][:slots] + norm_back(unit, inverse, row_of(gain_ref), grad[:slots])
        gtok_ref[0] = result

    @pl.when((step >= places["inputs"]) & (step < places["end"]))
    def early_inputs():
        inputs(step - places["inputs"])

    @pl.when(step == places["end"])
    def finish():
        for kind, a, stage in SUM_STEPS[places["end"]]:
            if kind == "input":
                inputs(clips - 1)
            else:
                perform((kind, a, stage))
        for a, (name, at, r, width_a, _) in enumerate(arrays):
            for who in range(2):
                full = full_bufs[a]
                if name == "fc1":
                    start = who * fc1_out.shape[1] // 2 + at
                    fc1_out[:, start : start + width_a] = full[who]
                elif name == "fc2":
                    fc2_out[at : at + r, who * width_a : (who + 1) * width_a] = full[who]
                elif name == "proj":
                    proj_out[:, who * width_a : (who + 1) * width_a] = full[who]
                else:
                    for side in range(2):
                        for part in range(3):
                            to = part * width + side * half + at * lanes
                            value = full[who, side, :, part * lanes : (part + 1) * lanes]
                            qkv_out[who * r : (who + 1) * r, to : to + lanes] = value
        vec_out[...] = vec_sum[bits + 2]
        for a in range(count):
            for stage in range(bits + 3):
                stage_copy(a, stage).wait_send()
        for clip in range(clips):
            grad_vert(clip).wait_send()
            dn_copy(clip).wait_send()
        for pair in range(pairs):
            kv_copy(clips - 1, pair).wait_send()
        for hop in range(bits + 2):
            vec_copy(hop).wait_send()


def step_places(clips, pairs):
    of_clip = 2 * pairs
    projections = [of_clip * (c + 1) + 2 + c for c in range(clips - 1)]
    begin = of_clip * (clips - 1) + clips - 1
    chunks = [begin + 2 * (pair + 1) + 1 + pair for pair in range(pairs - 1)]
    projections.append(begin + of_clip + pairs - 1)
    inputs = projections[-1] + 1
    pauses = projections[:-1] + chunks
    return {"projections": projections, "chunks": chunks, "pauses": pauses, "inputs": inputs, "end": inputs + clips - 1}


def attention_unit(step, places, clips, pairs):
    index = step
    for at in places["pauses"]:
        index = index - (step > at).astype(jnp.int32)
    index = jnp.minimum(index, 2 * clips * pairs - 1)
    clip = index // (2 * pairs)
    inside = index % (2 * pairs)
    last = clip == clips - 1
    return clip, jnp.where(last, inside % 2, inside // pairs), jnp.where(last, inside // 2, inside % pairs)


def backward(q, k, v, mask, part, lse, normed, weight_half, tokens, far, gmid, gain, small, db1, gmixed,
             dfc1, dfc2, dproj, clip_size):
    clips, slots, width = tokens.shape
    rows = gmid.shape[1]
    half = width // 2
    keys = k.shape[1]
    pairs = HEADS // 4
    lanes = 2 * DH
    bits = clip_size.bit_length() - 1
    hidden = db1.shape[1]
    arrays = sum_arrays(width, hidden, clip_size)
    places = step_places(clips, pairs)
    one = pl.Buffered(buffer_count=1)

    def of_pair(s):
        return attention_unit(s, places, clips, pairs)

    def of_keys(s):
        clip, _, pair = of_pair(s)
        return clip, 0, pair

    def of_projection(s):
        index = s * 0
        for at in places["projections"][:-1]:
            index = index + (s > at).astype(jnp.int32)
        return index, 0, 0

    def of_clip(s):
        return jnp.clip(s - places["inputs"], 0, clips - 1), 0, 0

    fixed = lambda shape: pl.BlockSpec(shape, lambda s: (0,) * len(shape), pipeline_mode=one)
    tok_pair = pl.BlockSpec((1, rows, lanes), of_pair)
    key_pair = pl.BlockSpec((1, keys, lanes), of_keys)
    anywhere = pl.BlockSpec(memory_space=pl.ANY)
    blocks = (2,) * bits
    r_fc1, r_fc2 = width // clip_size, hidden // clip_size
    dfc1 = dfc1.reshape((2,) + blocks + (r_fc1, hidden // 2))
    dfc2 = dfc2.reshape((2,) + blocks + (r_fc2, half))
    dproj = dproj.reshape((2,) + blocks + (r_fc1, half))
    vmem = lambda *shape: pltpu.VMEM(shape, bf16)
    wide = lambda *shape: pltpu.VMEM(shape, f32)
    scratch = [
        vmem(2, clips, rows, half),
        vmem(clips, 2 * rows, 3 * half),
        wide(pairs, 2, keys, lanes),
        vmem(pairs, 2, 2 * rows, lanes),
        vmem(clips, pairs, 2, 2 * rows, lanes),
        wide(clips, rows, width),
        vmem(clips, rows, width),
        vmem(clips, rows, width),
        wide(width, 3 * half),
        wide(8, half),
        wide(bits + 3, 16, width),
        wide(bits + 2, 16, width),
        vmem(*blocks, r_fc1, hidden // 4),
        vmem(*blocks, r_fc2 // 2, half),
        vmem(*blocks, r_fc1, half),
    ]
    scratch.append(vmem(pairs, 2, *blocks, r_fc1 // 2, half))
    for _, _, r, w, _ in arrays:
        scratch += [vmem(*((2,) * (bits - stage)), r, w) for stage in range(bits + 1)]
    scratch += [vmem(r, w) for name, _, r, w, _ in arrays if name != "qkv"]
    scratch += [vmem(2, 2, r, w) if name == "qkv" else vmem(2, r, w) for name, _, r, w, _ in arrays]
    dma = lambda *shape: pltpu.SemaphoreType.DMA(shape)
    count = len(arrays)
    scratch += [
        dma(clips), dma(clips), dma(clips), dma(clips, pairs), dma(clips, pairs), dma(clips), dma(clips),
        dma(count, bits + 3), dma(count, bits + 3), dma(count), dma(bits + 2), dma(bits + 2),
    ]
    shape = jax.ShapeDtypeStruct
    return pl.pallas_call(
        functools.partial(backward_kernel, (clips, slots, rows, bits, pairs, arrays)),
        grid=(places["end"] + 1,),
        in_specs=[
            tok_pair, key_pair, key_pair,
            pl.BlockSpec((1, 1, keys), lambda s: (of_pair(s)[0], 0, 0)),
            tok_pair, tok_pair,
            pl.BlockSpec((1, 2 * rows, width), of_projection),
            fixed(weight_half.shape),
            pl.BlockSpec((1, slots, width), of_projection),
            pl.BlockSpec((1, rows, width), of_projection),
            pl.BlockSpec((1, slots, width), of_clip),
            pl.BlockSpec((1, rows, width), of_clip),
            fixed((width,)), fixed((8, width)), fixed((1, hidden)),
            anywhere, anywhere, anywhere, anywhere,
        ],
        out_specs=[
            pl.BlockSpec((1, slots, width), of_clip),
            fixed((r_fc1, hidden)), fixed((r_fc2, width)), fixed((r_fc1, width)),
            fixed((r_fc1, 3 * width)), fixed((16, width)),
        ],
        out_shape=[
            shape((clips, slots, width), f32),
            shape((r_fc1, hidden), bf16),
            shape((r_fc2, width), bf16),
            shape((r_fc1, width), bf16),
            shape((r_fc1, 3 * width), bf16),
            shape((16, width), f32),
        ],
        scratch_shapes=scratch,
        compiler_params=params(collective_id=1, has_side_effects=True),
        cost_estimate=pl.CostEstimate(
            flops=2 * clips * rows * (5 * keys * width + 6 * width * width),
            bytes_accessed=60_000_000,
            transcendentals=clips * rows * keys * HEADS,
        ),
        name="backward",
    )(q, k, v, mask, part, lse, normed, weight_half, tokens, far, tokens, gmid, gain, small, db1, gmixed, dfc1, dfc2, dproj)


def outputs_kernel(fc1, fc2, proj, qkv, vec, gtok, fc1_out, fc2_out, proj_out, qkv_out, gtok_out, db1_out, *outs):
    gtok_out[...] = gtok[...]
    for src, dst in ((fc1, fc1_out), (fc2, fc2_out), (proj, proj_out), (qkv, qkv_out)):
        dst[...] = src[...].astype(f32)

    @pl.when(pl.program_id(0) == 0)
    def others():
        width = vec.shape[1]
        for i, dst in enumerate(outs):
            dst[...] = vec[i : i + 1].reshape(width)
        tall = db1_out.shape[0] // width
        db1_out[...] = jnp.concatenate([vec[8 + i : 9 + i] for i in range(tall)], axis=1).reshape(db1_out.shape[0])


def final_outputs(low_fc1, low_fc2, low_proj, low_qkv, summed, gtok, hidden):
    width = summed.shape[1]
    steps = gtok.shape[0]
    one = pl.Buffered(buffer_count=1)
    fixed = lambda shape: pl.BlockSpec(shape, lambda c: (0,) * len(shape), pipeline_mode=one)
    by_clip = pl.BlockSpec((1,) + gtok.shape[1:], lambda c: (c, 0, 0))
    shape = jax.ShapeDtypeStruct
    lows = (low_fc1, low_fc2, low_proj, low_qkv)

    def by_rows(a):
        if a.shape[0] % (16 * steps):
            return fixed(a.shape)
        return pl.BlockSpec((a.shape[0] // steps, a.shape[1]), lambda c: (c, 0))

    return pl.pallas_call(
        outputs_kernel,
        grid=(steps,),
        in_specs=[by_rows(a) for a in lows] + [fixed(summed.shape), by_clip],
        out_specs=[by_rows(a) for a in lows] + [by_clip, fixed((hidden,))] + [fixed((width,))] * 8,
        out_shape=[shape(a.shape, f32) for a in lows]
        + [shape(gtok.shape, f32), shape((hidden,), f32)]
        + [shape((width,), f32)] * 8,
        compiler_params=params(),
        name="final_outputs",
    )(*lows, summed, gtok)


def partner(kind):
    index = lax.axis_index("freq")
    if kind == "vert":
        return {"freq": (index + 2) % 4}
    return {"freq": index + 1 - 2 * (index % 2)}


def whole_forward_kernel(
    counts,
    tok_ref, qkv_ref, qb_ref, vb_ref, gain_ref, shift_ref, proj_ref, pb_ref, gain2_ref, shift2_ref,
    q_ref, k_ref, v_ref, normed_ref, mixed_ref, lse_ref, middle_ref, normed2_ref, mask_ref,
    held, send_sem, recv_sem,
):
    clips, slots, rows = counts
    clip = pl.program_id(0)
    pair = pl.program_id(1)
    width = tok_ref.shape[-1]

    def copy(kind, index):
        at = {"vert": 0, "core": 1, "diag": 2}[kind]
        return pltpu.make_async_remote_copy(
            src_ref=held.at[index, 0] if kind == "diag" else tok_ref.at[index],
            dst_ref=held.at[index, at],
            send_sem=send_sem.at[index, at],
            recv_sem=recv_sem.at[index, at],
            device_id=partner(kind),
            device_id_type=pl.DeviceIdType.MESH,
        )

    def project(slot, source):
        unit, _ = center_scale(source.astype(f32))
        normed = (unit * gain_ref[...] + shift_ref[...]).astype(bf16)
        if slot == 0:
            normed_ref[0] = normed
            query = (dot(normed, qkv_ref[:, :width]) + qb_ref[...]).astype(bf16)
            q_ref[0] = query * jnp.asarray(DH ** -0.5, bf16)
        both = dot(normed, qkv_ref[:, width:])
        k_ref[0, slot * rows : (slot + 1) * rows] = both[:, :width].astype(bf16)
        v_ref[0, slot * rows : (slot + 1) * rows] = (both[:, width:] + vb_ref[...]).astype(bf16)
        first = (slots // 16) * 16
        kept = source[first:].astype(f32)[slots - first : slots - first + 1, 0:1] + slots // 2
        lane = lax.broadcasted_iota(jnp.int32, (1, rows), 1).astype(f32)
        return (lane < kept).astype(f32)

    @pl.when((clip == 0) & (pair == 0))
    def enter():
        barrier = pltpu.get_barrier_semaphore()
        for kind in ("vert", "core"):
            pl.semaphore_signal(
                barrier, inc=1, device_id=partner(kind), device_id_type=pl.DeviceIdType.MESH
            )
        pl.semaphore_wait(barrier, 2)
        copy("vert", 0).start()
        for index in range(clips):
            copy("core", index).start()

    def pass_on(index):
        copy("vert", index).wait_recv()
        copy("diag", index).start()
        copy("vert", index).wait_send()

        @pl.when(index + 1 < clips)
        def more():
            copy("vert", index + 1).start()

    @pl.when(pair == 0)
    def project_all():
        live_own = project(0, tok_ref[clip])
        copy("core", clip).wait_recv()
        live_core = project(2, held[clip, 1])

        @pl.when(clip == 0)
        def first_pass():
            pass_on(clip)

        live_vert = project(1, held[clip, 0])
        copy("diag", clip).wait_recv()
        live_diag = project(3, held[clip, 2])
        mask_ref[0] = jnp.concatenate([live_own, live_vert, live_core, live_diag], axis=1)

    @pl.when((pair == 3) & (clip + 1 < clips))
    def next_pass():
        pass_on(clip + 1)

    lanes = pl.ds(pl.multiple_of(pair * 2 * DH, 2 * DH), 2 * DH)
    query = q_ref[0, :, lanes]
    keys = k_ref[0, :, lanes]
    values = v_ref[0, :, lanes]
    live = mask_ref[0] > 0.5
    outs, lses = [], []
    for head in range(2):
        scores = jnp.where(live, dot(only(query, head), keys, NT), MASKED)
        top = jnp.max(scores, axis=1, keepdims=True)
        exps = jnp.exp(scores - top)
        total = jnp.sum(exps, axis=1, keepdims=True)
        outs.append(dot(exps.astype(bf16), values) / total)
        lses.append(top + jnp.log(total))
    first = own_lanes(outs[0].shape, 0)
    mixed_ref[0, :, lanes] = jnp.where(first, outs[0], outs[1]).astype(bf16)
    lse_ref[0, :, lanes] = jnp.where(first, lses[0], lses[1])

    @pl.when(pair == pl.num_programs(1) - 1)
    def finish():
        middle = tok_ref[clip].astype(f32) + (dot(mixed_ref[0], proj_ref[...]) + pb_ref[...])
        middle_ref[0] = middle
        unit, _ = center_scale(middle)
        normed2_ref[0] = (unit * gain2_ref[...] + shift2_ref[...]).astype(bf16)
        copy("core", clip).wait_send()
        copy("diag", clip).wait_send()


def whole_forward(tok, slots, qkv_weight, vectors, proj_weight):
    clips, rows, width = tok.shape
    keys = 4 * rows
    pairs = HEADS // 2
    query_bias, value_bias, gain, shift, proj_bias, gain2, shift2 = vectors
    one = pl.Buffered(buffer_count=1)
    row = full((1, width))
    block = lambda n: pl.BlockSpec((1, n, width), lambda c, p: (c, 0, 0))
    flops = 2 * clips * (10 * rows * width * width + 2 * rows * keys * width)
    weight = lambda w: pl.BlockSpec(w.shape, lambda c, p: (0, 0), pipeline_mode=one)
    return pl.pallas_call(
        functools.partial(whole_forward_kernel, (clips, slots, rows)),
        grid=(clips, pairs),
        in_specs=[
            pl.BlockSpec(tok.shape, lambda c, p: (0, 0, 0), pipeline_mode=one),
            weight(qkv_weight), row, row, row, row, weight(proj_weight), row, row, row,
        ],
        out_specs=[block(rows), block(keys), block(keys)] + [block(rows)] * 5
        + [pl.BlockSpec((1, 1, keys), lambda c, p: (c, 0, 0))],
        out_shape=[
            jax.ShapeDtypeStruct((clips, rows, width), bf16),
            jax.ShapeDtypeStruct((clips, keys, width), bf16),
            jax.ShapeDtypeStruct((clips, keys, width), bf16),
            jax.ShapeDtypeStruct((clips, rows, width), bf16),
            jax.ShapeDtypeStruct((clips, rows, width), bf16),
            jax.ShapeDtypeStruct((clips, rows, width), f32),
            jax.ShapeDtypeStruct((clips, rows, width), f32),
            jax.ShapeDtypeStruct((clips, rows, width), bf16),
            jax.ShapeDtypeStruct((clips, 1, keys), f32),
        ],
        scratch_shapes=[
            pltpu.VMEM((clips, 3, rows, width), bf16),
            pltpu.SemaphoreType.DMA((clips, 3)),
            pltpu.SemaphoreType.DMA((clips, 3)),
        ],
        compiler_params=params(collective_id=0, has_side_effects=True),
        cost_estimate=pl.CostEstimate(
            flops=flops, bytes_accessed=40_000_000, transcendentals=clips * rows * keys * HEADS
        ),
        name="whole_forward",
    )(tok, qkv_weight, query_bias, value_bias, gain, shift, proj_weight, proj_bias, gain2, shift2)


def attend_back_kernel(q_ref, k_ref, v_ref, mask_ref, mixed_ref, lse_ref, grad_ref,
                       dq_ref, dkeep_ref, dsend_ref):
    query = q_ref[0]
    keys = k_ref[0]
    values = v_ref[0]
    grad = grad_ref[0]
    live = mask_ref[0] > 0.5
    product = grad.astype(f32) * mixed_ref[0].astype(f32)
    dqs, dk, dv = [], None, None
    for head in range(2):
        own_query = only(query, head)
        own_grad = only(grad, head)
        scores = jnp.where(live, dot(own_query, keys, NT), MASKED)
        probs = jnp.exp(scores - lse_ref[0, :, head * DH : head * DH + 1])
        delta = jnp.sum(only(product, head), axis=1, keepdims=True)
        dscores = (probs * (dot(own_grad, values, NT) - delta)).astype(bf16)
        dqs.append(dot(dscores, keys))
        more_k = dot(dscores, own_query, TN)
        more_v = dot(probs.astype(bf16), own_grad, TN)
        dk = more_k if dk is None else dk + more_k
        dv = more_v if dv is None else dv + more_v
    first = own_lanes(dqs[0].shape, 0)
    dq_ref[0] = (jnp.where(first, dqs[0], dqs[1]) * DH ** -0.5).astype(bf16)
    half = dk.shape[0] // 2
    dkeep_ref[0, 0] = dk[:half].astype(bf16)
    dkeep_ref[1, 0] = dv[:half].astype(bf16)
    dsend_ref[0, 0] = dk[half:].astype(bf16)
    dsend_ref[1, 0] = dv[half:].astype(bf16)


def attend_back(q, k, v, mask, mixed, lse, grad, first_pair, pairs):
    clips, rows, _ = q.shape
    keys = k.shape[1]
    lanes = 2 * DH
    tok = pl.BlockSpec((1, rows, lanes), lambda c, p: (c, 0, first_pair + p))
    key = pl.BlockSpec((1, keys, lanes), lambda c, p: (c, 0, first_pair + p))
    part = pl.BlockSpec((2, 1, keys // 2, lanes), lambda c, p: (0, c, 0, p))
    return pl.pallas_call(
        attend_back_kernel,
        grid=(clips, pairs),
        in_specs=[tok, key, key, pl.BlockSpec((1, 1, keys), lambda c, p: (c, 0, 0)), tok, tok, tok],
        out_specs=[pl.BlockSpec((1, rows, lanes), lambda c, p: (c, 0, p)), part, part],
        out_shape=[
            jax.ShapeDtypeStruct((clips, rows, pairs * lanes), bf16),
            jax.ShapeDtypeStruct((2, clips, keys // 2, pairs * lanes), bf16),
            jax.ShapeDtypeStruct((2, clips, keys // 2, pairs * lanes), bf16),
        ],
        compiler_params=params(),
        cost_estimate=pl.CostEstimate(
            flops=4 * 10 * clips * rows * keys * pairs * lanes,
            bytes_accessed=clips * pairs * lanes * (keys * 10 + rows * 12),
            transcendentals=clips * rows * keys * 2 * pairs,
        ),
        name="attend_back",
    )(q, k, v, mask, mixed, lse, grad)


def weight_kernel(normed_ref, dq_ref, dk0_ref, dk1_ref, dk2_ref, out_ref, dkv_ref, sums_ref):
    part = pl.program_id(0)
    @pl.when(part == 0)
    def query():
        grad = dq_ref[...]
        out_ref[0] = dot(normed_ref[...], grad, TN).astype(bf16)
        sums_ref[0] = column_sums(grad.astype(f32))
        dkv_ref[0] = jnp.zeros_like(dkv_ref[0])

    @pl.when(part > 0)
    def other():
        grad = (dk0_ref[0].astype(f32) + dk1_ref[0].astype(f32) + dk2_ref[0].astype(f32)).astype(bf16)
        dkv_ref[0] = grad
        out_ref[0] = dot(normed_ref[...], grad, TN).astype(bf16)
        sums_ref[0] = column_sums(grad.astype(f32))


def weight_grads(normed, dq, parts):
    total, width = normed.shape
    lanes = dq.shape[1]
    before = lambda j: (jnp.maximum(j - 1, 0), 0, 0)
    part = pl.BlockSpec((1, total, lanes), before)
    return pl.pallas_call(
        weight_kernel,
        grid=(3,),
        in_specs=[full((total, width)), full((total, lanes)), part, part, part],
        out_specs=[
            pl.BlockSpec((1, width, lanes), lambda j: (j, 0, 0)),
            part,
            pl.BlockSpec((1, 1, lanes), lambda j: (j, 0, 0)),
        ],
        out_shape=[
            jax.ShapeDtypeStruct((3, width, lanes), bf16),
            jax.ShapeDtypeStruct((2, total, lanes), bf16),
            jax.ShapeDtypeStruct((3, 1, lanes), f32),
        ],
        compiler_params=params(),
        cost_estimate=pl.CostEstimate(
            flops=6 * total * width * lanes, bytes_accessed=8_000_000, transcendentals=0
        ),
        name="weight_grads",
    )(normed, dq, *parts)


def input_kernel(counts, groups, *refs):
    clips, slots, rows = counts
    dqs = refs[:groups]
    dkvs = refs[groups : 2 * groups]
    qkv_ref, tok_ref, gmid_ref, gain_ref, shift_ref, out_ref, small_ref = refs[2 * groups :]
    clip = pl.program_id(0)
    width = tok_ref.shape[-1]
    lanes = width // groups
    grad = None
    for group in range(groups):
        for part in range(3):
            rows_grad = dqs[group][0] if part == 0 else dkvs[group][part - 1]
            at = part * width + group * lanes
            more = dot(rows_grad, qkv_ref[:, at : at + lanes], NT)
            grad = more if grad is None else grad + more
    unit, inverse = center_scale(tok_ref[0].astype(f32))
    result = gmid_ref[0] + norm_back(unit, inverse, gain_ref[...], grad)
    out_ref[0] = result[:slots]

    @pl.when(clip == 0)
    def start():
        small_ref[...] = jnp.zeros_like(small_ref)

    small_ref[0:1] += column_sums(grad * unit)
    small_ref[1:2] += column_sums(grad)


def input_grads(dqs, dkvs, qkv_weight, tokens, gmid, gain, shift, slots):
    clips, rows, width = tokens.shape
    groups = len(dqs)
    lanes = width // groups
    tok = pl.BlockSpec((1, rows, width), lambda c: (c, 0, 0))
    return pl.pallas_call(
        functools.partial(input_kernel, (clips, slots, rows), groups),
        grid=(clips,),
        in_specs=[pl.BlockSpec((1, rows, lanes), lambda c: (c, 0, 0))] * groups
        + [pl.BlockSpec((2, rows, lanes), lambda c: (0, c, 0))] * groups
        + [full(qkv_weight.shape), tok, tok, full((1, width)), full((1, width))],
        out_specs=[pl.BlockSpec((1, slots, width), lambda c: (c, 0, 0)), full((8, width))],
        out_shape=[
            jax.ShapeDtypeStruct((clips, slots, width), f32),
            jax.ShapeDtypeStruct((8, width), f32),
        ],
        compiler_params=params(),
        cost_estimate=pl.CostEstimate(
            flops=6 * clips * rows * width * width, bytes_accessed=16_000_000, transcendentals=0
        ),
        name="input_grads",
    )(*dqs, *dkvs, qkv_weight, tokens, gmid, gain, shift)


def swap_bit(array, axis, size, bit):
    return lax.ppermute(array, axis, [(i, i ^ (1 << bit)) for i in range(size)])


def add_low(left, right):
    return (left.astype(f32) + right.astype(f32)).astype(bf16)


def pick(array, index, dim):
    return lax.dynamic_index_in_dim(array, index, dim, keepdims=False)


def bit_of(axis, bit):
    return (lax.axis_index(axis) >> bit) & 1


def scatter_sum(split, clip_size, order):
    core = bit_of("freq", 0)
    vert = bit_of("freq", 1)
    bits = clip_size.bit_length() - 1
    lanes = split.shape[-1]
    value = add_low(pick(split, core, 0), swap_bit(pick(split, 1 - core, 0), "freq", 4, 0))
    rows = value.shape[0] // (2 * clip_size)
    value = value.reshape((2,) * bits + (2, rows, lanes))
    left = list(range(bits))[::-1]
    for bit in order:
        at = left.index(bit)
        mine = bit_of("clip", bit)
        value = add_low(
            pick(value, mine, at), swap_bit(pick(value, 1 - mine, at), "clip", clip_size, bit)
        )
        left.remove(bit)
    return add_low(pick(value, vert, 0), swap_bit(pick(value, 1 - vert, 0), "freq", 4, 1))


def gather_low(part):
    core = bit_of("freq", 0)
    vert = bit_of("freq", 1)
    other = swap_bit(part, "freq", 4, 1)
    tall = jnp.where(vert == 0, jnp.concatenate([part, other]), jnp.concatenate([other, part]))
    side = swap_bit(tall, "freq", 4, 0)
    return jnp.where(
        core == 0,
        jnp.concatenate([tall, side], axis=1),
        jnp.concatenate([side, tall], axis=1),
    ).astype(f32)


def total_sum(array, clip_size):
    for bit in range(2):
        array = array + swap_bit(array, "freq", 4, bit)
    for bit in range(clip_size.bit_length() - 1):
        array = array + swap_bit(array, "clip", clip_size, bit)
    return array


def on_device_plain(
    clip_size, tokens, kept_counts, attn_gain, attn_shift, qkv_weight, query_bias, value_bias,
    proj_weight, proj_bias, mlp_gain, mlp_shift, fc1_weight, fc1_bias, fc2_weight, fc2_bias, cotangent,
):
    clips, slots, width = tokens.shape
    rows = -(-slots // 16) * 16
    total = clips * rows
    bits = clip_size.bit_length() - 1
    forward_order = list(range(bits))
    second_order = forward_order[1:2] + forward_order[:1] + forward_order[2:]
    vec = lambda v: v.astype(f32)[None, :]
    kept = (kept_counts - slots // 2).astype(bf16)
    tok = jnp.concatenate(
        [tokens, jnp.broadcast_to(kept[:, :, None], (clips, rows - slots, width))], axis=1
    )
    vectors = [vec(v) for v in (query_bias, value_bias, attn_gain, attn_shift, proj_bias, mlp_gain, mlp_shift)]
    q, k, v, normed, mixed, lse, middle, normed2, mask = whole_forward(
        tok, slots, qkv_weight, vectors, proj_weight
    )
    flat = lambda a: a.reshape(total, width)
    layer_out, dfc1, dfc2, dproj, db1, small2, gmid, gmixed = mlp(
        kept_counts.reshape(clips), flat(normed2), flat(middle), cotangent, flat(mixed), fc1_weight, fc1_bias,
        fc2_weight, fc2_bias, mlp_gain, proj_weight, rows,
    )
    early = total_sum(jnp.concatenate([small2[:4].reshape(-1), db1.reshape(-1)])[None, :], clip_size)[0]
    sum_fc1 = gather_low(scatter_sum(dfc1, clip_size, forward_order))
    sum_fc2 = gather_low(scatter_sum(dfc2, clip_size, second_order))
    sum_proj = gather_low(scatter_sum(dproj, clip_size, forward_order))

    groups = 3
    pairs = HEADS // 2 // groups
    lanes = pairs * 2 * DH
    gmixed = gmixed.reshape(clips, rows, width)
    dqs, dkvs, sums, sharded = [], [], [], []
    for group in range(groups):
        dq, keep, send = attend_back(q, k, v, mask, mixed, lse, gmixed, group * pairs, pairs)
        got = swap_bit(send, "freq", 4, 0)
        across = swap_bit(add_low(keep[:, :, rows:], got[:, :, rows:]), "freq", 4, 1)
        parts = [a.reshape(2, total, lanes) for a in (keep[:, :, :rows], got[:, :, :rows], across)]
        dw, dkv, colsum = weight_grads(flat(normed), dq.reshape(total, lanes), parts)
        half = lanes // 2
        split = jnp.stack(
            [
                jnp.concatenate([dw[i, :, s * half : (s + 1) * half] for i in range(3)], axis=1)
                for s in range(2)
            ]
        )
        order = forward_order if group % 2 == 0 else second_order
        summed = gather_low(scatter_sum(split, clip_size, order))
        sharded.append(summed.reshape(summed.shape[0], 2, 3, half))
        dqs.append(dq)
        dkvs.append(dkv)
        sums.append(colsum)
    grad_tokens, small1 = input_grads(
        dqs, dkvs, qkv_weight, tok, gmid.reshape(clips, rows, width), vectors[2], vectors[3], slots
    )
    qkv = jnp.stack(sharded, axis=1)
    sum_qkv = qkv.transpose(0, 3, 1, 2, 4).reshape(qkv.shape[0], 3 * width)
    bias = jnp.concatenate(sums, axis=2)
    late = total_sum(
        jnp.concatenate([small1[0:1], small1[1:2], bias[0], bias[2]], axis=1), clip_size
    )[0]
    cut = lambda a, i: a[i * width : (i + 1) * width]
    return (
        layer_out, grad_tokens, cut(late, 0), cut(late, 1), sum_qkv, cut(late, 2), cut(late, 3),
        sum_proj, cut(early, 3), cut(early, 0), cut(early, 1), sum_fc1, early[4 * width :],
        sum_fc2, cut(early, 2),
    )


def on_device(
    clip_size, tokens, kept_counts, attn_gain, attn_shift, qkv_weight, query_bias, value_bias,
    proj_weight, proj_bias, mlp_gain, mlp_shift, fc1_weight, fc1_bias, fc2_weight, fc2_bias, cotangent,
):
    clips, slots, width = tokens.shape
    rows = -(-slots // 16) * 16
    if clip_size != 8 or width % (32 * clip_size):
        return on_device_plain(
            clip_size, tokens, kept_counts, attn_gain, attn_shift, qkv_weight, query_bias, value_bias,
            proj_weight, proj_bias, mlp_gain, mlp_shift, fc1_weight, fc1_bias, fc2_weight, fc2_bias, cotangent,
        )
    kept = kept_counts.reshape(clips)
    q, k, v, normed, far, weight_half, part, lse, mask, mixed, middle, normed2 = forward(
        kept, tokens, rows, qkv_weight, query_bias, value_bias, attn_gain, attn_shift,
        proj_weight, proj_bias, mlp_gain, mlp_shift,
    )
    flat = lambda a: a.reshape(clips * rows, width)
    layer_out, dfc1, dfc2, dproj, db1, small, gmid, gmixed = mlp(
        kept, flat(normed2), flat(middle), cotangent, flat(mixed), fc1_weight, fc1_bias,
        fc2_weight, fc2_bias, mlp_gain, proj_weight, rows,
    )
    by_clip = lambda a: a.reshape(clips, rows, width)
    gtok, low_fc1, low_fc2, low_proj, low_qkv, summed = backward(
        q, k, v, mask, part, lse, normed, weight_half, tokens, far, by_clip(gmid), attn_gain, small, db1,
        by_clip(gmixed), dfc1, dfc2, dproj, clip_size,
    )
    fc1, fc2, proj, qkv, grad_tokens, fc1_b, *rows_out = final_outputs(
        low_fc1, low_fc2, low_proj, low_qkv, summed, gtok, fc1_bias.shape[0]
    )
    return (
        layer_out, grad_tokens, rows_out[0], rows_out[1], qkv, rows_out[2], rows_out[3], proj, rows_out[7],
        rows_out[4], rows_out[5], fc1, fc1_b, fc2, rows_out[6],
    )


def solution(mesh):
    rows = P("clip", "freq", None)
    shard = P("clip", None)
    return jax.shard_map(
        functools.partial(on_device, mesh.shape["clip"]),
        mesh=mesh,
        in_specs=(rows, P("clip", "freq")) + (P(),) * 13 + (rows,),
        out_specs=(rows, rows, P(), P(), shard, P(), P(), shard, P(), P(), P(), shard, P(), shard, P()),
        check_vma=False,
    )
```

```python
import functools
import math

import jax
import jax.numpy as jnp
from jax import lax
from jax.experimental import pallas as pl
from jax.experimental.pallas import tpu as pltpu
from jax.sharding import PartitionSpec as P

HEADS = 12
DH = 64
EPS = 1e-06
MASKED = -1000000000.0
VMEM_BYTES = 60 * 1024 * 1024

f32 = jnp.float32
bf16 = jnp.bfloat16
NN = (((1,), (0,)), ((), ()))
NT = (((1,), (1,)), ((), ()))
TN = (((0,), (0,)), ((), ()))


def dot(left, right, dims=NN):
    return lax.dot_general(left, right, dims, preferred_element_type=f32)


def center_scale(rows):
    center = rows - jnp.mean(rows, axis=-1, keepdims=True)
    inverse = lax.rsqrt(jnp.mean(center * center, axis=-1, keepdims=True) + EPS)
    return center * inverse, inverse


def norm_back(unit, inverse, gain, grad):
    scaled = grad * gain
    return inverse * (
        scaled
        - jnp.mean(scaled, axis=-1, keepdims=True)
        - unit * jnp.mean(scaled * unit, axis=-1, keepdims=True)
    )


def column_sums(rows):
    return jnp.sum(rows, axis=0, keepdims=True)


def own_lanes(shape, head):
    lane = lax.broadcasted_iota(jnp.int32, shape, len(shape) - 1)
    return lane < DH if head == 0 else lane >= DH


def only(rows, head):
    return jnp.where(own_lanes(rows.shape, head), rows, jnp.zeros_like(rows))


def full(shape):
    return pl.BlockSpec(shape, lambda *ids: (0,) * len(shape))


def params(**more):
    return pltpu.CompilerParams(vmem_limit_bytes=VMEM_BYTES, **more)


def freq_places():
    freq = lax.axis_index("freq")
    core, vert = freq % 2, freq // 2
    return core, vert, {"freq": freq + 1 - 2 * core}, {"freq": (freq + 2) % 4}


def lane_slice(start, size):
    return pl.ds(pl.multiple_of(start, 2 * DH), size)


def row_of(ref):
    return ref[...].astype(f32).reshape(1, ref.shape[0])


def forward_kernel(
    counts,
    kept_ref, tok_ref, qkv_ref, qb_ref, vb_ref, gain_ref, shift_ref, proj_ref, pb_ref, gain2_ref, shift2_ref,
    q_out, k_out, v_out, normed_out, far_out, weight_out, part_ref, lse_ref, mask_ref, mixed_ref, middle_ref, normed2_ref,
    q_all, k_all, v_all, normed_all, weight, live_all, own, held, mix_send, mix_got, own_mix, vecs,
    tok_send, tok_recv, part_send, part_recv, out_sem, weight_sem,
):
    clips, slots, rows, pairs = counts
    clip = pl.program_id(0)
    turn = pl.program_id(1)
    slot = 1 - turn
    width = tok_ref.shape[-1]
    half = width // 2
    lanes = 2 * DH
    core, vert, core_dev, vert_dev = freq_places()
    mesh_id = pl.DeviceIdType.MESH

    def copy(kind, index):
        at = {"vert": 0, "core": 1, "diag": 2}[kind]
        return pltpu.make_async_remote_copy(
            src_ref=held.at[index, 0] if kind == "diag" else own.at[index],
            dst_ref=held.at[index, at],
            send_sem=tok_send.at[index, at],
            recv_sem=tok_recv.at[index, at],
            device_id=vert_dev if kind == "vert" else core_dev,
            device_id_type=mesh_id,
        )

    def mix_copy(index, which):
        return pltpu.make_async_remote_copy(
            src_ref=mix_send.at[index, which],
            dst_ref=mix_got.at[index, which],
            send_sem=part_send.at[index, which],
            recv_sem=part_recv.at[index, which],
            device_id=vert_dev,
            device_id_type=mesh_id,
        )

    def project(index, slot, source):
        unit, _ = center_scale(source.astype(f32))
        normed = (unit * vecs[2:3] + vecs[3:4]).astype(bf16)
        at = slice(slot * rows, (slot + 1) * rows)
        if slot < 2:
            normed_all[index, at] = normed
            query = (dot(normed, weight[:, :half]) + vecs[0:1, lane_slice(vert * half, half)]).astype(bf16)
            q_all[index, at] = query * jnp.asarray(DH ** -0.5, bf16)
        both = dot(normed, weight[:, half:])
        k_all[index, at] = both[:, :half].astype(bf16)
        v_all[index, at] = (both[:, half:] + vecs[1:2, lane_slice(vert * half, half)]).astype(bf16)
        first = (slots // 16) * 16
        kept = source[first:].astype(f32)[slots - first : slots - first + 1, 0:1] + slots // 2
        lane = lax.broadcasted_iota(jnp.int32, (1, rows), 1).astype(f32)
        live_all[index, slot] = (lane < kept).astype(f32)

    def out_copies(index):
        return [
            pltpu.make_async_copy(src.at[index], dst.at[index], out_sem.at[index, i])
            for i, (src, dst) in enumerate(
                ((q_all, q_out), (k_all, k_out), (v_all, v_out), (normed_all, normed_out))
            )
        ] + [pltpu.make_async_copy(held.at[index, 0], far_out.at[index], out_sem.at[index, 4])]

    def weight_copies():
        moves = []
        for pair in range(pairs):
            for part in range(3):
                src = weight.at[:, pl.ds(part * half + pair * lanes, lanes)]
                dst = weight_out.at[:, pl.ds((3 * pair + part) * lanes, lanes)]
                moves.append(pltpu.make_async_copy(src, dst, weight_sem.at[3 * pair + part]))
        return moves

    @pl.when((clip == 0) & (turn == 0))
    def enter():
        barrier = pltpu.get_barrier_semaphore()
        for device in (vert_dev, core_dev):
            pl.semaphore_signal(barrier, inc=1, device_id=device, device_id_type=mesh_id)
        first = (slots // 16) * 16
        for index in range(clips):
            kept = (kept_ref[index] - slots // 2).astype(f32).astype(bf16)
            own[index, first:] = jnp.broadcast_to(kept, (rows - first, width))
            own[index, :slots] = tok_ref[index]
        pl.semaphore_wait(barrier, 2)
        copy("vert", 0).start()
        for index in range(clips):
            copy("core", index).start()
        for i, ref in enumerate((qb_ref, vb_ref, gain_ref, shift_ref, pb_ref, gain2_ref, shift2_ref)):
            vecs[i : i + 1] = row_of(ref)
        for part in range(3):
            weight[:, part * half : (part + 1) * half] = qkv_ref[:, lane_slice(part * width + vert * half, half)]
        for move in weight_copies():
            move.start()

        def own_slots(index, carry):
            project(index, 0, own[index])
            return carry

        def core_slots(index, carry):
            copy("core", index).wait_recv()
            project(index, 2, held[index, 1])
            return carry

        lax.fori_loop(0, clips, own_slots, 0)
        lax.fori_loop(0, clips, core_slots, 0)
        copy("vert", 0).wait_recv()
        copy("diag", 0).start()
        copy("vert", 0).wait_send()
        if clips > 1:
            copy("vert", 1).start()

    @pl.when(turn == 0)
    def project_rest():
        project(clip, 1, held[clip, 0])
        copy("diag", clip).wait_recv()
        project(clip, 3, held[clip, 2])
        for i in range(4):
            mask_ref[0, :, i * rows : (i + 1) * rows] = live_all[clip, i]
        for move in out_copies(clip):
            move.start()

    for index in range(2, clips):
        @pl.when((turn == 1) & (clip == index - 2))
        def send_ahead(index=index):
            copy("vert", index - 1).wait_send()
            copy("vert", index).start()

    def finish(index):
        at = lane_slice(vert * half, half)
        mixed_ref[0, :, at] = own_mix[...]
        for which in range(pairs):
            mix_copy(index, which).wait_recv()
            at = lane_slice((1 - vert) * half + which * lanes, lanes)
            mixed_ref[0, :, at] = mix_got[index, which]
        middle = own[index].astype(f32) + (dot(mixed_ref[0], proj_ref[...]) + vecs[4:5])
        middle_ref[0] = middle
        unit, _ = center_scale(middle)
        normed2_ref[0] = (unit * vecs[5:6] + vecs[6:7]).astype(bf16)
        copy("core", index).wait_send()
        copy("diag", index).wait_send()
        for which in range(pairs):
            mix_copy(index, which).wait_send()

    at = pl.ds(pl.multiple_of(slot * rows, rows), rows)
    live = mask_ref[0] > 0.5
    ones = jnp.ones((4 * rows, lanes), bf16)
    for pair in range(pairs):
        here = slice(pair * lanes, (pair + 1) * lanes)
        keys = k_all[clip, :, here]
        values = jnp.concatenate([v_all[clip, :, here], ones], axis=1)
        query = q_all[clip, at, here]
        outs, lses = [], []
        for head in range(2):
            scores = jnp.where(live, dot(only(query, head), keys, NT), MASKED)
            top = jnp.max(scores, axis=1, keepdims=True)
            exps = jnp.exp(scores - top)
            both = dot(exps.astype(bf16), values)
            total = both[:, lanes:]
            outs.append(both[:, :lanes] / total)
            lses.append(top + jnp.log(total))
        first = own_lanes(outs[0].shape, 0)
        mixed = jnp.where(first, outs[0], outs[1]).astype(bf16)
        part_ref[0, at, here] = mixed
        lse_ref[0, at, here] = jnp.where(first, lses[0], lses[1])

    @pl.when(slot == 1)
    def give():
        for pair in range(pairs):
            mix_send[clip, pair] = part_ref[0, rows:, pair * lanes : (pair + 1) * lanes]
            mix_copy(clip, pair).start()

    @pl.when((turn == 0) & (clip > 0))
    def finish_before():
        finish(clip - 1)

    @pl.when(turn == 1)
    def keep_own():
        own_mix[...] = part_ref[0, :rows]

    @pl.when((turn == 1) & (clip + 1 < clips))
    def pass_on():
        copy("vert", clip + 1).wait_recv()
        copy("diag", clip + 1).start()

    @pl.when((turn == 1) & (clip == clips - 1))
    def finish_last():
        finish(clip)
        copy("vert", clips - 1).wait_send()

    @pl.when((turn == 1) & (clip == clips - 1))
    def leave():
        for move in weight_copies():
            move.wait()
        for index in range(clips):
            for move in out_copies(index):
                move.wait()


def forward(kept, tokens, rows, qkv_weight, query_bias, value_bias, gain, shift, proj_weight, proj_bias, gain2, shift2):
    clips, slots, width = tokens.shape
    keys = 4 * rows
    half = width // 2
    pairs = HEADS // 4
    lanes = 2 * DH
    one = pl.Buffered(buffer_count=1)
    block = lambda n, m: pl.BlockSpec((1, n, m), lambda c, p: (c, 0, 0))
    late = pl.BlockSpec((1, rows, width), lambda c, t: (jnp.maximum(c - 1 + t, 0), 0, 0))
    anywhere = pl.BlockSpec(memory_space=pl.ANY)
    whole = lambda a: pl.BlockSpec(a.shape, lambda c, p: (0,) * a.ndim, pipeline_mode=one)
    shape = jax.ShapeDtypeStruct
    flops = 2 * clips * (rows * width * width * 6 + 2 * rows * keys * width)
    vectors = (query_bias, value_bias, gain, shift)
    return pl.pallas_call(
        functools.partial(forward_kernel, (clips, slots, rows, pairs)),
        grid=(clips, 2),
        in_specs=[pl.BlockSpec(memory_space=pltpu.SMEM), whole(tokens), whole(qkv_weight)]
        + [whole(v) for v in vectors]
        + [whole(proj_weight)]
        + [whole(v) for v in (proj_bias, gain2, shift2)],
        out_specs=[
            anywhere, anywhere, anywhere, anywhere, anywhere, anywhere,
            block(2 * rows, half), block(2 * rows, half), block(1, keys),
            late, late, late,
        ],
        out_shape=[
            shape((clips, 2 * rows, half), bf16),
            shape((clips, keys, half), bf16),
            shape((clips, keys, half), bf16),
            shape((clips, 2 * rows, width), bf16),
            shape((clips, rows, width), bf16),
            shape((width, 3 * half), bf16),
            shape((clips, 2 * rows, half), bf16),
            shape((clips, 2 * rows, half), f32),
            shape((clips, 1, keys), f32),
            shape((clips, rows, width), bf16),
            shape((clips, rows, width), f32),
            shape((clips, rows, width), bf16),
        ],
        scratch_shapes=[
            pltpu.VMEM((clips, 2 * rows, half), bf16),
            pltpu.VMEM((clips, keys, half), bf16),
            pltpu.VMEM((clips, keys, half), bf16),
            pltpu.VMEM((clips, 2 * rows, width), bf16),
            pltpu.VMEM((width, 3 * half), bf16),
            pltpu.VMEM((clips, 4, 1, rows), f32),
            pltpu.VMEM((clips, rows, width), bf16),
            pltpu.VMEM((clips, 3, rows, width), bf16),
            pltpu.VMEM((clips, pairs, rows, lanes), bf16),
            pltpu.VMEM((clips, pairs, rows, lanes), bf16),
            pltpu.VMEM((rows, half), bf16),
            pltpu.VMEM((8, width), f32),
            pltpu.SemaphoreType.DMA((clips, 3)),
            pltpu.SemaphoreType.DMA((clips, 3)),
            pltpu.SemaphoreType.DMA((clips, pairs)),
            pltpu.SemaphoreType.DMA((clips, pairs)),
            pltpu.SemaphoreType.DMA((clips, 5)),
            pltpu.SemaphoreType.DMA((3 * pairs,)),
        ],
        compiler_params=params(collective_id=0, has_side_effects=True),
        cost_estimate=pl.CostEstimate(
            flops=flops, bytes_accessed=40_000_000, transcendentals=clips * rows * keys * HEADS
        ),
        name="forward",
    )(kept, tokens, qkv_weight, *vectors, proj_weight, proj_bias, gain2, shift2)


def mlp_kernel(
    counts,
    kept_ref, n2_ref, middle_hbm, cot_ref, mixed_hbm, fc1_ref, b1_ref, fc2_ref, b2_ref, gain_ref, proj_hbm,
    out_ref, dfc1_ref, dfc2_ref, dproj_ref, db1_ref, small_ref, gmid_hbm, gmixed_hbm,
    middle_ref, mixed_ref, proj_ref, gmixed_ref, in_sems, out_sems,
    n2t_ref, grad_ref, out_acc, dn_acc, hidden_ref, dact_ref, active_ref, dhid_ref, biases,
):
    clips, slots, rows, tile = counts
    step = pl.program_id(0)
    width = n2_ref.shape[-1]
    chunk = fc1_ref.shape[-1]
    total = clips * rows

    def live_rows(clip, size):
        slot = lax.broadcasted_iota(jnp.int32, (size, 1), 0)
        return (slot < kept_ref[clip]).astype(f32)

    def loads():
        pairs = ((middle_hbm, middle_ref), (mixed_hbm, mixed_ref), (proj_hbm, proj_ref))
        return [pltpu.make_async_copy(src, dst, in_sems.at[i]) for i, (src, dst) in enumerate(pairs)]

    def stores(clip):
        at = pl.ds(pl.multiple_of(clip * rows, rows), rows)
        pairs = ((middle_ref, gmid_hbm), (gmixed_ref, gmixed_hbm))
        return [
            pltpu.make_async_copy(src.at[at], dst.at[at], out_sems.at[clip, i]) for i, (src, dst) in enumerate(pairs)
        ]

    @pl.when(step == 0)
    def start():
        for load in loads():
            load.start()
        n2t_ref[...] = n2_ref[...].T
        first = (slots // 16) * 16
        for clip in range(clips):
            begin = clip * rows
            grad_ref[begin + first : begin + rows] = jnp.zeros((rows - first, width), bf16)
            grad_ref[begin : begin + slots] = cot_ref[clip] * live_rows(clip, slots).astype(bf16)
        all_biases = row_of(b1_ref)
        for i in range(all_biases.shape[1] // chunk):
            biases[i : i + 1] = all_biases[:, i * chunk : (i + 1) * chunk]
        out_acc[...] = jnp.zeros_like(out_acc)
        dn_acc[...] = jnp.zeros_like(dn_acc)

    bias = biases[pl.ds(step, 1), :]
    hidden_ref[...] = dot(n2_ref[...], fc1_ref[...])
    dact_ref[...] = dot(grad_ref[...], fc2_ref[...], NT)
    sums = jnp.zeros((tile, chunk), f32)
    for begin in range(0, total, tile):
        at = slice(begin, begin + tile)
        hidden = hidden_ref[at] + bias
        cdf = 0.5 * (1.0 + lax.erf(hidden * (0.5 ** 0.5)))
        active_ref[at] = (hidden * cdf).astype(bf16)
        slope = cdf + hidden * (jnp.exp(-0.5 * hidden * hidden) * (1.0 / math.sqrt(2.0 * math.pi)))
        dhid = (dact_ref[at] * slope).astype(bf16)
        dhid_ref[at] = dhid
        sums = sums + dhid.astype(f32)
    db1_ref[...] = column_sums(sums)
    active = active_ref[...]
    dhid = dhid_ref[...]
    out_acc[...] += dot(active, fc2_ref[...])
    dn_acc[...] += dot(dhid, fc1_ref[...], NT)
    dfc1_ref[0] = dot(n2t_ref[...], dhid).astype(bf16)
    dfc2 = dot(active, grad_ref[...], TN).astype(bf16)
    half = width // 2
    dfc2_ref[0] = dfc2[:, :half]
    dfc2_ref[1] = dfc2[:, half:]

    @pl.when(step == pl.num_programs(0) - 1)
    def finish():
        for load in loads():
            load.wait()
        gain = row_of(gain_ref)
        bias2 = row_of(b2_ref)
        small_ref[...] = jnp.zeros_like(small_ref)

        def finish_clip(clip, carry):
            at = pl.ds(pl.multiple_of(clip * rows, rows), rows)
            middle = middle_ref[at]
            layer = middle + (out_acc[at] + bias2)
            out_ref[clip] = (live_rows(clip, slots) * layer[:slots]).astype(bf16)
            unit, inverse = center_scale(middle)
            grad = dn_acc[at]
            out_grad = grad_ref[at].astype(f32)
            gmid = out_grad + norm_back(unit, inverse, gain, grad)
            middle_ref[at] = gmid
            low = gmid.astype(bf16)
            dhid_ref[at, :width] = low
            gmixed_ref[at] = dot(low, proj_ref[...], NT).astype(bf16)
            small_ref[0:1] += column_sums(grad * unit)
            small_ref[1:2] += column_sums(grad)
            small_ref[2:3] += column_sums(out_grad)
            small_ref[3:4] += column_sums(low.astype(f32))
            for store in stores(clip):
                store.start()
            return carry

        lax.fori_loop(0, clips, finish_clip, 0)
        dproj = dot(mixed_ref[...], dhid_ref[:, :width], TN).astype(bf16)
        dproj_ref[0] = dproj[:, :half]
        dproj_ref[1] = dproj[:, half:]
        for clip in range(clips):
            for store in stores(clip):
                store.wait()


def mlp(kept, n2, middle, cot, mixed, fc1, b1, fc2, b2, gain, proj, rows):
    clips, slots, _ = cot.shape
    total, width = n2.shape
    hidden = fc1.shape[1]
    chunk = 768
    steps = hidden // chunk
    half = steps // 2
    tile = 16
    whole = lambda a: pl.BlockSpec(a.shape, lambda j: (0,) * a.ndim, pipeline_mode=one)
    anywhere = pl.BlockSpec(memory_space=pl.ANY)
    one = pl.Buffered(buffer_count=1)
    big = pl.BlockSpec((total, width), lambda j: (0, 0), pipeline_mode=one)
    return pl.pallas_call(
        functools.partial(mlp_kernel, (clips, slots, rows, tile)),
        grid=(steps,),
        in_specs=[
            pl.BlockSpec(memory_space=pltpu.SMEM),
            big, anywhere, whole(cot), anywhere,
            pl.BlockSpec((width, chunk), lambda j: (0, j)),
            whole(b1),
            pl.BlockSpec((chunk, width), lambda j: (j, 0)),
            whole(b2), whole(gain), anywhere,
        ],
        out_specs=[
            full((clips, slots, width)),
            pl.BlockSpec((1, width, chunk), lambda j: (j // half, 0, j % half)),
            pl.BlockSpec((2, chunk, width // 2), lambda j: (0, j, 0)),
            full((2, width, width // 2)),
            pl.BlockSpec((1, chunk), lambda j: (0, j)),
            full((8, width)),
            anywhere,
            anywhere,
        ],
        out_shape=[
            jax.ShapeDtypeStruct((clips, slots, width), bf16),
            jax.ShapeDtypeStruct((2, width, hidden // 2), bf16),
            jax.ShapeDtypeStruct((2, hidden, width // 2), bf16),
            jax.ShapeDtypeStruct((2, width, width // 2), bf16),
            jax.ShapeDtypeStruct((1, hidden), f32),
            jax.ShapeDtypeStruct((8, width), f32),
            jax.ShapeDtypeStruct((total, width), f32),
            jax.ShapeDtypeStruct((total, width), bf16),
        ],
        scratch_shapes=[
            pltpu.VMEM((total, width), f32),
            pltpu.VMEM((total, width), bf16),
            pltpu.VMEM((width, width), bf16),
            pltpu.VMEM((total, width), bf16),
            pltpu.SemaphoreType.DMA((3,)),
            pltpu.SemaphoreType.DMA((clips, 2)),
            pltpu.VMEM((width, total), bf16),
            pltpu.VMEM((total, width), bf16),
            pltpu.VMEM((total, width), f32),
            pltpu.VMEM((total, width), f32),
            pltpu.VMEM((total, chunk), f32),
            pltpu.VMEM((total, chunk), f32),
            pltpu.VMEM((total, chunk), bf16),
            pltpu.VMEM((total, chunk), bf16),
            pltpu.VMEM((8, chunk), f32),
        ],
        compiler_params=params(),
        cost_estimate=pl.CostEstimate(
            flops=12 * total * width * hidden, bytes_accessed=40_000_000, transcendentals=2 * total * hidden
        ),
        name="mlp",
    )(kept, n2, middle, cot, mixed, fc1, b1, fc2, b2, gain, proj)


def sum_arrays(width, hidden, clip_size):
    rows = width // clip_size
    tall = hidden // clip_size
    first, second = (0, 1, 2), (1, 0, 2)
    chunks = [("qkv", i, rows // 2, width // 2, order) for i, order in enumerate(QKV_ORDERS)]
    return [
        ("fc1", 0, rows, hidden // 4, first),
        ("fc2", 0, tall // 2, width // 2, second),
        ("fc1", hidden // 4, rows, hidden // 4, first),
        ("fc2", tall // 2, tall // 2, width // 2, second),
        ("proj", 0, rows, width // 2, PROJ_ORDER),
    ] + chunks


PROJ_ORDER = (0, 1, 2)
QKV_ORDERS = ((0, 1, 2), (0, 1, 2), (1, 0, 2))
SUM_STEPS = {
    2: [("end", 0, 0), ("start", 0, 1), ("end", 1, 0), ("start", 1, 1)],
    3: [("end", 2, 0)],
    4: [("end", 3, 0), ("end", 4, 0)],
    6: [("start", 2, 1), ("start", 3, 1)],
    7: [("end", 0, 1), ("end", 1, 1)],
    9: [("end", 2, 1), ("start", 0, 2), ("start", 1, 2), ("end", 3, 1)],
    10: [("start", 2, 2), ("start", 3, 2)],
    11: [("end", 0, 2), ("start", 0, 3), ("end", 1, 2)],
    12: [("end", 2, 2), ("start", 1, 3), ("start", 4, 1), ("end", 3, 2)],
    13: [("end", 0, 3), ("start", 0, 4), ("start", 2, 3)],
    15: [("end", 5, 0), ("start", 5, 1), ("start", 3, 3), ("end", 0, 4), ("start", 0, 5),
        ("end", 1, 3), ("start", 1, 4), ("end", 4, 1)],
    16: [("end", 0, 5), ("start", 4, 2), ("end", 2, 3), ("start", 2, 4)],
    17: [("end", 5, 1), ("start", 5, 2), ("end", 6, 0), ("start", 6, 1), ("end", 7, 0),
        ("start", 7, 1), ("end", 1, 4), ("start", 1, 5), ("end", 2, 4), ("start", 2, 5),
        ("end", 3, 3), ("start", 3, 4), ("end", 4, 2), ("start", 4, 3)],
    18: [("end", 1, 5), ("end", 2, 5)],
    19: [("end", 5, 2), ("start", 5, 3), ("vec", 0, 0), ("end", 6, 1), ("start", 6, 2), ("end", 7, 1),
        ("start", 7, 2), ("end", 4, 3), ("start", 4, 4), ("vec", 1, 0), ("input", 2, 0),
        ("end", 6, 2), ("start", 6, 3), ("end", 5, 3), ("start", 5, 4), ("end", 7, 2),
        ("start", 7, 3), ("end", 3, 4), ("start", 3, 5), ("vec", 2, 0), ("end", 4, 4),
        ("start", 4, 5), ("end", 3, 5), ("end", 5, 4), ("start", 5, 5), ("end", 4, 5), ("end", 6, 3),
        ("start", 6, 4), ("end", 5, 5), ("end", 7, 3), ("start", 7, 4), ("vec", 3, 0), ("end", 6, 4),
        ("start", 6, 5), ("end", 7, 4), ("start", 7, 5), ("end", 6, 5), ("end", 7, 5), ("vec", 4, 0)],
}


def backward_kernel(
    meta,
    q_ref, k_ref, v_ref, mask_ref, part_ref, lse_ref, normed_ref, weight_ref, near_ref, far_ref,
    tok_ref, gmid_ref, gain_ref,
    small_ref, db1_ref, gmixed_ref, dfc1_ref, dfc2_ref, dproj_ref,
    gtok_ref, fc1_out, fc2_out, proj_out, qkv_out, vec_out,
    *scratch,
):
    clips, slots, rows, bits, pairs, arrays = meta
    width = weight_ref.shape[0]
    half = width // 2
    lanes = 2 * DH
    step = pl.program_id(0)
    places = step_places(clips, pairs)
    mesh_id = pl.DeviceIdType.MESH
    count = len(arrays)

    scratch = list(scratch)
    take = lambda n: [scratch.pop(0) for _ in range(n)]
    (grad_all, packed, kv_acc, kv_send, kv_got, acc, dn_send, dn_got, dw_acc, bias_acc, vec_sum, vec_got) = take(12)
    own_bufs = dict(zip(("fc1", "fc2", "proj"), take(3)))
    dw_low = scratch.pop(0)
    stage_bufs = [take(bits + 1) for _ in arrays]
    vert_bufs = take(5)
    full_bufs = take(count)
    (grad_sem, grad_out, grad_in, kv_out, kv_in, dn_out, dn_in, sum_out, sum_in, own_sem, vec_out_sem, vec_in_sem) = take(12)

    core, vert, core_dev, vert_dev = freq_places()
    place = lax.axis_index("clip")
    bit_at = [(place // 2 ** b) % 2 for b in range(bits)]
    clip_dev = [{"clip": place + (1 - 2 * bit_at[b]) * 2 ** b} for b in range(bits)]

    def remote(src, dst, send, recv, device):
        return pltpu.make_async_remote_copy(
            src_ref=src, dst_ref=dst, send_sem=send, recv_sem=recv, device_id=device, device_id_type=mesh_id
        )

    def grad_own(clip):
        src = gmixed_ref.at[clip, :, lane_slice(vert * half, half)]
        return pltpu.make_async_copy(src, grad_all.at[0, clip], grad_sem.at[clip])

    def grad_vert(clip):
        src = gmixed_ref.at[clip, :, lane_slice((1 - vert) * half, half)]
        return remote(src, grad_all.at[1, clip], grad_out.at[clip], grad_in.at[clip], vert_dev)

    def kv_copy(clip, pair):
        return remote(
            kv_send.at[pair], kv_got.at[clip, pair], kv_out.at[clip, pair], kv_in.at[clip, pair], core_dev
        )

    def dn_copy(clip):
        return remote(dn_send.at[clip], dn_got.at[clip], dn_out.at[clip], dn_in.at[clip], vert_dev)

    every = (slice(None),) * bits

    def piece(a, who):
        name, at, r, width_a, _ = arrays[a]
        if name == "fc1":
            return dfc1_ref.at[(who,) + every + (slice(None), pl.ds(at, width_a))]
        if name == "fc2":
            return dfc2_ref.at[(who,) + every + (pl.ds(at, r), slice(None))]
        if name == "proj":
            return dproj_ref.at[who]
        return dw_low.at[at, who]

    def chosen(a, stage, index_of):
        order = arrays[a][4]
        left = [b for b in range(bits)[::-1] if b not in order[: stage - 1]]
        bit = order[stage - 1]
        at = (slice(None),) * left.index(bit) + (index_of(bit),)
        return stage_bufs[a][stage - 1].at[at]

    def stage_copy(a, stage):
        sems = (sum_out.at[a, stage], sum_in.at[a, stage])
        full, packed_array = full_bufs[a], arrays[a][0] == "qkv"
        if stage == 0:
            return remote(piece(a, 1 - core), stage_bufs[a][0], *sems, core_dev)
        if stage <= bits:
            src = chosen(a, stage, lambda bit: 1 - bit_at[bit])
            return remote(src, stage_bufs[a][stage], *sems, clip_dev[arrays[a][4][stage - 1]])
        if stage == bits + 1:
            dst = full.at[core, vert] if packed_array else vert_bufs[a]
            return remote(stage_bufs[a][bits], dst, *sems, vert_dev)
        return remote(full.at[core], full.at[core], *sems, core_dev)

    def own_copy(a):
        return pltpu.make_async_copy(piece(a, core), own_bufs[arrays[a][0]], own_sem.at[a])

    def add_blocks(dst, src, lead):
        if lead == 0:
            dst[...] = dst[...] + src[...]
            return

        def add_one(i, carry):
            at = tuple((i // 2 ** (lead - 1 - j)) % 2 for j in range(lead))
            dst[at] = dst[at] + src[at]
            return carry

        lax.fori_loop(0, 2 ** lead, add_one, 0)

    def stage_end(a, stage):
        name = arrays[a][0]
        stage_copy(a, stage).wait_recv()
        if stage == 0:
            if name == "qkv":
                add_blocks(stage_bufs[a][0], dw_low.at[arrays[a][1], core], bits)
            else:
                own_copy(a).wait()
                add_blocks(stage_bufs[a][0], own_bufs[name], bits)
                if a + 2 < 4:
                    own_copy(a + 2).start()
        elif stage <= bits:
            add_blocks(stage_bufs[a][stage], chosen(a, stage, lambda bit: bit_at[bit]), bits - stage)
            if stage == bits and name == "qkv":
                full_bufs[a][core, vert] = stage_bufs[a][bits][...]
        elif stage == bits + 1 and name != "qkv":
            full_bufs[a][core] = stage_bufs[a][bits][...] + vert_bufs[a][...]

    def vec_copy(hop):
        device = ([core_dev] + clip_dev + [vert_dev])[hop]
        return remote(vec_sum.at[hop], vec_got.at[hop], vec_out_sem.at[hop], vec_in_sem.at[hop], device)

    def vec_end(hop):
        vec_copy(hop).wait_recv()
        vec_sum[hop + 1] = vec_sum[hop] + vec_got[hop]
        if hop < bits + 1:
            vec_copy(hop + 1).start()

    def perform(action):
        kind, a, stage = action
        if kind == "vec":
            vec_end(a)
        elif kind == "start":
            stage_copy(a, stage).start()
        else:
            stage_end(a, stage)

    @pl.when(step == 0)
    def enter():
        barrier = pltpu.get_barrier_semaphore()
        for clip in range(clips):
            grad_own(clip).start()
        for device in [core_dev, vert_dev] + clip_dev:
            pl.semaphore_signal(barrier, inc=1, device_id=device, device_id_type=mesh_id)
        pl.semaphore_wait(barrier, 2 + bits)
        for clip in range(clips):
            grad_vert(clip).start()
        for a in range(5):
            stage_copy(a, 0).start()
        for a in (0, 1, 4):
            own_copy(a).start()
        vec_sum[0] = jnp.zeros_like(vec_sum[0])
        bias_acc[...] = jnp.zeros_like(bias_acc)
        dw_acc[...] = jnp.zeros_like(dw_acc)
        vec_sum[0, 4:8] = small_ref[0:4]
        for i in range(db1_ref.shape[1] // width):
            vec_sum[0, 8 + i : 9 + i] = db1_ref[0:1, i * width : (i + 1) * width]

    for at in sorted(SUM_STEPS):
        if at < places["end"]:
            @pl.when(step == at)
            def run(at=at):
                for action in SUM_STEPS[at]:
                    perform(action)

    def head_back(head, query, keys, values, grad, mixed, lse, live):
        own_query, own_grad = only(query, head), only(grad, head)
        scores = jnp.where(live, dot(own_query, keys, NT), MASKED)
        probs = jnp.exp(scores - lse[:, head * DH : head * DH + 1])
        delta = jnp.sum(only(grad.astype(f32) * mixed.astype(f32), head), axis=1, keepdims=True)
        dscores = (probs * (dot(own_grad, values, NT) - delta)).astype(bf16)
        return probs.astype(bf16), dscores, dot(dscores, keys)

    def join_heads(dqs):
        first = own_lanes(dqs[0].shape, 0)
        return (jnp.where(first, dqs[0], dqs[1]) * DH ** -0.5).astype(bf16)

    def send_pair(clip, pair, dk, dv):
        for part, value in enumerate((dk, dv)):
            low = value.astype(bf16)
            packed[clip, :, lane_slice((3 * pair + part + 1) * lanes, lanes)] = low[: 2 * rows]
            kv_send[pair, part] = low[2 * rows :]
        kv_copy(clip, pair).start()

    clip_now, slot_now, pair_now = attention_unit(step, places, clips, pairs)

    def attend_single():
        clip, slot, pair = 0, slot_now, pair_now

        @pl.when((pair == 0) & (slot == 0))
        def own_grads():
            grad_own(clip).wait()

        @pl.when((pair == 0) & (slot == 1))
        def vert_grads():
            grad_vert(clip).wait_recv()

        at = pl.ds(pl.multiple_of(slot * rows, rows), rows)
        query, keys, values, live = q_ref[0, at], k_ref[0], v_ref[0], mask_ref[0] > 0.5
        grad = grad_all[slot, clip, :, lane_slice(pair * lanes, lanes)]
        dqs, dk, dv = [], 0.0, 0.0
        for head in range(2):
            probs, dscores, dq = head_back(head, query, keys, values, grad, part_ref[0, at], lse_ref[0, at], live)
            dqs.append(dq)
            dk = dk + dot(dscores, only(query, head), TN)
            dv = dv + dot(probs, only(grad, head), TN)
        packed[clip, at, lane_slice(3 * pair * lanes, lanes)] = join_heads(dqs)

        @pl.when(slot == 0)
        def keep():
            kv_acc[pair, 0] = dk
            kv_acc[pair, 1] = dv

        @pl.when(slot == 1)
        def send():
            send_pair(clip, pair, kv_acc[pair, 0] + dk, kv_acc[pair, 1] + dv)

    def attend_double():
        clip, pair = clip_now, pair_now

        @pl.when(pair == 0)
        def grads():
            grad_own(clip).wait()
            grad_vert(clip).wait_recv()

        kv_copy(clip - 1, pair).wait_send()
        keys, values, live = k_ref[0], v_ref[0], mask_ref[0] > 0.5
        here = lane_slice(pair * lanes, lanes)
        query = q_ref[0]
        grad = jnp.concatenate([grad_all[0, clip, :, here], grad_all[1, clip, :, here]], axis=0)
        dqs, dk, dv = [[], []], 0.0, 0.0
        for head in range(2):
            parts = []
            for slot in range(2):
                at = slice(slot * rows, (slot + 1) * rows)
                parts.append(
                    head_back(head, query[at], keys, values, grad[at], part_ref[0, at], lse_ref[0, at], live)
                )
                dqs[slot].append(parts[slot][2])
            probs, dscores = [jnp.concatenate([parts[0][i], parts[1][i]], axis=0) for i in range(2)]
            dk = dk + dot(dscores, only(query, head), TN)
            dv = dv + dot(probs, only(grad, head), TN)
        for slot in range(2):
            at = slice(slot * rows, (slot + 1) * rows)
            packed[clip, at, lane_slice(3 * pair * lanes, lanes)] = join_heads(dqs[slot])
        send_pair(clip, pair, dk, dv)

    is_attention = step < places["projections"][-1]
    for at in places["pauses"]:
        is_attention = is_attention & (step != at)
    pl.when(step < 2 * pairs)(attend_single)
    pl.when(is_attention & (step >= 2 * pairs))(attend_double)

    def take_pair(clip, pair):
        kv_copy(clip, pair).wait_recv()
        for part in range(2):
            at = lane_slice((3 * pair + part + 1) * lanes, lanes)
            packed[clip, :, at] = packed[clip, :, at] + kv_got[clip, pair, part]
        at = lane_slice(pair * lanes, lanes)
        for row, part in ((0, 0), (1, 2)):
            value = packed[clip, :, lane_slice((3 * pair + part) * lanes, lanes)]
            bias_acc[row : row + 1, at] += column_sums(value.astype(f32))

    def norm_sums(clip, back):
        near, _ = center_scale(near_ref[0].astype(f32))
        far, _ = center_scale(far_ref[0].astype(f32))
        vec_sum[0, 0:1] += column_sums(back[:slots] * near) + column_sums(back[rows:] * far)
        vec_sum[0, 1:2] += column_sums(back)

    def give_back(clip, back):
        acc[clip] = back[:rows]
        dn_send[clip] = back[rows:].astype(bf16)
        dn_copy(clip).start()

    def last_chunk(pair):
        at = lane_slice(3 * pair * lanes, 3 * lanes)
        more = dot(normed_ref[0], packed[clips - 1, :, at], TN)
        low = (dw_acc[:, at] + more).astype(bf16)
        r = arrays[5][2]
        for block in range(2 ** bits):
            index = tuple((block >> b) & 1 for b in range(bits)[::-1])
            for who in range(2):
                start = (2 * block + who) * r
                dw_low[(pair, who) + index] = low[start : start + r]

    early_steps = places["projections"][:-1]
    early = functools.reduce(jnp.logical_or, [step == at for at in early_steps])

    @pl.when(early)
    def projections():
        clip = sum((step > at).astype(jnp.int32) for at in early_steps)

        def take_one(pair, carry):
            take_pair(clip, pair)
            return carry

        lax.fori_loop(0, pairs, take_one, 0)
        grads = packed[clip]
        back = dot(grads, weight_ref[...], NT)
        give_back(clip, back)
        dw_acc[...] += dot(normed_ref[0], grads, TN)
        norm_sums(clip, back)

    chunk_steps = places["chunks"]

    @pl.when(functools.reduce(jnp.logical_or, [step == at for at in chunk_steps]))
    def chunk():
        pair = sum((step > at).astype(jnp.int32) for at in chunk_steps)
        take_pair(clips - 1, pair)
        last_chunk(pair)

    for pair in range(pairs - 1):
        @pl.when(step == chunk_steps[pair])
        def send_chunk(pair=pair):
            stage_copy(5 + pair, 0).start()

    @pl.when(step == places["projections"][-1])
    def last_projections():
        clip = clips - 1
        before = 3 * (pairs - 1) * lanes
        back = dot(packed[clip, :, :before], weight_ref[:, :before], NT)
        take_pair(clip, pairs - 1)
        last_chunk(pairs - 1)
        stage_copy(4 + pairs, 0).start()
        back = back + dot(packed[clip, :, before:], weight_ref[:, before:], NT)
        give_back(clip, back)
        norm_sums(clip, back)
        mine = lane_slice(vert * half, half)
        vec_sum[0, 2:3, mine] = bias_acc[0:1]
        vec_sum[0, 3:4, mine] = bias_acc[1:2]
        vec_copy(0).start()

    def inputs(clip):
        dn_copy(clip).wait_recv()
        grad = acc[clip] + dn_got[clip].astype(f32)
        unit, inverse = center_scale(tok_ref[0].astype(f32))
        result = gmid_ref[0][:slots] + norm_back(unit, inverse, row_of(gain_ref), grad[:slots])
        gtok_ref[0] = result

    @pl.when((step >= places["inputs"]) & (step < places["end"]))
    def early_inputs():
        inputs(step - places["inputs"])

    @pl.when(step == places["end"])
    def finish():
        for kind, a, stage in SUM_STEPS[places["end"]]:
            if kind == "input":
                inputs(clips - 1)
            else:
                perform((kind, a, stage))
        for a, (name, at, r, width_a, _) in enumerate(arrays):
            for who in range(2):
                full = full_bufs[a]
                if name == "fc1":
                    start = who * fc1_out.shape[1] // 2 + at
                    fc1_out[:, start : start + width_a] = full[who]
                elif name == "fc2":
                    fc2_out[at : at + r, who * width_a : (who + 1) * width_a] = full[who]
                elif name == "proj":
                    proj_out[:, who * width_a : (who + 1) * width_a] = full[who]
                else:
                    for side in range(2):
                        for part in range(3):
                            to = part * width + side * half + at * lanes
                            value = full[who, side, :, part * lanes : (part + 1) * lanes]
                            qkv_out[who * r : (who + 1) * r, to : to + lanes] = value
        vec_out[...] = vec_sum[bits + 2]
        for a in range(count):
            for stage in range(bits + 3):
                stage_copy(a, stage).wait_send()
        for clip in range(clips):
            grad_vert(clip).wait_send()
            dn_copy(clip).wait_send()
        for pair in range(pairs):
            kv_copy(clips - 1, pair).wait_send()
        for hop in range(bits + 2):
            vec_copy(hop).wait_send()


def step_places(clips, pairs):
    plan = ["attend"] * (2 * pairs)
    for clip in range(1, clips):
        for pair in range(pairs):
            plan.append("attend")
            if pair == 0:
                plan.append("project")
            elif clip == clips - 1:
                plan.append("chunk")
    projections = [i for i, kind in enumerate(plan) if kind == "project"] + [len(plan)]
    chunks = [i for i, kind in enumerate(plan) if kind == "chunk"]
    inputs = len(plan) + 1
    pauses = projections[:-1] + chunks
    return {"projections": projections, "chunks": chunks, "pauses": pauses, "inputs": inputs, "end": inputs + clips - 1}


def attention_unit(step, places, clips, pairs):
    index = step
    for at in places["pauses"]:
        index = index - (step > at).astype(jnp.int32)
    index = jnp.minimum(index, (clips + 1) * pairs - 1)
    slot = jnp.where(index < 2 * pairs, index // pairs, 0)
    clip = jnp.maximum(index // pairs - 1, 0)
    return clip, slot, index % pairs


def backward(q, k, v, mask, part, lse, normed, weight_half, tokens, far, gmid, gain, small, db1, gmixed,
             dfc1, dfc2, dproj, clip_size):
    clips, slots, width = tokens.shape
    rows = gmid.shape[1]
    half = width // 2
    keys = k.shape[1]
    pairs = HEADS // 4
    lanes = 2 * DH
    bits = clip_size.bit_length() - 1
    hidden = db1.shape[1]
    arrays = sum_arrays(width, hidden, clip_size)
    places = step_places(clips, pairs)
    one = pl.Buffered(buffer_count=1)

    def of_pair(s):
        clip, _, pair = attention_unit(s, places, clips, pairs)
        return clip, 0, pair

    def of_projection(s):
        index = s * 0
        for at in places["projections"][:-1]:
            index = index + (s > at).astype(jnp.int32)
        return index, 0, 0

    def of_clip(s):
        return jnp.clip(s - places["inputs"], 0, clips - 1), 0, 0

    fixed = lambda shape: pl.BlockSpec(shape, lambda s: (0,) * len(shape), pipeline_mode=one)
    tok_pair = pl.BlockSpec((1, 2 * rows, lanes), of_pair)
    key_pair = pl.BlockSpec((1, keys, lanes), of_pair)
    anywhere = pl.BlockSpec(memory_space=pl.ANY)
    blocks = (2,) * bits
    r_fc1, r_fc2 = width // clip_size, hidden // clip_size
    dfc1 = dfc1.reshape((2,) + blocks + (r_fc1, hidden // 2))
    dfc2 = dfc2.reshape((2,) + blocks + (r_fc2, half))
    dproj = dproj.reshape((2,) + blocks + (r_fc1, half))
    vmem = lambda *shape: pltpu.VMEM(shape, bf16)
    wide = lambda *shape: pltpu.VMEM(shape, f32)
    scratch = [
        vmem(2, clips, rows, half),
        vmem(clips, 2 * rows, 3 * half),
        wide(pairs, 2, keys, lanes),
        vmem(pairs, 2, 2 * rows, lanes),
        vmem(clips, pairs, 2, 2 * rows, lanes),
        wide(clips, rows, width),
        vmem(clips, rows, width),
        vmem(clips, rows, width),
        wide(width, 3 * half),
        wide(8, half),
        wide(bits + 3, 16, width),
        wide(bits + 2, 16, width),
        vmem(*blocks, r_fc1, hidden // 4),
        vmem(*blocks, r_fc2 // 2, half),
        vmem(*blocks, r_fc1, half),
    ]
    scratch.append(vmem(pairs, 2, *blocks, r_fc1 // 2, half))
    for _, _, r, w, _ in arrays:
        scratch += [vmem(*((2,) * (bits - stage)), r, w) for stage in range(bits + 1)]
    scratch += [vmem(r, w) for name, _, r, w, _ in arrays if name != "qkv"]
    scratch += [vmem(2, 2, r, w) if name == "qkv" else vmem(2, r, w) for name, _, r, w, _ in arrays]
    dma = lambda *shape: pltpu.SemaphoreType.DMA(shape)
    count = len(arrays)
    scratch += [
        dma(clips), dma(clips), dma(clips), dma(clips, pairs), dma(clips, pairs), dma(clips), dma(clips),
        dma(count, bits + 3), dma(count, bits + 3), dma(count), dma(bits + 2), dma(bits + 2),
    ]
    shape = jax.ShapeDtypeStruct
    return pl.pallas_call(
        functools.partial(backward_kernel, (clips, slots, rows, bits, pairs, arrays)),
        grid=(places["end"] + 1,),
        in_specs=[
            tok_pair, key_pair, key_pair,
            pl.BlockSpec((1, 1, keys), lambda s: (of_pair(s)[0], 0, 0)),
            tok_pair, tok_pair,
            pl.BlockSpec((1, 2 * rows, width), of_projection),
            fixed(weight_half.shape),
            pl.BlockSpec((1, slots, width), of_projection, pipeline_mode=one),
            pl.BlockSpec((1, rows, width), of_projection, pipeline_mode=one),
            pl.BlockSpec((1, slots, width), of_clip),
            pl.BlockSpec((1, rows, width), of_clip),
            fixed((width,)), fixed((8, width)), fixed((1, hidden)),
            anywhere, anywhere, anywhere, anywhere,
        ],
        out_specs=[
            pl.BlockSpec((1, slots, width), of_clip),
            fixed((r_fc1, hidden)), fixed((r_fc2, width)), fixed((r_fc1, width)),
            fixed((r_fc1, 3 * width)), fixed((16, width)),
        ],
        out_shape=[
            shape((clips, slots, width), f32),
            shape((r_fc1, hidden), bf16),
            shape((r_fc2, width), bf16),
            shape((r_fc1, width), bf16),
            shape((r_fc1, 3 * width), bf16),
            shape((16, width), f32),
        ],
        scratch_shapes=scratch,
        compiler_params=pltpu.CompilerParams(
            vmem_limit_bytes=63 * 1024 * 1024, collective_id=1, has_side_effects=True
        ),
        cost_estimate=pl.CostEstimate(
            flops=2 * clips * rows * (5 * keys * width + 6 * width * width),
            bytes_accessed=60_000_000,
            transcendentals=clips * rows * keys * HEADS,
        ),
        name="backward",
    )(q, k, v, mask, part, lse, normed, weight_half, tokens, far, tokens, gmid, gain, small, db1, gmixed, dfc1, dfc2, dproj)


def outputs_kernel(fc1, fc2, proj, qkv, vec, gtok, fc1_out, fc2_out, proj_out, qkv_out, gtok_out, db1_out, *outs):
    gtok_out[...] = gtok[...]
    for src, dst in ((fc1, fc1_out), (fc2, fc2_out), (proj, proj_out), (qkv, qkv_out)):
        dst[...] = src[...].astype(f32)

    @pl.when(pl.program_id(0) == 0)
    def others():
        width = vec.shape[1]
        for i, dst in enumerate(outs):
            dst[...] = vec[i : i + 1].reshape(width)
        tall = db1_out.shape[0] // width
        db1_out[...] = jnp.concatenate([vec[8 + i : 9 + i] for i in range(tall)], axis=1).reshape(db1_out.shape[0])


def final_outputs(low_fc1, low_fc2, low_proj, low_qkv, summed, gtok, hidden):
    width = summed.shape[1]
    steps = gtok.shape[0]
    one = pl.Buffered(buffer_count=1)
    fixed = lambda shape: pl.BlockSpec(shape, lambda c: (0,) * len(shape), pipeline_mode=one)
    by_clip = pl.BlockSpec((1,) + gtok.shape[1:], lambda c: (c, 0, 0))
    shape = jax.ShapeDtypeStruct
    lows = (low_fc1, low_fc2, low_proj, low_qkv)

    def by_rows(a):
        if a.shape[0] % (16 * steps):
            return fixed(a.shape)
        return pl.BlockSpec((a.shape[0] // steps, a.shape[1]), lambda c: (c, 0))

    return pl.pallas_call(
        outputs_kernel,
        grid=(steps,),
        in_specs=[by_rows(a) for a in lows] + [fixed(summed.shape), by_clip],
        out_specs=[by_rows(a) for a in lows] + [by_clip, fixed((hidden,))] + [fixed((width,))] * 8,
        out_shape=[shape(a.shape, f32) for a in lows]
        + [shape(gtok.shape, f32), shape((hidden,), f32)]
        + [shape((width,), f32)] * 8,
        compiler_params=params(),
        name="final_outputs",
    )(*lows, summed, gtok)


def partner(kind):
    index = lax.axis_index("freq")
    if kind == "vert":
        return {"freq": (index + 2) % 4}
    return {"freq": index + 1 - 2 * (index % 2)}


def whole_forward_kernel(
    counts,
    tok_ref, qkv_ref, qb_ref, vb_ref, gain_ref, shift_ref, proj_ref, pb_ref, gain2_ref, shift2_ref,
    q_ref, k_ref, v_ref, normed_ref, mixed_ref, lse_ref, middle_ref, normed2_ref, mask_ref,
    held, send_sem, recv_sem,
):
    clips, slots, rows = counts
    clip = pl.program_id(0)
    pair = pl.program_id(1)
    width = tok_ref.shape[-1]

    def copy(kind, index):
        at = {"vert": 0, "core": 1, "diag": 2}[kind]
        return pltpu.make_async_remote_copy(
            src_ref=held.at[index, 0] if kind == "diag" else tok_ref.at[index],
            dst_ref=held.at[index, at],
            send_sem=send_sem.at[index, at],
            recv_sem=recv_sem.at[index, at],
            device_id=partner(kind),
            device_id_type=pl.DeviceIdType.MESH,
        )

    def project(slot, source):
        unit, _ = center_scale(source.astype(f32))
        normed = (unit * gain_ref[...] + shift_ref[...]).astype(bf16)
        if slot == 0:
            normed_ref[0] = normed
            query = (dot(normed, qkv_ref[:, :width]) + qb_ref[...]).astype(bf16)
            q_ref[0] = query * jnp.asarray(DH ** -0.5, bf16)
        both = dot(normed, qkv_ref[:, width:])
        k_ref[0, slot * rows : (slot + 1) * rows] = both[:, :width].astype(bf16)
        v_ref[0, slot * rows : (slot + 1) * rows] = (both[:, width:] + vb_ref[...]).astype(bf16)
        first = (slots // 16) * 16
        kept = source[first:].astype(f32)[slots - first : slots - first + 1, 0:1] + slots // 2
        lane = lax.broadcasted_iota(jnp.int32, (1, rows), 1).astype(f32)
        return (lane < kept).astype(f32)

    @pl.when((clip == 0) & (pair == 0))
    def enter():
        barrier = pltpu.get_barrier_semaphore()
        for kind in ("vert", "core"):
            pl.semaphore_signal(
                barrier, inc=1, device_id=partner(kind), device_id_type=pl.DeviceIdType.MESH
            )
        pl.semaphore_wait(barrier, 2)
        copy("vert", 0).start()
        for index in range(clips):
            copy("core", index).start()

    def pass_on(index):
        copy("vert", index).wait_recv()
        copy("diag", index).start()
        copy("vert", index).wait_send()

        @pl.when(index + 1 < clips)
        def more():
            copy("vert", index + 1).start()

    @pl.when(pair == 0)
    def project_all():
        live_own = project(0, tok_ref[clip])
        copy("core", clip).wait_recv()
        live_core = project(2, held[clip, 1])

        @pl.when(clip == 0)
        def first_pass():
            pass_on(clip)

        live_vert = project(1, held[clip, 0])
        copy("diag", clip).wait_recv()
        live_diag = project(3, held[clip, 2])
        mask_ref[0] = jnp.concatenate([live_own, live_vert, live_core, live_diag], axis=1)

    @pl.when((pair == 3) & (clip + 1 < clips))
    def next_pass():
        pass_on(clip + 1)

    lanes = pl.ds(pl.multiple_of(pair * 2 * DH, 2 * DH), 2 * DH)
    query = q_ref[0, :, lanes]
    keys = k_ref[0, :, lanes]
    values = v_ref[0, :, lanes]
    live = mask_ref[0] > 0.5
    outs, lses = [], []
    for head in range(2):
        scores = jnp.where(live, dot(only(query, head), keys, NT), MASKED)
        top = jnp.max(scores, axis=1, keepdims=True)
        exps = jnp.exp(scores - top)
        total = jnp.sum(exps, axis=1, keepdims=True)
        outs.append(dot(exps.astype(bf16), values) / total)
        lses.append(top + jnp.log(total))
    first = own_lanes(outs[0].shape, 0)
    mixed_ref[0, :, lanes] = jnp.where(first, outs[0], outs[1]).astype(bf16)
    lse_ref[0, :, lanes] = jnp.where(first, lses[0], lses[1])

    @pl.when(pair == pl.num_programs(1) - 1)
    def finish():
        middle = tok_ref[clip].astype(f32) + (dot(mixed_ref[0], proj_ref[...]) + pb_ref[...])
        middle_ref[0] = middle
        unit, _ = center_scale(middle)
        normed2_ref[0] = (unit * gain2_ref[...] + shift2_ref[...]).astype(bf16)
        copy("core", clip).wait_send()
        copy("diag", clip).wait_send()


def whole_forward(tok, slots, qkv_weight, vectors, proj_weight):
    clips, rows, width = tok.shape
    keys = 4 * rows
    pairs = HEADS // 2
    query_bias, value_bias, gain, shift, proj_bias, gain2, shift2 = vectors
    one = pl.Buffered(buffer_count=1)
    row = full((1, width))
    block = lambda n: pl.BlockSpec((1, n, width), lambda c, p: (c, 0, 0))
    flops = 2 * clips * (10 * rows * width * width + 2 * rows * keys * width)
    weight = lambda w: pl.BlockSpec(w.shape, lambda c, p: (0, 0), pipeline_mode=one)
    return pl.pallas_call(
        functools.partial(whole_forward_kernel, (clips, slots, rows)),
        grid=(clips, pairs),
        in_specs=[
            pl.BlockSpec(tok.shape, lambda c, p: (0, 0, 0), pipeline_mode=one),
            weight(qkv_weight), row, row, row, row, weight(proj_weight), row, row, row,
        ],
        out_specs=[block(rows), block(keys), block(keys)] + [block(rows)] * 5
        + [pl.BlockSpec((1, 1, keys), lambda c, p: (c, 0, 0))],
        out_shape=[
            jax.ShapeDtypeStruct((clips, rows, width), bf16),
            jax.ShapeDtypeStruct((clips, keys, width), bf16),
            jax.ShapeDtypeStruct((clips, keys, width), bf16),
            jax.ShapeDtypeStruct((clips, rows, width), bf16),
            jax.ShapeDtypeStruct((clips, rows, width), bf16),
            jax.ShapeDtypeStruct((clips, rows, width), f32),
            jax.ShapeDtypeStruct((clips, rows, width), f32),
            jax.ShapeDtypeStruct((clips, rows, width), bf16),
            jax.ShapeDtypeStruct((clips, 1, keys), f32),
        ],
        scratch_shapes=[
            pltpu.VMEM((clips, 3, rows, width), bf16),
            pltpu.SemaphoreType.DMA((clips, 3)),
            pltpu.SemaphoreType.DMA((clips, 3)),
        ],
        compiler_params=params(collective_id=0, has_side_effects=True),
        cost_estimate=pl.CostEstimate(
            flops=flops, bytes_accessed=40_000_000, transcendentals=clips * rows * keys * HEADS
        ),
        name="whole_forward",
    )(tok, qkv_weight, query_bias, value_bias, gain, shift, proj_weight, proj_bias, gain2, shift2)


def attend_back_kernel(q_ref, k_ref, v_ref, mask_ref, mixed_ref, lse_ref, grad_ref,
                       dq_ref, dkeep_ref, dsend_ref):
    query = q_ref[0]
    keys = k_ref[0]
    values = v_ref[0]
    grad = grad_ref[0]
    live = mask_ref[0] > 0.5
    product = grad.astype(f32) * mixed_ref[0].astype(f32)
    dqs, dk, dv = [], None, None
    for head in range(2):
        own_query = only(query, head)
        own_grad = only(grad, head)
        scores = jnp.where(live, dot(own_query, keys, NT), MASKED)
        probs = jnp.exp(scores - lse_ref[0, :, head * DH : head * DH + 1])
        delta = jnp.sum(only(product, head), axis=1, keepdims=True)
        dscores = (probs * (dot(own_grad, values, NT) - delta)).astype(bf16)
        dqs.append(dot(dscores, keys))
        more_k = dot(dscores, own_query, TN)
        more_v = dot(probs.astype(bf16), own_grad, TN)
        dk = more_k if dk is None else dk + more_k
        dv = more_v if dv is None else dv + more_v
    first = own_lanes(dqs[0].shape, 0)
    dq_ref[0] = (jnp.where(first, dqs[0], dqs[1]) * DH ** -0.5).astype(bf16)
    half = dk.shape[0] // 2
    dkeep_ref[0, 0] = dk[:half].astype(bf16)
    dkeep_ref[1, 0] = dv[:half].astype(bf16)
    dsend_ref[0, 0] = dk[half:].astype(bf16)
    dsend_ref[1, 0] = dv[half:].astype(bf16)


def attend_back(q, k, v, mask, mixed, lse, grad, first_pair, pairs):
    clips, rows, _ = q.shape
    keys = k.shape[1]
    lanes = 2 * DH
    tok = pl.BlockSpec((1, rows, lanes), lambda c, p: (c, 0, first_pair + p))
    key = pl.BlockSpec((1, keys, lanes), lambda c, p: (c, 0, first_pair + p))
    part = pl.BlockSpec((2, 1, keys // 2, lanes), lambda c, p: (0, c, 0, p))
    return pl.pallas_call(
        attend_back_kernel,
        grid=(clips, pairs),
        in_specs=[tok, key, key, pl.BlockSpec((1, 1, keys), lambda c, p: (c, 0, 0)), tok, tok, tok],
        out_specs=[pl.BlockSpec((1, rows, lanes), lambda c, p: (c, 0, p)), part, part],
        out_shape=[
            jax.ShapeDtypeStruct((clips, rows, pairs * lanes), bf16),
            jax.ShapeDtypeStruct((2, clips, keys // 2, pairs * lanes), bf16),
            jax.ShapeDtypeStruct((2, clips, keys // 2, pairs * lanes), bf16),
        ],
        compiler_params=params(),
        cost_estimate=pl.CostEstimate(
            flops=4 * 10 * clips * rows * keys * pairs * lanes,
            bytes_accessed=clips * pairs * lanes * (keys * 10 + rows * 12),
            transcendentals=clips * rows * keys * 2 * pairs,
        ),
        name="attend_back",
    )(q, k, v, mask, mixed, lse, grad)


def weight_kernel(normed_ref, dq_ref, dk0_ref, dk1_ref, dk2_ref, out_ref, dkv_ref, sums_ref):
    part = pl.program_id(0)
    @pl.when(part == 0)
    def query():
        grad = dq_ref[...]
        out_ref[0] = dot(normed_ref[...], grad, TN).astype(bf16)
        sums_ref[0] = column_sums(grad.astype(f32))
        dkv_ref[0] = jnp.zeros_like(dkv_ref[0])

    @pl.when(part > 0)
    def other():
        grad = (dk0_ref[0].astype(f32) + dk1_ref[0].astype(f32) + dk2_ref[0].astype(f32)).astype(bf16)
        dkv_ref[0] = grad
        out_ref[0] = dot(normed_ref[...], grad, TN).astype(bf16)
        sums_ref[0] = column_sums(grad.astype(f32))


def weight_grads(normed, dq, parts):
    total, width = normed.shape
    lanes = dq.shape[1]
    before = lambda j: (jnp.maximum(j - 1, 0), 0, 0)
    part = pl.BlockSpec((1, total, lanes), before)
    return pl.pallas_call(
        weight_kernel,
        grid=(3,),
        in_specs=[full((total, width)), full((total, lanes)), part, part, part],
        out_specs=[
            pl.BlockSpec((1, width, lanes), lambda j: (j, 0, 0)),
            part,
            pl.BlockSpec((1, 1, lanes), lambda j: (j, 0, 0)),
        ],
        out_shape=[
            jax.ShapeDtypeStruct((3, width, lanes), bf16),
            jax.ShapeDtypeStruct((2, total, lanes), bf16),
            jax.ShapeDtypeStruct((3, 1, lanes), f32),
        ],
        compiler_params=params(),
        cost_estimate=pl.CostEstimate(
            flops=6 * total * width * lanes, bytes_accessed=8_000_000, transcendentals=0
        ),
        name="weight_grads",
    )(normed, dq, *parts)


def input_kernel(counts, groups, *refs):
    clips, slots, rows = counts
    dqs = refs[:groups]
    dkvs = refs[groups : 2 * groups]
    qkv_ref, tok_ref, gmid_ref, gain_ref, shift_ref, out_ref, small_ref = refs[2 * groups :]
    clip = pl.program_id(0)
    width = tok_ref.shape[-1]
    lanes = width // groups
    grad = None
    for group in range(groups):
        for part in range(3):
            rows_grad = dqs[group][0] if part == 0 else dkvs[group][part - 1]
            at = part * width + group * lanes
            more = dot(rows_grad, qkv_ref[:, at : at + lanes], NT)
            grad = more if grad is None else grad + more
    unit, inverse = center_scale(tok_ref[0].astype(f32))
    result = gmid_ref[0] + norm_back(unit, inverse, gain_ref[...], grad)
    out_ref[0] = result[:slots]

    @pl.when(clip == 0)
    def start():
        small_ref[...] = jnp.zeros_like(small_ref)

    small_ref[0:1] += column_sums(grad * unit)
    small_ref[1:2] += column_sums(grad)


def input_grads(dqs, dkvs, qkv_weight, tokens, gmid, gain, shift, slots):
    clips, rows, width = tokens.shape
    groups = len(dqs)
    lanes = width // groups
    tok = pl.BlockSpec((1, rows, width), lambda c: (c, 0, 0))
    return pl.pallas_call(
        functools.partial(input_kernel, (clips, slots, rows), groups),
        grid=(clips,),
        in_specs=[pl.BlockSpec((1, rows, lanes), lambda c: (c, 0, 0))] * groups
        + [pl.BlockSpec((2, rows, lanes), lambda c: (0, c, 0))] * groups
        + [full(qkv_weight.shape), tok, tok, full((1, width)), full((1, width))],
        out_specs=[pl.BlockSpec((1, slots, width), lambda c: (c, 0, 0)), full((8, width))],
        out_shape=[
            jax.ShapeDtypeStruct((clips, slots, width), f32),
            jax.ShapeDtypeStruct((8, width), f32),
        ],
        compiler_params=params(),
        cost_estimate=pl.CostEstimate(
            flops=6 * clips * rows * width * width, bytes_accessed=16_000_000, transcendentals=0
        ),
        name="input_grads",
    )(*dqs, *dkvs, qkv_weight, tokens, gmid, gain, shift)


def swap_bit(array, axis, size, bit):
    return lax.ppermute(array, axis, [(i, i ^ (1 << bit)) for i in range(size)])


def add_low(left, right):
    return (left.astype(f32) + right.astype(f32)).astype(bf16)


def pick(array, index, dim):
    return lax.dynamic_index_in_dim(array, index, dim, keepdims=False)


def bit_of(axis, bit):
    return (lax.axis_index(axis) >> bit) & 1


def scatter_sum(split, clip_size, order):
    core = bit_of("freq", 0)
    vert = bit_of("freq", 1)
    bits = clip_size.bit_length() - 1
    lanes = split.shape[-1]
    value = add_low(pick(split, core, 0), swap_bit(pick(split, 1 - core, 0), "freq", 4, 0))
    rows = value.shape[0] // (2 * clip_size)
    value = value.reshape((2,) * bits + (2, rows, lanes))
    left = list(range(bits))[::-1]
    for bit in order:
        at = left.index(bit)
        mine = bit_of("clip", bit)
        value = add_low(
            pick(value, mine, at), swap_bit(pick(value, 1 - mine, at), "clip", clip_size, bit)
        )
        left.remove(bit)
    return add_low(pick(value, vert, 0), swap_bit(pick(value, 1 - vert, 0), "freq", 4, 1))


def gather_low(part):
    core = bit_of("freq", 0)
    vert = bit_of("freq", 1)
    other = swap_bit(part, "freq", 4, 1)
    tall = jnp.where(vert == 0, jnp.concatenate([part, other]), jnp.concatenate([other, part]))
    side = swap_bit(tall, "freq", 4, 0)
    return jnp.where(
        core == 0,
        jnp.concatenate([tall, side], axis=1),
        jnp.concatenate([side, tall], axis=1),
    ).astype(f32)


def total_sum(array, clip_size):
    for bit in range(2):
        array = array + swap_bit(array, "freq", 4, bit)
    for bit in range(clip_size.bit_length() - 1):
        array = array + swap_bit(array, "clip", clip_size, bit)
    return array


def on_device_plain(
    clip_size, tokens, kept_counts, attn_gain, attn_shift, qkv_weight, query_bias, value_bias,
    proj_weight, proj_bias, mlp_gain, mlp_shift, fc1_weight, fc1_bias, fc2_weight, fc2_bias, cotangent,
):
    clips, slots, width = tokens.shape
    rows = -(-slots // 16) * 16
    total = clips * rows
    bits = clip_size.bit_length() - 1
    forward_order = list(range(bits))
    second_order = forward_order[1:2] + forward_order[:1] + forward_order[2:]
    vec = lambda v: v.astype(f32)[None, :]
    kept = (kept_counts - slots // 2).astype(bf16)
    tok = jnp.concatenate(
        [tokens, jnp.broadcast_to(kept[:, :, None], (clips, rows - slots, width))], axis=1
    )
    vectors = [vec(v) for v in (query_bias, value_bias, attn_gain, attn_shift, proj_bias, mlp_gain, mlp_shift)]
    q, k, v, normed, mixed, lse, middle, normed2, mask = whole_forward(
        tok, slots, qkv_weight, vectors, proj_weight
    )
    flat = lambda a: a.reshape(total, width)
    layer_out, dfc1, dfc2, dproj, db1, small2, gmid, gmixed = mlp(
        kept_counts.reshape(clips), flat(normed2), flat(middle), cotangent, flat(mixed), fc1_weight, fc1_bias,
        fc2_weight, fc2_bias, mlp_gain, proj_weight, rows,
    )
    early = total_sum(jnp.concatenate([small2[:4].reshape(-1), db1.reshape(-1)])[None, :], clip_size)[0]
    sum_fc1 = gather_low(scatter_sum(dfc1, clip_size, forward_order))
    sum_fc2 = gather_low(scatter_sum(dfc2, clip_size, second_order))
    sum_proj = gather_low(scatter_sum(dproj, clip_size, forward_order))

    groups = 3
    pairs = HEADS // 2 // groups
    lanes = pairs * 2 * DH
    gmixed = gmixed.reshape(clips, rows, width)
    dqs, dkvs, sums, sharded = [], [], [], []
    for group in range(groups):
        dq, keep, send = attend_back(q, k, v, mask, mixed, lse, gmixed, group * pairs, pairs)
        got = swap_bit(send, "freq", 4, 0)
        across = swap_bit(add_low(keep[:, :, rows:], got[:, :, rows:]), "freq", 4, 1)
        parts = [a.reshape(2, total, lanes) for a in (keep[:, :, :rows], got[:, :, :rows], across)]
        dw, dkv, colsum = weight_grads(flat(normed), dq.reshape(total, lanes), parts)
        half = lanes // 2
        split = jnp.stack(
            [
                jnp.concatenate([dw[i, :, s * half : (s + 1) * half] for i in range(3)], axis=1)
                for s in range(2)
            ]
        )
        order = forward_order if group % 2 == 0 else second_order
        summed = gather_low(scatter_sum(split, clip_size, order))
        sharded.append(summed.reshape(summed.shape[0], 2, 3, half))
        dqs.append(dq)
        dkvs.append(dkv)
        sums.append(colsum)
    grad_tokens, small1 = input_grads(
        dqs, dkvs, qkv_weight, tok, gmid.reshape(clips, rows, width), vectors[2], vectors[3], slots
    )
    qkv = jnp.stack(sharded, axis=1)
    sum_qkv = qkv.transpose(0, 3, 1, 2, 4).reshape(qkv.shape[0], 3 * width)
    bias = jnp.concatenate(sums, axis=2)
    late = total_sum(
        jnp.concatenate([small1[0:1], small1[1:2], bias[0], bias[2]], axis=1), clip_size
    )[0]
    cut = lambda a, i: a[i * width : (i + 1) * width]
    return (
        layer_out, grad_tokens, cut(late, 0), cut(late, 1), sum_qkv, cut(late, 2), cut(late, 3),
        sum_proj, cut(early, 3), cut(early, 0), cut(early, 1), sum_fc1, early[4 * width :],
        sum_fc2, cut(early, 2),
    )


def on_device(
    clip_size, tokens, kept_counts, attn_gain, attn_shift, qkv_weight, query_bias, value_bias,
    proj_weight, proj_bias, mlp_gain, mlp_shift, fc1_weight, fc1_bias, fc2_weight, fc2_bias, cotangent,
):
    clips, slots, width = tokens.shape
    rows = -(-slots // 16) * 16
    if clip_size != 8 or width % (32 * clip_size):
        return on_device_plain(
            clip_size, tokens, kept_counts, attn_gain, attn_shift, qkv_weight, query_bias, value_bias,
            proj_weight, proj_bias, mlp_gain, mlp_shift, fc1_weight, fc1_bias, fc2_weight, fc2_bias, cotangent,
        )
    kept = kept_counts.reshape(clips)
    q, k, v, normed, far, weight_half, part, lse, mask, mixed, middle, normed2 = forward(
        kept, tokens, rows, qkv_weight, query_bias, value_bias, attn_gain, attn_shift,
        proj_weight, proj_bias, mlp_gain, mlp_shift,
    )
    flat = lambda a: a.reshape(clips * rows, width)
    layer_out, dfc1, dfc2, dproj, db1, small, gmid, gmixed = mlp(
        kept, flat(normed2), flat(middle), cotangent, flat(mixed), fc1_weight, fc1_bias,
        fc2_weight, fc2_bias, mlp_gain, proj_weight, rows,
    )
    by_clip = lambda a: a.reshape(clips, rows, width)
    gtok, low_fc1, low_fc2, low_proj, low_qkv, summed = backward(
        q, k, v, mask, part, lse, normed, weight_half, tokens, far, by_clip(gmid), attn_gain, small, db1,
        by_clip(gmixed), dfc1, dfc2, dproj, clip_size,
    )
    fc1, fc2, proj, qkv, grad_tokens, fc1_b, *rows_out = final_outputs(
        low_fc1, low_fc2, low_proj, low_qkv, summed, gtok, fc1_bias.shape[0]
    )
    return (
        layer_out, grad_tokens, rows_out[0], rows_out[1], qkv, rows_out[2], rows_out[3], proj, rows_out[7],
        rows_out[4], rows_out[5], fc1, fc1_b, fc2, rows_out[6],
    )


def solution(mesh):
    rows = P("clip", "freq", None)
    shard = P("clip", None)
    return jax.shard_map(
        functools.partial(on_device, mesh.shape["clip"]),
        mesh=mesh,
        in_specs=(rows, P("clip", "freq")) + (P(),) * 13 + (rows,),
        out_specs=(rows, rows, P(), P(), shard, P(), P(), shard, P(), P(), P(), shard, P(), shard, P()),
        check_vma=False,
    )
```

```python
import functools
import math

import jax
import jax.numpy as jnp
from jax import lax
from jax.experimental import pallas as pl
from jax.experimental.pallas import tpu as pltpu
from jax.sharding import PartitionSpec as P

HEADS = 12
DH = 64
EPS = 1e-06
MASKED = -1000000000.0
VMEM_BYTES = 60 * 1024 * 1024

f32 = jnp.float32
bf16 = jnp.bfloat16
NN = (((1,), (0,)), ((), ()))
NT = (((1,), (1,)), ((), ()))
TN = (((0,), (0,)), ((), ()))


def dot(left, right, dims=NN):
    return lax.dot_general(left, right, dims, preferred_element_type=f32)


def center_scale(rows):
    center = rows - jnp.mean(rows, axis=-1, keepdims=True)
    inverse = lax.rsqrt(jnp.mean(center * center, axis=-1, keepdims=True) + EPS)
    return center * inverse, inverse


def norm_back(unit, inverse, gain, grad):
    scaled = grad * gain
    return inverse * (
        scaled
        - jnp.mean(scaled, axis=-1, keepdims=True)
        - unit * jnp.mean(scaled * unit, axis=-1, keepdims=True)
    )


def column_sums(rows):
    return jnp.sum(rows, axis=0, keepdims=True)


def own_lanes(shape, head):
    lane = lax.broadcasted_iota(jnp.int32, shape, len(shape) - 1)
    return lane < DH if head == 0 else lane >= DH


def only(rows, head):
    return jnp.where(own_lanes(rows.shape, head), rows, jnp.zeros_like(rows))


def full(shape):
    return pl.BlockSpec(shape, lambda *ids: (0,) * len(shape))


def params(**more):
    return pltpu.CompilerParams(vmem_limit_bytes=VMEM_BYTES, **more)


def freq_places():
    freq = lax.axis_index("freq")
    core, vert = freq % 2, freq // 2
    return core, vert, {"freq": freq + 1 - 2 * core}, {"freq": (freq + 2) % 4}


def lane_slice(start, size):
    return pl.ds(pl.multiple_of(start, 2 * DH), size)


def row_of(ref):
    return ref[...].astype(f32).reshape(1, ref.shape[0])


def forward_kernel(
    counts,
    kept_ref, tok_ref, qkv_ref, qb_ref, vb_ref, gain_ref, shift_ref, proj_ref, pb_ref, gain2_ref, shift2_ref,
    q_out, k_out, v_out, normed_out, far_out, weight_out, part_ref, lse_ref, mask_ref, mixed_ref, middle_ref, normed2_ref,
    q_all, k_all, v_all, normed_all, weight, live_all, own, held, mix_send, mix_got, own_mix, vecs,
    tok_send, tok_recv, part_send, part_recv, out_sem, weight_sem,
):
    clips, slots, rows, pairs = counts
    clip = pl.program_id(0)
    turn = pl.program_id(1)
    slot = 1 - turn
    width = tok_ref.shape[-1]
    half = width // 2
    lanes = 2 * DH
    core, vert, core_dev, vert_dev = freq_places()
    mesh_id = pl.DeviceIdType.MESH

    def copy(kind, index):
        at = {"vert": 0, "core": 1, "diag": 2}[kind]
        return pltpu.make_async_remote_copy(
            src_ref=held.at[index, 0] if kind == "diag" else own.at[index],
            dst_ref=held.at[index, at],
            send_sem=tok_send.at[index, at],
            recv_sem=tok_recv.at[index, at],
            device_id=vert_dev if kind == "vert" else core_dev,
            device_id_type=mesh_id,
        )

    def mix_copy(index, which):
        return pltpu.make_async_remote_copy(
            src_ref=mix_send.at[index, which],
            dst_ref=mix_got.at[index, which],
            send_sem=part_send.at[index, which],
            recv_sem=part_recv.at[index, which],
            device_id=vert_dev,
            device_id_type=mesh_id,
        )

    def project(index, slot, source):
        unit, _ = center_scale(source.astype(f32))
        normed = (unit * vecs[2:3] + vecs[3:4]).astype(bf16)
        at = slice(slot * rows, (slot + 1) * rows)
        if slot < 2:
            normed_all[index, at] = normed
            query = (dot(normed, weight[:, :half]) + vecs[0:1, lane_slice(vert * half, half)]).astype(bf16)
            q_all[index, at] = query * jnp.asarray(DH ** -0.5, bf16)
        both = dot(normed, weight[:, half:])
        k_all[index, at] = both[:, :half].astype(bf16)
        v_all[index, at] = (both[:, half:] + vecs[1:2, lane_slice(vert * half, half)]).astype(bf16)
        first = (slots // 16) * 16
        kept = source[first:].astype(f32)[slots - first : slots - first + 1, 0:1] + slots // 2
        lane = lax.broadcasted_iota(jnp.int32, (1, rows), 1).astype(f32)
        live_all[index, slot] = (lane < kept).astype(f32)

    def out_copies(index):
        return [
            pltpu.make_async_copy(src.at[index], dst.at[index], out_sem.at[index, i])
            for i, (src, dst) in enumerate(
                ((q_all, q_out), (k_all, k_out), (v_all, v_out), (normed_all, normed_out))
            )
        ] + [pltpu.make_async_copy(held.at[index, 0], far_out.at[index], out_sem.at[index, 4])]

    def weight_copies():
        moves = []
        for pair in range(pairs):
            for part in range(3):
                src = weight.at[:, pl.ds(part * half + pair * lanes, lanes)]
                dst = weight_out.at[:, pl.ds((3 * pair + part) * lanes, lanes)]
                moves.append(pltpu.make_async_copy(src, dst, weight_sem.at[3 * pair + part]))
        return moves

    @pl.when((clip == 0) & (turn == 0))
    def enter():
        barrier = pltpu.get_barrier_semaphore()
        for device in (vert_dev, core_dev):
            pl.semaphore_signal(barrier, inc=1, device_id=device, device_id_type=mesh_id)
        first = (slots // 16) * 16
        for index in range(clips):
            kept = (kept_ref[index] - slots // 2).astype(f32).astype(bf16)
            own[index, first:] = jnp.broadcast_to(kept, (rows - first, width))
            own[index, :slots] = tok_ref[index]
        pl.semaphore_wait(barrier, 2)
        copy("vert", 0).start()
        for index in range(clips):
            copy("core", index).start()
        for i, ref in enumerate((qb_ref, vb_ref, gain_ref, shift_ref, pb_ref, gain2_ref, shift2_ref)):
            vecs[i : i + 1] = row_of(ref)
        for part in range(3):
            weight[:, part * half : (part + 1) * half] = qkv_ref[:, lane_slice(part * width + vert * half, half)]
        for move in weight_copies():
            move.start()

        def own_slots(index, carry):
            project(index, 0, own[index])
            return carry

        def core_slots(index, carry):
            copy("core", index).wait_recv()
            project(index, 2, held[index, 1])
            return carry

        lax.fori_loop(0, clips, own_slots, 0)
        lax.fori_loop(0, clips, core_slots, 0)
        copy("vert", 0).wait_recv()
        copy("diag", 0).start()
        copy("vert", 0).wait_send()
        if clips > 1:
            copy("vert", 1).start()

    @pl.when(turn == 0)
    def project_rest():
        project(clip, 1, held[clip, 0])
        copy("diag", clip).wait_recv()
        project(clip, 3, held[clip, 2])
        for i in range(4):
            mask_ref[0, :, i * rows : (i + 1) * rows] = live_all[clip, i]
        for move in out_copies(clip):
            move.start()

    for index in range(2, clips):
        @pl.when((turn == 1) & (clip == index - 2))
        def send_ahead(index=index):
            copy("vert", index - 1).wait_send()
            copy("vert", index).start()

    def finish(index):
        at = lane_slice(vert * half, half)
        mixed_ref[0, :, at] = own_mix[...]
        for which in range(pairs):
            mix_copy(index, which).wait_recv()
            at = lane_slice((1 - vert) * half + which * lanes, lanes)
            mixed_ref[0, :, at] = mix_got[index, which]
        middle = own[index].astype(f32) + (dot(mixed_ref[0], proj_ref[...]) + vecs[4:5])
        middle_ref[0] = middle
        unit, _ = center_scale(middle)
        normed2_ref[0] = (unit * vecs[5:6] + vecs[6:7]).astype(bf16)
        copy("core", index).wait_send()
        copy("diag", index).wait_send()
        for which in range(pairs):
            mix_copy(index, which).wait_send()

    at = pl.ds(pl.multiple_of(slot * rows, rows), rows)
    live = mask_ref[0] > 0.5
    ones = jnp.ones((4 * rows, lanes), bf16)
    for pair in range(pairs):
        here = slice(pair * lanes, (pair + 1) * lanes)
        keys = k_all[clip, :, here]
        values = jnp.concatenate([v_all[clip, :, here], ones], axis=1)
        query = q_all[clip, at, here]
        outs, lses = [], []
        for head in range(2):
            scores = jnp.where(live, dot(only(query, head), keys, NT), MASKED)
            top = jnp.max(scores, axis=1, keepdims=True)
            exps = jnp.exp(scores - top)
            both = dot(exps.astype(bf16), values)
            total = both[:, lanes:]
            outs.append(both[:, :lanes] / total)
            lses.append(top + jnp.log(total))
        first = own_lanes(outs[0].shape, 0)
        mixed = jnp.where(first, outs[0], outs[1]).astype(bf16)
        part_ref[0, at, here] = mixed
        lse_ref[0, at, here] = jnp.where(first, lses[0], lses[1])

    @pl.when(slot == 1)
    def give():
        for pair in range(pairs):
            mix_send[clip, pair] = part_ref[0, rows:, pair * lanes : (pair + 1) * lanes]
            mix_copy(clip, pair).start()

    @pl.when((turn == 0) & (clip > 0))
    def finish_before():
        finish(clip - 1)

    @pl.when(turn == 1)
    def keep_own():
        own_mix[...] = part_ref[0, :rows]

    @pl.when((turn == 1) & (clip + 1 < clips))
    def pass_on():
        copy("vert", clip + 1).wait_recv()
        copy("diag", clip + 1).start()

    @pl.when((turn == 1) & (clip == clips - 1))
    def finish_last():
        finish(clip)
        copy("vert", clips - 1).wait_send()

    @pl.when((turn == 1) & (clip == clips - 1))
    def leave():
        for move in weight_copies():
            move.wait()
        for index in range(clips):
            for move in out_copies(index):
                move.wait()


def forward(kept, tokens, rows, qkv_weight, query_bias, value_bias, gain, shift, proj_weight, proj_bias, gain2, shift2):
    clips, slots, width = tokens.shape
    keys = 4 * rows
    half = width // 2
    pairs = HEADS // 4
    lanes = 2 * DH
    one = pl.Buffered(buffer_count=1)
    block = lambda n, m: pl.BlockSpec((1, n, m), lambda c, p: (c, 0, 0))
    late = pl.BlockSpec((1, rows, width), lambda c, t: (jnp.maximum(c - 1 + t, 0), 0, 0))
    anywhere = pl.BlockSpec(memory_space=pl.ANY)
    whole = lambda a: pl.BlockSpec(a.shape, lambda c, p: (0,) * a.ndim, pipeline_mode=one)
    shape = jax.ShapeDtypeStruct
    flops = 2 * clips * (rows * width * width * 6 + 2 * rows * keys * width)
    vectors = (query_bias, value_bias, gain, shift)
    return pl.pallas_call(
        functools.partial(forward_kernel, (clips, slots, rows, pairs)),
        grid=(clips, 2),
        in_specs=[pl.BlockSpec(memory_space=pltpu.SMEM), whole(tokens), whole(qkv_weight)]
        + [whole(v) for v in vectors]
        + [whole(proj_weight)]
        + [whole(v) for v in (proj_bias, gain2, shift2)],
        out_specs=[
            anywhere, anywhere, anywhere, anywhere, anywhere, anywhere,
            block(2 * rows, half), block(2 * rows, half), block(1, keys),
            late, late, late,
        ],
        out_shape=[
            shape((clips, 2 * rows, half), bf16),
            shape((clips, keys, half), bf16),
            shape((clips, keys, half), bf16),
            shape((clips, 2 * rows, width), bf16),
            shape((clips, rows, width), bf16),
            shape((width, 3 * half), bf16),
            shape((clips, 2 * rows, half), bf16),
            shape((clips, 2 * rows, half), f32),
            shape((clips, 1, keys), f32),
            shape((clips, rows, width), bf16),
            shape((clips, rows, width), f32),
            shape((clips, rows, width), bf16),
        ],
        scratch_shapes=[
            pltpu.VMEM((clips, 2 * rows, half), bf16),
            pltpu.VMEM((clips, keys, half), bf16),
            pltpu.VMEM((clips, keys, half), bf16),
            pltpu.VMEM((clips, 2 * rows, width), bf16),
            pltpu.VMEM((width, 3 * half), bf16),
            pltpu.VMEM((clips, 4, 1, rows), f32),
            pltpu.VMEM((clips, rows, width), bf16),
            pltpu.VMEM((clips, 3, rows, width), bf16),
            pltpu.VMEM((clips, pairs, rows, lanes), bf16),
            pltpu.VMEM((clips, pairs, rows, lanes), bf16),
            pltpu.VMEM((rows, half), bf16),
            pltpu.VMEM((8, width), f32),
            pltpu.SemaphoreType.DMA((clips, 3)),
            pltpu.SemaphoreType.DMA((clips, 3)),
            pltpu.SemaphoreType.DMA((clips, pairs)),
            pltpu.SemaphoreType.DMA((clips, pairs)),
            pltpu.SemaphoreType.DMA((clips, 5)),
            pltpu.SemaphoreType.DMA((3 * pairs,)),
        ],
        compiler_params=params(collective_id=0, has_side_effects=True),
        cost_estimate=pl.CostEstimate(
            flops=flops, bytes_accessed=40_000_000, transcendentals=clips * rows * keys * HEADS
        ),
        name="forward",
    )(kept, tokens, qkv_weight, *vectors, proj_weight, proj_bias, gain2, shift2)


def mlp_kernel(
    counts,
    kept_ref, n2_ref, middle_hbm, cot_ref, mixed_hbm, fc1_ref, b1_ref, fc2_ref, b2_ref, gain_ref, proj_hbm,
    out_ref, dfc1_ref, dfc2_ref, dproj_ref, db1_ref, small_ref, gmid_hbm, gmixed_hbm,
    middle_ref, mixed_ref, proj_ref, gmixed_ref, in_sems, out_sems,
    n2t_ref, grad_ref, out_acc, dn_acc, hidden_ref, dact_ref, active_ref, dhid_ref, biases,
):
    clips, slots, rows, tile = counts
    step = pl.program_id(0)
    width = n2_ref.shape[-1]
    chunk = fc1_ref.shape[-1]
    total = clips * rows

    def live_rows(clip, size):
        slot = lax.broadcasted_iota(jnp.int32, (size, 1), 0)
        return (slot < kept_ref[clip]).astype(f32)

    def loads():
        pairs = ((middle_hbm, middle_ref), (mixed_hbm, mixed_ref), (proj_hbm, proj_ref))
        return [pltpu.make_async_copy(src, dst, in_sems.at[i]) for i, (src, dst) in enumerate(pairs)]

    def stores(clip):
        at = pl.ds(pl.multiple_of(clip * rows, rows), rows)
        pairs = ((middle_ref, gmid_hbm), (gmixed_ref, gmixed_hbm))
        return [
            pltpu.make_async_copy(src.at[at], dst.at[at], out_sems.at[clip, i]) for i, (src, dst) in enumerate(pairs)
        ]

    @pl.when(step == 0)
    def start():
        for load in loads():
            load.start()
        n2t_ref[...] = n2_ref[...].T
        first = (slots // 16) * 16
        for clip in range(clips):
            begin = clip * rows
            grad_ref[begin + first : begin + rows] = jnp.zeros((rows - first, width), bf16)
            grad_ref[begin : begin + slots] = cot_ref[clip] * live_rows(clip, slots).astype(bf16)
        all_biases = row_of(b1_ref)
        for i in range(all_biases.shape[1] // chunk):
            biases[i : i + 1] = all_biases[:, i * chunk : (i + 1) * chunk]
        out_acc[...] = jnp.zeros_like(out_acc)
        dn_acc[...] = jnp.zeros_like(dn_acc)

    bias = biases[pl.ds(step, 1), :]
    hidden_ref[...] = dot(n2_ref[...], fc1_ref[...])
    dact_ref[...] = dot(grad_ref[...], fc2_ref[...], NT)
    sums = jnp.zeros((tile, chunk), f32)
    for begin in range(0, total, tile):
        at = slice(begin, begin + tile)
        hidden = hidden_ref[at] + bias
        cdf = 0.5 * (1.0 + lax.erf(hidden * (0.5 ** 0.5)))
        active_ref[at] = (hidden * cdf).astype(bf16)
        slope = cdf + hidden * (jnp.exp(-0.5 * hidden * hidden) * (1.0 / math.sqrt(2.0 * math.pi)))
        dhid = (dact_ref[at] * slope).astype(bf16)
        dhid_ref[at] = dhid
        sums = sums + dhid.astype(f32)
    db1_ref[...] = column_sums(sums)
    active = active_ref[...]
    dhid = dhid_ref[...]
    out_acc[...] += dot(active, fc2_ref[...])
    dn_acc[...] += dot(dhid, fc1_ref[...], NT)
    dfc1_ref[0] = dot(n2t_ref[...], dhid).astype(bf16)
    dfc2 = dot(active, grad_ref[...], TN).astype(bf16)
    half = width // 2
    dfc2_ref[0] = dfc2[:, :half]
    dfc2_ref[1] = dfc2[:, half:]

    @pl.when(step == pl.num_programs(0) - 1)
    def finish():
        for load in loads():
            load.wait()
        gain = row_of(gain_ref)
        bias2 = row_of(b2_ref)
        small_ref[...] = jnp.zeros_like(small_ref)

        def finish_clip(clip, carry):
            at = pl.ds(pl.multiple_of(clip * rows, rows), rows)
            middle = middle_ref[at]
            layer = middle + (out_acc[at] + bias2)
            out_ref[clip] = (live_rows(clip, slots) * layer[:slots]).astype(bf16)
            unit, inverse = center_scale(middle)
            grad = dn_acc[at]
            out_grad = grad_ref[at].astype(f32)
            gmid = out_grad + norm_back(unit, inverse, gain, grad)
            middle_ref[at] = gmid
            low = gmid.astype(bf16)
            dhid_ref[at, :width] = low
            gmixed_ref[at] = dot(low, proj_ref[...], NT).astype(bf16)
            small_ref[0:1] += column_sums(grad * unit)
            small_ref[1:2] += column_sums(grad)
            small_ref[2:3] += column_sums(out_grad)
            small_ref[3:4] += column_sums(low.astype(f32))
            for store in stores(clip):
                store.start()
            return carry

        lax.fori_loop(0, clips, finish_clip, 0)
        dproj = dot(mixed_ref[...], dhid_ref[:, :width], TN).astype(bf16)
        dproj_ref[0] = dproj[:, :half]
        dproj_ref[1] = dproj[:, half:]
        for clip in range(clips):
            for store in stores(clip):
                store.wait()


def mlp(kept, n2, middle, cot, mixed, fc1, b1, fc2, b2, gain, proj, rows):
    clips, slots, _ = cot.shape
    total, width = n2.shape
    hidden = fc1.shape[1]
    chunk = 768
    steps = hidden // chunk
    half = steps // 2
    tile = 16
    whole = lambda a: pl.BlockSpec(a.shape, lambda j: (0,) * a.ndim, pipeline_mode=one)
    anywhere = pl.BlockSpec(memory_space=pl.ANY)
    one = pl.Buffered(buffer_count=1)
    big = pl.BlockSpec((total, width), lambda j: (0, 0), pipeline_mode=one)
    return pl.pallas_call(
        functools.partial(mlp_kernel, (clips, slots, rows, tile)),
        grid=(steps,),
        in_specs=[
            pl.BlockSpec(memory_space=pltpu.SMEM),
            big, anywhere, whole(cot), anywhere,
            pl.BlockSpec((width, chunk), lambda j: (0, j)),
            whole(b1),
            pl.BlockSpec((chunk, width), lambda j: (j, 0)),
            whole(b2), whole(gain), anywhere,
        ],
        out_specs=[
            full((clips, slots, width)),
            pl.BlockSpec((1, width, chunk), lambda j: (j // half, 0, j % half)),
            pl.BlockSpec((2, chunk, width // 2), lambda j: (0, j, 0)),
            full((2, width, width // 2)),
            pl.BlockSpec((1, chunk), lambda j: (0, j)),
            full((8, width)),
            anywhere,
            anywhere,
        ],
        out_shape=[
            jax.ShapeDtypeStruct((clips, slots, width), bf16),
            jax.ShapeDtypeStruct((2, width, hidden // 2), bf16),
            jax.ShapeDtypeStruct((2, hidden, width // 2), bf16),
            jax.ShapeDtypeStruct((2, width, width // 2), bf16),
            jax.ShapeDtypeStruct((1, hidden), f32),
            jax.ShapeDtypeStruct((8, width), f32),
            jax.ShapeDtypeStruct((total, width), f32),
            jax.ShapeDtypeStruct((total, width), bf16),
        ],
        scratch_shapes=[
            pltpu.VMEM((total, width), f32),
            pltpu.VMEM((total, width), bf16),
            pltpu.VMEM((width, width), bf16),
            pltpu.VMEM((total, width), bf16),
            pltpu.SemaphoreType.DMA((3,)),
            pltpu.SemaphoreType.DMA((clips, 2)),
            pltpu.VMEM((width, total), bf16),
            pltpu.VMEM((total, width), bf16),
            pltpu.VMEM((total, width), f32),
            pltpu.VMEM((total, width), f32),
            pltpu.VMEM((total, chunk), f32),
            pltpu.VMEM((total, chunk), f32),
            pltpu.VMEM((total, chunk), bf16),
            pltpu.VMEM((total, chunk), bf16),
            pltpu.VMEM((8, chunk), f32),
        ],
        compiler_params=params(),
        cost_estimate=pl.CostEstimate(
            flops=12 * total * width * hidden, bytes_accessed=40_000_000, transcendentals=2 * total * hidden
        ),
        name="mlp",
    )(kept, n2, middle, cot, mixed, fc1, b1, fc2, b2, gain, proj)


def sum_arrays(width, hidden, clip_size):
    rows = width // clip_size
    tall = hidden // clip_size
    first, second = (0, 1, 2), (1, 0, 2)
    chunks = [("qkv", i, rows // 2, width // 2, order) for i, order in enumerate(QKV_ORDERS)]
    return [
        ("fc1", 0, rows, hidden // 4, first),
        ("fc2", 0, tall // 2, width // 2, second),
        ("fc1", hidden // 4, rows, hidden // 4, first),
        ("fc2", tall // 2, tall // 2, width // 2, second),
        ("proj", 0, rows, width // 2, PROJ_ORDER),
    ] + chunks


PROJ_ORDER = (1, 0, 2)
QKV_ORDERS = ((0, 1, 2), (0, 1, 2), (1, 0, 2))
SUM_STEPS = {
    2: [("end", 0, 0), ("start", 0, 1)],
    3: [("end", 1, 0), ("start", 1, 1)],
    4: [("end", 2, 0), ("end", 3, 0), ("end", 4, 0)],
    6: [("start", 2, 1)],
    7: [("end", 0, 1), ("start", 0, 2)],
    8: [("end", 1, 1), ("start", 3, 1)],
    9: [("start", 1, 2)],
    10: [("end", 0, 2), ("start", 0, 3), ("end", 2, 1)],
    11: [("start", 2, 2)],
    12: [("end", 1, 2), ("start", 1, 3), ("end", 3, 1), ("start", 3, 2)],
    13: [("end", 0, 3), ("start", 0, 4), ("start", 4, 1)],
    14: [("end", 2, 2), ("start", 2, 3)],
    15: [("end", 5, 0), ("start", 5, 1), ("end", 1, 3), ("start", 1, 4), ("end", 3, 2)],
    16: [("end", 0, 4), ("start", 0, 5), ("start", 3, 3)],
    17: [("end", 5, 1), ("start", 5, 2), ("end", 6, 0), ("start", 6, 1), ("end", 0, 5), ("end", 1, 4),
        ("start", 1, 5), ("end", 2, 3), ("start", 2, 4), ("end", 4, 1)],
    18: [("end", 7, 0), ("start", 7, 1), ("start", 4, 2)],
    19: [("end", 1, 5), ("vec", 0, 0), ("end", 3, 3), ("start", 3, 4), ("end", 5, 2), ("start", 5, 3),
        ("end", 6, 1), ("start", 6, 2), ("end", 7, 1), ("start", 7, 2), ("end", 4, 2),
        ("start", 4, 3), ("vec", 1, 0), ("input", 2, 0), ("end", 5, 3), ("start", 5, 4),
        ("end", 2, 4), ("start", 2, 5), ("end", 6, 2), ("start", 6, 3), ("end", 7, 2),
        ("start", 7, 3), ("end", 3, 4), ("start", 3, 5), ("end", 2, 5), ("vec", 2, 0), ("end", 4, 3),
        ("start", 4, 4), ("end", 5, 4), ("start", 5, 5), ("end", 3, 5), ("end", 6, 3),
        ("start", 6, 4), ("end", 5, 5), ("end", 7, 3), ("start", 7, 4), ("end", 4, 4),
        ("start", 4, 5), ("vec", 3, 0), ("end", 6, 4), ("start", 6, 5), ("end", 4, 5), ("end", 7, 4),
        ("start", 7, 5), ("end", 6, 5), ("vec", 4, 0), ("end", 7, 5)],
}


def backward_kernel(
    meta,
    q_ref, k_ref, v_ref, mask_ref, part_ref, lse_ref, normed_ref, weight_ref, near_ref, far_ref,
    tok_ref, gmid_ref, gain_ref,
    small_ref, db1_ref, gmixed_ref, dfc1_ref, dfc2_ref, dproj_ref,
    gtok_ref, fc1_out, fc2_out, proj_out, qkv_out, vec_out,
    *scratch,
):
    clips, slots, rows, bits, pairs, arrays = meta
    width = weight_ref.shape[0]
    half = width // 2
    lanes = 2 * DH
    step = pl.program_id(0)
    places = step_places(clips, pairs)
    mesh_id = pl.DeviceIdType.MESH
    count = len(arrays)

    scratch = list(scratch)
    take = lambda n: [scratch.pop(0) for _ in range(n)]
    (grad_all, packed, kv_acc, kv_send, kv_got, acc, dn_send, dn_got, dw_acc, bias_acc, vec_sum, vec_got) = take(12)
    own_bufs = dict(zip(("fc1", "fc2", "proj"), take(3)))
    dw_low = scratch.pop(0)
    stage_bufs = [take(bits + 1) for _ in arrays]
    vert_bufs = take(5)
    full_bufs = take(count)
    (grad_sem, grad_out, grad_in, kv_out, kv_in, dn_out, dn_in, sum_out, sum_in, own_sem, vec_out_sem, vec_in_sem) = take(12)

    core, vert, core_dev, vert_dev = freq_places()
    place = lax.axis_index("clip")
    bit_at = [(place // 2 ** b) % 2 for b in range(bits)]
    clip_dev = [{"clip": place + (1 - 2 * bit_at[b]) * 2 ** b} for b in range(bits)]

    def remote(src, dst, send, recv, device):
        return pltpu.make_async_remote_copy(
            src_ref=src, dst_ref=dst, send_sem=send, recv_sem=recv, device_id=device, device_id_type=mesh_id
        )

    def grad_own(clip):
        src = gmixed_ref.at[clip, :, lane_slice(vert * half, half)]
        return pltpu.make_async_copy(src, grad_all.at[0, clip], grad_sem.at[clip])

    def grad_vert(clip):
        src = gmixed_ref.at[clip, :, lane_slice((1 - vert) * half, half)]
        return remote(src, grad_all.at[1, clip], grad_out.at[clip], grad_in.at[clip], vert_dev)

    def kv_copy(clip, pair):
        return remote(
            kv_send.at[pair], kv_got.at[clip, pair], kv_out.at[clip, pair], kv_in.at[clip, pair], core_dev
        )

    def dn_copy(clip):
        return remote(dn_send.at[clip], dn_got.at[clip], dn_out.at[clip], dn_in.at[clip], vert_dev)

    every = (slice(None),) * bits

    def piece(a, who):
        name, at, r, width_a, _ = arrays[a]
        if name == "fc1":
            return dfc1_ref.at[(who,) + every + (slice(None), pl.ds(at, width_a))]
        if name == "fc2":
            return dfc2_ref.at[(who,) + every + (pl.ds(at, r), slice(None))]
        if name == "proj":
            return dproj_ref.at[who]
        return dw_low.at[at, who]

    def chosen(a, stage, index_of):
        order = arrays[a][4]
        left = [b for b in range(bits)[::-1] if b not in order[: stage - 1]]
        bit = order[stage - 1]
        at = (slice(None),) * left.index(bit) + (index_of(bit),)
        return stage_bufs[a][stage - 1].at[at]

    def stage_copy(a, stage):
        sems = (sum_out.at[a, stage], sum_in.at[a, stage])
        full, packed_array = full_bufs[a], arrays[a][0] == "qkv"
        if stage == 0:
            return remote(piece(a, 1 - core), stage_bufs[a][0], *sems, core_dev)
        if stage <= bits:
            src = chosen(a, stage, lambda bit: 1 - bit_at[bit])
            return remote(src, stage_bufs[a][stage], *sems, clip_dev[arrays[a][4][stage - 1]])
        if stage == bits + 1:
            dst = full.at[core, vert] if packed_array else vert_bufs[a]
            return remote(stage_bufs[a][bits], dst, *sems, vert_dev)
        return remote(full.at[core], full.at[core], *sems, core_dev)

    def own_copy(a):
        return pltpu.make_async_copy(piece(a, core), own_bufs[arrays[a][0]], own_sem.at[a])

    def add_blocks(dst, src, lead):
        if lead == 0:
            dst[...] = dst[...] + src[...]
            return

        def add_one(i, carry):
            at = tuple((i // 2 ** (lead - 1 - j)) % 2 for j in range(lead))
            dst[at] = dst[at] + src[at]
            return carry

        lax.fori_loop(0, 2 ** lead, add_one, 0)

    def stage_end(a, stage):
        name = arrays[a][0]
        stage_copy(a, stage).wait_recv()
        if stage == 0:
            if name == "qkv":
                add_blocks(stage_bufs[a][0], dw_low.at[arrays[a][1], core], bits)
            else:
                own_copy(a).wait()
                add_blocks(stage_bufs[a][0], own_bufs[name], bits)
                if a + 2 < 4:
                    own_copy(a + 2).start()
        elif stage <= bits:
            add_blocks(stage_bufs[a][stage], chosen(a, stage, lambda bit: bit_at[bit]), bits - stage)
            if stage == bits and name == "qkv":
                full_bufs[a][core, vert] = stage_bufs[a][bits][...]
        elif stage == bits + 1 and name != "qkv":
            full_bufs[a][core] = stage_bufs[a][bits][...] + vert_bufs[a][...]

    def vec_copy(hop):
        device = ([core_dev] + clip_dev + [vert_dev])[hop]
        return remote(vec_sum.at[hop], vec_got.at[hop], vec_out_sem.at[hop], vec_in_sem.at[hop], device)

    def vec_end(hop):
        vec_copy(hop).wait_recv()
        vec_sum[hop + 1] = vec_sum[hop] + vec_got[hop]
        if hop < bits + 1:
            vec_copy(hop + 1).start()

    def perform(action):
        kind, a, stage = action
        if kind == "vec":
            vec_end(a)
        elif kind == "start":
            stage_copy(a, stage).start()
        else:
            stage_end(a, stage)

    @pl.when(step == 0)
    def enter():
        barrier = pltpu.get_barrier_semaphore()
        for clip in range(clips):
            grad_own(clip).start()
        for device in [core_dev, vert_dev] + clip_dev:
            pl.semaphore_signal(barrier, inc=1, device_id=device, device_id_type=mesh_id)
        pl.semaphore_wait(barrier, 2 + bits)
        for clip in range(clips):
            grad_vert(clip).start()
        for a in range(5):
            stage_copy(a, 0).start()
        for a in (0, 1, 4):
            own_copy(a).start()
        vec_sum[0] = jnp.zeros_like(vec_sum[0])
        bias_acc[...] = jnp.zeros_like(bias_acc)
        dw_acc[...] = jnp.zeros_like(dw_acc)
        vec_sum[0, 4:8] = small_ref[0:4]
        for i in range(db1_ref.shape[1] // width):
            vec_sum[0, 8 + i : 9 + i] = db1_ref[0:1, i * width : (i + 1) * width]

    for at in sorted(SUM_STEPS):
        if at < places["end"]:
            @pl.when(step == at)
            def run(at=at):
                for action in SUM_STEPS[at]:
                    perform(action)

    def head_back(head, query, keys, values, grad, mixed, lse, live):
        own_query, own_grad = only(query, head), only(grad, head)
        scores = jnp.where(live, dot(own_query, keys, NT), MASKED)
        probs = jnp.exp(scores - lse[:, head * DH : head * DH + 1])
        delta = jnp.sum(only(grad.astype(f32) * mixed.astype(f32), head), axis=1, keepdims=True)
        dscores = (probs * (dot(own_grad, values, NT) - delta)).astype(bf16)
        return probs.astype(bf16), dscores, dot(dscores, keys)

    def join_heads(dqs):
        first = own_lanes(dqs[0].shape, 0)
        return (jnp.where(first, dqs[0], dqs[1]) * DH ** -0.5).astype(bf16)

    def send_pair(clip, pair, dk, dv):
        for part, value in enumerate((dk, dv)):
            low = value.astype(bf16)
            packed[clip, :, lane_slice((3 * pair + part + 1) * lanes, lanes)] = low[: 2 * rows]
            kv_send[pair, part] = low[2 * rows :]
        kv_copy(clip, pair).start()

    clip_now, slot_now, pair_now = attention_unit(step, places, clips, pairs)

    def attend_single():
        clip, slot, pair = 0, slot_now, pair_now

        @pl.when((pair == 0) & (slot == 0))
        def own_grads():
            grad_own(clip).wait()

        @pl.when((pair == 0) & (slot == 1))
        def vert_grads():
            grad_vert(clip).wait_recv()

        at = pl.ds(pl.multiple_of(slot * rows, rows), rows)
        query, keys, values, live = q_ref[0, at], k_ref[0], v_ref[0], mask_ref[0] > 0.5
        grad = grad_all[slot, clip, :, lane_slice(pair * lanes, lanes)]
        dqs, dk, dv = [], 0.0, 0.0
        for head in range(2):
            probs, dscores, dq = head_back(head, query, keys, values, grad, part_ref[0, at], lse_ref[0, at], live)
            dqs.append(dq)
            dk = dk + dot(dscores, only(query, head), TN)
            dv = dv + dot(probs, only(grad, head), TN)
        packed[clip, at, lane_slice(3 * pair * lanes, lanes)] = join_heads(dqs)

        @pl.when(slot == 0)
        def keep():
            kv_acc[pair, 0] = dk
            kv_acc[pair, 1] = dv

        @pl.when(slot == 1)
        def send():
            send_pair(clip, pair, kv_acc[pair, 0] + dk, kv_acc[pair, 1] + dv)

    def attend_double():
        clip, pair = clip_now, pair_now

        @pl.when(pair == 0)
        def grads():
            grad_own(clip).wait()
            grad_vert(clip).wait_recv()

        kv_copy(clip - 1, pair).wait_send()
        keys, values, live = k_ref[0], v_ref[0], mask_ref[0] > 0.5
        here = lane_slice(pair * lanes, lanes)
        query = q_ref[0]
        grad = jnp.concatenate([grad_all[0, clip, :, here], grad_all[1, clip, :, here]], axis=0)
        dqs, dk, dv = [[], []], 0.0, 0.0
        for head in range(2):
            parts = []
            for slot in range(2):
                at = slice(slot * rows, (slot + 1) * rows)
                parts.append(
                    head_back(head, query[at], keys, values, grad[at], part_ref[0, at], lse_ref[0, at], live)
                )
                dqs[slot].append(parts[slot][2])
            probs, dscores = [jnp.concatenate([parts[0][i], parts[1][i]], axis=0) for i in range(2)]
            dk = dk + dot(dscores, only(query, head), TN)
            dv = dv + dot(probs, only(grad, head), TN)
        for slot in range(2):
            at = slice(slot * rows, (slot + 1) * rows)
            packed[clip, at, lane_slice(3 * pair * lanes, lanes)] = join_heads(dqs[slot])
        send_pair(clip, pair, dk, dv)

    is_attention = step < places["projections"][-1]
    for at in places["pauses"]:
        is_attention = is_attention & (step != at)
    pl.when(step < 2 * pairs)(attend_single)
    pl.when(is_attention & (step >= 2 * pairs))(attend_double)

    def take_pair(clip, pair):
        kv_copy(clip, pair).wait_recv()
        for part in range(2):
            at = lane_slice((3 * pair + part + 1) * lanes, lanes)
            packed[clip, :, at] = packed[clip, :, at] + kv_got[clip, pair, part]
        at = lane_slice(pair * lanes, lanes)
        for row, part in ((0, 0), (1, 2)):
            value = packed[clip, :, lane_slice((3 * pair + part) * lanes, lanes)]
            bias_acc[row : row + 1, at] += column_sums(value.astype(f32))

    def norm_sums(clip, back):
        near, _ = center_scale(near_ref[0].astype(f32))
        far, _ = center_scale(far_ref[0].astype(f32))
        vec_sum[0, 0:1] += column_sums(back[:slots] * near) + column_sums(back[rows:] * far)
        vec_sum[0, 1:2] += column_sums(back)

    def give_back(clip, back):
        acc[clip] = back[:rows]
        dn_send[clip] = back[rows:].astype(bf16)
        dn_copy(clip).start()

    def last_chunk(pair):
        at = lane_slice(3 * pair * lanes, 3 * lanes)
        more = dot(normed_ref[0], packed[clips - 1, :, at], TN)
        low = (dw_acc[:, at] + more).astype(bf16)
        r = arrays[5][2]
        for block in range(2 ** bits):
            index = tuple((block >> b) & 1 for b in range(bits)[::-1])
            for who in range(2):
                start = (2 * block + who) * r
                dw_low[(pair, who) + index] = low[start : start + r]

    early_steps = places["projections"][:-1]
    early = functools.reduce(jnp.logical_or, [step == at for at in early_steps])

    @pl.when(early)
    def projections():
        clip = sum((step > at).astype(jnp.int32) for at in early_steps)

        def take_one(pair, carry):
            take_pair(clip, pair)
            return carry

        lax.fori_loop(0, pairs, take_one, 0)
        grads = packed[clip]
        back = dot(grads, weight_ref[...], NT)
        give_back(clip, back)
        dw_acc[...] += dot(normed_ref[0], grads, TN)
        norm_sums(clip, back)

    chunk_steps = places["chunks"]

    @pl.when(functools.reduce(jnp.logical_or, [step == at for at in chunk_steps]))
    def chunk():
        pair = sum((step > at).astype(jnp.int32) for at in chunk_steps)
        take_pair(clips - 1, pair)
        last_chunk(pair)

    for pair in range(pairs - 1):
        @pl.when(step == chunk_steps[pair])
        def send_chunk(pair=pair):
            stage_copy(5 + pair, 0).start()

    @pl.when(step == places["projections"][-1])
    def last_projections():
        clip = clips - 1
        before = 3 * (pairs - 1) * lanes
        back = dot(packed[clip, :, :before], weight_ref[:, :before], NT)
        take_pair(clip, pairs - 1)
        last_chunk(pairs - 1)
        stage_copy(4 + pairs, 0).start()
        back = back + dot(packed[clip, :, before:], weight_ref[:, before:], NT)
        give_back(clip, back)
        norm_sums(clip, back)
        mine = lane_slice(vert * half, half)
        vec_sum[0, 2:3, mine] = bias_acc[0:1]
        vec_sum[0, 3:4, mine] = bias_acc[1:2]
        vec_copy(0).start()

    def inputs(clip):
        dn_copy(clip).wait_recv()
        grad = acc[clip] + dn_got[clip].astype(f32)
        unit, inverse = center_scale(tok_ref[0].astype(f32))
        result = gmid_ref[0][:slots] + norm_back(unit, inverse, row_of(gain_ref), grad[:slots])
        gtok_ref[0] = result

    @pl.when((step >= places["inputs"]) & (step < places["end"]))
    def early_inputs():
        inputs(step - places["inputs"])

    @pl.when(step == places["end"])
    def finish():
        for kind, a, stage in SUM_STEPS[places["end"]]:
            if kind == "input":
                inputs(clips - 1)
            else:
                perform((kind, a, stage))
        for a, (name, at, r, width_a, _) in enumerate(arrays):
            for who in range(2):
                full = full_bufs[a]
                if name == "fc1":
                    start = who * fc1_out.shape[1] // 2 + at
                    fc1_out[:, start : start + width_a] = full[who]
                elif name == "fc2":
                    fc2_out[at : at + r, who * width_a : (who + 1) * width_a] = full[who]
                elif name == "proj":
                    proj_out[:, who * width_a : (who + 1) * width_a] = full[who]
                else:
                    for side in range(2):
                        for part in range(3):
                            to = part * width + side * half + at * lanes
                            value = full[who, side, :, part * lanes : (part + 1) * lanes]
                            qkv_out[who * r : (who + 1) * r, to : to + lanes] = value
        vec_out[...] = vec_sum[bits + 2]
        for a in range(count):
            for stage in range(bits + 3):
                stage_copy(a, stage).wait_send()
        for clip in range(clips):
            grad_vert(clip).wait_send()
            dn_copy(clip).wait_send()
        for pair in range(pairs):
            kv_copy(clips - 1, pair).wait_send()
        for hop in range(bits + 2):
            vec_copy(hop).wait_send()


def step_places(clips, pairs):
    plan = ["attend"] * (2 * pairs)
    for clip in range(1, clips):
        for pair in range(pairs):
            plan.append("attend")
            if pair == 0:
                plan.append("project")
            elif clip == clips - 1:
                plan.append("chunk")
    projections = [i for i, kind in enumerate(plan) if kind == "project"] + [len(plan)]
    chunks = [i for i, kind in enumerate(plan) if kind == "chunk"]
    inputs = len(plan) + 1
    pauses = projections[:-1] + chunks
    return {"projections": projections, "chunks": chunks, "pauses": pauses, "inputs": inputs, "end": inputs + clips - 1}


def attention_unit(step, places, clips, pairs):
    index = step
    for at in places["pauses"]:
        index = index - (step > at).astype(jnp.int32)
    index = jnp.minimum(index, (clips + 1) * pairs - 1)
    slot = jnp.where(index < 2 * pairs, index // pairs, 0)
    clip = jnp.maximum(index // pairs - 1, 0)
    return clip, slot, index % pairs


def backward(q, k, v, mask, part, lse, normed, weight_half, tokens, far, gmid, gain, small, db1, gmixed,
             dfc1, dfc2, dproj, clip_size):
    clips, slots, width = tokens.shape
    rows = gmid.shape[1]
    half = width // 2
    keys = k.shape[1]
    pairs = HEADS // 4
    lanes = 2 * DH
    bits = clip_size.bit_length() - 1
    hidden = db1.shape[1]
    arrays = sum_arrays(width, hidden, clip_size)
    places = step_places(clips, pairs)
    one = pl.Buffered(buffer_count=1)

    def of_pair(s):
        clip, _, pair = attention_unit(s, places, clips, pairs)
        return clip, 0, pair

    def of_projection(s):
        index = s * 0
        for at in places["projections"][:-1]:
            index = index + (s > at).astype(jnp.int32)
        return index, 0, 0

    def of_clip(s):
        return jnp.clip(s - places["inputs"], 0, clips - 1), 0, 0

    fixed = lambda shape: pl.BlockSpec(shape, lambda s: (0,) * len(shape), pipeline_mode=one)
    tok_pair = pl.BlockSpec((1, 2 * rows, lanes), of_pair)
    key_pair = pl.BlockSpec((1, keys, lanes), of_pair)
    anywhere = pl.BlockSpec(memory_space=pl.ANY)
    blocks = (2,) * bits
    r_fc1, r_fc2 = width // clip_size, hidden // clip_size
    dfc1 = dfc1.reshape((2,) + blocks + (r_fc1, hidden // 2))
    dfc2 = dfc2.reshape((2,) + blocks + (r_fc2, half))
    dproj = dproj.reshape((2,) + blocks + (r_fc1, half))
    vmem = lambda *shape: pltpu.VMEM(shape, bf16)
    wide = lambda *shape: pltpu.VMEM(shape, f32)
    scratch = [
        vmem(2, clips, rows, half),
        vmem(clips, 2 * rows, 3 * half),
        wide(pairs, 2, keys, lanes),
        vmem(pairs, 2, 2 * rows, lanes),
        vmem(clips, pairs, 2, 2 * rows, lanes),
        wide(clips, rows, width),
        vmem(clips, rows, width),
        vmem(clips, rows, width),
        wide(width, 3 * half),
        wide(8, half),
        wide(bits + 3, 16, width),
        wide(bits + 2, 16, width),
        vmem(*blocks, r_fc1, hidden // 4),
        vmem(*blocks, r_fc2 // 2, half),
        vmem(*blocks, r_fc1, half),
    ]
    scratch.append(vmem(pairs, 2, *blocks, r_fc1 // 2, half))
    for _, _, r, w, _ in arrays:
        scratch += [vmem(*((2,) * (bits - stage)), r, w) for stage in range(bits + 1)]
    scratch += [vmem(r, w) for name, _, r, w, _ in arrays if name != "qkv"]
    scratch += [vmem(2, 2, r, w) if name == "qkv" else vmem(2, r, w) for name, _, r, w, _ in arrays]
    dma = lambda *shape: pltpu.SemaphoreType.DMA(shape)
    count = len(arrays)
    scratch += [
        dma(clips), dma(clips), dma(clips), dma(clips, pairs), dma(clips, pairs), dma(clips), dma(clips),
        dma(count, bits + 3), dma(count, bits + 3), dma(count), dma(bits + 2), dma(bits + 2),
    ]
    shape = jax.ShapeDtypeStruct
    return pl.pallas_call(
        functools.partial(backward_kernel, (clips, slots, rows, bits, pairs, arrays)),
        grid=(places["end"] + 1,),
        in_specs=[
            tok_pair, key_pair, key_pair,
            pl.BlockSpec((1, 1, keys), lambda s: (of_pair(s)[0], 0, 0)),
            tok_pair, tok_pair,
            pl.BlockSpec((1, 2 * rows, width), of_projection),
            fixed(weight_half.shape),
            pl.BlockSpec((1, slots, width), of_projection, pipeline_mode=one),
            pl.BlockSpec((1, rows, width), of_projection, pipeline_mode=one),
            pl.BlockSpec((1, slots, width), of_clip),
            pl.BlockSpec((1, rows, width), of_clip),
            fixed((width,)), fixed((8, width)), fixed((1, hidden)),
            anywhere, anywhere, anywhere, anywhere,
        ],
        out_specs=[
            pl.BlockSpec((1, slots, width), of_clip),
            fixed((r_fc1, hidden)), fixed((r_fc2, width)), fixed((r_fc1, width)),
            fixed((r_fc1, 3 * width)), fixed((16, width)),
        ],
        out_shape=[
            shape((clips, slots, width), f32),
            shape((r_fc1, hidden), bf16),
            shape((r_fc2, width), bf16),
            shape((r_fc1, width), bf16),
            shape((r_fc1, 3 * width), bf16),
            shape((16, width), f32),
        ],
        scratch_shapes=scratch,
        compiler_params=pltpu.CompilerParams(
            vmem_limit_bytes=63 * 1024 * 1024, collective_id=1, has_side_effects=True
        ),
        cost_estimate=pl.CostEstimate(
            flops=2 * clips * rows * (5 * keys * width + 6 * width * width),
            bytes_accessed=60_000_000,
            transcendentals=clips * rows * keys * HEADS,
        ),
        name="backward",
    )(q, k, v, mask, part, lse, normed, weight_half, tokens, far, tokens, gmid, gain, small, db1, gmixed, dfc1, dfc2, dproj)


def outputs_kernel(fc1, fc2, proj, qkv, vec, gtok, fc1_out, fc2_out, proj_out, qkv_out, gtok_out, db1_out, *outs):
    gtok_out[...] = gtok[...]
    for src, dst in ((fc1, fc1_out), (fc2, fc2_out), (proj, proj_out), (qkv, qkv_out)):
        dst[...] = src[...].astype(f32)

    @pl.when(pl.program_id(0) == 0)
    def others():
        width = vec.shape[1]
        for i, dst in enumerate(outs):
            dst[...] = vec[i : i + 1].reshape(width)
        tall = db1_out.shape[0] // width
        db1_out[...] = jnp.concatenate([vec[8 + i : 9 + i] for i in range(tall)], axis=1).reshape(db1_out.shape[0])


def final_outputs(low_fc1, low_fc2, low_proj, low_qkv, summed, gtok, hidden):
    width = summed.shape[1]
    steps = gtok.shape[0]
    one = pl.Buffered(buffer_count=1)
    fixed = lambda shape: pl.BlockSpec(shape, lambda c: (0,) * len(shape), pipeline_mode=one)
    by_clip = pl.BlockSpec((1,) + gtok.shape[1:], lambda c: (c, 0, 0))
    shape = jax.ShapeDtypeStruct
    lows = (low_fc1, low_fc2, low_proj, low_qkv)

    def by_rows(a):
        if a.shape[0] % (16 * steps):
            return fixed(a.shape)
        return pl.BlockSpec((a.shape[0] // steps, a.shape[1]), lambda c: (c, 0))

    return pl.pallas_call(
        outputs_kernel,
        grid=(steps,),
        in_specs=[by_rows(a) for a in lows] + [fixed(summed.shape), by_clip],
        out_specs=[by_rows(a) for a in lows] + [by_clip, fixed((hidden,))] + [fixed((width,))] * 8,
        out_shape=[shape(a.shape, f32) for a in lows]
        + [shape(gtok.shape, f32), shape((hidden,), f32)]
        + [shape((width,), f32)] * 8,
        compiler_params=params(),
        name="final_outputs",
    )(*lows, summed, gtok)


def partner(kind):
    index = lax.axis_index("freq")
    if kind == "vert":
        return {"freq": (index + 2) % 4}
    return {"freq": index + 1 - 2 * (index % 2)}


def whole_forward_kernel(
    counts,
    tok_ref, qkv_ref, qb_ref, vb_ref, gain_ref, shift_ref, proj_ref, pb_ref, gain2_ref, shift2_ref,
    q_ref, k_ref, v_ref, normed_ref, mixed_ref, lse_ref, middle_ref, normed2_ref, mask_ref,
    held, send_sem, recv_sem,
):
    clips, slots, rows = counts
    clip = pl.program_id(0)
    pair = pl.program_id(1)
    width = tok_ref.shape[-1]

    def copy(kind, index):
        at = {"vert": 0, "core": 1, "diag": 2}[kind]
        return pltpu.make_async_remote_copy(
            src_ref=held.at[index, 0] if kind == "diag" else tok_ref.at[index],
            dst_ref=held.at[index, at],
            send_sem=send_sem.at[index, at],
            recv_sem=recv_sem.at[index, at],
            device_id=partner(kind),
            device_id_type=pl.DeviceIdType.MESH,
        )

    def project(slot, source):
        unit, _ = center_scale(source.astype(f32))
        normed = (unit * gain_ref[...] + shift_ref[...]).astype(bf16)
        if slot == 0:
            normed_ref[0] = normed
            query = (dot(normed, qkv_ref[:, :width]) + qb_ref[...]).astype(bf16)
            q_ref[0] = query * jnp.asarray(DH ** -0.5, bf16)
        both = dot(normed, qkv_ref[:, width:])
        k_ref[0, slot * rows : (slot + 1) * rows] = both[:, :width].astype(bf16)
        v_ref[0, slot * rows : (slot + 1) * rows] = (both[:, width:] + vb_ref[...]).astype(bf16)
        first = (slots // 16) * 16
        kept = source[first:].astype(f32)[slots - first : slots - first + 1, 0:1] + slots // 2
        lane = lax.broadcasted_iota(jnp.int32, (1, rows), 1).astype(f32)
        return (lane < kept).astype(f32)

    @pl.when((clip == 0) & (pair == 0))
    def enter():
        barrier = pltpu.get_barrier_semaphore()
        for kind in ("vert", "core"):
            pl.semaphore_signal(
                barrier, inc=1, device_id=partner(kind), device_id_type=pl.DeviceIdType.MESH
            )
        pl.semaphore_wait(barrier, 2)
        copy("vert", 0).start()
        for index in range(clips):
            copy("core", index).start()

    def pass_on(index):
        copy("vert", index).wait_recv()
        copy("diag", index).start()
        copy("vert", index).wait_send()

        @pl.when(index + 1 < clips)
        def more():
            copy("vert", index + 1).start()

    @pl.when(pair == 0)
    def project_all():
        live_own = project(0, tok_ref[clip])
        copy("core", clip).wait_recv()
        live_core = project(2, held[clip, 1])

        @pl.when(clip == 0)
        def first_pass():
            pass_on(clip)

        live_vert = project(1, held[clip, 0])
        copy("diag", clip).wait_recv()
        live_diag = project(3, held[clip, 2])
        mask_ref[0] = jnp.concatenate([live_own, live_vert, live_core, live_diag], axis=1)

    @pl.when((pair == 3) & (clip + 1 < clips))
    def next_pass():
        pass_on(clip + 1)

    lanes = pl.ds(pl.multiple_of(pair * 2 * DH, 2 * DH), 2 * DH)
    query = q_ref[0, :, lanes]
    keys = k_ref[0, :, lanes]
    values = v_ref[0, :, lanes]
    live = mask_ref[0] > 0.5
    outs, lses = [], []
    for head in range(2):
        scores = jnp.where(live, dot(only(query, head), keys, NT), MASKED)
        top = jnp.max(scores, axis=1, keepdims=True)
        exps = jnp.exp(scores - top)
        total = jnp.sum(exps, axis=1, keepdims=True)
        outs.append(dot(exps.astype(bf16), values) / total)
        lses.append(top + jnp.log(total))
    first = own_lanes(outs[0].shape, 0)
    mixed_ref[0, :, lanes] = jnp.where(first, outs[0], outs[1]).astype(bf16)
    lse_ref[0, :, lanes] = jnp.where(first, lses[0], lses[1])

    @pl.when(pair == pl.num_programs(1) - 1)
    def finish():
        middle = tok_ref[clip].astype(f32) + (dot(mixed_ref[0], proj_ref[...]) + pb_ref[...])
        middle_ref[0] = middle
        unit, _ = center_scale(middle)
        normed2_ref[0] = (unit * gain2_ref[...] + shift2_ref[...]).astype(bf16)
        copy("core", clip).wait_send()
        copy("diag", clip).wait_send()


def whole_forward(tok, slots, qkv_weight, vectors, proj_weight):
    clips, rows, width = tok.shape
    keys = 4 * rows
    pairs = HEADS // 2
    query_bias, value_bias, gain, shift, proj_bias, gain2, shift2 = vectors
    one = pl.Buffered(buffer_count=1)
    row = full((1, width))
    block = lambda n: pl.BlockSpec((1, n, width), lambda c, p: (c, 0, 0))
    flops = 2 * clips * (10 * rows * width * width + 2 * rows * keys * width)
    weight = lambda w: pl.BlockSpec(w.shape, lambda c, p: (0, 0), pipeline_mode=one)
    return pl.pallas_call(
        functools.partial(whole_forward_kernel, (clips, slots, rows)),
        grid=(clips, pairs),
        in_specs=[
            pl.BlockSpec(tok.shape, lambda c, p: (0, 0, 0), pipeline_mode=one),
            weight(qkv_weight), row, row, row, row, weight(proj_weight), row, row, row,
        ],
        out_specs=[block(rows), block(keys), block(keys)] + [block(rows)] * 5
        + [pl.BlockSpec((1, 1, keys), lambda c, p: (c, 0, 0))],
        out_shape=[
            jax.ShapeDtypeStruct((clips, rows, width), bf16),
            jax.ShapeDtypeStruct((clips, keys, width), bf16),
            jax.ShapeDtypeStruct((clips, keys, width), bf16),
            jax.ShapeDtypeStruct((clips, rows, width), bf16),
            jax.ShapeDtypeStruct((clips, rows, width), bf16),
            jax.ShapeDtypeStruct((clips, rows, width), f32),
            jax.ShapeDtypeStruct((clips, rows, width), f32),
            jax.ShapeDtypeStruct((clips, rows, width), bf16),
            jax.ShapeDtypeStruct((clips, 1, keys), f32),
        ],
        scratch_shapes=[
            pltpu.VMEM((clips, 3, rows, width), bf16),
            pltpu.SemaphoreType.DMA((clips, 3)),
            pltpu.SemaphoreType.DMA((clips, 3)),
        ],
        compiler_params=params(collective_id=0, has_side_effects=True),
        cost_estimate=pl.CostEstimate(
            flops=flops, bytes_accessed=40_000_000, transcendentals=clips * rows * keys * HEADS
        ),
        name="whole_forward",
    )(tok, qkv_weight, query_bias, value_bias, gain, shift, proj_weight, proj_bias, gain2, shift2)


def attend_back_kernel(q_ref, k_ref, v_ref, mask_ref, mixed_ref, lse_ref, grad_ref,
                       dq_ref, dkeep_ref, dsend_ref):
    query = q_ref[0]
    keys = k_ref[0]
    values = v_ref[0]
    grad = grad_ref[0]
    live = mask_ref[0] > 0.5
    product = grad.astype(f32) * mixed_ref[0].astype(f32)
    dqs, dk, dv = [], None, None
    for head in range(2):
        own_query = only(query, head)
        own_grad = only(grad, head)
        scores = jnp.where(live, dot(own_query, keys, NT), MASKED)
        probs = jnp.exp(scores - lse_ref[0, :, head * DH : head * DH + 1])
        delta = jnp.sum(only(product, head), axis=1, keepdims=True)
        dscores = (probs * (dot(own_grad, values, NT) - delta)).astype(bf16)
        dqs.append(dot(dscores, keys))
        more_k = dot(dscores, own_query, TN)
        more_v = dot(probs.astype(bf16), own_grad, TN)
        dk = more_k if dk is None else dk + more_k
        dv = more_v if dv is None else dv + more_v
    first = own_lanes(dqs[0].shape, 0)
    dq_ref[0] = (jnp.where(first, dqs[0], dqs[1]) * DH ** -0.5).astype(bf16)
    half = dk.shape[0] // 2
    dkeep_ref[0, 0] = dk[:half].astype(bf16)
    dkeep_ref[1, 0] = dv[:half].astype(bf16)
    dsend_ref[0, 0] = dk[half:].astype(bf16)
    dsend_ref[1, 0] = dv[half:].astype(bf16)


def attend_back(q, k, v, mask, mixed, lse, grad, first_pair, pairs):
    clips, rows, _ = q.shape
    keys = k.shape[1]
    lanes = 2 * DH
    tok = pl.BlockSpec((1, rows, lanes), lambda c, p: (c, 0, first_pair + p))
    key = pl.BlockSpec((1, keys, lanes), lambda c, p: (c, 0, first_pair + p))
    part = pl.BlockSpec((2, 1, keys // 2, lanes), lambda c, p: (0, c, 0, p))
    return pl.pallas_call(
        attend_back_kernel,
        grid=(clips, pairs),
        in_specs=[tok, key, key, pl.BlockSpec((1, 1, keys), lambda c, p: (c, 0, 0)), tok, tok, tok],
        out_specs=[pl.BlockSpec((1, rows, lanes), lambda c, p: (c, 0, p)), part, part],
        out_shape=[
            jax.ShapeDtypeStruct((clips, rows, pairs * lanes), bf16),
            jax.ShapeDtypeStruct((2, clips, keys // 2, pairs * lanes), bf16),
            jax.ShapeDtypeStruct((2, clips, keys // 2, pairs * lanes), bf16),
        ],
        compiler_params=params(),
        cost_estimate=pl.CostEstimate(
            flops=4 * 10 * clips * rows * keys * pairs * lanes,
            bytes_accessed=clips * pairs * lanes * (keys * 10 + rows * 12),
            transcendentals=clips * rows * keys * 2 * pairs,
        ),
        name="attend_back",
    )(q, k, v, mask, mixed, lse, grad)


def weight_kernel(normed_ref, dq_ref, dk0_ref, dk1_ref, dk2_ref, out_ref, dkv_ref, sums_ref):
    part = pl.program_id(0)
    @pl.when(part == 0)
    def query():
        grad = dq_ref[...]
        out_ref[0] = dot(normed_ref[...], grad, TN).astype(bf16)
        sums_ref[0] = column_sums(grad.astype(f32))
        dkv_ref[0] = jnp.zeros_like(dkv_ref[0])

    @pl.when(part > 0)
    def other():
        grad = (dk0_ref[0].astype(f32) + dk1_ref[0].astype(f32) + dk2_ref[0].astype(f32)).astype(bf16)
        dkv_ref[0] = grad
        out_ref[0] = dot(normed_ref[...], grad, TN).astype(bf16)
        sums_ref[0] = column_sums(grad.astype(f32))


def weight_grads(normed, dq, parts):
    total, width = normed.shape
    lanes = dq.shape[1]
    before = lambda j: (jnp.maximum(j - 1, 0), 0, 0)
    part = pl.BlockSpec((1, total, lanes), before)
    return pl.pallas_call(
        weight_kernel,
        grid=(3,),
        in_specs=[full((total, width)), full((total, lanes)), part, part, part],
        out_specs=[
            pl.BlockSpec((1, width, lanes), lambda j: (j, 0, 0)),
            part,
            pl.BlockSpec((1, 1, lanes), lambda j: (j, 0, 0)),
        ],
        out_shape=[
            jax.ShapeDtypeStruct((3, width, lanes), bf16),
            jax.ShapeDtypeStruct((2, total, lanes), bf16),
            jax.ShapeDtypeStruct((3, 1, lanes), f32),
        ],
        compiler_params=params(),
        cost_estimate=pl.CostEstimate(
            flops=6 * total * width * lanes, bytes_accessed=8_000_000, transcendentals=0
        ),
        name="weight_grads",
    )(normed, dq, *parts)


def input_kernel(counts, groups, *refs):
    clips, slots, rows = counts
    dqs = refs[:groups]
    dkvs = refs[groups : 2 * groups]
    qkv_ref, tok_ref, gmid_ref, gain_ref, shift_ref, out_ref, small_ref = refs[2 * groups :]
    clip = pl.program_id(0)
    width = tok_ref.shape[-1]
    lanes = width // groups
    grad = None
    for group in range(groups):
        for part in range(3):
            rows_grad = dqs[group][0] if part == 0 else dkvs[group][part - 1]
            at = part * width + group * lanes
            more = dot(rows_grad, qkv_ref[:, at : at + lanes], NT)
            grad = more if grad is None else grad + more
    unit, inverse = center_scale(tok_ref[0].astype(f32))
    result = gmid_ref[0] + norm_back(unit, inverse, gain_ref[...], grad)
    out_ref[0] = result[:slots]

    @pl.when(clip == 0)
    def start():
        small_ref[...] = jnp.zeros_like(small_ref)

    small_ref[0:1] += column_sums(grad * unit)
    small_ref[1:2] += column_sums(grad)


def input_grads(dqs, dkvs, qkv_weight, tokens, gmid, gain, shift, slots):
    clips, rows, width = tokens.shape
    groups = len(dqs)
    lanes = width // groups
    tok = pl.BlockSpec((1, rows, width), lambda c: (c, 0, 0))
    return pl.pallas_call(
        functools.partial(input_kernel, (clips, slots, rows), groups),
        grid=(clips,),
        in_specs=[pl.BlockSpec((1, rows, lanes), lambda c: (c, 0, 0))] * groups
        + [pl.BlockSpec((2, rows, lanes), lambda c: (0, c, 0))] * groups
        + [full(qkv_weight.shape), tok, tok, full((1, width)), full((1, width))],
        out_specs=[pl.BlockSpec((1, slots, width), lambda c: (c, 0, 0)), full((8, width))],
        out_shape=[
            jax.ShapeDtypeStruct((clips, slots, width), f32),
            jax.ShapeDtypeStruct((8, width), f32),
        ],
        compiler_params=params(),
        cost_estimate=pl.CostEstimate(
            flops=6 * clips * rows * width * width, bytes_accessed=16_000_000, transcendentals=0
        ),
        name="input_grads",
    )(*dqs, *dkvs, qkv_weight, tokens, gmid, gain, shift)


def swap_bit(array, axis, size, bit):
    return lax.ppermute(array, axis, [(i, i ^ (1 << bit)) for i in range(size)])


def add_low(left, right):
    return (left.astype(f32) + right.astype(f32)).astype(bf16)


def pick(array, index, dim):
    return lax.dynamic_index_in_dim(array, index, dim, keepdims=False)


def bit_of(axis, bit):
    return (lax.axis_index(axis) >> bit) & 1


def scatter_sum(split, clip_size, order):
    core = bit_of("freq", 0)
    vert = bit_of("freq", 1)
    bits = clip_size.bit_length() - 1
    lanes = split.shape[-1]
    value = add_low(pick(split, core, 0), swap_bit(pick(split, 1 - core, 0), "freq", 4, 0))
    rows = value.shape[0] // (2 * clip_size)
    value = value.reshape((2,) * bits + (2, rows, lanes))
    left = list(range(bits))[::-1]
    for bit in order:
        at = left.index(bit)
        mine = bit_of("clip", bit)
        value = add_low(
            pick(value, mine, at), swap_bit(pick(value, 1 - mine, at), "clip", clip_size, bit)
        )
        left.remove(bit)
    return add_low(pick(value, vert, 0), swap_bit(pick(value, 1 - vert, 0), "freq", 4, 1))


def gather_low(part):
    core = bit_of("freq", 0)
    vert = bit_of("freq", 1)
    other = swap_bit(part, "freq", 4, 1)
    tall = jnp.where(vert == 0, jnp.concatenate([part, other]), jnp.concatenate([other, part]))
    side = swap_bit(tall, "freq", 4, 0)
    return jnp.where(
        core == 0,
        jnp.concatenate([tall, side], axis=1),
        jnp.concatenate([side, tall], axis=1),
    ).astype(f32)


def total_sum(array, clip_size):
    for bit in range(2):
        array = array + swap_bit(array, "freq", 4, bit)
    for bit in range(clip_size.bit_length() - 1):
        array = array + swap_bit(array, "clip", clip_size, bit)
    return array


def on_device_plain(
    clip_size, tokens, kept_counts, attn_gain, attn_shift, qkv_weight, query_bias, value_bias,
    proj_weight, proj_bias, mlp_gain, mlp_shift, fc1_weight, fc1_bias, fc2_weight, fc2_bias, cotangent,
):
    clips, slots, width = tokens.shape
    rows = -(-slots // 16) * 16
    total = clips * rows
    bits = clip_size.bit_length() - 1
    forward_order = list(range(bits))
    second_order = forward_order[1:2] + forward_order[:1] + forward_order[2:]
    vec = lambda v: v.astype(f32)[None, :]
    kept = (kept_counts - slots // 2).astype(bf16)
    tok = jnp.concatenate(
        [tokens, jnp.broadcast_to(kept[:, :, None], (clips, rows - slots, width))], axis=1
    )
    vectors = [vec(v) for v in (query_bias, value_bias, attn_gain, attn_shift, proj_bias, mlp_gain, mlp_shift)]
    q, k, v, normed, mixed, lse, middle, normed2, mask = whole_forward(
        tok, slots, qkv_weight, vectors, proj_weight
    )
    flat = lambda a: a.reshape(total, width)
    layer_out, dfc1, dfc2, dproj, db1, small2, gmid, gmixed = mlp(
        kept_counts.reshape(clips), flat(normed2), flat(middle), cotangent, flat(mixed), fc1_weight, fc1_bias,
        fc2_weight, fc2_bias, mlp_gain, proj_weight, rows,
    )
    early = total_sum(jnp.concatenate([small2[:4].reshape(-1), db1.reshape(-1)])[None, :], clip_size)[0]
    sum_fc1 = gather_low(scatter_sum(dfc1, clip_size, forward_order))
    sum_fc2 = gather_low(scatter_sum(dfc2, clip_size, second_order))
    sum_proj = gather_low(scatter_sum(dproj, clip_size, forward_order))

    groups = 3
    pairs = HEADS // 2 // groups
    lanes = pairs * 2 * DH
    gmixed = gmixed.reshape(clips, rows, width)
    dqs, dkvs, sums, sharded = [], [], [], []
    for group in range(groups):
        dq, keep, send = attend_back(q, k, v, mask, mixed, lse, gmixed, group * pairs, pairs)
        got = swap_bit(send, "freq", 4, 0)
        across = swap_bit(add_low(keep[:, :, rows:], got[:, :, rows:]), "freq", 4, 1)
        parts = [a.reshape(2, total, lanes) for a in (keep[:, :, :rows], got[:, :, :rows], across)]
        dw, dkv, colsum = weight_grads(flat(normed), dq.reshape(total, lanes), parts)
        half = lanes // 2
        split = jnp.stack(
            [
                jnp.concatenate([dw[i, :, s * half : (s + 1) * half] for i in range(3)], axis=1)
                for s in range(2)
            ]
        )
        order = forward_order if group % 2 == 0 else second_order
        summed = gather_low(scatter_sum(split, clip_size, order))
        sharded.append(summed.reshape(summed.shape[0], 2, 3, half))
        dqs.append(dq)
        dkvs.append(dkv)
        sums.append(colsum)
    grad_tokens, small1 = input_grads(
        dqs, dkvs, qkv_weight, tok, gmid.reshape(clips, rows, width), vectors[2], vectors[3], slots
    )
    qkv = jnp.stack(sharded, axis=1)
    sum_qkv = qkv.transpose(0, 3, 1, 2, 4).reshape(qkv.shape[0], 3 * width)
    bias = jnp.concatenate(sums, axis=2)
    late = total_sum(
        jnp.concatenate([small1[0:1], small1[1:2], bias[0], bias[2]], axis=1), clip_size
    )[0]
    cut = lambda a, i: a[i * width : (i + 1) * width]
    return (
        layer_out, grad_tokens, cut(late, 0), cut(late, 1), sum_qkv, cut(late, 2), cut(late, 3),
        sum_proj, cut(early, 3), cut(early, 0), cut(early, 1), sum_fc1, early[4 * width :],
        sum_fc2, cut(early, 2),
    )


def on_device(
    clip_size, tokens, kept_counts, attn_gain, attn_shift, qkv_weight, query_bias, value_bias,
    proj_weight, proj_bias, mlp_gain, mlp_shift, fc1_weight, fc1_bias, fc2_weight, fc2_bias, cotangent,
):
    clips, slots, width = tokens.shape
    rows = -(-slots // 16) * 16
    if clip_size != 8 or width % (32 * clip_size):
        return on_device_plain(
            clip_size, tokens, kept_counts, attn_gain, attn_shift, qkv_weight, query_bias, value_bias,
            proj_weight, proj_bias, mlp_gain, mlp_shift, fc1_weight, fc1_bias, fc2_weight, fc2_bias, cotangent,
        )
    kept = kept_counts.reshape(clips)
    q, k, v, normed, far, weight_half, part, lse, mask, mixed, middle, normed2 = forward(
        kept, tokens, rows, qkv_weight, query_bias, value_bias, attn_gain, attn_shift,
        proj_weight, proj_bias, mlp_gain, mlp_shift,
    )
    flat = lambda a: a.reshape(clips * rows, width)
    layer_out, dfc1, dfc2, dproj, db1, small, gmid, gmixed = mlp(
        kept, flat(normed2), flat(middle), cotangent, flat(mixed), fc1_weight, fc1_bias,
        fc2_weight, fc2_bias, mlp_gain, proj_weight, rows,
    )
    by_clip = lambda a: a.reshape(clips, rows, width)
    gtok, low_fc1, low_fc2, low_proj, low_qkv, summed = backward(
        q, k, v, mask, part, lse, normed, weight_half, tokens, far, by_clip(gmid), attn_gain, small, db1,
        by_clip(gmixed), dfc1, dfc2, dproj, clip_size,
    )
    fc1, fc2, proj, qkv, grad_tokens, fc1_b, *rows_out = final_outputs(
        low_fc1, low_fc2, low_proj, low_qkv, summed, gtok, fc1_bias.shape[0]
    )
    return (
        layer_out, grad_tokens, rows_out[0], rows_out[1], qkv, rows_out[2], rows_out[3], proj, rows_out[7],
        rows_out[4], rows_out[5], fc1, fc1_b, fc2, rows_out[6],
    )


def solution(mesh):
    rows = P("clip", "freq", None)
    shard = P("clip", None)
    return jax.shard_map(
        functools.partial(on_device, mesh.shape["clip"]),
        mesh=mesh,
        in_specs=(rows, P("clip", "freq")) + (P(),) * 13 + (rows,),
        out_specs=(rows, rows, P(), P(), shard, P(), P(), shard, P(), P(), P(), shard, P(), shard, P()),
        check_vma=False,
    )
```

```python
import functools
import math

import jax
import jax.numpy as jnp
from jax import lax
from jax.experimental import pallas as pl
from jax.experimental.pallas import tpu as pltpu
from jax.sharding import PartitionSpec as P

HEADS = 12
DH = 64
EPS = 1e-06
MASKED = -1000000000.0
VMEM_BYTES = 60 * 1024 * 1024

f32 = jnp.float32
bf16 = jnp.bfloat16
NN = (((1,), (0,)), ((), ()))
NT = (((1,), (1,)), ((), ()))
TN = (((0,), (0,)), ((), ()))


def dot(left, right, dims=NN):
    return lax.dot_general(left, right, dims, preferred_element_type=f32)


def center_scale(rows):
    center = rows - jnp.mean(rows, axis=-1, keepdims=True)
    inverse = lax.rsqrt(jnp.mean(center * center, axis=-1, keepdims=True) + EPS)
    return center * inverse, inverse


def norm_back(unit, inverse, gain, grad):
    scaled = grad * gain
    return inverse * (
        scaled
        - jnp.mean(scaled, axis=-1, keepdims=True)
        - unit * jnp.mean(scaled * unit, axis=-1, keepdims=True)
    )


def column_sums(rows):
    return jnp.sum(rows, axis=0, keepdims=True)


def own_lanes(shape, head):
    lane = lax.broadcasted_iota(jnp.int32, shape, len(shape) - 1)
    return lane < DH if head == 0 else lane >= DH


def only(rows, head):
    return jnp.where(own_lanes(rows.shape, head), rows, jnp.zeros_like(rows))


def full(shape):
    return pl.BlockSpec(shape, lambda *ids: (0,) * len(shape))


def params(**more):
    return pltpu.CompilerParams(vmem_limit_bytes=VMEM_BYTES, **more)


def freq_places():
    freq = lax.axis_index("freq")
    core, vert = freq % 2, freq // 2
    return core, vert, {"freq": freq + 1 - 2 * core}, {"freq": (freq + 2) % 4}


def lane_slice(start, size):
    return pl.ds(pl.multiple_of(start, 2 * DH), size)


def row_of(ref):
    return ref[...].astype(f32).reshape(1, ref.shape[0])


def forward_kernel(
    counts,
    kept_ref, tok_ref, qkv_ref, qb_ref, vb_ref, gain_ref, shift_ref, proj_ref, pb_ref, gain2_ref, shift2_ref,
    q_out, k_out, v_out, normed_out, far_out, weight_out, part_ref, lse_ref, mask_ref, mixed_ref, middle_ref, normed2_ref,
    q_all, k_all, v_all, normed_all, weight, live_all, own, held, mix_send, mix_got, own_mix, vecs,
    tok_send, tok_recv, part_send, part_recv, out_sem, weight_sem,
):
    clips, slots, rows, pairs = counts
    clip = pl.program_id(0)
    turn = pl.program_id(1)
    slot = 1 - turn
    width = tok_ref.shape[-1]
    half = width // 2
    lanes = 2 * DH
    core, vert, core_dev, vert_dev = freq_places()
    mesh_id = pl.DeviceIdType.MESH

    def copy(kind, index):
        at = {"vert": 0, "core": 1, "diag": 2}[kind]
        return pltpu.make_async_remote_copy(
            src_ref=held.at[index, 0] if kind == "diag" else own.at[index],
            dst_ref=held.at[index, at],
            send_sem=tok_send.at[index, at],
            recv_sem=tok_recv.at[index, at],
            device_id=vert_dev if kind == "vert" else core_dev,
            device_id_type=mesh_id,
        )

    def mix_copy(index, which):
        return pltpu.make_async_remote_copy(
            src_ref=mix_send.at[index, which],
            dst_ref=mix_got.at[index, which],
            send_sem=part_send.at[index, which],
            recv_sem=part_recv.at[index, which],
            device_id=vert_dev,
            device_id_type=mesh_id,
        )

    def project(index, slot, source):
        unit, _ = center_scale(source.astype(f32))
        normed = (unit * vecs[2:3] + vecs[3:4]).astype(bf16)
        at = slice(slot * rows, (slot + 1) * rows)
        if slot < 2:
            normed_all[index, at] = normed
            query = (dot(normed, weight[:, :half]) + vecs[0:1, lane_slice(vert * half, half)]).astype(bf16)
            q_all[index, at] = query * jnp.asarray(DH ** -0.5, bf16)
        both = dot(normed, weight[:, half:])
        k_all[index, at] = both[:, :half].astype(bf16)
        v_all[index, at] = (both[:, half:] + vecs[1:2, lane_slice(vert * half, half)]).astype(bf16)
        first = (slots // 16) * 16
        kept = source[first:].astype(f32)[slots - first : slots - first + 1, 0:1] + slots // 2
        lane = lax.broadcasted_iota(jnp.int32, (1, rows), 1).astype(f32)
        live_all[index, slot] = (lane < kept).astype(f32)

    def out_copies(index):
        return [
            pltpu.make_async_copy(src.at[index], dst.at[index], out_sem.at[index, i])
            for i, (src, dst) in enumerate(
                ((q_all, q_out), (k_all, k_out), (v_all, v_out), (normed_all, normed_out))
            )
        ] + [pltpu.make_async_copy(held.at[index, 0], far_out.at[index], out_sem.at[index, 4])]

    def weight_copies():
        moves = []
        for pair in range(pairs):
            for part in range(3):
                src = weight.at[:, pl.ds(part * half + pair * lanes, lanes)]
                dst = weight_out.at[:, pl.ds((3 * pair + part) * lanes, lanes)]
                moves.append(pltpu.make_async_copy(src, dst, weight_sem.at[3 * pair + part]))
        return moves

    @pl.when((clip == 0) & (turn == 0))
    def enter():
        barrier = pltpu.get_barrier_semaphore()
        for device in (vert_dev, core_dev):
            pl.semaphore_signal(barrier, inc=1, device_id=device, device_id_type=mesh_id)
        first = (slots // 16) * 16
        for index in range(clips):
            kept = (kept_ref[index] - slots // 2).astype(f32).astype(bf16)
            own[index, first:] = jnp.broadcast_to(kept, (rows - first, width))
            own[index, :slots] = tok_ref[index]
        pl.semaphore_wait(barrier, 2)
        copy("vert", 0).start()
        for index in range(clips):
            copy("core", index).start()
        for i, ref in enumerate((qb_ref, vb_ref, gain_ref, shift_ref, pb_ref, gain2_ref, shift2_ref)):
            vecs[i : i + 1] = row_of(ref)
        for part in range(3):
            weight[:, part * half : (part + 1) * half] = qkv_ref[:, lane_slice(part * width + vert * half, half)]
        for move in weight_copies():
            move.start()

        def own_slots(index, carry):
            project(index, 0, own[index])
            return carry

        def core_slots(index, carry):
            copy("core", index).wait_recv()
            project(index, 2, held[index, 1])
            return carry

        lax.fori_loop(0, clips, own_slots, 0)
        lax.fori_loop(0, clips, core_slots, 0)
        copy("vert", 0).wait_recv()
        copy("diag", 0).start()
        copy("vert", 0).wait_send()
        if clips > 1:
            copy("vert", 1).start()

    @pl.when(turn == 0)
    def project_rest():
        project(clip, 1, held[clip, 0])
        copy("diag", clip).wait_recv()
        project(clip, 3, held[clip, 2])
        for i in range(4):
            mask_ref[0, :, i * rows : (i + 1) * rows] = live_all[clip, i]
        for move in out_copies(clip):
            move.start()

    for index in range(2, clips):
        @pl.when((turn == 1) & (clip == index - 2))
        def send_ahead(index=index):
            copy("vert", index - 1).wait_send()
            copy("vert", index).start()

    def finish(index):
        at = lane_slice(vert * half, half)
        mixed_ref[0, :, at] = own_mix[...]
        for which in range(pairs):
            mix_copy(index, which).wait_recv()
            at = lane_slice((1 - vert) * half + which * lanes, lanes)
            mixed_ref[0, :, at] = mix_got[index, which]
        middle = own[index].astype(f32) + (dot(mixed_ref[0], proj_ref[...]) + vecs[4:5])
        middle_ref[0] = middle
        unit, _ = center_scale(middle)
        normed2_ref[0] = (unit * vecs[5:6] + vecs[6:7]).astype(bf16)
        copy("core", index).wait_send()
        copy("diag", index).wait_send()
        for which in range(pairs):
            mix_copy(index, which).wait_send()

    at = pl.ds(pl.multiple_of(slot * rows, rows), rows)
    live = mask_ref[0] > 0.5
    ones = jnp.ones((4 * rows, lanes), bf16)
    for pair in range(pairs):
        here = slice(pair * lanes, (pair + 1) * lanes)
        keys = k_all[clip, :, here]
        values = jnp.concatenate([v_all[clip, :, here], ones], axis=1)
        query = q_all[clip, at, here]
        outs, lses = [], []
        for head in range(2):
            scores = jnp.where(live, dot(only(query, head), keys, NT), MASKED)
            top = jnp.max(scores, axis=1, keepdims=True)
            exps = jnp.exp(scores - top)
            both = dot(exps.astype(bf16), values)
            total = both[:, lanes:]
            outs.append(both[:, :lanes] / total)
            lses.append(top + jnp.log(total))
        first = own_lanes(outs[0].shape, 0)
        mixed = jnp.where(first, outs[0], outs[1]).astype(bf16)
        part_ref[0, at, here] = mixed
        lse_ref[0, at, here] = jnp.where(first, lses[0], lses[1])

    @pl.when(slot == 1)
    def give():
        for pair in range(pairs):
            mix_send[clip, pair] = part_ref[0, rows:, pair * lanes : (pair + 1) * lanes]
            mix_copy(clip, pair).start()

    @pl.when((turn == 0) & (clip > 0))
    def finish_before():
        finish(clip - 1)

    @pl.when(turn == 1)
    def keep_own():
        own_mix[...] = part_ref[0, :rows]

    @pl.when((turn == 1) & (clip + 1 < clips))
    def pass_on():
        copy("vert", clip + 1).wait_recv()
        copy("diag", clip + 1).start()

    @pl.when((turn == 1) & (clip == clips - 1))
    def finish_last():
        finish(clip)
        copy("vert", clips - 1).wait_send()

    @pl.when((turn == 1) & (clip == clips - 1))
    def leave():
        for move in weight_copies():
            move.wait()
        for index in range(clips):
            for move in out_copies(index):
                move.wait()


def forward(kept, tokens, rows, qkv_weight, query_bias, value_bias, gain, shift, proj_weight, proj_bias, gain2, shift2):
    clips, slots, width = tokens.shape
    keys = 4 * rows
    half = width // 2
    pairs = HEADS // 4
    lanes = 2 * DH
    one = pl.Buffered(buffer_count=1)
    block = lambda n, m: pl.BlockSpec((1, n, m), lambda c, p: (c, 0, 0))
    late = pl.BlockSpec((1, rows, width), lambda c, t: (jnp.maximum(c - 1 + t, 0), 0, 0))
    anywhere = pl.BlockSpec(memory_space=pl.ANY)
    whole = lambda a: pl.BlockSpec(a.shape, lambda c, p: (0,) * a.ndim, pipeline_mode=one)
    shape = jax.ShapeDtypeStruct
    flops = 2 * clips * (rows * width * width * 6 + 2 * rows * keys * width)
    vectors = (query_bias, value_bias, gain, shift)
    return pl.pallas_call(
        functools.partial(forward_kernel, (clips, slots, rows, pairs)),
        grid=(clips, 2),
        in_specs=[pl.BlockSpec(memory_space=pltpu.SMEM), whole(tokens), whole(qkv_weight)]
        + [whole(v) for v in vectors]
        + [whole(proj_weight)]
        + [whole(v) for v in (proj_bias, gain2, shift2)],
        out_specs=[
            anywhere, anywhere, anywhere, anywhere, anywhere, anywhere,
            block(2 * rows, half), block(2 * rows, half), block(1, keys),
            late, late, late,
        ],
        out_shape=[
            shape((clips, 2 * rows, half), bf16),
            shape((clips, keys, half), bf16),
            shape((clips, keys, half), bf16),
            shape((clips, 2 * rows, width), bf16),
            shape((clips, rows, width), bf16),
            shape((width, 3 * half), bf16),
            shape((clips, 2 * rows, half), bf16),
            shape((clips, 2 * rows, half), f32),
            shape((clips, 1, keys), f32),
            shape((clips, rows, width), bf16),
            shape((clips, rows, width), f32),
            shape((clips, rows, width), bf16),
        ],
        scratch_shapes=[
            pltpu.VMEM((clips, 2 * rows, half), bf16),
            pltpu.VMEM((clips, keys, half), bf16),
            pltpu.VMEM((clips, keys, half), bf16),
            pltpu.VMEM((clips, 2 * rows, width), bf16),
            pltpu.VMEM((width, 3 * half), bf16),
            pltpu.VMEM((clips, 4, 1, rows), f32),
            pltpu.VMEM((clips, rows, width), bf16),
            pltpu.VMEM((clips, 3, rows, width), bf16),
            pltpu.VMEM((clips, pairs, rows, lanes), bf16),
            pltpu.VMEM((clips, pairs, rows, lanes), bf16),
            pltpu.VMEM((rows, half), bf16),
            pltpu.VMEM((8, width), f32),
            pltpu.SemaphoreType.DMA((clips, 3)),
            pltpu.SemaphoreType.DMA((clips, 3)),
            pltpu.SemaphoreType.DMA((clips, pairs)),
            pltpu.SemaphoreType.DMA((clips, pairs)),
            pltpu.SemaphoreType.DMA((clips, 5)),
            pltpu.SemaphoreType.DMA((3 * pairs,)),
        ],
        compiler_params=params(collective_id=0, has_side_effects=True),
        cost_estimate=pl.CostEstimate(
            flops=flops, bytes_accessed=40_000_000, transcendentals=clips * rows * keys * HEADS
        ),
        name="forward",
    )(kept, tokens, qkv_weight, *vectors, proj_weight, proj_bias, gain2, shift2)


def mlp_kernel(
    counts,
    kept_ref, n2_ref, middle_hbm, cot_ref, mixed_hbm, fc1_ref, b1_ref, fc2_ref, b2_ref, gain_ref, proj_hbm,
    out_ref, dfc1_ref, dfc2_ref, dproj_ref, db1_ref, small_ref, gmid_hbm, gmixed_hbm,
    middle_ref, mixed_ref, proj_ref, gmixed_ref, in_sems, out_sems,
    n2t_ref, grad_ref, out_acc, dn_acc, hidden_ref, dact_ref, active_ref, dhid_ref, biases,
):
    clips, slots, rows, tile = counts
    step = pl.program_id(0)
    width = n2_ref.shape[-1]
    chunk = fc1_ref.shape[-1]
    total = clips * rows

    def live_rows(clip, size):
        slot = lax.broadcasted_iota(jnp.int32, (size, 1), 0)
        return (slot < kept_ref[clip]).astype(f32)

    def loads():
        pairs = ((middle_hbm, middle_ref), (mixed_hbm, mixed_ref), (proj_hbm, proj_ref))
        return [pltpu.make_async_copy(src, dst, in_sems.at[i]) for i, (src, dst) in enumerate(pairs)]

    def stores(clip):
        at = pl.ds(pl.multiple_of(clip * rows, rows), rows)
        pairs = ((middle_ref, gmid_hbm), (gmixed_ref, gmixed_hbm))
        return [
            pltpu.make_async_copy(src.at[at], dst.at[at], out_sems.at[clip, i]) for i, (src, dst) in enumerate(pairs)
        ]

    @pl.when(step == 0)
    def start():
        for load in loads():
            load.start()
        n2t_ref[...] = n2_ref[...].T
        first = (slots // 16) * 16
        for clip in range(clips):
            begin = clip * rows
            grad_ref[begin + first : begin + rows] = jnp.zeros((rows - first, width), bf16)
            grad_ref[begin : begin + slots] = cot_ref[clip] * live_rows(clip, slots).astype(bf16)
        all_biases = row_of(b1_ref)
        for i in range(all_biases.shape[1] // chunk):
            biases[i : i + 1] = all_biases[:, i * chunk : (i + 1) * chunk]
        out_acc[...] = jnp.zeros_like(out_acc)
        dn_acc[...] = jnp.zeros_like(dn_acc)

    bias = biases[pl.ds(step, 1), :]
    hidden_ref[...] = dot(n2_ref[...], fc1_ref[...])
    dact_ref[...] = dot(grad_ref[...], fc2_ref[...], NT)
    sums = jnp.zeros((tile, chunk), f32)
    for begin in range(0, total, tile):
        at = slice(begin, begin + tile)
        hidden = hidden_ref[at] + bias
        cdf = 0.5 * (1.0 + lax.erf(hidden * (0.5 ** 0.5)))
        active_ref[at] = (hidden * cdf).astype(bf16)
        slope = cdf + hidden * (jnp.exp(-0.5 * hidden * hidden) * (1.0 / math.sqrt(2.0 * math.pi)))
        dhid = (dact_ref[at] * slope).astype(bf16)
        dhid_ref[at] = dhid
        sums = sums + dhid.astype(f32)
    db1_ref[...] = column_sums(sums)
    active = active_ref[...]
    dhid = dhid_ref[...]
    out_acc[...] += dot(active, fc2_ref[...])
    dn_acc[...] += dot(dhid, fc1_ref[...], NT)
    dfc1_ref[0] = dot(n2t_ref[...], dhid).astype(bf16)
    dfc2 = dot(active, grad_ref[...], TN).astype(bf16)
    half = width // 2
    dfc2_ref[0] = dfc2[:, :half]
    dfc2_ref[1] = dfc2[:, half:]

    @pl.when(step == pl.num_programs(0) - 1)
    def finish():
        for load in loads():
            load.wait()
        gain = row_of(gain_ref)
        bias2 = row_of(b2_ref)
        small_ref[...] = jnp.zeros_like(small_ref)

        def finish_clip(clip, carry):
            at = pl.ds(pl.multiple_of(clip * rows, rows), rows)
            middle = middle_ref[at]
            layer = middle + (out_acc[at] + bias2)
            out_ref[clip] = (live_rows(clip, slots) * layer[:slots]).astype(bf16)
            unit, inverse = center_scale(middle)
            grad = dn_acc[at]
            out_grad = grad_ref[at].astype(f32)
            gmid = out_grad + norm_back(unit, inverse, gain, grad)
            middle_ref[at] = gmid
            low = gmid.astype(bf16)
            dhid_ref[at, :width] = low
            gmixed_ref[at] = dot(low, proj_ref[...], NT).astype(bf16)
            small_ref[0:1] += column_sums(grad * unit)
            small_ref[1:2] += column_sums(grad)
            small_ref[2:3] += column_sums(out_grad)
            small_ref[3:4] += column_sums(low.astype(f32))
            for store in stores(clip):
                store.start()
            return carry

        lax.fori_loop(0, clips, finish_clip, 0)
        dproj = dot(mixed_ref[...], dhid_ref[:, :width], TN).astype(bf16)
        dproj_ref[0] = dproj[:, :half]
        dproj_ref[1] = dproj[:, half:]
        for clip in range(clips):
            for store in stores(clip):
                store.wait()


def mlp(kept, n2, middle, cot, mixed, fc1, b1, fc2, b2, gain, proj, rows):
    clips, slots, _ = cot.shape
    total, width = n2.shape
    hidden = fc1.shape[1]
    chunk = 768
    steps = hidden // chunk
    half = steps // 2
    tile = 16
    whole = lambda a: pl.BlockSpec(a.shape, lambda j: (0,) * a.ndim, pipeline_mode=one)
    anywhere = pl.BlockSpec(memory_space=pl.ANY)
    one = pl.Buffered(buffer_count=1)
    big = pl.BlockSpec((total, width), lambda j: (0, 0), pipeline_mode=one)
    return pl.pallas_call(
        functools.partial(mlp_kernel, (clips, slots, rows, tile)),
        grid=(steps,),
        in_specs=[
            pl.BlockSpec(memory_space=pltpu.SMEM),
            big, anywhere, whole(cot), anywhere,
            pl.BlockSpec((width, chunk), lambda j: (0, j)),
            whole(b1),
            pl.BlockSpec((chunk, width), lambda j: (j, 0)),
            whole(b2), whole(gain), anywhere,
        ],
        out_specs=[
            full((clips, slots, width)),
            pl.BlockSpec((1, width, chunk), lambda j: (j // half, 0, j % half)),
            pl.BlockSpec((2, chunk, width // 2), lambda j: (0, j, 0)),
            full((2, width, width // 2)),
            pl.BlockSpec((1, chunk), lambda j: (0, j)),
            full((8, width)),
            anywhere,
            anywhere,
        ],
        out_shape=[
            jax.ShapeDtypeStruct((clips, slots, width), bf16),
            jax.ShapeDtypeStruct((2, width, hidden // 2), bf16),
            jax.ShapeDtypeStruct((2, hidden, width // 2), bf16),
            jax.ShapeDtypeStruct((2, width, width // 2), bf16),
            jax.ShapeDtypeStruct((1, hidden), f32),
            jax.ShapeDtypeStruct((8, width), f32),
            jax.ShapeDtypeStruct((total, width), f32),
            jax.ShapeDtypeStruct((total, width), bf16),
        ],
        scratch_shapes=[
            pltpu.VMEM((total, width), f32),
            pltpu.VMEM((total, width), bf16),
            pltpu.VMEM((width, width), bf16),
            pltpu.VMEM((total, width), bf16),
            pltpu.SemaphoreType.DMA((3,)),
            pltpu.SemaphoreType.DMA((clips, 2)),
            pltpu.VMEM((width, total), bf16),
            pltpu.VMEM((total, width), bf16),
            pltpu.VMEM((total, width), f32),
            pltpu.VMEM((total, width), f32),
            pltpu.VMEM((total, chunk), f32),
            pltpu.VMEM((total, chunk), f32),
            pltpu.VMEM((total, chunk), bf16),
            pltpu.VMEM((total, chunk), bf16),
            pltpu.VMEM((8, chunk), f32),
        ],
        compiler_params=params(),
        cost_estimate=pl.CostEstimate(
            flops=12 * total * width * hidden, bytes_accessed=40_000_000, transcendentals=2 * total * hidden
        ),
        name="mlp",
    )(kept, n2, middle, cot, mixed, fc1, b1, fc2, b2, gain, proj)


def sum_arrays(width, hidden, clip_size):
    rows = width // clip_size
    tall = hidden // clip_size
    first, second = (0, 1, 2), (1, 0, 2)
    chunks = [("qkv", i, rows // 2, width // 2, order) for i, order in enumerate(QKV_ORDERS)]
    return [
        ("fc1", 0, rows, hidden // 4, first),
        ("fc2", 0, tall // 2, width // 2, second),
        ("fc1", hidden // 4, rows, hidden // 4, first),
        ("fc2", tall // 2, tall // 2, width // 2, second),
        ("proj", 0, rows, width // 2, PROJ_ORDER),
    ] + chunks


PROJ_ORDER = (1, 0, 2)
QKV_ORDERS = ((0, 1, 2), (0, 1, 2), (1, 0, 2))
SUM_STEPS = {
    2: [("end", 0, 0), ("start", 0, 1)],
    3: [("end", 1, 0), ("start", 1, 1)],
    4: [("end", 2, 0), ("end", 3, 0), ("end", 4, 0)],
    6: [("start", 2, 1)],
    7: [("end", 0, 1), ("start", 0, 2)],
    8: [("end", 1, 1), ("start", 3, 1)],
    9: [("start", 1, 2)],
    10: [("end", 0, 2), ("start", 0, 3), ("end", 2, 1)],
    11: [("start", 2, 2)],
    12: [("end", 1, 2), ("start", 1, 3), ("end", 3, 1), ("start", 3, 2)],
    13: [("end", 0, 3), ("start", 0, 4), ("start", 4, 1)],
    14: [("end", 2, 2), ("start", 2, 3)],
    15: [("end", 5, 0), ("start", 5, 1), ("end", 1, 3), ("start", 1, 4), ("end", 3, 2)],
    16: [("end", 0, 4), ("start", 0, 5), ("start", 3, 3)],
    17: [("end", 5, 1), ("start", 5, 2), ("end", 6, 0), ("start", 6, 1), ("end", 0, 5), ("end", 1, 4),
        ("start", 1, 5), ("end", 2, 3), ("start", 2, 4), ("end", 4, 1)],
    18: [("end", 7, 0), ("start", 7, 1), ("start", 4, 2)],
    19: [("end", 1, 5), ("vec", 0, 0), ("end", 3, 3), ("start", 3, 4), ("end", 5, 2), ("start", 5, 3),
        ("end", 6, 1), ("start", 6, 2), ("end", 7, 1), ("start", 7, 2), ("end", 4, 2),
        ("start", 4, 3), ("vec", 1, 0), ("input", 2, 0), ("end", 5, 3), ("start", 5, 4),
        ("end", 2, 4), ("start", 2, 5), ("end", 6, 2), ("start", 6, 3), ("end", 7, 2),
        ("start", 7, 3), ("end", 3, 4), ("start", 3, 5), ("end", 2, 5), ("vec", 2, 0), ("end", 4, 3),
        ("start", 4, 4), ("end", 5, 4), ("start", 5, 5), ("end", 3, 5), ("end", 6, 3),
        ("start", 6, 4), ("end", 5, 5), ("end", 7, 3), ("start", 7, 4), ("end", 4, 4),
        ("start", 4, 5), ("vec", 3, 0), ("end", 6, 4), ("start", 6, 5), ("end", 4, 5), ("end", 7, 4),
        ("start", 7, 5), ("end", 6, 5), ("vec", 4, 0), ("end", 7, 5)],
}


def backward_kernel(
    meta,
    q_ref, k_ref, v_ref, mask_ref, part_ref, lse_ref, normed_ref, weight_ref, near_ref, far_ref,
    tok_ref, gmid_ref, gain_ref,
    small_ref, db1_ref, gmixed_ref, dfc1_ref, dfc2_ref, dproj_ref,
    gtok_ref, fc1_out, fc2_out, proj_out, qkv_out, vec_out,
    *scratch,
):
    clips, slots, rows, bits, pairs, arrays = meta
    width = weight_ref.shape[0]
    half = width // 2
    lanes = 2 * DH
    step = pl.program_id(0)
    places = step_places(clips, pairs)
    mesh_id = pl.DeviceIdType.MESH
    count = len(arrays)

    scratch = list(scratch)
    take = lambda n: [scratch.pop(0) for _ in range(n)]
    (grad_all, packed, kv_acc, kv_send, kv_got, acc, dn_send, dn_got, dw_acc, bias_acc, vec_sum, vec_got) = take(12)
    own_bufs = dict(zip(("fc1", "fc2", "proj"), take(3)))
    dw_low = scratch.pop(0)
    stage_bufs = [take(bits + 1) for _ in arrays]
    vert_bufs = take(5)
    full_bufs = take(count)
    (grad_sem, grad_out, grad_in, kv_out, kv_in, dn_out, dn_in, sum_out, sum_in, own_sem, vec_out_sem, vec_in_sem) = take(12)

    core, vert, core_dev, vert_dev = freq_places()
    place = lax.axis_index("clip")
    bit_at = [(place // 2 ** b) % 2 for b in range(bits)]
    clip_dev = [{"clip": place + (1 - 2 * bit_at[b]) * 2 ** b} for b in range(bits)]

    def remote(src, dst, send, recv, device):
        return pltpu.make_async_remote_copy(
            src_ref=src, dst_ref=dst, send_sem=send, recv_sem=recv, device_id=device, device_id_type=mesh_id
        )

    def grad_own(clip):
        src = gmixed_ref.at[clip, :, lane_slice(vert * half, half)]
        return pltpu.make_async_copy(src, grad_all.at[0, clip], grad_sem.at[clip])

    def grad_vert(clip):
        src = gmixed_ref.at[clip, :, lane_slice((1 - vert) * half, half)]
        return remote(src, grad_all.at[1, clip], grad_out.at[clip], grad_in.at[clip], vert_dev)

    def kv_copy(clip, pair):
        return remote(
            kv_send.at[pair], kv_got.at[clip, pair], kv_out.at[clip, pair], kv_in.at[clip, pair], core_dev
        )

    def dn_copy(clip):
        return remote(dn_send.at[clip], dn_got.at[clip], dn_out.at[clip], dn_in.at[clip], vert_dev)

    every = (slice(None),) * bits

    def piece(a, who):
        name, at, r, width_a, _ = arrays[a]
        if name == "fc1":
            return dfc1_ref.at[(who,) + every + (slice(None), pl.ds(at, width_a))]
        if name == "fc2":
            return dfc2_ref.at[(who,) + every + (pl.ds(at, r), slice(None))]
        if name == "proj":
            return dproj_ref.at[who]
        return dw_low.at[at, who]

    def chosen(a, stage, index_of):
        order = arrays[a][4]
        left = [b for b in range(bits)[::-1] if b not in order[: stage - 1]]
        bit = order[stage - 1]
        at = (slice(None),) * left.index(bit) + (index_of(bit),)
        return stage_bufs[a][stage - 1].at[at]

    def stage_copy(a, stage):
        sems = (sum_out.at[a, stage], sum_in.at[a, stage])
        full, packed_array = full_bufs[a], arrays[a][0] == "qkv"
        if stage == 0:
            return remote(piece(a, 1 - core), stage_bufs[a][0], *sems, core_dev)
        if stage <= bits:
            src = chosen(a, stage, lambda bit: 1 - bit_at[bit])
            return remote(src, stage_bufs[a][stage], *sems, clip_dev[arrays[a][4][stage - 1]])
        if stage == bits + 1:
            dst = full.at[core, vert] if packed_array else vert_bufs[a]
            return remote(stage_bufs[a][bits], dst, *sems, vert_dev)
        return remote(full.at[core], full.at[core], *sems, core_dev)

    def own_copy(a):
        return pltpu.make_async_copy(piece(a, core), own_bufs[arrays[a][0]], own_sem.at[a])

    def add_blocks(dst, src, lead):
        if lead == 0:
            dst[...] = dst[...] + src[...]
            return

        def add_one(i, carry):
            at = tuple((i // 2 ** (lead - 1 - j)) % 2 for j in range(lead))
            dst[at] = dst[at] + src[at]
            return carry

        lax.fori_loop(0, 2 ** lead, add_one, 0)

    def stage_end(a, stage):
        name = arrays[a][0]
        stage_copy(a, stage).wait_recv()
        if stage == 0:
            if name == "qkv":
                add_blocks(stage_bufs[a][0], dw_low.at[arrays[a][1], core], bits)
            else:
                own_copy(a).wait()
                add_blocks(stage_bufs[a][0], own_bufs[name], bits)
                if a + 2 < 4:
                    own_copy(a + 2).start()
        elif stage <= bits:
            add_blocks(stage_bufs[a][stage], chosen(a, stage, lambda bit: bit_at[bit]), bits - stage)
            if stage == bits and name == "qkv":
                full_bufs[a][core, vert] = stage_bufs[a][bits][...]
        elif stage == bits + 1 and name != "qkv":
            full_bufs[a][core] = stage_bufs[a][bits][...] + vert_bufs[a][...]

    def vec_copy(hop):
        device = ([core_dev] + clip_dev + [vert_dev])[hop]
        return remote(vec_sum.at[hop], vec_got.at[hop], vec_out_sem.at[hop], vec_in_sem.at[hop], device)

    def vec_end(hop):
        vec_copy(hop).wait_recv()
        vec_sum[hop + 1] = vec_sum[hop] + vec_got[hop]
        if hop < bits + 1:
            vec_copy(hop + 1).start()

    def perform(action):
        kind, a, stage = action
        if kind == "vec":
            vec_end(a)
        elif kind == "start":
            stage_copy(a, stage).start()
        else:
            stage_end(a, stage)

    @pl.when(step == 0)
    def enter():
        barrier = pltpu.get_barrier_semaphore()
        for clip in range(clips):
            grad_own(clip).start()
        for device in [core_dev, vert_dev] + clip_dev:
            pl.semaphore_signal(barrier, inc=1, device_id=device, device_id_type=mesh_id)
        vec_sum[0] = jnp.zeros_like(vec_sum[0])
        bias_acc[...] = jnp.zeros_like(bias_acc)
        dw_acc[...] = jnp.zeros_like(dw_acc)
        vec_sum[0, 4:8] = small_ref[0:4]
        for i in range(db1_ref.shape[1] // width):
            vec_sum[0, 8 + i : 9 + i] = db1_ref[0:1, i * width : (i + 1) * width]
        pl.semaphore_wait(barrier, 2 + bits)
        for clip in range(clips):
            grad_vert(clip).start()
        for a in range(5):
            stage_copy(a, 0).start()
        for a in (0, 1, 4):
            own_copy(a).start()

    for at in sorted(SUM_STEPS):
        if at < places["end"]:
            @pl.when(step == at)
            def run(at=at):
                for action in SUM_STEPS[at]:
                    perform(action)

    def head_back(head, query, keys, values, grad, mixed, lse, live):
        own_query, own_grad = only(query, head), only(grad, head)
        scores = jnp.where(live, dot(own_query, keys, NT), MASKED)
        probs = jnp.exp(scores - lse[:, head * DH : head * DH + 1])
        delta = jnp.sum(only(grad.astype(f32) * mixed.astype(f32), head), axis=1, keepdims=True)
        dscores = (probs * (dot(own_grad, values, NT) - delta)).astype(bf16)
        return probs.astype(bf16), dscores, dot(dscores, keys)

    def join_heads(dqs):
        first = own_lanes(dqs[0].shape, 0)
        return (jnp.where(first, dqs[0], dqs[1]) * DH ** -0.5).astype(bf16)

    def send_pair(clip, pair, dk, dv):
        for part, value in enumerate((dk, dv)):
            low = value.astype(bf16)
            packed[clip, :, lane_slice((3 * pair + part + 1) * lanes, lanes)] = low[: 2 * rows]
            kv_send[pair, part] = low[2 * rows :]
        kv_copy(clip, pair).start()

    clip_now, slot_now, pair_now = attention_unit(step, places, clips, pairs)

    def attend_single():
        clip, slot, pair = 0, slot_now, pair_now

        @pl.when((pair == 0) & (slot == 0))
        def own_grads():
            grad_own(clip).wait()

        @pl.when((pair == 0) & (slot == 1))
        def vert_grads():
            grad_vert(clip).wait_recv()

        at = pl.ds(pl.multiple_of(slot * rows, rows), rows)
        query, keys, values, live = q_ref[0, at], k_ref[0], v_ref[0], mask_ref[0] > 0.5
        grad = grad_all[slot, clip, :, lane_slice(pair * lanes, lanes)]
        dqs, dk, dv = [], 0.0, 0.0
        for head in range(2):
            probs, dscores, dq = head_back(head, query, keys, values, grad, part_ref[0, at], lse_ref[0, at], live)
            dqs.append(dq)
            dk = dk + dot(dscores, only(query, head), TN)
            dv = dv + dot(probs, only(grad, head), TN)
        packed[clip, at, lane_slice(3 * pair * lanes, lanes)] = join_heads(dqs)

        @pl.when(slot == 0)
        def keep():
            kv_acc[pair, 0] = dk
            kv_acc[pair, 1] = dv

        @pl.when(slot == 1)
        def send():
            send_pair(clip, pair, kv_acc[pair, 0] + dk, kv_acc[pair, 1] + dv)

    def attend_double():
        clip, pair = clip_now, pair_now

        @pl.when(pair == 0)
        def grads():
            grad_own(clip).wait()
            grad_vert(clip).wait_recv()

        kv_copy(clip - 1, pair).wait_send()
        keys, values, live = k_ref[0], v_ref[0], mask_ref[0] > 0.5
        here = lane_slice(pair * lanes, lanes)
        query = q_ref[0]
        grad = jnp.concatenate([grad_all[0, clip, :, here], grad_all[1, clip, :, here]], axis=0)
        dqs, dk, dv = [[], []], 0.0, 0.0
        for head in range(2):
            parts = []
            for slot in range(2):
                at = slice(slot * rows, (slot + 1) * rows)
                parts.append(
                    head_back(head, query[at], keys, values, grad[at], part_ref[0, at], lse_ref[0, at], live)
                )
                dqs[slot].append(parts[slot][2])
            probs, dscores = [jnp.concatenate([parts[0][i], parts[1][i]], axis=0) for i in range(2)]
            dk = dk + dot(dscores, only(query, head), TN)
            dv = dv + dot(probs, only(grad, head), TN)
        for slot in range(2):
            at = slice(slot * rows, (slot + 1) * rows)
            packed[clip, at, lane_slice(3 * pair * lanes, lanes)] = join_heads(dqs[slot])
        send_pair(clip, pair, dk, dv)

    is_attention = step < places["projections"][-1]
    for at in places["pauses"]:
        is_attention = is_attention & (step != at)
    pl.when(step < 2 * pairs)(attend_single)
    pl.when(is_attention & (step >= 2 * pairs))(attend_double)

    def take_pair(clip, pair):
        kv_copy(clip, pair).wait_recv()
        for part in range(2):
            at = lane_slice((3 * pair + part + 1) * lanes, lanes)
            packed[clip, :, at] = packed[clip, :, at] + kv_got[clip, pair, part]
        at = lane_slice(pair * lanes, lanes)
        for row, part in ((0, 0), (1, 2)):
            value = packed[clip, :, lane_slice((3 * pair + part) * lanes, lanes)]
            bias_acc[row : row + 1, at] += column_sums(value.astype(f32))

    def norm_sums(clip, back):
        near, _ = center_scale(near_ref[0].astype(f32))
        far, _ = center_scale(far_ref[0].astype(f32))
        vec_sum[0, 0:1] += column_sums(back[:slots] * near) + column_sums(back[rows:] * far)
        vec_sum[0, 1:2] += column_sums(back)

    def give_back(clip, back):
        acc[clip] = back[:rows]
        dn_send[clip] = back[rows:].astype(bf16)
        dn_copy(clip).start()

    def last_chunk(pair):
        at = lane_slice(3 * pair * lanes, 3 * lanes)
        more = dot(normed_ref[0], packed[clips - 1, :, at], TN)
        low = (dw_acc[:, at] + more).astype(bf16)
        r = arrays[5][2]
        for block in range(2 ** bits):
            index = tuple((block >> b) & 1 for b in range(bits)[::-1])
            for who in range(2):
                start = (2 * block + who) * r
                dw_low[(pair, who) + index] = low[start : start + r]

    early_steps = places["projections"][:-1]
    early = functools.reduce(jnp.logical_or, [step == at for at in early_steps])

    @pl.when(early)
    def projections():
        clip = sum((step > at).astype(jnp.int32) for at in early_steps)

        def take_one(pair, carry):
            take_pair(clip, pair)
            return carry

        lax.fori_loop(0, pairs, take_one, 0)
        grads = packed[clip]
        back = dot(grads, weight_ref[...], NT)
        give_back(clip, back)
        dw_acc[...] += dot(normed_ref[0], grads, TN)
        norm_sums(clip, back)

    chunk_steps = places["chunks"]

    @pl.when(functools.reduce(jnp.logical_or, [step == at for at in chunk_steps]))
    def chunk():
        pair = sum((step > at).astype(jnp.int32) for at in chunk_steps)
        take_pair(clips - 1, pair)
        last_chunk(pair)

    for pair in range(pairs - 1):
        @pl.when(step == chunk_steps[pair])
        def send_chunk(pair=pair):
            stage_copy(5 + pair, 0).start()

    @pl.when(step == places["projections"][-1])
    def last_projections():
        clip = clips - 1
        before = 3 * (pairs - 1) * lanes
        back = dot(packed[clip, :, :before], weight_ref[:, :before], NT)
        take_pair(clip, pairs - 1)
        last_chunk(pairs - 1)
        stage_copy(4 + pairs, 0).start()
        back = back + dot(packed[clip, :, before:], weight_ref[:, before:], NT)
        give_back(clip, back)
        norm_sums(clip, back)
        mine = lane_slice(vert * half, half)
        vec_sum[0, 2:3, mine] = bias_acc[0:1]
        vec_sum[0, 3:4, mine] = bias_acc[1:2]
        vec_copy(0).start()

    def inputs(clip):
        dn_copy(clip).wait_recv()
        grad = acc[clip] + dn_got[clip].astype(f32)
        unit, inverse = center_scale(tok_ref[0].astype(f32))
        result = gmid_ref[0][:slots] + norm_back(unit, inverse, row_of(gain_ref), grad[:slots])
        gtok_ref[0] = result

    @pl.when((step >= places["inputs"]) & (step < places["end"]))
    def early_inputs():
        inputs(step - places["inputs"])

    @pl.when(step == places["end"])
    def finish():
        for kind, a, stage in SUM_STEPS[places["end"]]:
            if kind == "input":
                inputs(clips - 1)
            else:
                perform((kind, a, stage))
        for a, (name, at, r, width_a, _) in enumerate(arrays):
            for who in range(2):
                full = full_bufs[a]
                if name == "fc1":
                    start = who * fc1_out.shape[1] // 2 + at
                    fc1_out[:, start : start + width_a] = full[who]
                elif name == "fc2":
                    fc2_out[at : at + r, who * width_a : (who + 1) * width_a] = full[who]
                elif name == "proj":
                    proj_out[:, who * width_a : (who + 1) * width_a] = full[who]
                else:
                    for side in range(2):
                        for part in range(3):
                            to = part * width + side * half + at * lanes
                            value = full[who, side, :, part * lanes : (part + 1) * lanes]
                            qkv_out[who * r : (who + 1) * r, to : to + lanes] = value
        vec_out[...] = vec_sum[bits + 2]
        for a in range(count):
            for stage in range(bits + 3):
                stage_copy(a, stage).wait_send()
        for clip in range(clips):
            grad_vert(clip).wait_send()
            dn_copy(clip).wait_send()
        for pair in range(pairs):
            kv_copy(clips - 1, pair).wait_send()
        for hop in range(bits + 2):
            vec_copy(hop).wait_send()


def step_places(clips, pairs):
    plan = ["attend"] * (2 * pairs)
    for clip in range(1, clips):
        for pair in range(pairs):
            plan.append("attend")
            if pair == 0:
                plan.append("project")
            elif clip == clips - 1:
                plan.append("chunk")
    projections = [i for i, kind in enumerate(plan) if kind == "project"] + [len(plan)]
    chunks = [i for i, kind in enumerate(plan) if kind == "chunk"]
    inputs = len(plan) + 1
    pauses = projections[:-1] + chunks
    return {"projections": projections, "chunks": chunks, "pauses": pauses, "inputs": inputs, "end": inputs + clips - 1}


def attention_unit(step, places, clips, pairs):
    index = step
    for at in places["pauses"]:
        index = index - (step > at).astype(jnp.int32)
    index = jnp.minimum(index, (clips + 1) * pairs - 1)
    slot = jnp.where(index < 2 * pairs, index // pairs, 0)
    clip = jnp.maximum(index // pairs - 1, 0)
    return clip, slot, index % pairs


def backward(q, k, v, mask, part, lse, normed, weight_half, tokens, far, gmid, gain, small, db1, gmixed,
             dfc1, dfc2, dproj, clip_size):
    clips, slots, width = tokens.shape
    rows = gmid.shape[1]
    half = width // 2
    keys = k.shape[1]
    pairs = HEADS // 4
    lanes = 2 * DH
    bits = clip_size.bit_length() - 1
    hidden = db1.shape[1]
    arrays = sum_arrays(width, hidden, clip_size)
    places = step_places(clips, pairs)
    one = pl.Buffered(buffer_count=1)

    def of_pair(s):
        clip, _, pair = attention_unit(s, places, clips, pairs)
        return clip, 0, pair

    def of_projection(s):
        index = s * 0
        for at in places["projections"][:-1]:
            index = index + (s > at).astype(jnp.int32)
        return index, 0, 0

    def of_clip(s):
        return jnp.clip(s - places["inputs"], 0, clips - 1), 0, 0

    fixed = lambda shape: pl.BlockSpec(shape, lambda s: (0,) * len(shape), pipeline_mode=one)
    tok_pair = pl.BlockSpec((1, 2 * rows, lanes), of_pair)
    key_pair = pl.BlockSpec((1, keys, lanes), of_pair)
    anywhere = pl.BlockSpec(memory_space=pl.ANY)
    blocks = (2,) * bits
    r_fc1, r_fc2 = width // clip_size, hidden // clip_size
    dfc1 = dfc1.reshape((2,) + blocks + (r_fc1, hidden // 2))
    dfc2 = dfc2.reshape((2,) + blocks + (r_fc2, half))
    dproj = dproj.reshape((2,) + blocks + (r_fc1, half))
    vmem = lambda *shape: pltpu.VMEM(shape, bf16)
    wide = lambda *shape: pltpu.VMEM(shape, f32)
    scratch = [
        vmem(2, clips, rows, half),
        vmem(clips, 2 * rows, 3 * half),
        wide(pairs, 2, keys, lanes),
        vmem(pairs, 2, 2 * rows, lanes),
        vmem(clips, pairs, 2, 2 * rows, lanes),
        wide(clips, rows, width),
        vmem(clips, rows, width),
        vmem(clips, rows, width),
        wide(width, 3 * half),
        wide(8, half),
        wide(bits + 3, 16, width),
        wide(bits + 2, 16, width),
        vmem(*blocks, r_fc1, hidden // 4),
        vmem(*blocks, r_fc2 // 2, half),
        vmem(*blocks, r_fc1, half),
    ]
    scratch.append(vmem(pairs, 2, *blocks, r_fc1 // 2, half))
    for _, _, r, w, _ in arrays:
        scratch += [vmem(*((2,) * (bits - stage)), r, w) for stage in range(bits + 1)]
    scratch += [vmem(r, w) for name, _, r, w, _ in arrays if name != "qkv"]
    scratch += [vmem(2, 2, r, w) if name == "qkv" else vmem(2, r, w) for name, _, r, w, _ in arrays]
    dma = lambda *shape: pltpu.SemaphoreType.DMA(shape)
    count = len(arrays)
    scratch += [
        dma(clips), dma(clips), dma(clips), dma(clips, pairs), dma(clips, pairs), dma(clips), dma(clips),
        dma(count, bits + 3), dma(count, bits + 3), dma(count), dma(bits + 2), dma(bits + 2),
    ]
    shape = jax.ShapeDtypeStruct
    return pl.pallas_call(
        functools.partial(backward_kernel, (clips, slots, rows, bits, pairs, arrays)),
        grid=(places["end"] + 1,),
        in_specs=[
            tok_pair, key_pair, key_pair,
            pl.BlockSpec((1, 1, keys), lambda s: (of_pair(s)[0], 0, 0)),
            tok_pair, tok_pair,
            pl.BlockSpec((1, 2 * rows, width), of_projection),
            fixed(weight_half.shape),
            pl.BlockSpec((1, slots, width), of_projection, pipeline_mode=one),
            pl.BlockSpec((1, rows, width), of_projection, pipeline_mode=one),
            pl.BlockSpec((1, slots, width), of_clip),
            pl.BlockSpec((1, rows, width), of_clip),
            fixed((width,)), fixed((8, width)), fixed((1, hidden)),
            anywhere, anywhere, anywhere, anywhere,
        ],
        out_specs=[
            pl.BlockSpec((1, slots, width), of_clip),
            fixed((r_fc1, hidden)), fixed((r_fc2, width)), fixed((r_fc1, width)),
            fixed((r_fc1, 3 * width)), fixed((16, width)),
        ],
        out_shape=[
            shape((clips, slots, width), f32),
            shape((r_fc1, hidden), bf16),
            shape((r_fc2, width), bf16),
            shape((r_fc1, width), bf16),
            shape((r_fc1, 3 * width), bf16),
            shape((16, width), f32),
        ],
        scratch_shapes=scratch,
        compiler_params=pltpu.CompilerParams(
            vmem_limit_bytes=63 * 1024 * 1024, collective_id=1, has_side_effects=True
        ),
        cost_estimate=pl.CostEstimate(
            flops=2 * clips * rows * (5 * keys * width + 6 * width * width),
            bytes_accessed=60_000_000,
            transcendentals=clips * rows * keys * HEADS,
        ),
        name="backward",
    )(q, k, v, mask, part, lse, normed, weight_half, tokens, far, tokens, gmid, gain, small, db1, gmixed, dfc1, dfc2, dproj)


def outputs_kernel(fc1, fc2, proj, qkv, vec, gtok, fc1_out, fc2_out, proj_out, qkv_out, gtok_out, db1_out, *outs):
    gtok_out[...] = gtok[...]
    for src, dst in ((fc1, fc1_out), (fc2, fc2_out), (proj, proj_out), (qkv, qkv_out)):
        dst[...] = src[...].astype(f32)

    @pl.when(pl.program_id(0) == 0)
    def others():
        width = vec.shape[1]
        for i, dst in enumerate(outs):
            dst[...] = vec[i : i + 1].reshape(width)
        tall = db1_out.shape[0] // width
        db1_out[...] = jnp.concatenate([vec[8 + i : 9 + i] for i in range(tall)], axis=1).reshape(db1_out.shape[0])


def final_outputs(low_fc1, low_fc2, low_proj, low_qkv, summed, gtok, hidden):
    width = summed.shape[1]
    steps = gtok.shape[0]
    one = pl.Buffered(buffer_count=1)
    fixed = lambda shape: pl.BlockSpec(shape, lambda c: (0,) * len(shape), pipeline_mode=one)
    by_clip = pl.BlockSpec((1,) + gtok.shape[1:], lambda c: (c, 0, 0))
    shape = jax.ShapeDtypeStruct
    lows = (low_fc1, low_fc2, low_proj, low_qkv)

    def by_rows(a):
        if a.shape[0] % (16 * steps):
            return fixed(a.shape)
        return pl.BlockSpec((a.shape[0] // steps, a.shape[1]), lambda c: (c, 0))

    return pl.pallas_call(
        outputs_kernel,
        grid=(steps,),
        in_specs=[by_rows(a) for a in lows] + [fixed(summed.shape), by_clip],
        out_specs=[by_rows(a) for a in lows] + [by_clip, fixed((hidden,))] + [fixed((width,))] * 8,
        out_shape=[shape(a.shape, f32) for a in lows]
        + [shape(gtok.shape, f32), shape((hidden,), f32)]
        + [shape((width,), f32)] * 8,
        compiler_params=params(),
        name="final_outputs",
    )(*lows, summed, gtok)


def partner(kind):
    index = lax.axis_index("freq")
    if kind == "vert":
        return {"freq": (index + 2) % 4}
    return {"freq": index + 1 - 2 * (index % 2)}


def whole_forward_kernel(
    counts,
    tok_ref, qkv_ref, qb_ref, vb_ref, gain_ref, shift_ref, proj_ref, pb_ref, gain2_ref, shift2_ref,
    q_ref, k_ref, v_ref, normed_ref, mixed_ref, lse_ref, middle_ref, normed2_ref, mask_ref,
    held, send_sem, recv_sem,
):
    clips, slots, rows = counts
    clip = pl.program_id(0)
    pair = pl.program_id(1)
    width = tok_ref.shape[-1]

    def copy(kind, index):
        at = {"vert": 0, "core": 1, "diag": 2}[kind]
        return pltpu.make_async_remote_copy(
            src_ref=held.at[index, 0] if kind == "diag" else tok_ref.at[index],
            dst_ref=held.at[index, at],
            send_sem=send_sem.at[index, at],
            recv_sem=recv_sem.at[index, at],
            device_id=partner(kind),
            device_id_type=pl.DeviceIdType.MESH,
        )

    def project(slot, source):
        unit, _ = center_scale(source.astype(f32))
        normed = (unit * gain_ref[...] + shift_ref[...]).astype(bf16)
        if slot == 0:
            normed_ref[0] = normed
            query = (dot(normed, qkv_ref[:, :width]) + qb_ref[...]).astype(bf16)
            q_ref[0] = query * jnp.asarray(DH ** -0.5, bf16)
        both = dot(normed, qkv_ref[:, width:])
        k_ref[0, slot * rows : (slot + 1) * rows] = both[:, :width].astype(bf16)
        v_ref[0, slot * rows : (slot + 1) * rows] = (both[:, width:] + vb_ref[...]).astype(bf16)
        first = (slots // 16) * 16
        kept = source[first:].astype(f32)[slots - first : slots - first + 1, 0:1] + slots // 2
        lane = lax.broadcasted_iota(jnp.int32, (1, rows), 1).astype(f32)
        return (lane < kept).astype(f32)

    @pl.when((clip == 0) & (pair == 0))
    def enter():
        barrier = pltpu.get_barrier_semaphore()
        for kind in ("vert", "core"):
            pl.semaphore_signal(
                barrier, inc=1, device_id=partner(kind), device_id_type=pl.DeviceIdType.MESH
            )
        pl.semaphore_wait(barrier, 2)
        copy("vert", 0).start()
        for index in range(clips):
            copy("core", index).start()

    def pass_on(index):
        copy("vert", index).wait_recv()
        copy("diag", index).start()
        copy("vert", index).wait_send()

        @pl.when(index + 1 < clips)
        def more():
            copy("vert", index + 1).start()

    @pl.when(pair == 0)
    def project_all():
        live_own = project(0, tok_ref[clip])
        copy("core", clip).wait_recv()
        live_core = project(2, held[clip, 1])

        @pl.when(clip == 0)
        def first_pass():
            pass_on(clip)

        live_vert = project(1, held[clip, 0])
        copy("diag", clip).wait_recv()
        live_diag = project(3, held[clip, 2])
        mask_ref[0] = jnp.concatenate([live_own, live_vert, live_core, live_diag], axis=1)

    @pl.when((pair == 3) & (clip + 1 < clips))
    def next_pass():
        pass_on(clip + 1)

    lanes = pl.ds(pl.multiple_of(pair * 2 * DH, 2 * DH), 2 * DH)
    query = q_ref[0, :, lanes]
    keys = k_ref[0, :, lanes]
    values = v_ref[0, :, lanes]
    live = mask_ref[0] > 0.5
    outs, lses = [], []
    for head in range(2):
        scores = jnp.where(live, dot(only(query, head), keys, NT), MASKED)
        top = jnp.max(scores, axis=1, keepdims=True)
        exps = jnp.exp(scores - top)
        total = jnp.sum(exps, axis=1, keepdims=True)
        outs.append(dot(exps.astype(bf16), values) / total)
        lses.append(top + jnp.log(total))
    first = own_lanes(outs[0].shape, 0)
    mixed_ref[0, :, lanes] = jnp.where(first, outs[0], outs[1]).astype(bf16)
    lse_ref[0, :, lanes] = jnp.where(first, lses[0], lses[1])

    @pl.when(pair == pl.num_programs(1) - 1)
    def finish():
        middle = tok_ref[clip].astype(f32) + (dot(mixed_ref[0], proj_ref[...]) + pb_ref[...])
        middle_ref[0] = middle
        unit, _ = center_scale(middle)
        normed2_ref[0] = (unit * gain2_ref[...] + shift2_ref[...]).astype(bf16)
        copy("core", clip).wait_send()
        copy("diag", clip).wait_send()


def whole_forward(tok, slots, qkv_weight, vectors, proj_weight):
    clips, rows, width = tok.shape
    keys = 4 * rows
    pairs = HEADS // 2
    query_bias, value_bias, gain, shift, proj_bias, gain2, shift2 = vectors
    one = pl.Buffered(buffer_count=1)
    row = full((1, width))
    block = lambda n: pl.BlockSpec((1, n, width), lambda c, p: (c, 0, 0))
    flops = 2 * clips * (10 * rows * width * width + 2 * rows * keys * width)
    weight = lambda w: pl.BlockSpec(w.shape, lambda c, p: (0, 0), pipeline_mode=one)
    return pl.pallas_call(
        functools.partial(whole_forward_kernel, (clips, slots, rows)),
        grid=(clips, pairs),
        in_specs=[
            pl.BlockSpec(tok.shape, lambda c, p: (0, 0, 0), pipeline_mode=one),
            weight(qkv_weight), row, row, row, row, weight(proj_weight), row, row, row,
        ],
        out_specs=[block(rows), block(keys), block(keys)] + [block(rows)] * 5
        + [pl.BlockSpec((1, 1, keys), lambda c, p: (c, 0, 0))],
        out_shape=[
            jax.ShapeDtypeStruct((clips, rows, width), bf16),
            jax.ShapeDtypeStruct((clips, keys, width), bf16),
            jax.ShapeDtypeStruct((clips, keys, width), bf16),
            jax.ShapeDtypeStruct((clips, rows, width), bf16),
            jax.ShapeDtypeStruct((clips, rows, width), bf16),
            jax.ShapeDtypeStruct((clips, rows, width), f32),
            jax.ShapeDtypeStruct((clips, rows, width), f32),
            jax.ShapeDtypeStruct((clips, rows, width), bf16),
            jax.ShapeDtypeStruct((clips, 1, keys), f32),
        ],
        scratch_shapes=[
            pltpu.VMEM((clips, 3, rows, width), bf16),
            pltpu.SemaphoreType.DMA((clips, 3)),
            pltpu.SemaphoreType.DMA((clips, 3)),
        ],
        compiler_params=params(collective_id=0, has_side_effects=True),
        cost_estimate=pl.CostEstimate(
            flops=flops, bytes_accessed=40_000_000, transcendentals=clips * rows * keys * HEADS
        ),
        name="whole_forward",
    )(tok, qkv_weight, query_bias, value_bias, gain, shift, proj_weight, proj_bias, gain2, shift2)


def attend_back_kernel(q_ref, k_ref, v_ref, mask_ref, mixed_ref, lse_ref, grad_ref,
                       dq_ref, dkeep_ref, dsend_ref):
    query = q_ref[0]
    keys = k_ref[0]
    values = v_ref[0]
    grad = grad_ref[0]
    live = mask_ref[0] > 0.5
    product = grad.astype(f32) * mixed_ref[0].astype(f32)
    dqs, dk, dv = [], None, None
    for head in range(2):
        own_query = only(query, head)
        own_grad = only(grad, head)
        scores = jnp.where(live, dot(own_query, keys, NT), MASKED)
        probs = jnp.exp(scores - lse_ref[0, :, head * DH : head * DH + 1])
        delta = jnp.sum(only(product, head), axis=1, keepdims=True)
        dscores = (probs * (dot(own_grad, values, NT) - delta)).astype(bf16)
        dqs.append(dot(dscores, keys))
        more_k = dot(dscores, own_query, TN)
        more_v = dot(probs.astype(bf16), own_grad, TN)
        dk = more_k if dk is None else dk + more_k
        dv = more_v if dv is None else dv + more_v
    first = own_lanes(dqs[0].shape, 0)
    dq_ref[0] = (jnp.where(first, dqs[0], dqs[1]) * DH ** -0.5).astype(bf16)
    half = dk.shape[0] // 2
    dkeep_ref[0, 0] = dk[:half].astype(bf16)
    dkeep_ref[1, 0] = dv[:half].astype(bf16)
    dsend_ref[0, 0] = dk[half:].astype(bf16)
    dsend_ref[1, 0] = dv[half:].astype(bf16)


def attend_back(q, k, v, mask, mixed, lse, grad, first_pair, pairs):
    clips, rows, _ = q.shape
    keys = k.shape[1]
    lanes = 2 * DH
    tok = pl.BlockSpec((1, rows, lanes), lambda c, p: (c, 0, first_pair + p))
    key = pl.BlockSpec((1, keys, lanes), lambda c, p: (c, 0, first_pair + p))
    part = pl.BlockSpec((2, 1, keys // 2, lanes), lambda c, p: (0, c, 0, p))
    return pl.pallas_call(
        attend_back_kernel,
        grid=(clips, pairs),
        in_specs=[tok, key, key, pl.BlockSpec((1, 1, keys), lambda c, p: (c, 0, 0)), tok, tok, tok],
        out_specs=[pl.BlockSpec((1, rows, lanes), lambda c, p: (c, 0, p)), part, part],
        out_shape=[
            jax.ShapeDtypeStruct((clips, rows, pairs * lanes), bf16),
            jax.ShapeDtypeStruct((2, clips, keys // 2, pairs * lanes), bf16),
            jax.ShapeDtypeStruct((2, clips, keys // 2, pairs * lanes), bf16),
        ],
        compiler_params=params(),
        cost_estimate=pl.CostEstimate(
            flops=4 * 10 * clips * rows * keys * pairs * lanes,
            bytes_accessed=clips * pairs * lanes * (keys * 10 + rows * 12),
            transcendentals=clips * rows * keys * 2 * pairs,
        ),
        name="attend_back",
    )(q, k, v, mask, mixed, lse, grad)


def weight_kernel(normed_ref, dq_ref, dk0_ref, dk1_ref, dk2_ref, out_ref, dkv_ref, sums_ref):
    part = pl.program_id(0)
    @pl.when(part == 0)
    def query():
        grad = dq_ref[...]
        out_ref[0] = dot(normed_ref[...], grad, TN).astype(bf16)
        sums_ref[0] = column_sums(grad.astype(f32))
        dkv_ref[0] = jnp.zeros_like(dkv_ref[0])

    @pl.when(part > 0)
    def other():
        grad = (dk0_ref[0].astype(f32) + dk1_ref[0].astype(f32) + dk2_ref[0].astype(f32)).astype(bf16)
        dkv_ref[0] = grad
        out_ref[0] = dot(normed_ref[...], grad, TN).astype(bf16)
        sums_ref[0] = column_sums(grad.astype(f32))


def weight_grads(normed, dq, parts):
    total, width = normed.shape
    lanes = dq.shape[1]
    before = lambda j: (jnp.maximum(j - 1, 0), 0, 0)
    part = pl.BlockSpec((1, total, lanes), before)
    return pl.pallas_call(
        weight_kernel,
        grid=(3,),
        in_specs=[full((total, width)), full((total, lanes)), part, part, part],
        out_specs=[
            pl.BlockSpec((1, width, lanes), lambda j: (j, 0, 0)),
            part,
            pl.BlockSpec((1, 1, lanes), lambda j: (j, 0, 0)),
        ],
        out_shape=[
            jax.ShapeDtypeStruct((3, width, lanes), bf16),
            jax.ShapeDtypeStruct((2, total, lanes), bf16),
            jax.ShapeDtypeStruct((3, 1, lanes), f32),
        ],
        compiler_params=params(),
        cost_estimate=pl.CostEstimate(
            flops=6 * total * width * lanes, bytes_accessed=8_000_000, transcendentals=0
        ),
        name="weight_grads",
    )(normed, dq, *parts)


def input_kernel(counts, groups, *refs):
    clips, slots, rows = counts
    dqs = refs[:groups]
    dkvs = refs[groups : 2 * groups]
    qkv_ref, tok_ref, gmid_ref, gain_ref, shift_ref, out_ref, small_ref = refs[2 * groups :]
    clip = pl.program_id(0)
    width = tok_ref.shape[-1]
    lanes = width // groups
    grad = None
    for group in range(groups):
        for part in range(3):
            rows_grad = dqs[group][0] if part == 0 else dkvs[group][part - 1]
            at = part * width + group * lanes
            more = dot(rows_grad, qkv_ref[:, at : at + lanes], NT)
            grad = more if grad is None else grad + more
    unit, inverse = center_scale(tok_ref[0].astype(f32))
    result = gmid_ref[0] + norm_back(unit, inverse, gain_ref[...], grad)
    out_ref[0] = result[:slots]

    @pl.when(clip == 0)
    def start():
        small_ref[...] = jnp.zeros_like(small_ref)

    small_ref[0:1] += column_sums(grad * unit)
    small_ref[1:2] += column_sums(grad)


def input_grads(dqs, dkvs, qkv_weight, tokens, gmid, gain, shift, slots):
    clips, rows, width = tokens.shape
    groups = len(dqs)
    lanes = width // groups
    tok = pl.BlockSpec((1, rows, width), lambda c: (c, 0, 0))
    return pl.pallas_call(
        functools.partial(input_kernel, (clips, slots, rows), groups),
        grid=(clips,),
        in_specs=[pl.BlockSpec((1, rows, lanes), lambda c: (c, 0, 0))] * groups
        + [pl.BlockSpec((2, rows, lanes), lambda c: (0, c, 0))] * groups
        + [full(qkv_weight.shape), tok, tok, full((1, width)), full((1, width))],
        out_specs=[pl.BlockSpec((1, slots, width), lambda c: (c, 0, 0)), full((8, width))],
        out_shape=[
            jax.ShapeDtypeStruct((clips, slots, width), f32),
            jax.ShapeDtypeStruct((8, width), f32),
        ],
        compiler_params=params(),
        cost_estimate=pl.CostEstimate(
            flops=6 * clips * rows * width * width, bytes_accessed=16_000_000, transcendentals=0
        ),
        name="input_grads",
    )(*dqs, *dkvs, qkv_weight, tokens, gmid, gain, shift)


def swap_bit(array, axis, size, bit):
    return lax.ppermute(array, axis, [(i, i ^ (1 << bit)) for i in range(size)])


def add_low(left, right):
    return (left.astype(f32) + right.astype(f32)).astype(bf16)


def pick(array, index, dim):
    return lax.dynamic_index_in_dim(array, index, dim, keepdims=False)


def bit_of(axis, bit):
    return (lax.axis_index(axis) >> bit) & 1


def scatter_sum(split, clip_size, order):
    core = bit_of("freq", 0)
    vert = bit_of("freq", 1)
    bits = clip_size.bit_length() - 1
    lanes = split.shape[-1]
    value = add_low(pick(split, core, 0), swap_bit(pick(split, 1 - core, 0), "freq", 4, 0))
    rows = value.shape[0] // (2 * clip_size)
    value = value.reshape((2,) * bits + (2, rows, lanes))
    left = list(range(bits))[::-1]
    for bit in order:
        at = left.index(bit)
        mine = bit_of("clip", bit)
        value = add_low(
            pick(value, mine, at), swap_bit(pick(value, 1 - mine, at), "clip", clip_size, bit)
        )
        left.remove(bit)
    return add_low(pick(value, vert, 0), swap_bit(pick(value, 1 - vert, 0), "freq", 4, 1))


def gather_low(part):
    core = bit_of("freq", 0)
    vert = bit_of("freq", 1)
    other = swap_bit(part, "freq", 4, 1)
    tall = jnp.where(vert == 0, jnp.concatenate([part, other]), jnp.concatenate([other, part]))
    side = swap_bit(tall, "freq", 4, 0)
    return jnp.where(
        core == 0,
        jnp.concatenate([tall, side], axis=1),
        jnp.concatenate([side, tall], axis=1),
    ).astype(f32)


def total_sum(array, clip_size):
    for bit in range(2):
        array = array + swap_bit(array, "freq", 4, bit)
    for bit in range(clip_size.bit_length() - 1):
        array = array + swap_bit(array, "clip", clip_size, bit)
    return array


def on_device_plain(
    clip_size, tokens, kept_counts, attn_gain, attn_shift, qkv_weight, query_bias, value_bias,
    proj_weight, proj_bias, mlp_gain, mlp_shift, fc1_weight, fc1_bias, fc2_weight, fc2_bias, cotangent,
):
    clips, slots, width = tokens.shape
    rows = -(-slots // 16) * 16
    total = clips * rows
    bits = clip_size.bit_length() - 1
    forward_order = list(range(bits))
    second_order = forward_order[1:2] + forward_order[:1] + forward_order[2:]
    vec = lambda v: v.astype(f32)[None, :]
    kept = (kept_counts - slots // 2).astype(bf16)
    tok = jnp.concatenate(
        [tokens, jnp.broadcast_to(kept[:, :, None], (clips, rows - slots, width))], axis=1
    )
    vectors = [vec(v) for v in (query_bias, value_bias, attn_gain, attn_shift, proj_bias, mlp_gain, mlp_shift)]
    q, k, v, normed, mixed, lse, middle, normed2, mask = whole_forward(
        tok, slots, qkv_weight, vectors, proj_weight
    )
    flat = lambda a: a.reshape(total, width)
    layer_out, dfc1, dfc2, dproj, db1, small2, gmid, gmixed = mlp(
        kept_counts.reshape(clips), flat(normed2), flat(middle), cotangent, flat(mixed), fc1_weight, fc1_bias,
        fc2_weight, fc2_bias, mlp_gain, proj_weight, rows,
    )
    early = total_sum(jnp.concatenate([small2[:4].reshape(-1), db1.reshape(-1)])[None, :], clip_size)[0]
    sum_fc1 = gather_low(scatter_sum(dfc1, clip_size, forward_order))
    sum_fc2 = gather_low(scatter_sum(dfc2, clip_size, second_order))
    sum_proj = gather_low(scatter_sum(dproj, clip_size, forward_order))

    groups = 3
    pairs = HEADS // 2 // groups
    lanes = pairs * 2 * DH
    gmixed = gmixed.reshape(clips, rows, width)
    dqs, dkvs, sums, sharded = [], [], [], []
    for group in range(groups):
        dq, keep, send = attend_back(q, k, v, mask, mixed, lse, gmixed, group * pairs, pairs)
        got = swap_bit(send, "freq", 4, 0)
        across = swap_bit(add_low(keep[:, :, rows:], got[:, :, rows:]), "freq", 4, 1)
        parts = [a.reshape(2, total, lanes) for a in (keep[:, :, :rows], got[:, :, :rows], across)]
        dw, dkv, colsum = weight_grads(flat(normed), dq.reshape(total, lanes), parts)
        half = lanes // 2
        split = jnp.stack(
            [
                jnp.concatenate([dw[i, :, s * half : (s + 1) * half] for i in range(3)], axis=1)
                for s in range(2)
            ]
        )
        order = forward_order if group % 2 == 0 else second_order
        summed = gather_low(scatter_sum(split, clip_size, order))
        sharded.append(summed.reshape(summed.shape[0], 2, 3, half))
        dqs.append(dq)
        dkvs.append(dkv)
        sums.append(colsum)
    grad_tokens, small1 = input_grads(
        dqs, dkvs, qkv_weight, tok, gmid.reshape(clips, rows, width), vectors[2], vectors[3], slots
    )
    qkv = jnp.stack(sharded, axis=1)
    sum_qkv = qkv.transpose(0, 3, 1, 2, 4).reshape(qkv.shape[0], 3 * width)
    bias = jnp.concatenate(sums, axis=2)
    late = total_sum(
        jnp.concatenate([small1[0:1], small1[1:2], bias[0], bias[2]], axis=1), clip_size
    )[0]
    cut = lambda a, i: a[i * width : (i + 1) * width]
    return (
        layer_out, grad_tokens, cut(late, 0), cut(late, 1), sum_qkv, cut(late, 2), cut(late, 3),
        sum_proj, cut(early, 3), cut(early, 0), cut(early, 1), sum_fc1, early[4 * width :],
        sum_fc2, cut(early, 2),
    )


def on_device(
    clip_size, tokens, kept_counts, attn_gain, attn_shift, qkv_weight, query_bias, value_bias,
    proj_weight, proj_bias, mlp_gain, mlp_shift, fc1_weight, fc1_bias, fc2_weight, fc2_bias, cotangent,
):
    clips, slots, width = tokens.shape
    rows = -(-slots // 16) * 16
    if clip_size != 8 or width % (32 * clip_size):
        return on_device_plain(
            clip_size, tokens, kept_counts, attn_gain, attn_shift, qkv_weight, query_bias, value_bias,
            proj_weight, proj_bias, mlp_gain, mlp_shift, fc1_weight, fc1_bias, fc2_weight, fc2_bias, cotangent,
        )
    kept = kept_counts.reshape(clips)
    q, k, v, normed, far, weight_half, part, lse, mask, mixed, middle, normed2 = forward(
        kept, tokens, rows, qkv_weight, query_bias, value_bias, attn_gain, attn_shift,
        proj_weight, proj_bias, mlp_gain, mlp_shift,
    )
    flat = lambda a: a.reshape(clips * rows, width)
    layer_out, dfc1, dfc2, dproj, db1, small, gmid, gmixed = mlp(
        kept, flat(normed2), flat(middle), cotangent, flat(mixed), fc1_weight, fc1_bias,
        fc2_weight, fc2_bias, mlp_gain, proj_weight, rows,
    )
    by_clip = lambda a: a.reshape(clips, rows, width)
    gtok, low_fc1, low_fc2, low_proj, low_qkv, summed = backward(
        q, k, v, mask, part, lse, normed, weight_half, tokens, far, by_clip(gmid), attn_gain, small, db1,
        by_clip(gmixed), dfc1, dfc2, dproj, clip_size,
    )
    fc1, fc2, proj, qkv, grad_tokens, fc1_b, *rows_out = final_outputs(
        low_fc1, low_fc2, low_proj, low_qkv, summed, gtok, fc1_bias.shape[0]
    )
    return (
        layer_out, grad_tokens, rows_out[0], rows_out[1], qkv, rows_out[2], rows_out[3], proj, rows_out[7],
        rows_out[4], rows_out[5], fc1, fc1_b, fc2, rows_out[6],
    )


def solution(mesh):
    rows = P("clip", "freq", None)
    shard = P("clip", None)
    return jax.shard_map(
        functools.partial(on_device, mesh.shape["clip"]),
        mesh=mesh,
        in_specs=(rows, P("clip", "freq")) + (P(),) * 13 + (rows,),
        out_specs=(rows, rows, P(), P(), shard, P(), P(), shard, P(), P(), P(), shard, P(), shard, P()),
        check_vma=False,
    )
```
